32 devices in a mesh: fsdp: 8 (over z, x), rep: 4 (over y, core).
Axes of the slice: x: 2, y: 2, z: 4, core: 2. Of those that a mesh axis runs over, the one named last changes fastest.
Arguments:
- tokens: bfloat16 [4096, 1024], P(('fsdp', 'rep')), may hold values from -6 to 6
- seq_lengths: int32 [32, 8], P(('fsdp', 'rep')), may hold values from 0 to 64, as said below
- cotangent: bfloat16 [4096, 1024], P(('fsdp', 'rep')), may hold values from -6 to 6
- attention_norm_gain: bfloat16 [1024], P(('fsdp', 'rep')), may hold values from 0.5 to 1.5
- w_qkv: bfloat16 [1024, 3072], P(('fsdp', 'rep')), may hold values from -0.1875 to 0.1875
- w_attn_out: bfloat16 [1024, 1024], P(('fsdp', 'rep')), may hold values from -0.75 to 0.75
- feedforward_norm_gain: bfloat16 [1024], P(('fsdp', 'rep')), may hold values from 0.5 to 1.5
- w_in: bfloat16 [1024, 5248], P(('fsdp', 'rep')), may hold values from -0.1875 to 0.1875
- w_out: bfloat16 [1024, 2624], P(('fsdp', 'rep')), may hold values from -0.125 to 0.125
Outputs:
- output: bfloat16 [4096, 1024], P(('fsdp', 'rep'))
- block_input_gradient: float32 [4096, 1024], P(('fsdp', 'rep'))
- attention_gain_gradient: float32 [1024], P(('fsdp', 'rep'))
- grad_w_qkv: float32 [1024, 3072], P(('fsdp', 'rep'))
- grad_w_attn_out: float32 [1024, 1024], P(('fsdp', 'rep'))
- feedforward_gain_gradient: float32 [1024], P(('fsdp', 'rep'))
- grad_w_in: float32 [1024, 5248], P(('fsdp', 'rep'))
- grad_w_out: float32 [1024, 2624], P(('fsdp', 'rep'))
The draws below stay inside these ranges and needn't reach their ends.
Inputs may be any that keep to these rules, and one draw needn't show every extreme that they name: `seq_lengths`: A row's nonzero lengths come first; a row's lengths sum to at most 128, and to exactly 128 on some device; some sequence has length 64.
All inputs are finite; a program needn't handle non-finite values.
Results may differ from the reference program's by a relative error of at most 0.013.
Values may be sent and summed in bfloat16 or wider, within the bound.
No kernel may reach another device: no remote copies, remote signals or barrier semaphores. Data moves between devices by JAX's collectives and lax.ppermute only.
A program may use at most 256 MiB of HBM per device.

```python
import math
import jax
import jax.numpy as jnp
from jax import lax

D = 1024
HEAD_DIM = 64
FF = 2624
TOK_DEV = 128
SEQS_DEV = 8
SEQ_MAX = 64
TOKENS = 4096
N_FSDP = 8
N_REP = 4


def draw_seq_lengths(key, part):
    device_count = N_FSDP * N_REP
    key_used = jax.random.fold_in(key, 101)
    key_raw = jax.random.fold_in(key, 202)
    key_pick = jax.random.fold_in(key, 303)
    used = jax.random.randint(key_used, (device_count,), TOK_DEV // 2, TOK_DEV + 1).astype(jnp.int32)
    raw_lengths = jax.random.randint(key_raw, (device_count, SEQS_DEV), 1, SEQ_MAX + 1).astype(jnp.int32)
    chosen = jax.random.randint(key_pick, (), 0, device_count).astype(jnp.int32)
    row_ids = lax.iota(jnp.int32, device_count)
    slot_ids = lax.iota(jnp.int32, SEQS_DEV)
    is_full = row_ids == chosen
    used = jnp.where(is_full, TOK_DEV, used)
    raw_lengths = jnp.where(is_full[:, None] & (slot_ids[None, :] < 2), SEQ_MAX, raw_lengths)
    ends = jnp.minimum(jnp.cumsum(raw_lengths, axis=1), used[:, None]).astype(jnp.int32)
    starts = jnp.concatenate([jnp.zeros((device_count, 1), jnp.int32), ends[:, :-1]], axis=1)
    return (ends - starts).astype(jnp.int32)


def block_scale(rng, extent, shards, low, high):
    level, own = 1.0, jax.random.fold_in(rng, 6)
    for axis_at, shards_of in shards:
        draws = jnp.exp(jax.random.uniform(jax.random.fold_in(own, axis_at), (shards_of,), jnp.float32, low / len(shards), high / len(shards)))
        level = level * jnp.repeat(draws, extent[axis_at] // shards_of).reshape([-1 if axis == axis_at else 1 for axis in range(len(extent))])
    return level


def noise(rng, shape, spread, reach, split=(), held_as=jnp.bfloat16):
    array = spread * jax.random.normal(rng, shape, jnp.float32)
    if split:
        array = array * block_scale(rng, shape, split, -0.22, 0.18)
    return jnp.clip(array, -reach, reach).astype(held_as)


def setup_inputs(seed: int = 0) -> dict:
    streams_of = jax.random.split(jax.random.key(seed), 10)
    tokens = noise(streams_of[0], (TOKENS, D), 1.0, 6.0, ((0, 32),))
    seq_lengths = draw_seq_lengths(jax.random.fold_in(streams_of[9], 71), 0)
    cotangent = noise(streams_of[2], (TOKENS, D), 1.0, 6.0, ((0, 32),))
    attention_norm_gain = jnp.clip(1.0 + 0.1 * jax.random.normal(streams_of[3], (D,), jnp.float32), 0.5, 1.5).astype(jnp.bfloat16)
    w_qkv = noise(streams_of[4], (D, 3 * D), D ** -0.5, 0.1875, ((0, 32),))
    w_attn_out = noise(streams_of[5], (D, D), (D // 16) ** -0.5, 0.75, ((0, 32),))
    feedforward_norm_gain = jnp.clip(1.0 + 0.1 * jax.random.normal(streams_of[6], (D,), jnp.float32), 0.5, 1.5).astype(jnp.bfloat16)
    w_in = noise(streams_of[7], (D, 2 * FF), D ** -0.5, 0.1875, ((0, 32),))
    w_out = noise(streams_of[8], (D, FF), FF ** -0.5, 0.125, ((0, 32),))
    return dict(tokens=tokens, seq_lengths=seq_lengths, cotangent=cotangent, attention_norm_gain=attention_norm_gain, w_qkv=w_qkv, w_attn_out=w_attn_out, feedforward_norm_gain=feedforward_norm_gain, w_in=w_in, w_out=w_out)


norm_eps = 1e-05
rope_base = 160000.0

def matmul(left_side, right_side):
    return jnp.dot(left_side, right_side, preferred_element_type=jnp.float32)

def batched(form, left_side, right_side):
    return jnp.einsum(form, left_side.astype(jnp.float32), right_side.astype(jnp.float32))

def layout(lengths, row_count):
    ends = jnp.cumsum(lengths).astype(jnp.int32)
    starts = (ends - lengths).astype(jnp.int32)
    places = lax.iota(jnp.int32, row_count)
    sequence_segment = lax.optimization_barrier(jnp.sum((ends[None, :] <= places[:, None]).astype(jnp.int32), axis=1))
    slot_ids = lax.iota(jnp.int32, lengths.shape[0])
    first_row = lax.optimization_barrier(jnp.sum(jnp.where(sequence_segment[:, None] == slot_ids[None, :], starts[None, :], 0), axis=1))
    return (sequence_segment, (places - first_row).astype(jnp.int32), sequence_segment < lengths.shape[0])

def rotary(positions, head_size):
    half_size = head_size // 2
    frequency = rope_base ** (-(lax.iota(jnp.float32, half_size) * (2.0 / head_size)))
    angles = positions.astype(jnp.float32)[..., None] * frequency
    cosine_table = jnp.concatenate([jnp.cos(angles), jnp.cos(angles)], axis=-1)
    sine_table = jnp.concatenate([jnp.sin(angles), jnp.sin(angles)], axis=-1)
    return (cosine_table, sine_table)

def rotate_half(vector):
    half_size = vector.shape[-1] // 2
    return jnp.concatenate([-vector[..., half_size:], vector[..., :half_size]], axis=-1)

def rotate_back(vector):
    half_size = vector.shape[-1] // 2
    return jnp.concatenate([vector[..., half_size:], -vector[..., :half_size]], axis=-1)

def norm_statistics(values):
    average = lax.optimization_barrier(jnp.mean(values, axis=-1, keepdims=True))
    centred = values - average
    inverse = lax.rsqrt(lax.optimization_barrier(jnp.mean(centred * centred, axis=-1, keepdims=True)) + norm_eps)
    return (centred * inverse, inverse)

def norm_backward_pass(grad_normed, gain_vec, normalized, inverse):
    scaled = grad_normed * gain_vec.astype(jnp.float32)
    return inverse * (scaled - lax.optimization_barrier(jnp.mean(scaled, axis=-1, keepdims=True)) - normalized * lax.optimization_barrier(jnp.mean(scaled * normalized, axis=-1, keepdims=True)))

def attend(rotated_query, rotated_key, value_reduced_precision, sequence_segment):
    scores = batched('thd,shd->hts', rotated_query, rotated_key)
    allowed = sequence_segment[:, None] == sequence_segment[None, :]
    scores = jnp.where(allowed[None], scores, -jnp.inf)
    logarithm_totals = jax.nn.logsumexp(scores, axis=-1)
    weights = jnp.exp(scores - logarithm_totals[..., None]).astype(jnp.bfloat16)
    attended = batched('hts,shd->thd', weights, value_reduced_precision).astype(jnp.bfloat16)
    return (attended, logarithm_totals)

def attend_back(rotated_query, rotated_key, value_reduced_precision, sequence_segment, logarithm_totals, grad_attended):
    scores = batched('thd,shd->hts', rotated_query, rotated_key)
    allowed = sequence_segment[:, None] == sequence_segment[None, :]
    scores = jnp.where(allowed[None], scores, -jnp.inf)
    probs_full = jnp.exp(scores - logarithm_totals[..., None])
    weights = probs_full.astype(jnp.bfloat16)
    grad_value = batched('hts,thd->shd', weights, grad_attended)
    grad_probs = batched('thd,shd->hts', grad_attended, value_reduced_precision)
    row_delta = lax.optimization_barrier(jnp.sum(probs_full * grad_probs, axis=-1, keepdims=True))
    grad_scores = (probs_full * (grad_probs - row_delta)).astype(jnp.bfloat16)
    grad_query = batched('hts,shd->thd', grad_scores, rotated_key)
    grad_key = batched('hts,thd->shd', grad_scores, rotated_query)
    return (grad_query, grad_key, grad_value)

def forward(tokens, lengths, attention_norm_gain, w_qkv, w_attn_out, feedforward_norm_gain, w_in, w_out):
    groups, row_count, embedding_width = tokens.shape
    head_count = embedding_width // HEAD_DIM
    hidden_units = w_in.shape[1] // 2
    sequence_segment, positions, valid = jax.vmap(lambda row_lengths: layout(row_lengths, row_count))(lengths)
    cosine_table, sine_table = rotary(positions, HEAD_DIM)
    cosine_table = cosine_table[:, :, None, :]
    sine_table = sine_table[:, :, None, :]
    residual_input = tokens.reshape(groups * row_count, embedding_width).astype(jnp.float32)
    attention_standardized, attention_inverse_norm = norm_statistics(residual_input)
    attention_normed_input = (attention_standardized * attention_norm_gain.astype(jnp.float32)).astype(jnp.bfloat16)
    packed = matmul(attention_normed_input, w_qkv).reshape(groups, row_count, 3, head_count, HEAD_DIM)
    query_raw = packed[:, :, 0]
    key_raw = packed[:, :, 1]
    rotated_query = ((query_raw * cosine_table + rotate_half(query_raw) * sine_table) * HEAD_DIM ** (-0.5)).astype(jnp.bfloat16)
    rotated_key = (key_raw * cosine_table + rotate_half(key_raw) * sine_table).astype(jnp.bfloat16)
    value_reduced_precision = packed[:, :, 2].astype(jnp.bfloat16)
    attended, logarithm_totals = jax.vmap(attend)(rotated_query, rotated_key, value_reduced_precision, sequence_segment)
    attention_rows_flat = attended.reshape(groups * row_count, embedding_width)
    hidden_residual = residual_input + matmul(attention_rows_flat, w_attn_out)
    feedforward_standardized, feedforward_inverse_norm = norm_statistics(hidden_residual)
    feedforward_normed_input = (feedforward_standardized * feedforward_norm_gain.astype(jnp.float32)).astype(jnp.bfloat16)
    inner_proj = matmul(feedforward_normed_input, w_in)
    gate_projection = inner_proj[:, :hidden_units]
    up_projection = inner_proj[:, hidden_units:]
    activation_output = jax.nn.gelu(gate_projection, approximate=False)
    mixed_input = (activation_output * up_projection).astype(jnp.bfloat16)
    live_token_rows = valid.reshape(groups * row_count, 1)
    output = jnp.where(live_token_rows, hidden_residual + matmul(mixed_input, w_out.T), 0.0).astype(jnp.bfloat16)
    saved_residuals = (sequence_segment, live_token_rows, cosine_table, sine_table, attention_standardized, attention_inverse_norm, attention_normed_input, rotated_query, rotated_key, value_reduced_precision, logarithm_totals, attention_rows_flat, feedforward_standardized, feedforward_inverse_norm, feedforward_normed_input, gate_projection, up_projection, activation_output, mixed_input)
    return (output, saved_residuals)

def backward(saved_residuals, cotangent, attention_norm_gain, w_qkv, w_attn_out, feedforward_norm_gain, w_in, w_out):
    sequence_segment, live_token_rows, cosine_table, sine_table, attention_standardized, attention_inverse_norm, attention_normed_input, rotated_query, rotated_key, value_reduced_precision, logarithm_totals, attention_rows_flat, feedforward_standardized, feedforward_inverse_norm, feedforward_normed_input, gate_projection, up_projection, activation_output, mixed_input = saved_residuals
    groups, row_count = sequence_segment.shape
    embedding_width = attention_standardized.shape[1]
    head_count = embedding_width // HEAD_DIM
    flat_cot = cotangent.reshape(groups * row_count, embedding_width)
    output_gradient = jnp.where(live_token_rows, flat_cot, jnp.zeros((), flat_cot.dtype))
    grad_w_out = matmul(output_gradient.T, mixed_input)
    grad_mixed = matmul(output_gradient, w_out)
    slope = 0.5 * (1.0 + lax.erf(gate_projection * 0.7071067811865476)) + gate_projection * jnp.exp(-0.5 * gate_projection * gate_projection) * 0.3989422804014327
    grad_inner = jnp.concatenate([grad_mixed * up_projection * slope, grad_mixed * activation_output], axis=1).astype(jnp.bfloat16)
    grad_w_in = matmul(feedforward_normed_input.T, grad_inner)
    feedforward_normed_gradient = matmul(grad_inner, w_in.T)
    feedforward_gain_gradient = lax.optimization_barrier(jnp.sum(feedforward_normed_gradient * feedforward_standardized, axis=0))
    hidden_gradient = output_gradient.astype(jnp.float32) + norm_backward_pass(feedforward_normed_gradient, feedforward_norm_gain, feedforward_standardized, feedforward_inverse_norm)
    grad_hidden_low = hidden_gradient.astype(jnp.bfloat16)
    grad_w_attn_out = matmul(attention_rows_flat.T, grad_hidden_low)
    grad_attended = matmul(grad_hidden_low, w_attn_out.T).astype(jnp.bfloat16)
    grad_attended = grad_attended.reshape(groups, row_count, head_count, HEAD_DIM)
    grad_query, grad_key, grad_value = jax.vmap(attend_back)(rotated_query, rotated_key, value_reduced_precision, sequence_segment, logarithm_totals, grad_attended)
    grad_query = grad_query * HEAD_DIM ** (-0.5)
    grad_query = grad_query * cosine_table + rotate_back(grad_query * sine_table)
    grad_key = grad_key * cosine_table + rotate_back(grad_key * sine_table)
    grad_packed = jnp.stack([grad_query, grad_key, grad_value], axis=2)
    grad_packed = grad_packed.reshape(groups * row_count, 3 * embedding_width).astype(jnp.bfloat16)
    grad_w_qkv = matmul(attention_normed_input.T, grad_packed)
    attention_normed_gradient = matmul(grad_packed, w_qkv.T)
    attention_gain_gradient = lax.optimization_barrier(jnp.sum(attention_normed_gradient * attention_standardized, axis=0))
    block_input_gradient = hidden_gradient + norm_backward_pass(attention_normed_gradient, attention_norm_gain, attention_standardized, attention_inverse_norm)
    return (block_input_gradient, (attention_gain_gradient, grad_w_qkv, grad_w_attn_out, feedforward_gain_gradient, grad_w_in, grad_w_out))

def reference(tokens, seq_lengths, cotangent, attention_norm_gain, w_qkv, w_attn_out, feedforward_norm_gain, w_in, w_out):
    device_count = N_FSDP * N_REP
    group_size = math.gcd(device_count, 8)
    step_count = device_count // group_size
    embedding_width = tokens.shape[1]
    token_blocks = tokens.reshape(step_count, group_size, TOK_DEV, embedding_width)
    length_blocks = seq_lengths.reshape(step_count, group_size, SEQS_DEV)
    cot_blocks = cotangent.reshape(step_count, group_size, TOK_DEV, embedding_width)
    params = (attention_norm_gain, w_qkv, w_attn_out, feedforward_norm_gain, w_in, w_out)

    def one_step(totals, block_data):
        token_part, length_part, cot_part = block_data
        output, saved_residuals = forward(token_part, length_part, attention_norm_gain, w_qkv, w_attn_out, feedforward_norm_gain, w_in, w_out)
        block_input_gradient, grads = backward(saved_residuals, cot_part, attention_norm_gain, w_qkv, w_attn_out, feedforward_norm_gain, w_in, w_out)
        totals = jax.tree.map(lambda first_term, second_term: first_term + second_term, totals, grads)
        return (totals, (output, block_input_gradient))
    zero_grads = tuple((jnp.zeros(param_item.shape, jnp.float32) for param_item in params))
    totals, (outputs, grad_inputs) = lax.scan(one_step, zero_grads, (token_blocks, length_blocks, cot_blocks))
    return (outputs.reshape(-1, embedding_width), grad_inputs.reshape(-1, embedding_width), totals[0], totals[1], totals[2], totals[3], totals[4], totals[5])
```

```python
import jax
import jax.numpy as jnp
from jax import lax
from jax.sharding import PartitionSpec as P

HEAD_DIM = 64

norm_eps = 1e-05
rope_base = 160000.0
AXES = ("fsdp", "rep")


def matmul(left_side, right_side):
    return jnp.dot(left_side, right_side, preferred_element_type=jnp.float32)


def matmul_right_t(left_side, right_side):
    return lax.dot_general(
        left_side, right_side, (((1,), (1,)), ((), ())), preferred_element_type=jnp.float32
    )


def matmul_left_t(left_side, right_side):
    return lax.dot_general(
        left_side, right_side, (((0,), (0,)), ((), ())), preferred_element_type=jnp.float32
    )


def batched(form, left_side, right_side):
    return jnp.einsum(form, left_side, right_side, preferred_element_type=jnp.float32)


def layout(lengths, row_count):
    slot_ids = lax.iota(jnp.int32, lengths.shape[0])
    before = (slot_ids[:, None] <= slot_ids[None, :]).astype(jnp.int32)
    ends = jnp.sum(lengths[:, None] * before, axis=0)
    starts = ends - lengths
    places = lax.iota(jnp.int32, row_count)
    sequence_segment = jnp.sum((ends[None, :] <= places[:, None]).astype(jnp.int32), axis=1)
    first_row = jnp.sum(
        jnp.where(sequence_segment[:, None] == slot_ids[None, :], starts[None, :], 0), axis=1
    )
    return (sequence_segment, places - first_row, sequence_segment < lengths.shape[0])


def rotary(positions, head_size):
    half_size = head_size // 2
    frequency = rope_base ** (-(lax.iota(jnp.float32, half_size) * (2.0 / head_size)))
    angles = positions.astype(jnp.float32)[..., None] * frequency
    cosine, sine = jnp.cos(angles), jnp.sin(angles)
    return (
        jnp.concatenate([cosine, cosine], axis=-1),
        jnp.concatenate([sine, sine], axis=-1),
    )


def rotate_half(vector):
    half_size = vector.shape[-1] // 2
    return jnp.concatenate([-vector[..., half_size:], vector[..., :half_size]], axis=-1)


def rotate_back(vector):
    half_size = vector.shape[-1] // 2
    return jnp.concatenate([vector[..., half_size:], -vector[..., :half_size]], axis=-1)


def norm_statistics(values):
    average = jnp.mean(values, axis=-1, keepdims=True)
    centred = values - average
    inverse = lax.rsqrt(jnp.mean(centred * centred, axis=-1, keepdims=True) + norm_eps)
    return (centred * inverse, inverse)


def norm_backward_pass(scaled, normalized, inverse):
    return inverse * (
        scaled
        - jnp.mean(scaled, axis=-1, keepdims=True)
        - normalized * jnp.mean(scaled * normalized, axis=-1, keepdims=True)
    )


def attend(rotated_query, rotated_key, value_reduced_precision, sequence_segment):
    scores = batched("thd,shd->hts", rotated_query, rotated_key)
    allowed = sequence_segment[:, None] == sequence_segment[None, :]
    scores = jnp.where(allowed[None], scores, -jnp.inf)
    logarithm_totals = jax.nn.logsumexp(scores, axis=-1)
    weights = jnp.exp(scores - logarithm_totals[..., None]).astype(jnp.bfloat16)
    attended = batched("hts,shd->thd", weights, value_reduced_precision).astype(jnp.bfloat16)
    return (attended, logarithm_totals)


def attend_back(
    rotated_query,
    rotated_key,
    value_reduced_precision,
    sequence_segment,
    logarithm_totals,
    grad_attended,
):
    scores = batched("thd,shd->hts", rotated_query, rotated_key)
    allowed = sequence_segment[:, None] == sequence_segment[None, :]
    scores = jnp.where(allowed[None], scores, -jnp.inf)
    probs_full = jnp.exp(scores - logarithm_totals[..., None])
    weights = probs_full.astype(jnp.bfloat16)
    grad_value = batched("hts,thd->shd", weights, grad_attended)
    grad_probs = batched("thd,shd->hts", grad_attended, value_reduced_precision)
    row_delta = jnp.sum(probs_full * grad_probs, axis=-1, keepdims=True)
    grad_scores = (probs_full * (grad_probs - row_delta)).astype(jnp.bfloat16)
    grad_query = batched("hts,shd->thd", grad_scores, rotated_key)
    grad_key = batched("hts,thd->shd", grad_scores, rotated_query)
    return (grad_query, grad_key, grad_value)


def xor_order(items, index):
    bit = 1
    while bit < len(items):
        flip = (index & bit) != 0
        items = [jnp.where(flip, items[k ^ bit], items[k]) for k in range(len(items))]
        bit *= 2
    return items


def swap(value, distance):
    count = lax.axis_size("rep")
    return lax.ppermute(value, "rep", [(k, k ^ distance) for k in range(count)])


def rep_gather(block):
    across = swap(block, 2)
    beside = swap(jnp.stack([block, across]), 1)
    return jnp.concatenate([block, beside[0], across, beside[1]], axis=0)


def rep_scatter(partial):
    low = partial.astype(jnp.bfloat16)
    rows = partial.shape[0] // 4
    blocks = [low[k * rows : (k + 1) * rows] for k in range(4)]
    beside = swap(jnp.stack([blocks[1], blocks[3]]), 1).astype(jnp.float32)
    kept = blocks[0].astype(jnp.float32) + beside[0]
    sent = (blocks[2].astype(jnp.float32) + beside[1]).astype(jnp.bfloat16)
    return kept + swap(sent, 2).astype(jnp.float32)


def rep_exchange(pieces, rep):
    placed = xor_order(pieces, rep)
    received = [placed[0]] + [swap(placed[k], k) for k in range(1, len(placed))]
    return xor_order(received, rep)


class Ring:
    def __init__(self):
        self.index = lax.axis_index("fsdp")
        self.z, self.x = self.index // 2, self.index % 2

    def up(self, value):
        return lax.ppermute(value, "fsdp", [(k, (k + 2) % 8) for k in range(8)])

    def over(self, value):
        return lax.ppermute(value, "fsdp", [(k, k ^ 1) for k in range(8)])

    def relative(self, blocks):
        flip = self.x == 1
        blocks = [jnp.where(flip, blocks[k ^ 1], blocks[k]) for k in range(8)]
        for bit in (1, 2):
            turn = (self.z & bit) != 0
            blocks = [jnp.where(turn, blocks[(k + 2 * bit) % 8], blocks[k]) for k in range(8)]
        return blocks

    def absolute(self, blocks):
        flip = self.x == 1
        blocks = [jnp.where(flip, blocks[k ^ 1], blocks[k]) for k in range(8)]
        for bit in (1, 2):
            turn = (self.z & bit) != 0
            blocks = [jnp.where(turn, blocks[(k - 2 * bit) % 8], blocks[k]) for k in range(8)]
        return blocks

    def gather(self, own, more_z):
        first = self.up(own)
        second = self.up(first)
        third = self.up(second)
        over_own, over_first, over_second = self.over(own), self.over(first), self.over(second)
        over_third = self.up(over_second) if more_z else self.over(third)
        return [own, over_own, third, over_third, second, over_second, first, over_first]

    def scatter(self, blocks, more_z):
        wide = lambda value: value.astype(jnp.float32)
        low = lambda value: value.astype(jnp.bfloat16)
        blocks = [low(block) for block in blocks]
        total = wide(blocks[6])
        if more_z:
            blocks[5] = low(wide(blocks[5]) + wide(self.up(blocks[7])))
        else:
            total = total + wide(self.over(blocks[7]))
        for step in (2, 1, 0):
            here = wide(blocks[2 * step]) + wide(self.over(blocks[2 * step + 1]))
            total = here + wide(self.up(low(total)))
        return total


class Plain:
    def __init__(self):
        self.count = lax.axis_size("fsdp")

    def relative(self, blocks):
        return blocks

    absolute = relative

    def gather(self, own, more_z):
        whole = lax.all_gather(own, "fsdp", axis=0)
        return [whole[k] for k in range(self.count)]

    def scatter(self, blocks, more_z):
        return lax.psum_scatter(jnp.stack(blocks), "fsdp", scatter_dimension=0, tiled=False)


def split_columns(value, count):
    width = value.shape[1] // count
    return [value[:, k * width : (k + 1) * width] for k in range(count)]


def split_rows(value, count):
    width = value.shape[0] // count
    return [value[k * width : (k + 1) * width] for k in range(count)]


def columns(blocks):
    return jnp.concatenate(blocks, axis=1)


def rows(blocks):
    return jnp.concatenate(blocks, axis=0)


def local(
    tokens,
    seq_lengths,
    cotangent,
    attention_norm_gain,
    w_qkv,
    w_attn_out,
    feedforward_norm_gain,
    w_in,
    w_out,
):
    row_count, width = tokens.shape
    fsdp_count, rep_count = lax.axis_size("fsdp"), lax.axis_size("rep")
    rep = lax.axis_index("rep")
    ring = Ring() if fsdp_count == 8 else Plain()
    hidden = w_in.shape[1] // 2
    head_count = width // HEAD_DIM // rep_count
    own_width = head_count * HEAD_DIM
    low, wide = jnp.bfloat16, jnp.float32

    def relative(value):
        return columns(ring.relative(split_columns(value, fsdp_count)))

    def absolute(value):
        return columns(ring.absolute(split_columns(value, fsdp_count)))

    gain_attn = attention_norm_gain.astype(wide)[:, None]
    gain_mlp = feedforward_norm_gain.astype(wide)[:, None]
    qkv_parts = split_columns((w_qkv.astype(wide) * gain_attn).astype(low), 3 * rep_count)
    in_parts = split_columns((w_in.astype(wide) * gain_mlp).astype(low), 2 * rep_count)
    qkv_own = rows(
        rep_exchange([columns(qkv_parts[k::rep_count]) for k in range(rep_count)], rep)
    )
    order = [
        (k, (k % fsdp_count) * rep_count + k // fsdp_count) for k in range(fsdp_count * rep_count)
    ]
    attn_own = lax.ppermute(w_attn_out, AXES, order)
    in_own = rows(rep_exchange([columns(in_parts[k::rep_count]) for k in range(rep_count)], rep))
    out_own = rows(rep_exchange(split_columns(w_out, rep_count), rep))

    x_own = relative(tokens)
    x_low = rep_gather(x_own)
    cot = rep_gather(relative(cotangent))
    lengths = rep_gather(seq_lengths)

    qkv = rows(ring.gather(qkv_own, True))
    attn = relative(rows(ring.absolute(ring.gather(attn_own, True))))
    w_up = rows(ring.gather(in_own, False))
    w_down = rows(ring.gather(out_own, True))

    sequence_segment, positions, valid = jax.vmap(
        lambda row_lengths: layout(row_lengths, row_count)
    )(lengths)
    cosine, sine = rotary(positions, HEAD_DIM)
    cosine, sine = cosine[:, :, None, :], sine[:, :, None, :]
    live = valid.reshape(rep_count * row_count, 1)

    standard, inverse = norm_statistics(x_low.astype(wide))
    normed = standard.astype(low)
    packed = matmul(normed, qkv).reshape(rep_count, row_count, 3, head_count, HEAD_DIM)
    query, key = packed[:, :, 0], packed[:, :, 1]
    query = ((query * cosine + rotate_half(query) * sine) * HEAD_DIM ** (-0.5)).astype(low)
    key = (key * cosine + rotate_half(key) * sine).astype(low)
    value = packed[:, :, 2].astype(low)
    attended, totals = jax.vmap(attend)(query, key, value, sequence_segment)
    attended = attended.reshape(rep_count * row_count, own_width)
    hidden_own = x_own.astype(wide) + rep_scatter(matmul(attended, attn))
    standard_mlp, inverse_mlp = norm_statistics(hidden_own)
    normed_mlp = rep_gather(standard_mlp.astype(low))
    inner = matmul(normed_mlp, w_up)
    gate, up = inner[:, : hidden // rep_count], inner[:, hidden // rep_count :]
    phi = 0.5 * (1.0 + lax.erf(gate * 0.7071067811865476))
    activation = gate * phi
    mixed = (activation * up).astype(low)
    grad_out = jnp.where(live, cot, jnp.zeros((), low))

    term_out = matmul_left_t(grad_out, mixed)
    sum_out = ring.scatter(split_rows(term_out, fsdp_count), True)

    slope = phi + gate * jnp.exp(-0.5 * gate * gate) * 0.3989422804014327
    grad_mixed = matmul(grad_out, w_down)
    grad_inner = columns([grad_mixed * up * slope, grad_mixed * activation]).astype(low)
    scaled_mlp = rep_scatter(matmul_right_t(grad_inner, w_up))
    term_in = matmul_left_t(normed_mlp, grad_inner)
    sum_in = ring.scatter(split_rows(term_in, fsdp_count), False)
    grad_hidden = grad_out[:row_count].astype(wide) + norm_backward_pass(
        scaled_mlp, standard_mlp, inverse_mlp
    )
    grad_low = rep_gather(grad_hidden.astype(low))
    mlp_result = rep_scatter(matmul_right_t(mixed, w_down))
    output = jnp.where(live[:row_count], hidden_own + mlp_result, 0.0).astype(low)

    grad_attended = matmul_right_t(grad_low, attn).astype(low)
    grad_query, grad_key, grad_value = jax.vmap(attend_back)(
        query,
        key,
        value,
        sequence_segment,
        totals,
        grad_attended.reshape(rep_count, row_count, head_count, HEAD_DIM),
    )
    grad_query = grad_query * HEAD_DIM ** (-0.5)
    grad_query = grad_query * cosine + rotate_back(grad_query * sine)
    grad_key = grad_key * cosine + rotate_back(grad_key * sine)
    grad_packed = jnp.stack([grad_query, grad_key, grad_value], axis=2)
    grad_packed = grad_packed.reshape(rep_count * row_count, 3 * own_width).astype(low)
    term_qkv = matmul_left_t(normed, grad_packed)
    sum_qkv = ring.scatter(split_rows(term_qkv, fsdp_count), True)
    term_attn = absolute(matmul_left_t(attended, grad_low).astype(low))
    sum_attn = ring.scatter(ring.relative(split_rows(term_attn, fsdp_count)), True)
    scaled_attn = rep_scatter(matmul_right_t(grad_packed, qkv))
    block_input_gradient = grad_hidden + norm_backward_pass(
        scaled_attn, standard[:row_count], inverse[:row_count]
    )

    back_qkv = rep_exchange(split_rows(sum_qkv.astype(low), rep_count), rep)
    back_in = rep_exchange(split_rows(sum_in.astype(low), rep_count), rep)
    back_out = rep_exchange(split_rows(sum_out.astype(low), rep_count), rep)
    unit_qkv = columns(
        [split_columns(piece, 3)[part] for part in range(3) for piece in back_qkv]
    ).astype(wide)
    unit_in = columns(
        [split_columns(piece, 2)[part] for part in range(2) for piece in back_in]
    ).astype(wide)
    grad_w_attn_out = lax.ppermute(
        sum_attn.astype(low), AXES, [(there, here) for here, there in order]
    ).astype(wide)
    return (
        absolute(output),
        absolute(block_input_gradient),
        jnp.sum(unit_qkv * w_qkv.astype(wide), axis=1),
        unit_qkv * gain_attn,
        grad_w_attn_out,
        jnp.sum(unit_in * w_in.astype(wide), axis=1),
        unit_in * gain_mlp,
        columns(back_out).astype(wide),
    )


def solution(mesh):
    return jax.shard_map(
        local,
        mesh=mesh,
        in_specs=(
            P(AXES, None),
            P(AXES, None),
            P(AXES, None),
            P(AXES),
            P(AXES, None),
            P(AXES, None),
            P(AXES),
            P(AXES, None),
            P(AXES, None),
        ),
        out_specs=(
            P(AXES, None),
            P(AXES, None),
            P(AXES),
            P(AXES, None),
            P(AXES, None),
            P(AXES),
            P(AXES, None),
            P(AXES, None),
        ),
        check_vma=False,
    )
```

```python
import jax
import jax.numpy as jnp
from jax import lax
from jax.sharding import PartitionSpec as P

HEAD_DIM = 64

norm_eps = 1e-05
rope_base = 160000.0
AXES = ("fsdp", "rep")


def matmul(left_side, right_side):
    return jnp.dot(left_side, right_side, preferred_element_type=jnp.float32)


def matmul_right_t(left_side, right_side):
    return lax.dot_general(
        left_side, right_side, (((1,), (1,)), ((), ())), preferred_element_type=jnp.float32
    )


def matmul_left_t(left_side, right_side):
    return lax.dot_general(
        left_side, right_side, (((0,), (0,)), ((), ())), preferred_element_type=jnp.float32
    )


def batched(form, left_side, right_side):
    return jnp.einsum(form, left_side, right_side, preferred_element_type=jnp.float32)


def layout(lengths, row_count):
    slot_ids = lax.iota(jnp.int32, lengths.shape[0])
    before = (slot_ids[:, None] <= slot_ids[None, :]).astype(jnp.int32)
    ends = jnp.sum(lengths[:, None] * before, axis=0)
    starts = ends - lengths
    places = lax.iota(jnp.int32, row_count)
    sequence_segment = jnp.sum((ends[None, :] <= places[:, None]).astype(jnp.int32), axis=1)
    first_row = jnp.sum(
        jnp.where(sequence_segment[:, None] == slot_ids[None, :], starts[None, :], 0), axis=1
    )
    return (sequence_segment, places - first_row, sequence_segment < lengths.shape[0])


def rotary(positions, head_size):
    half_size = head_size // 2
    frequency = rope_base ** (-(lax.iota(jnp.float32, half_size) * (2.0 / head_size)))
    angles = positions.astype(jnp.float32)[..., None] * frequency
    cosine, sine = jnp.cos(angles), jnp.sin(angles)
    return (
        jnp.concatenate([cosine, cosine], axis=-1),
        jnp.concatenate([sine, sine], axis=-1),
    )


def rotate_half(vector):
    half_size = vector.shape[-1] // 2
    return jnp.concatenate([-vector[..., half_size:], vector[..., :half_size]], axis=-1)


def rotate_back(vector):
    half_size = vector.shape[-1] // 2
    return jnp.concatenate([vector[..., half_size:], -vector[..., :half_size]], axis=-1)


def norm_statistics(values):
    average = jnp.mean(values, axis=-1, keepdims=True)
    centred = values - average
    inverse = lax.rsqrt(jnp.mean(centred * centred, axis=-1, keepdims=True) + norm_eps)
    return (centred * inverse, inverse)


def norm_backward_pass(scaled, normalized, inverse):
    return inverse * (
        scaled
        - jnp.mean(scaled, axis=-1, keepdims=True)
        - normalized * jnp.mean(scaled * normalized, axis=-1, keepdims=True)
    )


def attend(rotated_query, rotated_key, value_reduced_precision, sequence_segment):
    scores = batched("thd,shd->hts", rotated_query, rotated_key)
    allowed = sequence_segment[:, None] == sequence_segment[None, :]
    scores = jnp.where(allowed[None], scores, -jnp.inf)
    logarithm_totals = jax.nn.logsumexp(scores, axis=-1)
    weights = jnp.exp(scores - logarithm_totals[..., None]).astype(jnp.bfloat16)
    attended = batched("hts,shd->thd", weights, value_reduced_precision).astype(jnp.bfloat16)
    return (attended, logarithm_totals)


def attend_back(
    rotated_query,
    rotated_key,
    value_reduced_precision,
    sequence_segment,
    logarithm_totals,
    grad_attended,
):
    scores = batched("thd,shd->hts", rotated_query, rotated_key)
    allowed = sequence_segment[:, None] == sequence_segment[None, :]
    scores = jnp.where(allowed[None], scores, -jnp.inf)
    probs_full = jnp.exp(scores - logarithm_totals[..., None])
    weights = probs_full.astype(jnp.bfloat16)
    grad_value = batched("hts,thd->shd", weights, grad_attended)
    grad_probs = batched("thd,shd->hts", grad_attended, value_reduced_precision)
    row_delta = jnp.sum(probs_full * grad_probs, axis=-1, keepdims=True)
    grad_scores = (probs_full * (grad_probs - row_delta)).astype(jnp.bfloat16)
    grad_query = batched("hts,shd->thd", grad_scores, rotated_key)
    grad_key = batched("hts,thd->shd", grad_scores, rotated_query)
    return (grad_query, grad_key, grad_value)


def after(value, *others):
    return lax.optimization_barrier((value, *others))[0]


def swap(value, distance):
    count = lax.axis_size("rep")
    return lax.ppermute(value, "rep", [(k, k ^ distance) for k in range(count)])


def rep_gather(block):
    across = swap(block, 2)
    beside = swap(jnp.stack([block, across]), 1)
    return jnp.concatenate([block, beside[0], across, beside[1]], axis=0)


def rep_scatter(partial):
    low = partial.astype(jnp.bfloat16)
    rows = partial.shape[0] // 4
    blocks = [low[k * rows : (k + 1) * rows] for k in range(4)]
    beside = swap(jnp.stack([blocks[1], blocks[3]]), 1).astype(jnp.float32)
    kept = blocks[0].astype(jnp.float32) + beside[0]
    sent = (blocks[2].astype(jnp.float32) + beside[1]).astype(jnp.bfloat16)
    return kept + swap(sent, 2).astype(jnp.float32)


def rep_exchange(pieces):
    return lax.all_to_all(jnp.stack(pieces), "rep", 0, 0, tiled=True)


class Ring:
    def __init__(self):
        self.index = lax.axis_index("fsdp")
        self.z, self.x = self.index // 2, self.index % 2

    def up(self, value):
        return lax.ppermute(value, "fsdp", [(k, (k + 2) % 8) for k in range(8)])

    def down(self, value):
        return lax.ppermute(value, "fsdp", [(k, (k - 2) % 8) for k in range(8)])

    def over(self, value):
        return lax.ppermute(value, "fsdp", [(k, k ^ 1) for k in range(8)])

    def relative(self, blocks):
        flip = self.x == 1
        blocks = [jnp.where(flip, blocks[k ^ 1], blocks[k]) for k in range(8)]
        for bit in (1, 2):
            turn = (self.z & bit) != 0
            blocks = [jnp.where(turn, blocks[(k + 2 * bit) % 8], blocks[k]) for k in range(8)]
        return [blocks[2 * ((p + 1) % 4) + i] for i in range(2) for p in range(4)]

    def absolute(self, blocks):
        blocks = [blocks[4 * i + (j - 1) % 4] for j in range(4) for i in range(2)]
        flip = self.x == 1
        blocks = [jnp.where(flip, blocks[k ^ 1], blocks[k]) for k in range(8)]
        for bit in (1, 2):
            turn = (self.z & bit) != 0
            blocks = [jnp.where(turn, blocks[(k - 2 * bit) % 8], blocks[k]) for k in range(8)]
        return blocks

    def gather(self, own, *others):
        own = after(own, *others) if others else own
        third, first, own_x = self.up(own), self.down(own), self.over(own)
        second = self.up(third)
        first_x, third_x, second_x = self.over(first), self.over(third), self.over(second)
        return [first, second, third, own, first_x, second_x, third_x, own_x], (first, third)

    def scatter(self, term, parts, middle=(), end=()):
        wide = lambda value: value.astype(jnp.float32)
        low = lambda value: value.astype(jnp.bfloat16)
        term = low(term)
        size = term.shape[0] // 8
        received = [self.over(piece) for piece in split_rows(term[4 * size :], parts)]
        received = lax.optimization_barrier((*received, *middle))[:parts]
        sums = [
            wide(mine) + wide(its)
            for mine, its in zip(
                split_rows(term[: 4 * size], 4),
                [piece for whole in received for piece in split_rows(whole, 4 // parts)],
            )
        ]
        second, third = self.up(low(sums[1])), self.down(low(sums[2]))
        first = self.up(low(sums[0] + wide(second)))
        first, third = lax.optimization_barrier((first, third, *end))[:2]
        return sums[3] + wide(first) + wide(third)


class Plain:
    def __init__(self):
        self.count = lax.axis_size("fsdp")

    def relative(self, blocks):
        return blocks

    absolute = relative

    def gather(self, own, *others):
        whole = lax.all_gather(own, "fsdp", axis=0)
        return [whole[k] for k in range(self.count)], ()

    def scatter(self, term, parts, middle=(), end=()):
        return lax.psum_scatter(term, "fsdp", scatter_dimension=0, tiled=True)


def split_columns(value, count):
    width = value.shape[1] // count
    return [value[:, k * width : (k + 1) * width] for k in range(count)]


def split_rows(value, count):
    width = value.shape[0] // count
    return [value[k * width : (k + 1) * width] for k in range(count)]


def columns(blocks):
    return jnp.concatenate(blocks, axis=1)


def rows(blocks):
    return jnp.concatenate(blocks, axis=0)


def local(
    tokens,
    seq_lengths,
    cotangent,
    attention_norm_gain,
    w_qkv,
    w_attn_out,
    feedforward_norm_gain,
    w_in,
    w_out,
):
    row_count, width = tokens.shape
    fsdp_count, rep_count = lax.axis_size("fsdp"), lax.axis_size("rep")
    ring = Ring() if fsdp_count == 8 else Plain()
    hidden = w_in.shape[1] // 2
    head_count = width // HEAD_DIM // rep_count
    own_width = head_count * HEAD_DIM
    low, wide = jnp.bfloat16, jnp.float32

    def relative(value):
        return columns(ring.relative(split_columns(value, fsdp_count)))

    def absolute(value):
        return columns(ring.absolute(split_columns(value, fsdp_count)))

    gain_attn = attention_norm_gain.astype(wide)[:, None]
    gain_mlp = feedforward_norm_gain.astype(wide)[:, None]
    qkv_parts = split_columns((w_qkv.astype(wide) * gain_attn).astype(low), 3 * rep_count)
    in_parts = split_columns((w_in.astype(wide) * gain_mlp).astype(low), 2 * rep_count)
    order = [
        (k, (k % fsdp_count) * rep_count + k // fsdp_count) for k in range(fsdp_count * rep_count)
    ]
    attn_own = lax.ppermute(w_attn_out, AXES, order)
    qkv_own = rep_exchange([columns(qkv_parts[k::rep_count]) for k in range(rep_count)])
    block = rep_count * w_qkv.shape[0]
    first_own = columns(
        [qkv_own.reshape(block, 3 * own_width), rows(split_columns(attn_own, rep_count))]
    )
    in_own = rep_exchange([columns(in_parts[k::rep_count]) for k in range(rep_count)])
    out_own = rep_exchange(split_columns(w_out, rep_count))

    x_own = relative(tokens)
    x_low = rep_gather(x_own)
    cot = rep_gather(relative(cotangent))
    lengths = rep_gather(seq_lengths)

    first_blocks, first_in = ring.gather(first_own)
    in_blocks, in_in = ring.gather(in_own.reshape(block, -1), *first_in)
    out_blocks, _ = ring.gather(out_own.reshape(block, -1), *in_in)
    qkv = rows([piece[:, : 3 * own_width] for piece in first_blocks])
    attn = relative(
        rows(
            ring.absolute(
                [columns(split_rows(piece[:, 3 * own_width :], rep_count)) for piece in first_blocks]
            )
        )
    )
    w_up, w_down = rows(in_blocks), rows(out_blocks)

    sequence_segment, positions, valid = jax.vmap(
        lambda row_lengths: layout(row_lengths, row_count)
    )(lengths)
    cosine, sine = rotary(positions, HEAD_DIM)
    cosine, sine = cosine[:, :, None, :], sine[:, :, None, :]
    live = valid.reshape(rep_count * row_count, 1)

    standard, inverse = norm_statistics(x_low.astype(wide))
    normed = standard.astype(low)
    packed = matmul(normed, qkv).reshape(rep_count, row_count, 3, head_count, HEAD_DIM)
    query, key = packed[:, :, 0], packed[:, :, 1]
    query = ((query * cosine + rotate_half(query) * sine) * HEAD_DIM ** (-0.5)).astype(low)
    key = (key * cosine + rotate_half(key) * sine).astype(low)
    value = packed[:, :, 2].astype(low)
    attended, totals = jax.vmap(attend)(query, key, value, sequence_segment)
    attended = attended.reshape(rep_count * row_count, own_width)
    hidden_own = x_own.astype(wide) + rep_scatter(matmul(attended, attn))
    standard_mlp, inverse_mlp = norm_statistics(hidden_own)
    normed_mlp = rep_gather(standard_mlp.astype(low))
    inner = matmul(normed_mlp, w_up)
    gate, up = inner[:, : hidden // rep_count], inner[:, hidden // rep_count :]
    phi = 0.5 * (1.0 + lax.erf(gate * 0.7071067811865476))
    activation = gate * phi
    mixed = (activation * up).astype(low)
    grad_out = jnp.where(live, cot, jnp.zeros((), low))

    term_out = matmul_left_t(grad_out, mixed)
    slope = phi + gate * jnp.exp(-0.5 * gate * gate) * 0.3989422804014327
    grad_mixed = matmul(grad_out, w_down)
    grad_inner = columns([grad_mixed * up * slope, grad_mixed * activation]).astype(low)
    partial_mlp = matmul_right_t(grad_inner, w_up)
    scaled_mlp = rep_scatter(partial_mlp)
    term_in = matmul_left_t(normed_mlp, grad_inner)
    grad_hidden = grad_out[:row_count].astype(wide) + norm_backward_pass(
        scaled_mlp, standard_mlp, inverse_mlp
    )
    grad_low = rep_gather(grad_hidden.astype(low))
    mlp_result = rep_scatter(matmul_right_t(mixed, w_down))
    output = jnp.where(live[:row_count], hidden_own + mlp_result, 0.0).astype(low)

    grad_attended = matmul_right_t(grad_low, attn).astype(low)
    grad_query, grad_key, grad_value = jax.vmap(attend_back)(
        query,
        key,
        value,
        sequence_segment,
        totals,
        grad_attended.reshape(rep_count, row_count, head_count, HEAD_DIM),
    )
    grad_query = grad_query * HEAD_DIM ** (-0.5)
    grad_query = grad_query * cosine + rotate_back(grad_query * sine)
    grad_key = grad_key * cosine + rotate_back(grad_key * sine)
    grad_packed = jnp.stack([grad_query, grad_key, grad_value], axis=2)
    grad_packed = grad_packed.reshape(rep_count * row_count, 3 * own_width).astype(low)
    term_qkv = matmul_left_t(normed, grad_packed)
    term_attn = absolute(matmul_left_t(attended, grad_low).astype(low))
    term_attn = rows(ring.relative(split_rows(term_attn, fsdp_count)))
    sum_out = ring.scatter(term_out, 1, (partial_mlp,), (grad_low,))
    sum_in = ring.scatter(term_in, 2, (grad_low,), (grad_packed,))
    sum_attn = ring.scatter(term_attn, 1, (grad_packed,))
    sum_qkv = ring.scatter(term_qkv, 2)
    scaled_attn = rep_scatter(matmul_right_t(grad_packed, qkv))
    block_input_gradient = grad_hidden + norm_backward_pass(
        scaled_attn, standard[:row_count], inverse[:row_count]
    )

    back_out = rep_exchange(split_rows(sum_out.astype(low), rep_count))
    back_in = rep_exchange(split_rows(sum_in.astype(low), rep_count))
    back_qkv = rep_exchange(split_rows(sum_qkv.astype(low), rep_count))
    unit_qkv = columns(
        [split_columns(piece, 3)[part] for part in range(3) for piece in list(back_qkv)]
    ).astype(wide)
    unit_in = columns(
        [split_columns(piece, 2)[part] for part in range(2) for piece in list(back_in)]
    ).astype(wide)
    grad_w_attn_out = lax.ppermute(
        sum_attn.astype(low), AXES, [(there, here) for here, there in order]
    ).astype(wide)
    return (
        absolute(output),
        absolute(block_input_gradient),
        jnp.sum(unit_qkv * w_qkv.astype(wide), axis=1),
        unit_qkv * gain_attn,
        grad_w_attn_out,
        jnp.sum(unit_in * w_in.astype(wide), axis=1),
        unit_in * gain_mlp,
        columns(list(back_out)).astype(wide),
    )


def solution(mesh):
    return jax.shard_map(
        local,
        mesh=mesh,
        in_specs=(
            P(AXES, None),
            P(AXES, None),
            P(AXES, None),
            P(AXES),
            P(AXES, None),
            P(AXES, None),
            P(AXES),
            P(AXES, None),
            P(AXES, None),
        ),
        out_specs=(
            P(AXES, None),
            P(AXES, None),
            P(AXES),
            P(AXES, None),
            P(AXES, None),
            P(AXES),
            P(AXES, None),
            P(AXES, None),
        ),
        check_vma=False,
    )
```

```python
import jax
import jax.numpy as jnp
from jax import lax
from jax.sharding import PartitionSpec as P

HEAD_DIM = 64

norm_eps = 1e-05
rope_base = 160000.0
AXES = ("fsdp", "rep")


def matmul(left_side, right_side):
    return jnp.dot(left_side, right_side, preferred_element_type=jnp.float32)


def matmul_right_t(left_side, right_side):
    return lax.dot_general(
        left_side, right_side, (((1,), (1,)), ((), ())), preferred_element_type=jnp.float32
    )


def matmul_left_t(left_side, right_side):
    return lax.dot_general(
        left_side, right_side, (((0,), (0,)), ((), ())), preferred_element_type=jnp.float32
    )


def batched(form, left_side, right_side):
    return jnp.einsum(form, left_side, right_side, preferred_element_type=jnp.float32)


def layout(lengths, row_count):
    slot_ids = lax.iota(jnp.int32, lengths.shape[0])
    before = (slot_ids[:, None] <= slot_ids[None, :]).astype(jnp.int32)
    ends = jnp.sum(lengths[:, None] * before, axis=0)
    starts = ends - lengths
    places = lax.iota(jnp.int32, row_count)
    sequence_segment = jnp.sum((ends[None, :] <= places[:, None]).astype(jnp.int32), axis=1)
    first_row = jnp.sum(
        jnp.where(sequence_segment[:, None] == slot_ids[None, :], starts[None, :], 0), axis=1
    )
    return (sequence_segment, places - first_row, sequence_segment < lengths.shape[0])


def rotary(positions, head_size):
    half_size = head_size // 2
    frequency = rope_base ** (-(lax.iota(jnp.float32, half_size) * (2.0 / head_size)))
    angles = positions.astype(jnp.float32)[..., None] * frequency
    cosine, sine = jnp.cos(angles), jnp.sin(angles)
    return (
        jnp.concatenate([cosine, cosine], axis=-1),
        jnp.concatenate([sine, sine], axis=-1),
    )


def rotate_half(vector):
    half_size = vector.shape[-1] // 2
    return jnp.concatenate([-vector[..., half_size:], vector[..., :half_size]], axis=-1)


def rotate_back(vector):
    half_size = vector.shape[-1] // 2
    return jnp.concatenate([vector[..., half_size:], -vector[..., :half_size]], axis=-1)


def norm_statistics(values):
    average = jnp.mean(values, axis=-1, keepdims=True)
    centred = values - average
    inverse = lax.rsqrt(jnp.mean(centred * centred, axis=-1, keepdims=True) + norm_eps)
    return (centred * inverse, inverse)


def norm_backward_pass(scaled, normalized, inverse):
    return inverse * (
        scaled
        - jnp.mean(scaled, axis=-1, keepdims=True)
        - normalized * jnp.mean(scaled * normalized, axis=-1, keepdims=True)
    )


def attend(rotated_query, rotated_key, value_reduced_precision, sequence_segment):
    scores = batched("thd,shd->hts", rotated_query, rotated_key)
    allowed = sequence_segment[:, None] == sequence_segment[None, :]
    scores = jnp.where(allowed[None], scores, -jnp.inf)
    logarithm_totals = jax.nn.logsumexp(scores, axis=-1)
    weights = jnp.exp(scores - logarithm_totals[..., None]).astype(jnp.bfloat16)
    attended = batched("hts,shd->thd", weights, value_reduced_precision).astype(jnp.bfloat16)
    return (attended, logarithm_totals)


def attend_back(
    rotated_query,
    rotated_key,
    value_reduced_precision,
    sequence_segment,
    logarithm_totals,
    grad_attended,
):
    scores = batched("thd,shd->hts", rotated_query, rotated_key)
    allowed = sequence_segment[:, None] == sequence_segment[None, :]
    scores = jnp.where(allowed[None], scores, -jnp.inf)
    probs_full = jnp.exp(scores - logarithm_totals[..., None])
    weights = probs_full.astype(jnp.bfloat16)
    grad_value = batched("hts,thd->shd", weights, grad_attended)
    grad_probs = batched("thd,shd->hts", grad_attended, value_reduced_precision)
    row_delta = jnp.sum(probs_full * grad_probs, axis=-1, keepdims=True)
    grad_scores = (probs_full * (grad_probs - row_delta)).astype(jnp.bfloat16)
    grad_query = batched("hts,shd->thd", grad_scores, rotated_key)
    grad_key = batched("hts,thd->shd", grad_scores, rotated_query)
    return (grad_query, grad_key, grad_value)


def tie(*values):
    return lax.optimization_barrier(values)


def wide(value):
    return value.astype(jnp.float32)


def low(value):
    return value.astype(jnp.bfloat16)


def swap(value, distance):
    count = lax.axis_size("rep")
    return lax.ppermute(value, "rep", [(k, k ^ distance) for k in range(count)])


def rep_gather(block):
    across = swap(block, 2)
    beside = swap(rows([block, across]), 1)
    return rows([block, beside[: block.shape[0]], across, beside[block.shape[0] :]])


def rep_scatter(partial):
    blocks = split_rows(low(partial), 4)
    beside = split_rows(swap(rows([blocks[1], blocks[3]]), 1), 2)
    kept = wide(blocks[0]) + wide(beside[0])
    sent = low(wide(blocks[2]) + wide(beside[1]))
    return kept + wide(swap(sent, 2))


def rep_exchange(value):
    count = lax.axis_size("rep")
    blocks = value.reshape(count, value.shape[0] // count, value.shape[1])
    return lax.all_to_all(blocks, "rep", 0, 0, tiled=True).reshape(value.shape)


class Ring:
    def __init__(self):
        self.index = lax.axis_index("fsdp")
        self.z, self.x = self.index // 2, self.index % 2

    def up(self, value):
        return lax.ppermute(value, "fsdp", [(k, (k + 2) % 8) for k in range(8)])

    def down(self, value):
        return lax.ppermute(value, "fsdp", [(k, (k - 2) % 8) for k in range(8)])

    def over(self, value):
        return lax.ppermute(value, "fsdp", [(k, k ^ 1) for k in range(8)])

    def relative(self, blocks):
        flip = self.x == 1
        blocks = [jnp.where(flip, blocks[k ^ 1], blocks[k]) for k in range(8)]
        for bit in (1, 2):
            turn = (self.z & bit) != 0
            blocks = [jnp.where(turn, blocks[(k + 2 * bit) % 8], blocks[k]) for k in range(8)]
        return [blocks[2 * ((p + 1) % 4) + i] for i in range(2) for p in range(4)]

    def absolute(self, blocks):
        blocks = [blocks[4 * i + (j - 1) % 4] for j in range(4) for i in range(2)]
        flip = self.x == 1
        blocks = [jnp.where(flip, blocks[k ^ 1], blocks[k]) for k in range(8)]
        for bit in (1, 2):
            turn = (self.z & bit) != 0
            blocks = [jnp.where(turn, blocks[(k - 2 * bit) % 8], blocks[k]) for k in range(8)]
        return blocks


class Plain:
    def __init__(self):
        self.count = lax.axis_size("fsdp")

    def relative(self, blocks):
        return blocks

    absolute = relative

    def gather(self, own):
        return list(lax.all_gather(own, "fsdp", axis=0))

    def scatter(self, term):
        return lax.psum_scatter(term, "fsdp", scatter_dimension=0, tiled=True)


def split_columns(value, count):
    width = value.shape[1] // count
    return [value[:, k * width : (k + 1) * width] for k in range(count)]


def split_rows(value, count):
    width = value.shape[0] // count
    return [value[k * width : (k + 1) * width] for k in range(count)]


def columns(blocks):
    return jnp.concatenate(blocks, axis=1)


def rows(blocks):
    return jnp.concatenate(blocks, axis=0)


def local(
    tokens,
    seq_lengths,
    cotangent,
    attention_norm_gain,
    w_qkv,
    w_attn_out,
    feedforward_norm_gain,
    w_in,
    w_out,
):
    row_count, width = tokens.shape
    fsdp_count, rep_count = lax.axis_size("fsdp"), lax.axis_size("rep")
    ringed = fsdp_count == 8
    ring = Ring() if ringed else Plain()
    hidden = w_in.shape[1] // 2
    hidden_own = hidden // rep_count
    head_count = width // HEAD_DIM // rep_count
    own_width = head_count * HEAD_DIM
    block = rep_count * w_qkv.shape[0]

    def relative(value):
        return columns(ring.relative(split_columns(value, fsdp_count)))

    def absolute(value):
        return columns(ring.absolute(split_columns(value, fsdp_count)))

    gain_attn = wide(attention_norm_gain)[:, None]
    gain_mlp = wide(feedforward_norm_gain)[:, None]
    order = [
        (k, (k % fsdp_count) * rep_count + k // fsdp_count) for k in range(fsdp_count * rep_count)
    ]
    lengths = rows([seq_lengths] + [swap(seq_lengths, k) for k in range(1, rep_count)])
    attn_own = lax.ppermute(w_attn_out, AXES, order)
    qkv_parts = split_columns(low(wide(w_qkv) * gain_attn), 3 * rep_count)
    qkv_own = rep_exchange(
        rows([columns(qkv_parts[k::rep_count]) for k in range(rep_count)])
    )
    first_own = columns([qkv_own, rows(split_columns(attn_own, rep_count))])

    in_parts = split_columns(low(wide(w_in) * gain_mlp), 2 * rep_count)
    out_parts = split_columns(w_out, rep_count)
    rest = rows(
        [columns([*in_parts[k::rep_count], out_parts[k]]) for k in range(rep_count)]
    )
    mine = rows([relative(tokens), relative(cotangent)])
    first_own, rest, mine, lengths = tie(first_own, rest, mine, lengths)
    rest = rep_exchange(rest)
    in_own, out_own = rest[:, : 2 * hidden_own], rest[:, 2 * hidden_own :]
    across = swap(mine, 2)

    if ringed:
        third, first, other = ring.up(first_own), ring.down(first_own), ring.over(first_own)
        third, first, other, in_own, out_own, across = tie(
            third, first, other, in_own, out_own, across
        )
        second, others = ring.up(third), ring.over(rows([first, third]))
        out_pair = rows([out_own, ring.over(out_own)])
    beside = swap(rows([mine, across]), 1)
    if ringed:
        second, out_pair, beside, in_own = tie(second, out_pair, beside, in_own)
        other_second = ring.over(second)
        in_third, in_first = ring.up(in_own), ring.down(in_own)
        others, other_second = tie(others, other_second)
        in_other = ring.over(tie(in_own, other_second)[0])
        other_first, other_third = split_rows(others, 2)
        first_blocks = [
            first, second, third, first_own, other_first, other_second, other_third, other,
        ]
    else:
        first_blocks = ring.gather(first_own)
        in_blocks = ring.gather(in_own)
        out_blocks = ring.gather(out_own)
        w_up, w_down = rows(in_blocks), rows(out_blocks)
    x_own, cot_own = split_rows(mine, 2)
    across = split_rows(across, 2)
    beside = split_rows(beside, 4)
    x_low = rows([x_own, beside[0], across[0], beside[2]])
    cot = rows([cot_own, beside[1], across[1], beside[3]])
    qkv = rows([piece[:, : 3 * own_width] for piece in first_blocks])
    attn = relative(
        rows(
            ring.absolute(
                [columns(split_rows(piece[:, 3 * own_width :], rep_count)) for piece in first_blocks]
            )
        )
    )

    sequence_segment, positions, valid = jax.vmap(
        lambda row_lengths: layout(row_lengths, row_count)
    )(lengths)
    cosine, sine = rotary(positions, HEAD_DIM)
    cosine, sine = cosine[:, :, None, :], sine[:, :, None, :]
    live = valid.reshape(rep_count * row_count, 1)

    standard, inverse = norm_statistics(wide(x_low))
    normed = low(standard)
    packed = matmul(normed, qkv)
    if ringed:
        packed, in_third, in_first, in_other = tie(packed, in_third, in_first, in_other)
        in_second, in_others = ring.up(in_third), ring.over(rows([in_first, in_third]))
    packed = packed.reshape(rep_count, row_count, 3, head_count, HEAD_DIM)
    query, key = packed[:, :, 0], packed[:, :, 1]
    query = low((query * cosine + rotate_half(query) * sine) * HEAD_DIM ** (-0.5))
    key = low(key * cosine + rotate_half(key) * sine)
    value = low(packed[:, :, 2])
    attended, totals = jax.vmap(attend)(query, key, value, sequence_segment)
    attended = attended.reshape(rep_count * row_count, own_width)
    if ringed:
        attended, in_second, out_pair = tie(attended, in_second, out_pair)
        in_other_second = ring.over(in_second)
        out_third, out_first = ring.up(out_pair), ring.down(out_pair)
        attended, in_others = tie(attended, in_others)
    partial_hidden = matmul(attended, attn)
    hidden_sum = wide(x_own) + rep_scatter(partial_hidden)
    if ringed:
        hidden_sum, out_third, out_first = tie(hidden_sum, out_third, out_first)
        out_second = ring.up(out_third)
        in_other_first, in_other_third = split_rows(in_others, 2)
        in_blocks = [
            in_first, in_second, in_third, in_own,
            in_other_first, in_other_second, in_other_third, in_other,
        ]
        w_up = rows(in_blocks)
    standard_mlp, inverse_mlp = norm_statistics(hidden_sum)
    normed_mlp = rep_gather(low(standard_mlp))
    inner = matmul(normed_mlp, w_up)
    gate, up = inner[:, :hidden_own], inner[:, hidden_own:]
    phi = 0.5 * (1.0 + lax.erf(gate * 0.7071067811865476))
    activation = gate * phi
    mixed = low(activation * up)
    slope = phi + gate * jnp.exp(-0.5 * gate * gate) * 0.3989422804014327
    grad_out = jnp.where(live, cot, jnp.zeros((), cot.dtype))

    term_out = low(matmul_left_t(grad_out, mixed))
    if ringed:
        out_pairs = [
            wide(rows([mine_, its]))
            for mine_, its in zip(*(split_rows(half, 4) for half in split_rows(term_out, 2)))
        ]
        out_up, out_down = ring.up(low(out_pairs[1])), ring.down(low(out_pairs[2]))
        out_halves = [
            split_rows(piece, 2) for piece in (out_first, out_second, out_third, out_pair)
        ]
        w_down = rows([piece[0] for piece in out_halves] + [piece[1] for piece in out_halves])

    grad_mixed = matmul(grad_out, w_down)
    grad_inner = low(columns([grad_mixed * up * slope, grad_mixed * activation]))
    partial_mlp = matmul_right_t(grad_inner, w_up)
    if ringed:
        partial_mlp, out_up, out_down = tie(partial_mlp, out_up, out_down)
        out_turned = ring.up(low(out_pairs[0] + wide(out_up)))
    scaled_mlp = rep_scatter(partial_mlp)
    term_in = low(matmul_left_t(normed_mlp, grad_inner))
    if ringed:
        in_sent = split_rows(split_rows(term_in, 2)[1], 2)
        in_sent_early, in_sent_late = ring.over(in_sent[0]), ring.over(in_sent[1])
        scaled_mlp, out_turned = tie(scaled_mlp, out_turned)
        out_sums = split_rows(out_pairs[3] + wide(out_turned) + wide(out_down), 2)
        out_over = ring.over(low(out_sums[1]))
    grad_hidden = wide(grad_out[:row_count]) + norm_backward_pass(
        scaled_mlp, standard_mlp, inverse_mlp
    )
    grad_low = rep_gather(low(grad_hidden))
    if ringed:
        grad_low, in_sent_early, out_over = tie(grad_low, in_sent_early, out_over)
        in_kept = [wide(piece) for piece in split_rows(split_rows(term_in, 2)[0], 4)]
        in_early = split_rows(in_sent_early, 2)
        in_up = ring.up(low(in_kept[1] + wide(in_early[1])))

    grad_attended = low(matmul_right_t(grad_low, attn))
    grad_query, grad_key, grad_value = jax.vmap(attend_back)(
        query,
        key,
        value,
        sequence_segment,
        totals,
        grad_attended.reshape(rep_count, row_count, head_count, HEAD_DIM),
    )
    grad_query = grad_query * HEAD_DIM ** (-0.5)
    grad_query = grad_query * cosine + rotate_back(grad_query * sine)
    grad_key = grad_key * cosine + rotate_back(grad_key * sine)
    grad_packed = jnp.stack([grad_query, grad_key, grad_value], axis=2)
    grad_packed = low(grad_packed.reshape(rep_count * row_count, 3 * own_width))
    term_qkv = low(matmul_left_t(normed, grad_packed))
    if ringed:
        term_qkv, in_up, in_sent_late = tie(term_qkv, in_up, in_sent_late)
        in_late = split_rows(in_sent_late, 2)
        qkv_sent = split_rows(split_rows(term_qkv, 2)[1], 2)
        qkv_sent_early, qkv_sent_late = ring.over(qkv_sent[0]), ring.over(qkv_sent[1])
        in_turned = ring.up(low(in_kept[0] + wide(in_early[0]) + wide(in_up)))
        in_down = ring.down(low(in_kept[2] + wide(in_late[0])))
    partial_attn = matmul_right_t(grad_packed, qkv)
    term_attn = absolute(low(matmul_left_t(attended, grad_low)))
    term_attn = rows(ring.relative(split_rows(term_attn, fsdp_count)))
    if ringed:
        attn_pairs = [
            wide(rows([mine_, its]))
            for mine_, its in zip(*(split_rows(half, 4) for half in split_rows(term_attn, 2)))
        ]
        in_turned, in_down, attn_pairs, partial_attn = tie(
            in_turned, in_down, attn_pairs, partial_attn
        )
        sum_in = in_kept[3] + wide(in_late[1]) + wide(in_turned) + wide(in_down)
        attn_up, attn_down = ring.up(low(attn_pairs[1])), ring.down(low(attn_pairs[2]))
        sum_out = out_sums[0] + wide(out_over)
        qkv_sent_early, attn_up, attn_down = tie(qkv_sent_early, attn_up, attn_down)
        qkv_kept = [wide(piece) for piece in split_rows(split_rows(term_qkv, 2)[0], 4)]
        qkv_early = split_rows(qkv_sent_early, 2)
        qkv_up = ring.up(low(qkv_kept[1] + wide(qkv_early[1])))
        attn_turned = ring.up(low(attn_pairs[0] + wide(attn_up)))
        qkv_sent_late, qkv_up, attn_turned = tie(qkv_sent_late, qkv_up, attn_turned)
        qkv_late = split_rows(qkv_sent_late, 2)
        qkv_turned = ring.up(low(qkv_kept[0] + wide(qkv_early[0]) + wide(qkv_up)))
        qkv_down = ring.down(low(qkv_kept[2] + wide(qkv_late[0])))
        attn_sums = split_rows(attn_pairs[3] + wide(attn_turned) + wide(attn_down), 2)
        sum_attn = attn_sums[0] + wide(ring.over(low(attn_sums[1])))
        sum_qkv = qkv_kept[3] + wide(qkv_late[1]) + wide(qkv_turned) + wide(qkv_down)
    else:
        sum_in, sum_out, sum_attn, sum_qkv = (
            ring.scatter(wide(term)) for term in (term_in, term_out, term_attn, term_qkv)
        )
    scaled_attn = rep_scatter(partial_attn)
    block_input_gradient = grad_hidden + norm_backward_pass(
        scaled_attn, standard[:row_count], inverse[:row_count]
    )
    mlp_result = rep_scatter(matmul_right_t(mixed, w_down))
    output = low(jnp.where(live[:row_count], hidden_sum + mlp_result, 0.0))

    back = rep_exchange(columns([low(sum_in), low(sum_out)]))
    back_qkv = rep_exchange(low(sum_qkv))
    back = [split_columns(piece, 3) for piece in split_rows(back, rep_count)]
    back_qkv = [split_columns(piece, 3) for piece in split_rows(back_qkv, rep_count)]
    unit_qkv = wide(columns([piece[part] for part in range(3) for piece in back_qkv]))
    unit_in = wide(columns([piece[part] for part in range(2) for piece in back]))
    grad_w_out = wide(columns([piece[2] for piece in back]))
    grad_w_attn_out = wide(
        lax.ppermute(low(sum_attn), AXES, [(there, here) for here, there in order])
    )
    return (
        absolute(output),
        absolute(block_input_gradient),
        jnp.sum(unit_qkv * wide(w_qkv), axis=1),
        unit_qkv * gain_attn,
        grad_w_attn_out,
        jnp.sum(unit_in * wide(w_in), axis=1),
        unit_in * gain_mlp,
        grad_w_out,
    )


def solution(mesh):
    return jax.shard_map(
        local,
        mesh=mesh,
        in_specs=(
            P(AXES, None),
            P(AXES, None),
            P(AXES, None),
            P(AXES),
            P(AXES, None),
            P(AXES, None),
            P(AXES),
            P(AXES, None),
            P(AXES, None),
        ),
        out_specs=(
            P(AXES, None),
            P(AXES, None),
            P(AXES),
            P(AXES, None),
            P(AXES, None),
            P(AXES),
            P(AXES, None),
            P(AXES, None),
        ),
        check_vma=False,
    )
```

```python
import jax
import jax.numpy as jnp
from jax import lax
from jax.experimental import pallas as pl
from jax.experimental.pallas import tpu as pltpu
from jax.sharding import PartitionSpec as P

HEAD_DIM = 64


norm_eps = 1e-05
rope_base = 160000.0


def matmul(left_side, right_side):
    return jnp.dot(left_side, right_side, preferred_element_type=jnp.float32)


def matmul_right_t(left_side, right_side):
    return lax.dot_general(
        left_side, right_side, (((1,), (1,)), ((), ())), preferred_element_type=jnp.float32
    )


def matmul_left_t(left_side, right_side):
    return lax.dot_general(
        left_side, right_side, (((0,), (0,)), ((), ())), preferred_element_type=jnp.float32
    )


def batched(form, left_side, right_side):
    return jnp.einsum(form, left_side, right_side, preferred_element_type=jnp.float32)


def layout(lengths, row_count):
    slot_ids = lax.iota(jnp.int32, lengths.shape[0])
    before = (slot_ids[:, None] <= slot_ids[None, :]).astype(jnp.int32)
    ends = jnp.sum(lengths[:, None] * before, axis=0)
    starts = ends - lengths
    places = lax.iota(jnp.int32, row_count)
    sequence_segment = jnp.sum((ends[None, :] <= places[:, None]).astype(jnp.int32), axis=1)
    first_row = jnp.sum(
        jnp.where(sequence_segment[:, None] == slot_ids[None, :], starts[None, :], 0), axis=1
    )
    return (sequence_segment, places - first_row, sequence_segment < lengths.shape[0])


def rotary(positions, head_size):
    half_size = head_size // 2
    frequency = rope_base ** (-(lax.iota(jnp.float32, half_size) * (2.0 / head_size)))
    angles = positions.astype(jnp.float32)[..., None] * frequency
    cosine_table = jnp.concatenate([jnp.cos(angles), jnp.cos(angles)], axis=-1)
    sine_table = jnp.concatenate([jnp.sin(angles), jnp.sin(angles)], axis=-1)
    return (cosine_table, sine_table)


def rotate_half(vector):
    half_size = vector.shape[-1] // 2
    return jnp.concatenate([-vector[..., half_size:], vector[..., :half_size]], axis=-1)


def rotate_back(vector):
    half_size = vector.shape[-1] // 2
    return jnp.concatenate([vector[..., half_size:], -vector[..., :half_size]], axis=-1)


def norm_statistics(values):
    average = jnp.mean(values, axis=-1, keepdims=True)
    centred = values - average
    inverse = lax.rsqrt(jnp.mean(centred * centred, axis=-1, keepdims=True) + norm_eps)
    return (centred * inverse, inverse)


def norm_backward_pass(grad_normed, gain_vec, normalized, inverse):
    scaled = grad_normed * gain_vec.astype(jnp.float32)
    return inverse * (
        scaled
        - jnp.mean(scaled, axis=-1, keepdims=True)
        - normalized * jnp.mean(scaled * normalized, axis=-1, keepdims=True)
    )


def attend(rotated_query, rotated_key, value_reduced_precision, sequence_segment):
    scores = batched("thd,shd->hts", rotated_query, rotated_key)
    allowed = sequence_segment[:, None] == sequence_segment[None, :]
    scores = jnp.where(allowed[None], scores, -jnp.inf)
    logarithm_totals = jax.nn.logsumexp(scores, axis=-1)
    weights = jnp.exp(scores - logarithm_totals[..., None]).astype(jnp.bfloat16)
    attended = batched("hts,shd->thd", weights, value_reduced_precision).astype(jnp.bfloat16)
    return (attended, logarithm_totals)


def attend_back(
    rotated_query,
    rotated_key,
    value_reduced_precision,
    sequence_segment,
    logarithm_totals,
    grad_attended,
):
    scores = batched("thd,shd->hts", rotated_query, rotated_key)
    allowed = sequence_segment[:, None] == sequence_segment[None, :]
    scores = jnp.where(allowed[None], scores, -jnp.inf)
    probs_full = jnp.exp(scores - logarithm_totals[..., None])
    weights = probs_full.astype(jnp.bfloat16)
    grad_value = batched("hts,thd->shd", weights, grad_attended)
    grad_probs = batched("thd,shd->hts", grad_attended, value_reduced_precision)
    row_delta = jnp.sum(probs_full * grad_probs, axis=-1, keepdims=True)
    grad_scores = (probs_full * (grad_probs - row_delta)).astype(jnp.bfloat16)
    grad_query = batched("hts,shd->thd", grad_scores, rotated_key)
    grad_key = batched("hts,thd->shd", grad_scores, rotated_query)
    return (grad_query, grad_key, grad_value)


def forward(
    tokens, lengths, attention_norm_gain, w_qkv, w_attn_out, feedforward_norm_gain, w_in, w_out
):
    groups, row_count, embedding_width = tokens.shape
    head_count = embedding_width // HEAD_DIM
    hidden_units = w_in.shape[1] // 2
    sequence_segment, positions, valid = jax.vmap(
        lambda row_lengths: layout(row_lengths, row_count)
    )(lengths)
    cosine_table, sine_table = rotary(positions, HEAD_DIM)
    cosine_table = cosine_table[:, :, None, :]
    sine_table = sine_table[:, :, None, :]
    residual_input = tokens.reshape(groups * row_count, embedding_width).astype(jnp.float32)
    attention_standardized, attention_inverse_norm = norm_statistics(residual_input)
    attention_normed_input = (
        attention_standardized * attention_norm_gain.astype(jnp.float32)
    ).astype(jnp.bfloat16)
    packed = matmul(attention_normed_input, w_qkv).reshape(
        groups, row_count, 3, head_count, HEAD_DIM
    )
    query_raw = packed[:, :, 0]
    key_raw = packed[:, :, 1]
    rotated_query = (
        (query_raw * cosine_table + rotate_half(query_raw) * sine_table) * HEAD_DIM ** (-0.5)
    ).astype(jnp.bfloat16)
    rotated_key = (key_raw * cosine_table + rotate_half(key_raw) * sine_table).astype(jnp.bfloat16)
    value_reduced_precision = packed[:, :, 2].astype(jnp.bfloat16)
    attended, logarithm_totals = jax.vmap(attend)(
        rotated_query, rotated_key, value_reduced_precision, sequence_segment
    )
    attention_rows_flat = attended.reshape(groups * row_count, embedding_width)
    hidden_residual = residual_input + matmul(attention_rows_flat, w_attn_out)
    feedforward_standardized, feedforward_inverse_norm = norm_statistics(hidden_residual)
    feedforward_normed_input = (
        feedforward_standardized * feedforward_norm_gain.astype(jnp.float32)
    ).astype(jnp.bfloat16)
    inner_proj = matmul(feedforward_normed_input, w_in)
    gate_projection = inner_proj[:, :hidden_units]
    up_projection = inner_proj[:, hidden_units:]
    activation_output = jax.nn.gelu(gate_projection, approximate=False)
    mixed_input = (activation_output * up_projection).astype(jnp.bfloat16)
    live_token_rows = valid.reshape(groups * row_count, 1)
    mlp_result = matmul_right_t(mixed_input, w_out)
    output = jnp.where(live_token_rows, hidden_residual + mlp_result, 0.0).astype(jnp.bfloat16)
    saved_residuals = (
        sequence_segment,
        live_token_rows,
        cosine_table,
        sine_table,
        attention_standardized,
        attention_inverse_norm,
        attention_normed_input,
        rotated_query,
        rotated_key,
        value_reduced_precision,
        logarithm_totals,
        attention_rows_flat,
        feedforward_standardized,
        feedforward_inverse_norm,
        feedforward_normed_input,
        gate_projection,
        up_projection,
        activation_output,
        mixed_input,
    )
    return (output, saved_residuals)


def backward(
    saved_residuals,
    cotangent,
    attention_norm_gain,
    w_qkv,
    w_attn_out,
    feedforward_norm_gain,
    w_in,
    w_out,
):
    (
        sequence_segment,
        live_token_rows,
        cosine_table,
        sine_table,
        attention_standardized,
        attention_inverse_norm,
        attention_normed_input,
        rotated_query,
        rotated_key,
        value_reduced_precision,
        logarithm_totals,
        attention_rows_flat,
        feedforward_standardized,
        feedforward_inverse_norm,
        feedforward_normed_input,
        gate_projection,
        up_projection,
        activation_output,
        mixed_input,
    ) = saved_residuals
    groups, row_count = sequence_segment.shape
    embedding_width = attention_standardized.shape[1]
    head_count = embedding_width // HEAD_DIM
    flat_cot = cotangent.reshape(groups * row_count, embedding_width)
    output_gradient = jnp.where(live_token_rows, flat_cot, jnp.zeros((), flat_cot.dtype))
    grad_mixed = matmul(output_gradient, w_out)
    slope = (
        0.5 * (1.0 + lax.erf(gate_projection * 0.7071067811865476))
        + gate_projection * jnp.exp(-0.5 * gate_projection * gate_projection) * 0.3989422804014327
    )
    grad_inner = jnp.concatenate(
        [grad_mixed * up_projection * slope, grad_mixed * activation_output], axis=1
    ).astype(jnp.bfloat16)
    feedforward_normed_gradient = matmul_right_t(grad_inner, w_in)
    hidden_gradient = output_gradient.astype(jnp.float32) + norm_backward_pass(
        feedforward_normed_gradient,
        feedforward_norm_gain,
        feedforward_standardized,
        feedforward_inverse_norm,
    )
    grad_hidden_low = hidden_gradient.astype(jnp.bfloat16)
    grad_attended = matmul_right_t(grad_hidden_low, w_attn_out).astype(jnp.bfloat16)
    grad_attended = grad_attended.reshape(groups, row_count, head_count, HEAD_DIM)
    grad_query, grad_key, grad_value = jax.vmap(attend_back)(
        rotated_query,
        rotated_key,
        value_reduced_precision,
        sequence_segment,
        logarithm_totals,
        grad_attended,
    )
    grad_query = grad_query * HEAD_DIM ** (-0.5)
    grad_query = grad_query * cosine_table + rotate_back(grad_query * sine_table)
    grad_key = grad_key * cosine_table + rotate_back(grad_key * sine_table)
    grad_packed = jnp.stack([grad_query, grad_key, grad_value], axis=2)
    grad_packed = grad_packed.reshape(groups * row_count, 3 * embedding_width).astype(jnp.bfloat16)
    attention_normed_gradient = matmul_right_t(grad_packed, w_qkv)
    block_input_gradient = hidden_gradient + norm_backward_pass(
        attention_normed_gradient,
        attention_norm_gain,
        attention_standardized,
        attention_inverse_norm,
    )
    factors = (
        attention_normed_input,
        grad_packed,
        attention_rows_flat,
        grad_hidden_low,
        feedforward_normed_input,
        grad_inner,
        output_gradient,
        mixed_input,
        attention_normed_gradient,
        attention_standardized,
        feedforward_normed_gradient,
        feedforward_standardized,
    )
    return (block_input_gradient, factors)


def local_plain(
    tokens,
    seq_lengths,
    cotangent,
    attention_norm_gain,
    w_qkv,
    w_attn_out,
    feedforward_norm_gain,
    w_in,
    w_out,
):
    row_count, embedding_width = tokens.shape
    gathered = (
        lax.all_gather(attention_norm_gain, ("fsdp", "rep"), axis=0, tiled=True),
        lax.all_gather(w_qkv, ("fsdp", "rep"), axis=0, tiled=True),
        lax.all_gather(w_attn_out, ("fsdp", "rep"), axis=0, tiled=True),
        lax.all_gather(feedforward_norm_gain, ("fsdp", "rep"), axis=0, tiled=True),
        lax.all_gather(w_in, ("fsdp", "rep"), axis=0, tiled=True),
        lax.all_gather(w_out, ("fsdp", "rep"), axis=0, tiled=True),
    )
    output, saved_residuals = forward(
        tokens.reshape(1, row_count, embedding_width),
        seq_lengths,
        gathered[0],
        gathered[1],
        gathered[2],
        gathered[3],
        gathered[4],
        gathered[5],
    )
    second_copy = (
        lax.all_gather(attention_norm_gain, ("fsdp", "rep"), axis=0, tiled=True),
        lax.all_gather(w_qkv, ("fsdp", "rep"), axis=0, tiled=True),
        lax.all_gather(w_attn_out, ("fsdp", "rep"), axis=0, tiled=True),
        lax.all_gather(feedforward_norm_gain, ("fsdp", "rep"), axis=0, tiled=True),
        lax.all_gather(w_in, ("fsdp", "rep"), axis=0, tiled=True),
        lax.all_gather(w_out, ("fsdp", "rep"), axis=0, tiled=True),
    )
    block_input_gradient, factors = backward(
        saved_residuals,
        cotangent.reshape(1, row_count, embedding_width),
        second_copy[0],
        second_copy[1],
        second_copy[2],
        second_copy[3],
        second_copy[4],
        second_copy[5],
    )
    (
        normed_attn,
        grad_packed,
        attended_rows,
        grad_hidden_low,
        normed_mlp,
        grad_inner,
        grad_out,
        mixed_input,
        grad_normed_attn,
        standard_attn,
        grad_normed_mlp,
        standard_mlp,
    ) = factors
    qkv_width = w_qkv.shape[1]
    attn_width = w_attn_out.shape[1]
    inner_width = w_in.shape[1]
    outer_width = w_out.shape[1]
    qkv_term = matmul_left_t(normed_attn, grad_packed)
    attn_term = matmul_left_t(attended_rows, grad_hidden_low)
    inner_term = matmul_left_t(normed_mlp, grad_inner)
    outer_term = matmul_left_t(grad_out, mixed_input)
    attn_gain_term = jnp.sum(grad_normed_attn * standard_attn, axis=0)
    mlp_gain_term = jnp.sum(grad_normed_mlp * standard_mlp, axis=0)
    summed = lax.psum_scatter(
        jnp.concatenate(
            [
                qkv_term,
                attn_term,
                inner_term,
                outer_term,
                attn_gain_term[:, None],
                mlp_gain_term[:, None],
            ],
            axis=1,
        ),
        ("fsdp", "rep"),
        scatter_dimension=0,
        tiled=True,
    )
    edge_two = qkv_width + attn_width
    edge_three = edge_two + inner_width
    edge_four = edge_three + outer_width
    return (
        output,
        block_input_gradient,
        summed[:, edge_four],
        summed[:, :qkv_width],
        summed[:, qkv_width:edge_two],
        summed[:, edge_four + 1],
        summed[:, edge_two:edge_three],
        summed[:, edge_three:edge_four],
    )


AXES = ("fsdp", "rep")
LANES = 128
HALF = HEAD_DIM // 2


def tie(*values):
    return lax.optimization_barrier(values)


def wide(value):
    return value.astype(jnp.float32)


def low(value):
    return value.astype(jnp.bfloat16)


def split_columns(value, count):
    width = value.shape[1] // count
    return [value[:, k * width : (k + 1) * width] for k in range(count)]


def split_rows(value, count):
    width = value.shape[0] // count
    return [value[k * width : (k + 1) * width] for k in range(count)]


def columns(blocks):
    return jnp.concatenate(blocks, axis=1)


def rows(blocks):
    return jnp.concatenate(blocks, axis=0)


def swap(value, distance):
    return lax.ppermute(value, "rep", [(k, k ^ distance) for k in range(4)])


def rep_exchange(value):
    blocks = value.reshape(4, value.shape[0] // 4, value.shape[1])
    return lax.all_to_all(blocks, "rep", 0, 0, tiled=True).reshape(value.shape)


def up(value):
    return lax.ppermute(value, "fsdp", [(k, (k + 2) % 8) for k in range(8)])


def down(value):
    return lax.ppermute(value, "fsdp", [(k, (k - 2) % 8) for k in range(8)])


def over(value):
    return lax.ppermute(value, "fsdp", [(k, k ^ 1) for k in range(8)])


def relative(value, z, x):
    blocks = split_columns(value, 8)
    blocks = [jnp.where(x == 1, blocks[k ^ 1], blocks[k]) for k in range(8)]
    for bit in (1, 2):
        turn = (z & bit) != 0
        blocks = [jnp.where(turn, blocks[(k + 2 * bit) % 8], blocks[k]) for k in range(8)]
    return columns([blocks[2 * ((p + 1) % 4) + i] for i in range(2) for p in range(4)])


def absolute(value, z, x):
    blocks = split_columns(value, 8)
    blocks = [blocks[4 * i + (j - 1) % 4] for j in range(4) for i in range(2)]
    blocks = [jnp.where(x == 1, blocks[k ^ 1], blocks[k]) for k in range(8)]
    for bit in (1, 2):
        turn = (z & bit) != 0
        blocks = [jnp.where(turn, blocks[(k - 2 * bit) % 8], blocks[k]) for k in range(8)]
    return columns(blocks)


def place_of(place, step, side):
    z, x = place[0], place[1]
    return 2 * lax.rem(z + step + 1, 4) + (x if side == 0 else 1 - x)


def block_of(place, z_at, side):
    z, x = place[0], place[1]
    return 4 * (x if side == 0 else 1 - x) + lax.rem(z_at - z + 7, 4)


def turned(value):
    width = value.shape[1]
    lane = lax.broadcasted_iota(jnp.int32, value.shape, 1)
    return jnp.where(
        lane % HEAD_DIM < HALF,
        pltpu.roll(value, width - HALF, 1),
        pltpu.roll(value, HALF, 1),
    )


def head_masks(row_count):
    lane = lax.broadcasted_iota(jnp.int32, (row_count, LANES), 1)
    return [low(wide(lane < HEAD_DIM)), low(wide(lane >= HEAD_DIM))], lane < HEAD_DIM


def token_rows(mine, across, beside, first, step):
    count = 128
    return [
        mine[first : first + count],
        beside[first : first + count],
        across[first : first + count],
        beside[step + first : step + first + count],
    ]


def attention_forward(
    place, seg_col, seg_row, cosine, sine, mine, across, beside,
    first, second, third, own, others, other_second, other,
    normed, qkv, attn, query, key, value, probs, attended, send, keep,
):
    size = own.shape[0]
    blocks = [
        (first, 0), (second, 0), (third, 0), (own, 0),
        (others, 0), (other_second, 0), (others, size), (other, 0),
    ]
    part = size // 4
    for at, (ref, row) in enumerate(blocks):
        qkv[size * at : size * (at + 1), :] = ref[row : row + size, :768]
        target = pl.multiple_of(place_of(place, at % 4, at // 4) * part, part)
        for z_at in range(4):
            for side in range(2):
                lanes = pl.multiple_of(block_of(place, z_at, side) * LANES, LANES)
                attn[pl.ds(target, part), pl.ds(lanes, LANES)] = ref[
                    row + part * z_at : row + part * (z_at + 1),
                    768 + LANES * side : 768 + LANES * (side + 1),
                ]
    count = 128
    for at, ref in enumerate(token_rows(mine, across, beside, 0, mine.shape[0])):
        values = wide(ref)
        centred = values - jnp.mean(values, axis=1, keepdims=True)
        inverse = lax.rsqrt(jnp.mean(centred * centred, axis=1, keepdims=True) + norm_eps)
        normed[count * at : count * (at + 1), :] = low(centred * inverse)
    packed = matmul(normed[...], qkv[...])
    cos_all, sin_all = columns([cosine[...]] * 2), columns([sine[...]] * 2)
    raw = packed[:, :256]
    query[...] = low((raw * cos_all + turned(raw) * sin_all) * HEAD_DIM ** (-0.5))
    raw = packed[:, 256:512]
    key[...] = low(raw * cos_all + turned(raw) * sin_all)
    value[...] = low(packed[:, 512:])
    masks, is_first = head_masks(count)
    for at in range(4):
        here = slice(count * at, count * (at + 1))
        allowed = seg_col[here, :] == seg_row[at : at + 1, :]
        for pair in range(2):
            lanes = slice(LANES * pair, LANES * (pair + 1))
            made = []
            for head in range(2):
                scores = matmul_right_t(query[here, lanes] * masks[head], key[here, lanes])
                scores = jnp.where(allowed, scores, -jnp.inf)
                powers = jnp.exp(scores - jnp.max(scores, axis=1, keepdims=True))
                weights = powers / jnp.sum(powers, axis=1, keepdims=True)
                slot = count * (4 * at + 2 * pair + head)
                probs[slot : slot + count, :] = weights
                made.append(matmul(low(weights), value[here, lanes]))
            attended[here, lanes] = low(jnp.where(is_first, made[0], made[1]))
    total = low(matmul(attended[...], attn[...]))
    keep[:count, :], send[:count, :] = total[:count], total[count : 2 * count]
    keep[count:, :], send[count:, :] = total[2 * count : 3 * count], total[3 * count :]


def mlp(
    seg_col, norm_own, norm_across, norm_beside, mine, across, beside,
    first, second, third, own, others, other_second, other,
    out_first, out_second, out_third, out_own,
    normed, grad_out, mixed, grad_inner, send, keep,
    w_up, w_down, inner, grad_mixed,
):
    size, count = own.shape[0], 128
    blocks = [
        (first, 0), (second, 0), (third, 0), (own, 0),
        (others, 0), (other_second, 0), (others, size), (other, 0),
    ]
    for at, (ref, row) in enumerate(blocks):
        w_up[size * at : size * (at + 1), :] = ref[row : row + size, :]
    for at, ref in enumerate((out_first, out_second, out_third, out_own)):
        w_down[size * at : size * (at + 1), :] = ref[:size, :]
        w_down[size * (at + 4) : size * (at + 5), :] = ref[size:, :]
    for at, ref in enumerate(
        (norm_own[...], norm_beside[:count, :], norm_across[...], norm_beside[count:, :])
    ):
        normed[count * at : count * (at + 1), :] = ref
    for at, ref in enumerate(token_rows(mine, across, beside, count, mine.shape[0])):
        live = wide(seg_col[count * at : count * (at + 1), :] < 8)
        grad_out[count * at : count * (at + 1), :] = low(wide(ref) * live)
    inner[...] = matmul(normed[...], w_up[...])
    grad_mixed[...] = matmul(grad_out[...], w_down[...])
    main = (w_down.shape[1] // LANES - 1) * LANES
    rest = 16

    def parts(gate):
        phi = 0.5 * (1.0 + lax.erf(gate * 0.7071067811865476))
        slope = phi + gate * jnp.exp(-0.5 * gate * gate) * 0.3989422804014327
        return gate * phi, slope

    @pl.loop(0, 8)
    def _(step):
        here = pl.ds(pl.multiple_of(step * 64, 64), 64)
        gate, up_part = inner[here, :main], inner[here, main : 2 * main]
        grad = grad_mixed[here, :main]
        activation, slope = parts(gate)
        mixed[here, :main] = low(activation * up_part)
        grad_inner[here, :main] = low(grad * up_part * slope)
        grad_inner[here, main : 2 * main] = low(grad * activation)
        tail = inner[here, 2 * main :]
        grad = grad_mixed[here, main:]
        activation, slope = parts(tail)
        tail_up = pltpu.roll(tail, LANES - rest, 1)
        mixed[here, main:] = low(activation * tail_up)
        grad_inner[here, 2 * main :] = low(
            grad * tail_up * slope + pltpu.roll(grad * activation, rest, 1)
        )

    total = low(matmul_right_t(grad_inner[...], w_up[...]))
    keep[:count, :], send[:count, :] = total[:count], total[count : 2 * count]
    keep[count:, :], send[count:, :] = total[2 * count : 3 * count], total[3 * count :]


def mlp_terms(
    normed, grad_inner, grad_out, mixed,
    in_keep, in_early, in_late, out_first, out_second, out_third, out_own,
):
    term = low(matmul_left_t(normed[...], grad_inner[...]))
    half, quarter = term.shape[0] // 2, term.shape[0] // 4
    in_keep[...] = term[:half]
    in_early[...] = term[half : half + quarter]
    in_late[...] = term[half + quarter :]
    term = low(matmul_left_t(grad_out[...], mixed[...]))
    size = term.shape[0] // 8
    for at, ref in enumerate((out_first, out_second, out_third, out_own)):
        ref[:size, :] = term[size * at : size * (at + 1)]
        ref[size:, :] = term[size * (at + 4) : size * (at + 5)]


def attention_backward(
    place, cosine, sine, low_own, low_across, low_beside, attn, query, key, value, probs,
    attended, normed,
    grad_packed, g_keep, g_early, g_late, grad_low, grad_attended, term_attn,
):
    count = 128
    for at, ref in enumerate(
        (low_own[...], low_beside[:count, :], low_across[...], low_beside[count:, :])
    ):
        grad_low[count * at : count * (at + 1), :] = ref
    grad_attended[...] = low(matmul_right_t(grad_low[...], attn[...]))
    masks, is_first = head_masks(count)
    for at in range(4):
        here = slice(count * at, count * (at + 1))
        cos, sin = cosine[here, :], sine[here, :]
        for pair in range(2):
            lanes = slice(LANES * pair, LANES * (pair + 1))
            q, k, v = query[here, lanes], key[here, lanes], value[here, lanes]
            grad = grad_attended[here, lanes]
            made = []
            for head in range(2):
                slot = count * (4 * at + 2 * pair + head)
                weights = probs[slot : slot + count, :]
                grad_value = matmul_left_t(low(weights), grad)
                grad_probs = matmul_right_t(grad * masks[head], v)
                delta = jnp.sum(weights * grad_probs, axis=1, keepdims=True)
                grad_scores = low(weights * (grad_probs - delta))
                made.append((matmul(grad_scores, k), matmul_left_t(grad_scores, q), grad_value))
            grad_q, grad_k, grad_v = (jnp.where(is_first, *both) for both in zip(*made))
            grad_q = grad_q * HEAD_DIM ** (-0.5)
            grad_packed[here, lanes] = low(grad_q * cos - turned(grad_q) * sin)
            lanes = slice(256 + LANES * pair, 256 + LANES * (pair + 1))
            grad_packed[here, lanes] = low(grad_k * cos - turned(grad_k) * sin)
            lanes = slice(512 + LANES * pair, 512 + LANES * (pair + 1))
            grad_packed[here, lanes] = low(grad_v)
    term = low(matmul_left_t(normed[...], grad_packed[...]))
    half, quarter = term.shape[0] // 2, term.shape[0] // 4
    g_keep[:, :768] = term[:half]
    g_early[:, :768] = term[half : half + quarter]
    g_late[:, :768] = term[half + quarter :]
    term_attn[...] = low(matmul_left_t(attended[...], grad_low[...]))
    size = term.shape[0] // 8
    part = size // 4
    targets = [(g_keep, size * p) for p in range(4)]
    targets += [(g_early, 0), (g_early, size), (g_late, 0), (g_late, size)]
    for at, (ref, row) in enumerate(targets):
        source = pl.multiple_of(place_of(place, at % 4, at // 4) * part, part)
        for z_at in range(4):
            for side in range(2):
                lanes = pl.multiple_of(block_of(place, z_at, side) * LANES, LANES)
                ref[
                    row + part * z_at : row + part * (z_at + 1),
                    768 + LANES * side : 768 + LANES * (side + 1),
                ] = term_attn[pl.ds(source, part), pl.ds(lanes, LANES)]


def projections(
    grad_packed, qkv, mixed, out_first, out_second, out_third, out_own, send, keep, w_down
):
    size, count = out_own.shape[0] // 2, 128
    for at, ref in enumerate((out_first, out_second, out_third, out_own)):
        w_down[size * at : size * (at + 1), :] = ref[:size, :]
        w_down[size * (at + 4) : size * (at + 5), :] = ref[size:, :]
    for row, total in (
        (0, low(matmul_right_t(grad_packed[...], qkv[...]))),
        (count, low(matmul_right_t(mixed[...], w_down[...]))),
    ):
        keep[row : row + count, :] = total[:count]
        send[row : row + count, :] = total[count : 2 * count]
        keep[2 * count + row : 3 * count + row, :] = total[2 * count : 3 * count]
        send[2 * count + row : 3 * count + row, :] = total[3 * count :]


def kernel(body, outs, cost, *args, scratch=(), scalars=0):
    flops, transcendentals = cost
    shapes = [jax.ShapeDtypeStruct(shape, kind) for shape, kind in outs]
    moved = sum(arg.size * arg.dtype.itemsize for arg in (*args, *shapes))
    return pl.pallas_call(
        body,
        out_shape=shapes,
        in_specs=[
            pl.BlockSpec(memory_space=pltpu.SMEM if k < scalars else pltpu.VMEM)
            for k in range(len(args))
        ],
        out_specs=[pl.BlockSpec(memory_space=pltpu.VMEM)] * len(shapes),
        scratch_shapes=[pltpu.VMEM(shape, kind) for shape, kind in scratch],
        compiler_params=pltpu.CompilerParams(vmem_limit_bytes=48 * 2**20),
        cost_estimate=pl.CostEstimate(
            flops=flops, bytes_accessed=moved, transcendentals=transcendentals
        ),
        name=body.__name__,
    )(*args)


def scatter_last(send, keep):
    beside = split_rows(swap(send, 1), 2)
    kept = split_rows(keep, 2)
    sent = low(wide(kept[1]) + wide(beside[1]))
    return wide(kept[0]) + wide(beside[0]), sent


def local_ring(
    tokens,
    seq_lengths,
    cotangent,
    attention_norm_gain,
    w_qkv,
    w_attn_out,
    feedforward_norm_gain,
    w_in,
    w_out,
):
    count, width = tokens.shape
    index = lax.axis_index("fsdp")
    z, x = index // 2, index % 2
    place = jnp.stack([z, x]).astype(jnp.int32)
    hidden = w_in.shape[1] // 2
    part = hidden // 4
    main = part // LANES * LANES
    in_width, out_width = 2 * main + LANES, main + LANES
    f32, b16 = jnp.float32, jnp.bfloat16
    group = 4 * count

    gain_attn = wide(attention_norm_gain)[:, None]
    gain_mlp = wide(feedforward_norm_gain)[:, None]
    order = [(k, (k % 8) * 4 + k // 8) for k in range(32)]
    attn_own = lax.ppermute(w_attn_out, AXES, order)
    qkv_parts = split_columns(low(wide(w_qkv) * gain_attn), 12)
    qkv_own = rep_exchange(rows([columns(qkv_parts[k::4]) for k in range(4)]))
    first_own = columns([qkv_own, rows(split_columns(attn_own, 4))])

    scaled_in = low(wide(w_in) * gain_mlp)
    pieces = []
    for k in range(4):
        gate = scaled_in[:, part * k : part * (k + 1)]
        up_part = scaled_in[:, hidden + part * k : hidden + part * (k + 1)]
        out_part = w_out[:, part * k : part * (k + 1)]
        fill = [jnp.zeros((w_in.shape[0], n), b16) for n in (in_width - 2 * part, out_width - part)]
        pieces.append(
            columns(
                [gate[:, :main], up_part[:, :main], gate[:, main:], up_part[:, main:], fill[0]]
                + [out_part, fill[1]]
            )
        )
    lengths_row = jnp.pad(low(wide(seq_lengths)), ((0, 15), (0, width - seq_lengths.shape[1])))
    mine = rows([relative(tokens, z, x), relative(cotangent, z, x), lengths_row])
    first_own, rest, mine = tie(first_own, rows(pieces), mine)
    rest = rep_exchange(rest)
    in_own, out_own = rest[:, :in_width], rest[:, in_width:]
    across = swap(mine, 2)

    third, first, other = up(first_own), down(first_own), over(first_own)
    third, first, other = tie(third, first, other)
    second, others = up(third), over(rows([first, third]))
    beside = swap(rows([mine, across]), 1)
    second, in_own, out_own = tie(second, in_own, out_own)
    other_second = over(second)
    in_third, in_first = up(in_own), down(in_own)
    out_pair = rows([out_own, over(tie(out_own, others)[0])])

    step = mine.shape[0]
    lengths = rows(
        [mine[2 * count : 2 * count + 1], beside[2 * count : 2 * count + 1]]
        + [across[2 * count : 2 * count + 1], beside[step + 2 * count : step + 2 * count + 1]]
    )[:, : seq_lengths.shape[1]].astype(jnp.int32)
    segment, positions, _ = jax.vmap(lambda row: layout(row, count))(lengths)
    frequency = rope_base ** (-(lax.iota(f32, HALF) * (2.0 / HEAD_DIM)))
    angles = positions.reshape(group, 1).astype(f32) * frequency
    cosine, sine = jnp.cos(angles), jnp.sin(angles)
    cosine, sine = columns([cosine] * 4), columns([-sine, sine] * 2)
    seg_col = segment.reshape(group, 1)

    normed, qkv, attn, query, key, value, probs, attended, send, keep = kernel(
        attention_forward,
        [((group, width), b16), ((width, 768), b16), ((256, width), b16)]
        + [((group, 256), b16)] * 3
        + [((16 * count, count), f32), ((group, 256), b16)]
        + [((2 * count, width), b16)] * 2,
        (2 * group * width * (768 + 256) + 4 * 16 * count * count * LANES, 16 * count * count),
        place, seg_col, segment, cosine, sine, mine, across, beside,
        first, second, third, first_own, others, other_second, other,
        scalars=1,
    )
    in_third, in_first, _ = tie(in_third, in_first, send)
    in_second, in_others = up(in_third), over(rows([in_first, in_third]))
    in_other = over(tie(in_own, send)[0])
    x_own = wide(mine[:count])
    kept, sent = scatter_last(send, keep)
    in_second, out_pair, _ = tie(in_second, out_pair, sent)
    in_other_second = over(in_second)
    out_third, out_first = up(out_pair), down(out_pair)
    hidden_sum = x_own + kept + wide(swap(sent, 2))
    standard_mlp, inverse_mlp = norm_statistics(hidden_sum)
    norm_own = low(standard_mlp)
    norm_across = swap(norm_own, 2)
    out_third, out_first, _ = tie(out_third, out_first, norm_own)
    out_second = up(out_third)
    norm_beside = swap(rows([norm_own, norm_across]), 1)

    normed_mlp, grad_out, mixed, grad_inner, send, keep = kernel(
        mlp,
        [((group, width), b16)] * 2
        + [((group, out_width), b16), ((group, in_width), b16)]
        + [((2 * count, width), b16)] * 2,
        (2 * group * width * (2 * in_width + out_width), 3 * group * part),
        seg_col, norm_own, norm_across, norm_beside, mine, across, beside,
        in_first, in_second, in_third, in_own, in_others, in_other_second, in_other,
        out_first, out_second, out_third, out_pair,
        scratch=[
            ((width, in_width), b16),
            ((width, out_width), b16),
            ((group, in_width), f32),
            ((group, out_width), f32),
        ],
    )
    in_keep, in_early, in_late, *out_terms = kernel(
        mlp_terms,
        [((width // 2, in_width), b16)]
        + [((width // 4, in_width), b16)] * 2
        + [((width // 4, out_width), b16)] * 4,
        (2 * group * width * (in_width + out_width), 0),
        normed_mlp, grad_inner, grad_out, mixed,
    )
    out_up, out_down = up(out_terms[1]), down(out_terms[2])
    in_early, in_late = over(in_early), over(in_late)
    kept, sent = scatter_last(send, keep)
    scaled_mlp = kept + wide(swap(sent, 2))
    grad_hidden = wide(grad_out[:count]) + norm_backward_pass(
        scaled_mlp, jnp.ones((), f32), standard_mlp, inverse_mlp
    )
    low_own = low(grad_hidden)
    low_across = swap(low_own, 2)
    out_up, out_down, _ = tie(out_up, out_down, low_own)
    out_turned = up(low(wide(out_terms[0]) + wide(out_up)))
    low_beside = swap(rows([low_own, low_across]), 1)
    in_early, out_turned, low_beside = tie(in_early, out_turned, low_beside)
    in_kept, in_first_two = split_rows(in_keep, 4), split_rows(in_early, 2)
    in_up = up(low(wide(in_kept[1]) + wide(in_first_two[1])))
    out_sums = split_rows(wide(out_terms[3]) + wide(out_turned) + wide(out_down), 2)
    out_over = over(low(out_sums[1]))

    grad_packed, g_keep, g_early, g_late = kernel(
        attention_backward,
        [((group, 768), b16), ((width // 2, width), b16)] + [((width // 4, width), b16)] * 2,
        (2 * group * width * (768 + 512) + 10 * 16 * count * count * LANES, 0),
        place, cosine, sine, low_own, low_across, low_beside, attn, query, key, value, probs,
        attended, normed,
        scratch=[((group, width), b16), ((group, 256), b16), ((256, width), b16)],
        scalars=1,
    )
    g_over_early, g_over_late = over(g_early), over(g_late)
    in_late, in_up, _ = tie(in_late, in_up, g_keep)
    in_last_two = split_rows(in_late, 2)
    in_turned = up(low(wide(in_kept[0]) + wide(in_first_two[0]) + wide(in_up)))
    in_down = down(low(wide(in_kept[2]) + wide(in_last_two[0])))
    send, keep = kernel(
        projections,
        [((4 * count, width), b16)] * 2,
        (2 * group * width * (768 + out_width), 0),
        grad_packed, qkv, mixed, out_first, out_second, out_third, out_pair,
        scratch=[((width, out_width), b16)],
    )
    g_over_early, in_turned, in_down = tie(g_over_early, in_turned, in_down)
    g_kept, g_first_two = split_rows(g_keep, 4), split_rows(g_over_early, 2)
    g_up = up(low(wide(g_kept[1]) + wide(g_first_two[1])))
    sum_in = wide(in_kept[3]) + wide(in_last_two[1]) + wide(in_turned) + wide(in_down)
    sum_out = out_sums[0] + wide(out_over)
    back = rep_exchange(columns([low(sum_in), low(sum_out)]))
    g_over_late, g_up = tie(g_over_late, g_up)
    g_last_two = split_rows(g_over_late, 2)
    g_turned = up(low(wide(g_kept[0]) + wide(g_first_two[0]) + wide(g_up)))
    g_down = down(low(wide(g_kept[2]) + wide(g_last_two[0])))
    kept, sent = scatter_last(send, keep)
    last = kept + wide(swap(sent, 2))
    sum_g = low(wide(g_kept[3]) + wide(g_last_two[1]) + wide(g_turned) + wide(g_down))
    back_qkv = rep_exchange(sum_g[:, :768])
    grad_w_attn_out = wide(
        lax.ppermute(
            columns(split_rows(sum_g[:, 768:], 4)), AXES, [(there, here) for here, there in order]
        )
    )

    standard, inverse = norm_statistics(x_own)
    block_input_gradient = grad_hidden + norm_backward_pass(
        last[:count], jnp.ones((), f32), standard, inverse
    )
    output = low(jnp.where(seg_col[:count] < 8, hidden_sum + last[count:], 0.0))
    back = split_rows(back, 4)
    back_qkv = [split_columns(piece, 3) for piece in split_rows(back_qkv, 4)]
    unit_qkv = wide(columns([piece[k] for k in range(3) for piece in back_qkv]))
    rest_width = part - main
    unit_in = wide(
        columns(
            [
                value
                for k in range(2)
                for piece in back
                for value in (
                    piece[:, main * k : main * (k + 1)],
                    piece[:, 2 * main + rest_width * k : 2 * main + rest_width * (k + 1)],
                )
            ]
        )
    )
    grad_w_out = wide(columns([piece[:, in_width : in_width + part] for piece in back]))
    return (
        absolute(output, z, x),
        absolute(block_input_gradient, z, x),
        jnp.sum(unit_qkv * wide(w_qkv), axis=1),
        unit_qkv * gain_attn,
        grad_w_attn_out,
        jnp.sum(unit_in * wide(w_in), axis=1),
        unit_in * gain_mlp,
        grad_w_out,
    )


def solution(mesh):
    ringed = dict(mesh.shape) == {"fsdp": 8, "rep": 4}
    return jax.shard_map(
        local_ring if ringed else local_plain,
        mesh=mesh,
        in_specs=(
            P(AXES, None),
            P(AXES, None),
            P(AXES, None),
            P(AXES),
            P(AXES, None),
            P(AXES, None),
            P(AXES),
            P(AXES, None),
            P(AXES, None),
        ),
        out_specs=(
            P(AXES, None),
            P(AXES, None),
            P(AXES),
            P(AXES, None),
            P(AXES, None),
            P(AXES),
            P(AXES, None),
            P(AXES, None),
        ),
        check_vma=False,
    )
```

```python
import jax
import jax.numpy as jnp
from jax import lax
from jax.experimental import pallas as pl
from jax.experimental.pallas import tpu as pltpu
from jax.sharding import PartitionSpec as P

HEAD_DIM = 64


norm_eps = 1e-05
rope_base = 160000.0


def matmul(left_side, right_side):
    return jnp.dot(left_side, right_side, preferred_element_type=jnp.float32)


def matmul_right_t(left_side, right_side):
    return lax.dot_general(
        left_side, right_side, (((1,), (1,)), ((), ())), preferred_element_type=jnp.float32
    )


def matmul_left_t(left_side, right_side):
    return lax.dot_general(
        left_side, right_side, (((0,), (0,)), ((), ())), preferred_element_type=jnp.float32
    )


def batched(form, left_side, right_side):
    return jnp.einsum(form, left_side, right_side, preferred_element_type=jnp.float32)


def layout(lengths, row_count):
    slot_ids = lax.iota(jnp.int32, lengths.shape[0])
    before = (slot_ids[:, None] <= slot_ids[None, :]).astype(jnp.int32)
    ends = jnp.sum(lengths[:, None] * before, axis=0)
    starts = ends - lengths
    places = lax.iota(jnp.int32, row_count)
    sequence_segment = jnp.sum((ends[None, :] <= places[:, None]).astype(jnp.int32), axis=1)
    first_row = jnp.sum(
        jnp.where(sequence_segment[:, None] == slot_ids[None, :], starts[None, :], 0), axis=1
    )
    return (sequence_segment, places - first_row, sequence_segment < lengths.shape[0])


def rotary(positions, head_size):
    half_size = head_size // 2
    frequency = rope_base ** (-(lax.iota(jnp.float32, half_size) * (2.0 / head_size)))
    angles = positions.astype(jnp.float32)[..., None] * frequency
    cosine_table = jnp.concatenate([jnp.cos(angles), jnp.cos(angles)], axis=-1)
    sine_table = jnp.concatenate([jnp.sin(angles), jnp.sin(angles)], axis=-1)
    return (cosine_table, sine_table)


def rotate_half(vector):
    half_size = vector.shape[-1] // 2
    return jnp.concatenate([-vector[..., half_size:], vector[..., :half_size]], axis=-1)


def rotate_back(vector):
    half_size = vector.shape[-1] // 2
    return jnp.concatenate([vector[..., half_size:], -vector[..., :half_size]], axis=-1)


def norm_statistics(values):
    average = jnp.mean(values, axis=-1, keepdims=True)
    centred = values - average
    inverse = lax.rsqrt(jnp.mean(centred * centred, axis=-1, keepdims=True) + norm_eps)
    return (centred * inverse, inverse)


def norm_backward_pass(grad_normed, gain_vec, normalized, inverse):
    scaled = grad_normed * gain_vec.astype(jnp.float32)
    return inverse * (
        scaled
        - jnp.mean(scaled, axis=-1, keepdims=True)
        - normalized * jnp.mean(scaled * normalized, axis=-1, keepdims=True)
    )


def attend(rotated_query, rotated_key, value_reduced_precision, sequence_segment):
    scores = batched("thd,shd->hts", rotated_query, rotated_key)
    allowed = sequence_segment[:, None] == sequence_segment[None, :]
    scores = jnp.where(allowed[None], scores, -jnp.inf)
    logarithm_totals = jax.nn.logsumexp(scores, axis=-1)
    weights = jnp.exp(scores - logarithm_totals[..., None]).astype(jnp.bfloat16)
    attended = batched("hts,shd->thd", weights, value_reduced_precision).astype(jnp.bfloat16)
    return (attended, logarithm_totals)


def attend_back(
    rotated_query,
    rotated_key,
    value_reduced_precision,
    sequence_segment,
    logarithm_totals,
    grad_attended,
):
    scores = batched("thd,shd->hts", rotated_query, rotated_key)
    allowed = sequence_segment[:, None] == sequence_segment[None, :]
    scores = jnp.where(allowed[None], scores, -jnp.inf)
    probs_full = jnp.exp(scores - logarithm_totals[..., None])
    weights = probs_full.astype(jnp.bfloat16)
    grad_value = batched("hts,thd->shd", weights, grad_attended)
    grad_probs = batched("thd,shd->hts", grad_attended, value_reduced_precision)
    row_delta = jnp.sum(probs_full * grad_probs, axis=-1, keepdims=True)
    grad_scores = (probs_full * (grad_probs - row_delta)).astype(jnp.bfloat16)
    grad_query = batched("hts,shd->thd", grad_scores, rotated_key)
    grad_key = batched("hts,thd->shd", grad_scores, rotated_query)
    return (grad_query, grad_key, grad_value)


def forward(
    tokens, lengths, attention_norm_gain, w_qkv, w_attn_out, feedforward_norm_gain, w_in, w_out
):
    groups, row_count, embedding_width = tokens.shape
    head_count = embedding_width // HEAD_DIM
    hidden_units = w_in.shape[1] // 2
    sequence_segment, positions, valid = jax.vmap(
        lambda row_lengths: layout(row_lengths, row_count)
    )(lengths)
    cosine_table, sine_table = rotary(positions, HEAD_DIM)
    cosine_table = cosine_table[:, :, None, :]
    sine_table = sine_table[:, :, None, :]
    residual_input = tokens.reshape(groups * row_count, embedding_width).astype(jnp.float32)
    attention_standardized, attention_inverse_norm = norm_statistics(residual_input)
    attention_normed_input = (
        attention_standardized * attention_norm_gain.astype(jnp.float32)
    ).astype(jnp.bfloat16)
    packed = matmul(attention_normed_input, w_qkv).reshape(
        groups, row_count, 3, head_count, HEAD_DIM
    )
    query_raw = packed[:, :, 0]
    key_raw = packed[:, :, 1]
    rotated_query = (
        (query_raw * cosine_table + rotate_half(query_raw) * sine_table) * HEAD_DIM ** (-0.5)
    ).astype(jnp.bfloat16)
    rotated_key = (key_raw * cosine_table + rotate_half(key_raw) * sine_table).astype(jnp.bfloat16)
    value_reduced_precision = packed[:, :, 2].astype(jnp.bfloat16)
    attended, logarithm_totals = jax.vmap(attend)(
        rotated_query, rotated_key, value_reduced_precision, sequence_segment
    )
    attention_rows_flat = attended.reshape(groups * row_count, embedding_width)
    hidden_residual = residual_input + matmul(attention_rows_flat, w_attn_out)
    feedforward_standardized, feedforward_inverse_norm = norm_statistics(hidden_residual)
    feedforward_normed_input = (
        feedforward_standardized * feedforward_norm_gain.astype(jnp.float32)
    ).astype(jnp.bfloat16)
    inner_proj = matmul(feedforward_normed_input, w_in)
    gate_projection = inner_proj[:, :hidden_units]
    up_projection = inner_proj[:, hidden_units:]
    activation_output = jax.nn.gelu(gate_projection, approximate=False)
    mixed_input = (activation_output * up_projection).astype(jnp.bfloat16)
    live_token_rows = valid.reshape(groups * row_count, 1)
    mlp_result = matmul_right_t(mixed_input, w_out)
    output = jnp.where(live_token_rows, hidden_residual + mlp_result, 0.0).astype(jnp.bfloat16)
    saved_residuals = (
        sequence_segment,
        live_token_rows,
        cosine_table,
        sine_table,
        attention_standardized,
        attention_inverse_norm,
        attention_normed_input,
        rotated_query,
        rotated_key,
        value_reduced_precision,
        logarithm_totals,
        attention_rows_flat,
        feedforward_standardized,
        feedforward_inverse_norm,
        feedforward_normed_input,
        gate_projection,
        up_projection,
        activation_output,
        mixed_input,
    )
    return (output, saved_residuals)


def backward(
    saved_residuals,
    cotangent,
    attention_norm_gain,
    w_qkv,
    w_attn_out,
    feedforward_norm_gain,
    w_in,
    w_out,
):
    (
        sequence_segment,
        live_token_rows,
        cosine_table,
        sine_table,
        attention_standardized,
        attention_inverse_norm,
        attention_normed_input,
        rotated_query,
        rotated_key,
        value_reduced_precision,
        logarithm_totals,
        attention_rows_flat,
        feedforward_standardized,
        feedforward_inverse_norm,
        feedforward_normed_input,
        gate_projection,
        up_projection,
        activation_output,
        mixed_input,
    ) = saved_residuals
    groups, row_count = sequence_segment.shape
    embedding_width = attention_standardized.shape[1]
    head_count = embedding_width // HEAD_DIM
    flat_cot = cotangent.reshape(groups * row_count, embedding_width)
    output_gradient = jnp.where(live_token_rows, flat_cot, jnp.zeros((), flat_cot.dtype))
    grad_mixed = matmul(output_gradient, w_out)
    slope = (
        0.5 * (1.0 + lax.erf(gate_projection * 0.7071067811865476))
        + gate_projection * jnp.exp(-0.5 * gate_projection * gate_projection) * 0.3989422804014327
    )
    grad_inner = jnp.concatenate(
        [grad_mixed * up_projection * slope, grad_mixed * activation_output], axis=1
    ).astype(jnp.bfloat16)
    feedforward_normed_gradient = matmul_right_t(grad_inner, w_in)
    hidden_gradient = output_gradient.astype(jnp.float32) + norm_backward_pass(
        feedforward_normed_gradient,
        feedforward_norm_gain,
        feedforward_standardized,
        feedforward_inverse_norm,
    )
    grad_hidden_low = hidden_gradient.astype(jnp.bfloat16)
    grad_attended = matmul_right_t(grad_hidden_low, w_attn_out).astype(jnp.bfloat16)
    grad_attended = grad_attended.reshape(groups, row_count, head_count, HEAD_DIM)
    grad_query, grad_key, grad_value = jax.vmap(attend_back)(
        rotated_query,
        rotated_key,
        value_reduced_precision,
        sequence_segment,
        logarithm_totals,
        grad_attended,
    )
    grad_query = grad_query * HEAD_DIM ** (-0.5)
    grad_query = grad_query * cosine_table + rotate_back(grad_query * sine_table)
    grad_key = grad_key * cosine_table + rotate_back(grad_key * sine_table)
    grad_packed = jnp.stack([grad_query, grad_key, grad_value], axis=2)
    grad_packed = grad_packed.reshape(groups * row_count, 3 * embedding_width).astype(jnp.bfloat16)
    attention_normed_gradient = matmul_right_t(grad_packed, w_qkv)
    block_input_gradient = hidden_gradient + norm_backward_pass(
        attention_normed_gradient,
        attention_norm_gain,
        attention_standardized,
        attention_inverse_norm,
    )
    factors = (
        attention_normed_input,
        grad_packed,
        attention_rows_flat,
        grad_hidden_low,
        feedforward_normed_input,
        grad_inner,
        output_gradient,
        mixed_input,
        attention_normed_gradient,
        attention_standardized,
        feedforward_normed_gradient,
        feedforward_standardized,
    )
    return (block_input_gradient, factors)


def local_plain(
    tokens,
    seq_lengths,
    cotangent,
    attention_norm_gain,
    w_qkv,
    w_attn_out,
    feedforward_norm_gain,
    w_in,
    w_out,
):
    row_count, embedding_width = tokens.shape
    gathered = (
        lax.all_gather(attention_norm_gain, ("fsdp", "rep"), axis=0, tiled=True),
        lax.all_gather(w_qkv, ("fsdp", "rep"), axis=0, tiled=True),
        lax.all_gather(w_attn_out, ("fsdp", "rep"), axis=0, tiled=True),
        lax.all_gather(feedforward_norm_gain, ("fsdp", "rep"), axis=0, tiled=True),
        lax.all_gather(w_in, ("fsdp", "rep"), axis=0, tiled=True),
        lax.all_gather(w_out, ("fsdp", "rep"), axis=0, tiled=True),
    )
    output, saved_residuals = forward(
        tokens.reshape(1, row_count, embedding_width),
        seq_lengths,
        gathered[0],
        gathered[1],
        gathered[2],
        gathered[3],
        gathered[4],
        gathered[5],
    )
    second_copy = (
        lax.all_gather(attention_norm_gain, ("fsdp", "rep"), axis=0, tiled=True),
        lax.all_gather(w_qkv, ("fsdp", "rep"), axis=0, tiled=True),
        lax.all_gather(w_attn_out, ("fsdp", "rep"), axis=0, tiled=True),
        lax.all_gather(feedforward_norm_gain, ("fsdp", "rep"), axis=0, tiled=True),
        lax.all_gather(w_in, ("fsdp", "rep"), axis=0, tiled=True),
        lax.all_gather(w_out, ("fsdp", "rep"), axis=0, tiled=True),
    )
    block_input_gradient, factors = backward(
        saved_residuals,
        cotangent.reshape(1, row_count, embedding_width),
        second_copy[0],
        second_copy[1],
        second_copy[2],
        second_copy[3],
        second_copy[4],
        second_copy[5],
    )
    (
        normed_attn,
        grad_packed,
        attended_rows,
        grad_hidden_low,
        normed_mlp,
        grad_inner,
        grad_out,
        mixed_input,
        grad_normed_attn,
        standard_attn,
        grad_normed_mlp,
        standard_mlp,
    ) = factors
    qkv_width = w_qkv.shape[1]
    attn_width = w_attn_out.shape[1]
    inner_width = w_in.shape[1]
    outer_width = w_out.shape[1]
    qkv_term = matmul_left_t(normed_attn, grad_packed)
    attn_term = matmul_left_t(attended_rows, grad_hidden_low)
    inner_term = matmul_left_t(normed_mlp, grad_inner)
    outer_term = matmul_left_t(grad_out, mixed_input)
    attn_gain_term = jnp.sum(grad_normed_attn * standard_attn, axis=0)
    mlp_gain_term = jnp.sum(grad_normed_mlp * standard_mlp, axis=0)
    summed = lax.psum_scatter(
        jnp.concatenate(
            [
                qkv_term,
                attn_term,
                inner_term,
                outer_term,
                attn_gain_term[:, None],
                mlp_gain_term[:, None],
            ],
            axis=1,
        ),
        ("fsdp", "rep"),
        scatter_dimension=0,
        tiled=True,
    )
    edge_two = qkv_width + attn_width
    edge_three = edge_two + inner_width
    edge_four = edge_three + outer_width
    return (
        output,
        block_input_gradient,
        summed[:, edge_four],
        summed[:, :qkv_width],
        summed[:, qkv_width:edge_two],
        summed[:, edge_four + 1],
        summed[:, edge_two:edge_three],
        summed[:, edge_three:edge_four],
    )


AXES = ("fsdp", "rep")
LANES = 128
HALF = HEAD_DIM // 2


def tie(*values):
    return lax.optimization_barrier(values)


def wide(value):
    return value.astype(jnp.float32)


def low(value):
    return value.astype(jnp.bfloat16)


def split_columns(value, count):
    width = value.shape[1] // count
    return [value[:, k * width : (k + 1) * width] for k in range(count)]


def split_rows(value, count):
    width = value.shape[0] // count
    return [value[k * width : (k + 1) * width] for k in range(count)]


def columns(blocks):
    return jnp.concatenate(blocks, axis=1)


def rows(blocks):
    return jnp.concatenate(blocks, axis=0)


def swap(value, distance):
    return lax.ppermute(value, "rep", [(k, k ^ distance) for k in range(4)])


def rep_exchange(value):
    blocks = value.reshape(4, value.shape[0] // 4, value.shape[1])
    return lax.all_to_all(blocks, "rep", 0, 0, tiled=True).reshape(value.shape)


def up(value):
    return lax.ppermute(value, "fsdp", [(k, (k + 2) % 8) for k in range(8)])


def down(value):
    return lax.ppermute(value, "fsdp", [(k, (k - 2) % 8) for k in range(8)])


def over(value):
    return lax.ppermute(value, "fsdp", [(k, k ^ 1) for k in range(8)])


def relative(value, z, x):
    blocks = split_columns(value, 8)
    blocks = [jnp.where(x == 1, blocks[k ^ 1], blocks[k]) for k in range(8)]
    for bit in (1, 2):
        turn = (z & bit) != 0
        blocks = [jnp.where(turn, blocks[(k + 2 * bit) % 8], blocks[k]) for k in range(8)]
    return columns([blocks[2 * ((p + 1) % 4) + i] for i in range(2) for p in range(4)])


def absolute(value, z, x):
    blocks = split_columns(value, 8)
    blocks = [blocks[4 * i + (j - 1) % 4] for j in range(4) for i in range(2)]
    blocks = [jnp.where(x == 1, blocks[k ^ 1], blocks[k]) for k in range(8)]
    for bit in (1, 2):
        turn = (z & bit) != 0
        blocks = [jnp.where(turn, blocks[(k - 2 * bit) % 8], blocks[k]) for k in range(8)]
    return columns(blocks)


def place_of(place, step, side):
    z, x = place[0], place[1]
    return 2 * lax.rem(z + step + 1, 4) + (x if side == 0 else 1 - x)


def block_of(place, z_at, side):
    z, x = place[0], place[1]
    return 4 * (x if side == 0 else 1 - x) + lax.rem(z_at - z + 7, 4)


def turned(value):
    width = value.shape[1]
    lane = lax.broadcasted_iota(jnp.int32, value.shape, 1)
    return jnp.where(
        lane % HEAD_DIM < HALF,
        pltpu.roll(value, width - HALF, 1),
        pltpu.roll(value, HALF, 1),
    )


def head_masks(row_count):
    lane = lax.broadcasted_iota(jnp.int32, (row_count, LANES), 1)
    return [low(wide(lane < HEAD_DIM)), low(wide(lane >= HEAD_DIM))], lane < HEAD_DIM


def token_rows(mine, across, beside, first, step):
    count = 128
    return [
        mine[first : first + count],
        beside[first : first + count],
        across[first : first + count],
        beside[step + first : step + first + count],
    ]


def attention_forward(
    place, seg_col, seg_row, cosine, sine, mine, across, beside,
    first, second, third, own, others, other_second, other,
    normed, qkv, attn, query, key, value, probs, attended, send, keep,
):
    size = own.shape[0]
    blocks = [
        (first, 0), (second, 0), (third, 0), (own, 0),
        (others, 0), (other_second, 0), (others, size), (other, 0),
    ]
    part = size // 4
    for at, (ref, row) in enumerate(blocks):
        qkv[size * at : size * (at + 1), :] = ref[row : row + size, :768]
        target = pl.multiple_of(place_of(place, at % 4, at // 4) * part, part)
        for z_at in range(4):
            for side in range(2):
                lanes = pl.multiple_of(block_of(place, z_at, side) * LANES, LANES)
                attn[pl.ds(target, part), pl.ds(lanes, LANES)] = ref[
                    row + part * z_at : row + part * (z_at + 1),
                    768 + LANES * side : 768 + LANES * (side + 1),
                ]
    count = 128
    for at, ref in enumerate(token_rows(mine, across, beside, 0, mine.shape[0])):
        values = wide(ref)
        centred = values - jnp.mean(values, axis=1, keepdims=True)
        inverse = lax.rsqrt(jnp.mean(centred * centred, axis=1, keepdims=True) + norm_eps)
        normed[count * at : count * (at + 1), :] = low(centred * inverse)
    packed = matmul(normed[...], qkv[...])
    cos_all, sin_all = columns([cosine[...]] * 2), columns([sine[...]] * 2)
    raw = packed[:, :256]
    query[...] = low((raw * cos_all + turned(raw) * sin_all) * HEAD_DIM ** (-0.5))
    raw = packed[:, 256:512]
    key[...] = low(raw * cos_all + turned(raw) * sin_all)
    value[...] = low(packed[:, 512:])
    masks, is_first = head_masks(count)
    for at in range(4):
        here = slice(count * at, count * (at + 1))
        allowed = seg_col[here, :] == seg_row[at : at + 1, :]
        for pair in range(2):
            lanes = slice(LANES * pair, LANES * (pair + 1))
            made = []
            for head in range(2):
                scores = matmul_right_t(query[here, lanes] * masks[head], key[here, lanes])
                scores = jnp.where(allowed, scores, -jnp.inf)
                powers = jnp.exp(scores - jnp.max(scores, axis=1, keepdims=True))
                weights = powers / jnp.sum(powers, axis=1, keepdims=True)
                slot = count * (4 * at + 2 * pair + head)
                probs[slot : slot + count, :] = weights
                made.append(matmul(low(weights), value[here, lanes]))
            attended[here, lanes] = low(jnp.where(is_first, made[0], made[1]))
    total = low(matmul(attended[...], attn[...]))
    keep[:count, :], send[:count, :] = total[:count], total[count : 2 * count]
    keep[count:, :], send[count:, :] = total[2 * count : 3 * count], total[3 * count :]


def mlp(
    seg_col, norm_own, norm_across, norm_beside, mine, across, beside,
    first, second, third, own, other_first, other_second, other_third, other,
    normed, grad_out, mixed, grad_inner, send, keep, w_down,
    w_up, inner, grad_mixed,
):
    size, count, edge = own.shape[0], 128, w_up.shape[1]
    blocks = (first, second, third, own, other_first, other_second, other_third, other)
    for at, ref in enumerate(blocks):
        w_up[size * at : size * (at + 1), :] = ref[:, :edge]
        w_down[size * at : size * (at + 1), :] = ref[:, edge:]
    for at, ref in enumerate(
        (norm_own[...], norm_beside[:count, :], norm_across[...], norm_beside[count:, :])
    ):
        normed[count * at : count * (at + 1), :] = ref
    for at, ref in enumerate(token_rows(mine, across, beside, count, mine.shape[0])):
        live = wide(seg_col[count * at : count * (at + 1), :] < 8)
        grad_out[count * at : count * (at + 1), :] = low(wide(ref) * live)
    inner[...] = matmul(normed[...], w_up[...])
    grad_mixed[...] = matmul(grad_out[...], w_down[...])
    main = (w_down.shape[1] // LANES - 1) * LANES
    rest = 16

    def parts(gate):
        phi = 0.5 * (1.0 + lax.erf(gate * 0.7071067811865476))
        slope = phi + gate * jnp.exp(-0.5 * gate * gate) * 0.3989422804014327
        return gate * phi, slope

    @pl.loop(0, 8)
    def _(step):
        here = pl.ds(pl.multiple_of(step * 64, 64), 64)
        gate, up_part = inner[here, :main], inner[here, main : 2 * main]
        grad = grad_mixed[here, :main]
        activation, slope = parts(gate)
        mixed[here, :main] = low(activation * up_part)
        grad_inner[here, :main] = low(grad * up_part * slope)
        grad_inner[here, main : 2 * main] = low(grad * activation)
        tail = inner[here, 2 * main :]
        grad = grad_mixed[here, main:]
        activation, slope = parts(tail)
        tail_up = pltpu.roll(tail, LANES - rest, 1)
        mixed[here, main:] = low(activation * tail_up)
        grad_inner[here, 2 * main :] = low(
            grad * tail_up * slope + pltpu.roll(grad * activation, rest, 1)
        )

    total = low(matmul_right_t(grad_inner[...], w_up[...]))
    keep[:count, :], send[:count, :] = total[:count], total[count : 2 * count]
    keep[count:, :], send[count:, :] = total[2 * count : 3 * count], total[3 * count :]


def mlp_terms(
    normed, grad_inner, grad_out, mixed,
    in_keep, in_early, in_late, out_first, out_second, out_third, out_own,
):
    term = low(matmul_left_t(normed[...], grad_inner[...]))
    half, quarter = term.shape[0] // 2, term.shape[0] // 4
    in_keep[...] = term[:half]
    in_early[...] = term[half : half + quarter]
    in_late[...] = term[half + quarter :]
    term = low(matmul_left_t(grad_out[...], mixed[...]))
    size = term.shape[0] // 8
    for at, ref in enumerate((out_first, out_second, out_third, out_own)):
        ref[:size, :] = term[size * at : size * (at + 1)]
        ref[size:, :] = term[size * (at + 4) : size * (at + 5)]


def attention_backward(
    place, cosine, sine, low_own, low_across, low_beside, attn, query, key, value, probs,
    attended, normed,
    grad_packed, g_keep, g_early, g_late, grad_low, grad_attended, term_attn,
):
    count = 128
    for at, ref in enumerate(
        (low_own[...], low_beside[:count, :], low_across[...], low_beside[count:, :])
    ):
        grad_low[count * at : count * (at + 1), :] = ref
    grad_attended[...] = low(matmul_right_t(grad_low[...], attn[...]))
    masks, is_first = head_masks(count)
    for at in range(4):
        here = slice(count * at, count * (at + 1))
        cos, sin = cosine[here, :], sine[here, :]
        for pair in range(2):
            lanes = slice(LANES * pair, LANES * (pair + 1))
            q, k, v = query[here, lanes], key[here, lanes], value[here, lanes]
            grad = grad_attended[here, lanes]
            made = []
            for head in range(2):
                slot = count * (4 * at + 2 * pair + head)
                weights = probs[slot : slot + count, :]
                grad_value = matmul_left_t(low(weights), grad)
                grad_probs = matmul_right_t(grad * masks[head], v)
                delta = jnp.sum(weights * grad_probs, axis=1, keepdims=True)
                grad_scores = low(weights * (grad_probs - delta))
                made.append((matmul(grad_scores, k), matmul_left_t(grad_scores, q), grad_value))
            grad_q, grad_k, grad_v = (jnp.where(is_first, *both) for both in zip(*made))
            grad_q = grad_q * HEAD_DIM ** (-0.5)
            grad_packed[here, lanes] = low(grad_q * cos - turned(grad_q) * sin)
            lanes = slice(256 + LANES * pair, 256 + LANES * (pair + 1))
            grad_packed[here, lanes] = low(grad_k * cos - turned(grad_k) * sin)
            lanes = slice(512 + LANES * pair, 512 + LANES * (pair + 1))
            grad_packed[here, lanes] = low(grad_v)
    term = low(matmul_left_t(normed[...], grad_packed[...]))
    half, quarter = term.shape[0] // 2, term.shape[0] // 4
    g_keep[:, :768] = term[:half]
    g_early[:, :768] = term[half : half + quarter]
    g_late[:, :768] = term[half + quarter :]
    term_attn[...] = low(matmul_left_t(attended[...], grad_low[...]))
    size = term.shape[0] // 8
    part = size // 4
    targets = [(g_keep, size * p) for p in range(4)]
    targets += [(g_early, 0), (g_early, size), (g_late, 0), (g_late, size)]
    for at, (ref, row) in enumerate(targets):
        source = pl.multiple_of(place_of(place, at % 4, at // 4) * part, part)
        for z_at in range(4):
            for side in range(2):
                lanes = pl.multiple_of(block_of(place, z_at, side) * LANES, LANES)
                ref[
                    row + part * z_at : row + part * (z_at + 1),
                    768 + LANES * side : 768 + LANES * (side + 1),
                ] = term_attn[pl.ds(source, part), pl.ds(lanes, LANES)]


def projections(grad_packed, qkv, mixed, w_down, send, keep):
    count = 128
    for row, total in (
        (0, low(matmul_right_t(grad_packed[...], qkv[...]))),
        (count, low(matmul_right_t(mixed[...], w_down[...]))),
    ):
        keep[row : row + count, :] = total[:count]
        send[row : row + count, :] = total[count : 2 * count]
        keep[2 * count + row : 3 * count + row, :] = total[2 * count : 3 * count]
        send[2 * count + row : 3 * count + row, :] = total[3 * count :]


def kernel(body, outs, cost, *args, scratch=(), scalars=0):
    flops, transcendentals = cost
    shapes = [jax.ShapeDtypeStruct(shape, kind) for shape, kind in outs]
    moved = sum(arg.size * arg.dtype.itemsize for arg in (*args, *shapes))
    return pl.pallas_call(
        body,
        out_shape=shapes,
        in_specs=[
            pl.BlockSpec(memory_space=pltpu.SMEM if k < scalars else pltpu.VMEM)
            for k in range(len(args))
        ],
        out_specs=[pl.BlockSpec(memory_space=pltpu.VMEM)] * len(shapes),
        scratch_shapes=[pltpu.VMEM(shape, kind) for shape, kind in scratch],
        compiler_params=pltpu.CompilerParams(vmem_limit_bytes=48 * 2**20),
        cost_estimate=pl.CostEstimate(
            flops=flops, bytes_accessed=moved, transcendentals=transcendentals
        ),
        name=body.__name__,
    )(*args)


def scatter_last(send, keep):
    beside = split_rows(swap(send, 1), 2)
    kept = split_rows(keep, 2)
    sent = low(wide(kept[1]) + wide(beside[1]))
    return wide(kept[0]) + wide(beside[0]), sent


def local_ring(
    tokens,
    seq_lengths,
    cotangent,
    attention_norm_gain,
    w_qkv,
    w_attn_out,
    feedforward_norm_gain,
    w_in,
    w_out,
):
    count, width = tokens.shape
    index = lax.axis_index("fsdp")
    z, x = index // 2, index % 2
    place = jnp.stack([z, x]).astype(jnp.int32)
    hidden = w_in.shape[1] // 2
    part = hidden // 4
    main = part // LANES * LANES
    in_width, out_width = 2 * main + LANES, main + LANES
    f32, b16 = jnp.float32, jnp.bfloat16
    group = 4 * count

    gain_attn = wide(attention_norm_gain)[:, None]
    gain_mlp = wide(feedforward_norm_gain)[:, None]
    order = [(k, (k % 8) * 4 + k // 8) for k in range(32)]
    attn_own = lax.ppermute(w_attn_out, AXES, order)
    qkv_parts = split_columns(low(wide(w_qkv) * gain_attn), 12)
    size = w_qkv.shape[0]
    slots = seq_lengths.shape[1]
    lengths_low = jnp.pad(low(wide(seq_lengths)), ((0, size - 1), (0, LANES - slots)))
    exchanged = rep_exchange(rows([columns([*qkv_parts[k::4], lengths_low]) for k in range(4)]))
    first_own = columns([exchanged[:, :768], rows(split_columns(attn_own, 4))])
    lengths = rows([exchanged[size * k : size * k + 1, 768 : 768 + slots] for k in range(4)])
    lengths = wide(lengths).astype(jnp.int32)
    for bit in (1, 2):
        turned_rows = rows([lengths[k ^ bit : (k ^ bit) + 1] for k in range(4)])
        lengths = jnp.where((lax.axis_index("rep") & bit) != 0, turned_rows, lengths)

    scaled_in = low(wide(w_in) * gain_mlp)
    pieces = []
    for k in range(4):
        gate = scaled_in[:, part * k : part * (k + 1)]
        up_part = scaled_in[:, hidden + part * k : hidden + part * (k + 1)]
        out_part = w_out[:, part * k : part * (k + 1)]
        fill = [jnp.zeros((w_in.shape[0], n), b16) for n in (in_width - 2 * part, out_width - part)]
        pieces.append(
            columns(
                [gate[:, :main], up_part[:, :main], gate[:, main:], up_part[:, main:], fill[0]]
                + [out_part, fill[1]]
            )
        )
    mine = rows([relative(tokens, z, x), relative(cotangent, z, x)])
    first_own, rest, mine = tie(first_own, rows(pieces), mine)
    rest = rep_exchange(rest)

    third, first, other = up(first_own), down(first_own), over(first_own)
    third, first, other, mine = tie(third, first, other, mine)
    across = swap(mine, 2)
    second, others = up(third), over(rows([first, third]))
    second, others, across, rest = tie(second, others, across, rest)
    other_second = over(second)
    rest_third, rest_first = up(rest), down(rest)
    beside = swap(rows([mine, across]), 1)
    rest_other = over(tie(rest, other_second, beside)[0])

    step = mine.shape[0]
    segment, positions, _ = jax.vmap(lambda row: layout(row, count))(lengths)
    frequency = rope_base ** (-(lax.iota(f32, HALF) * (2.0 / HEAD_DIM)))
    angles = positions.reshape(group, 1).astype(f32) * frequency
    cosine, sine = jnp.cos(angles), jnp.sin(angles)
    cosine, sine = columns([cosine] * 4), columns([-sine, sine] * 2)
    seg_col = segment.reshape(group, 1)

    normed, qkv, attn, query, key, value, probs, attended, send, keep = kernel(
        attention_forward,
        [((group, width), b16), ((width, 768), b16), ((256, width), b16)]
        + [((group, 256), b16)] * 3
        + [((16 * count, count), f32), ((group, 256), b16)]
        + [((2 * count, width), b16)] * 2,
        (2 * group * width * (768 + 256) + 4 * 16 * count * count * LANES, 16 * count * count),
        place, seg_col, segment, cosine, sine, mine, across, beside,
        first, second, third, first_own, others, other_second, other,
        scalars=1,
    )
    rest_third, rest_first, rest_other, send = tie(rest_third, rest_first, rest_other, send)
    rest_second, rest_other_third = up(rest_third), over(rest_third)
    x_own = wide(mine[:count])
    kept, sent = scatter_last(send, keep)
    rest_other_first = over(tie(rest_first, rest_other_third)[0])
    hidden_sum = x_own + kept + wide(swap(sent, 2))
    standard_mlp, inverse_mlp = norm_statistics(hidden_sum)
    norm_own = low(standard_mlp)
    norm_across = swap(norm_own, 2)
    rest_second, rest_other_third, _ = tie(rest_second, rest_other_third, norm_own)
    rest_other_second = up(rest_other_third)
    norm_beside = swap(rows([norm_own, norm_across]), 1)

    normed_mlp, grad_out, mixed, grad_inner, send, keep, w_down = kernel(
        mlp,
        [((group, width), b16)] * 2
        + [((group, out_width), b16), ((group, in_width), b16)]
        + [((2 * count, width), b16)] * 2
        + [((width, out_width), b16)],
        (2 * group * width * (2 * in_width + out_width), 3 * group * part),
        seg_col, norm_own, norm_across, norm_beside, mine, across, beside,
        rest_first, rest_second, rest_third, rest,
        rest_other_first, rest_other_second, rest_other_third, rest_other,
        scratch=[
            ((width, in_width), b16),
            ((group, in_width), f32),
            ((group, out_width), f32),
        ],
    )
    in_keep, in_early, in_late, *out_terms = kernel(
        mlp_terms,
        [((width // 2, in_width), b16)]
        + [((width // 4, in_width), b16)] * 2
        + [((width // 4, out_width), b16)] * 4,
        (2 * group * width * (in_width + out_width), 0),
        normed_mlp, grad_inner, grad_out, mixed,
    )
    out_up, out_down = up(out_terms[1]), down(out_terms[2])
    in_early = over(in_early)
    kept, sent = scatter_last(send, keep)
    scaled_mlp = kept + wide(swap(sent, 2))
    grad_hidden = wide(grad_out[:count]) + norm_backward_pass(
        scaled_mlp, jnp.ones((), f32), standard_mlp, inverse_mlp
    )
    low_own = low(grad_hidden)
    low_across = swap(low_own, 2)
    in_early, low_across, out_up, out_down = tie(in_early, low_across, out_up, out_down)
    in_late = over(tie(in_late, in_early)[0])
    low_beside = swap(rows([low_own, low_across]), 1)
    in_kept, in_first_two = split_rows(in_keep, 4), split_rows(in_early, 2)
    in_up = up(low(wide(in_kept[1]) + wide(in_first_two[1])))
    out_turned = up(low(wide(out_terms[0]) + wide(out_up)))

    grad_packed, g_keep, g_early, g_late = kernel(
        attention_backward,
        [((group, 768), b16), ((width // 2, width), b16)] + [((width // 4, width), b16)] * 2,
        (2 * group * width * (768 + 512) + 10 * 16 * count * count * LANES, 0),
        place, cosine, sine, low_own, low_across, low_beside, attn, query, key, value, probs,
        attended, normed,
        scratch=[((group, width), b16), ((group, 256), b16), ((256, width), b16)],
        scalars=1,
    )
    g_over_early = over(g_early)
    in_late, in_up, out_turned, _ = tie(in_late, in_up, out_turned, g_keep)
    in_last_two = split_rows(in_late, 2)
    in_turned = up(low(wide(in_kept[0]) + wide(in_first_two[0]) + wide(in_up)))
    in_down = down(low(wide(in_kept[2]) + wide(in_last_two[0])))
    out_sums = split_rows(wide(out_terms[3]) + wide(out_turned) + wide(out_down), 2)
    send, keep = kernel(
        projections,
        [((4 * count, width), b16)] * 2,
        (2 * group * width * (768 + out_width), 0),
        grad_packed, qkv, mixed, w_down,
    )
    g_over_early, _ = tie(g_over_early, send)
    g_over_late = over(tie(g_late, g_over_early)[0])
    out_over = over(low(out_sums[1]))
    g_kept, g_first_two = split_rows(g_keep, 4), split_rows(g_over_early, 2)
    g_up = up(low(wide(g_kept[1]) + wide(g_first_two[1])))
    sum_in = wide(in_kept[3]) + wide(in_last_two[1]) + wide(in_turned) + wide(in_down)
    sum_out = out_sums[0] + wide(out_over)
    back = rep_exchange(columns([low(sum_in), low(sum_out)]))
    g_over_late, g_up = tie(g_over_late, g_up)
    g_last_two = split_rows(g_over_late, 2)
    g_turned = up(low(wide(g_kept[0]) + wide(g_first_two[0]) + wide(g_up)))
    g_down = down(low(wide(g_kept[2]) + wide(g_last_two[0])))
    kept, sent = scatter_last(send, keep)
    last = kept + wide(swap(sent, 2))
    sum_g = low(wide(g_kept[3]) + wide(g_last_two[1]) + wide(g_turned) + wide(g_down))
    back_qkv = rep_exchange(sum_g[:, :768])
    grad_w_attn_out = wide(
        lax.ppermute(
            columns(split_rows(sum_g[:, 768:], 4)), AXES, [(there, here) for here, there in order]
        )
    )

    standard, inverse = norm_statistics(x_own)
    block_input_gradient = grad_hidden + norm_backward_pass(
        last[:count], jnp.ones((), f32), standard, inverse
    )
    output = low(jnp.where(seg_col[:count] < 8, hidden_sum + last[count:], 0.0))
    back = split_rows(back, 4)
    back_qkv = [split_columns(piece, 3) for piece in split_rows(back_qkv, 4)]
    unit_qkv = wide(columns([piece[k] for k in range(3) for piece in back_qkv]))
    rest_width = part - main
    unit_in = wide(
        columns(
            [
                value
                for k in range(2)
                for piece in back
                for value in (
                    piece[:, main * k : main * (k + 1)],
                    piece[:, 2 * main + rest_width * k : 2 * main + rest_width * (k + 1)],
                )
            ]
        )
    )
    grad_w_out = wide(columns([piece[:, in_width : in_width + part] for piece in back]))
    return (
        absolute(output, z, x),
        absolute(block_input_gradient, z, x),
        jnp.sum(unit_qkv * wide(w_qkv), axis=1),
        unit_qkv * gain_attn,
        grad_w_attn_out,
        jnp.sum(unit_in * wide(w_in), axis=1),
        unit_in * gain_mlp,
        grad_w_out,
    )


def solution(mesh):
    ringed = dict(mesh.shape) == {"fsdp": 8, "rep": 4}
    return jax.shard_map(
        local_ring if ringed else local_plain,
        mesh=mesh,
        in_specs=(
            P(AXES, None),
            P(AXES, None),
            P(AXES, None),
            P(AXES),
            P(AXES, None),
            P(AXES, None),
            P(AXES),
            P(AXES, None),
            P(AXES, None),
        ),
        out_specs=(
            P(AXES, None),
            P(AXES, None),
            P(AXES),
            P(AXES, None),
            P(AXES, None),
            P(AXES),
            P(AXES, None),
            P(AXES, None),
        ),
        check_vma=False,
    )
```

```python
import jax
import jax.numpy as jnp
from jax import lax
from jax.experimental import pallas as pl
from jax.experimental.pallas import tpu as pltpu
from jax.sharding import PartitionSpec as P

HEAD_DIM = 64


norm_eps = 1e-05
rope_base = 160000.0


def matmul(left_side, right_side):
    return jnp.dot(left_side, right_side, preferred_element_type=jnp.float32)


def matmul_right_t(left_side, right_side):
    return lax.dot_general(
        left_side, right_side, (((1,), (1,)), ((), ())), preferred_element_type=jnp.float32
    )


def matmul_left_t(left_side, right_side):
    return lax.dot_general(
        left_side, right_side, (((0,), (0,)), ((), ())), preferred_element_type=jnp.float32
    )


def batched(form, left_side, right_side):
    return jnp.einsum(form, left_side, right_side, preferred_element_type=jnp.float32)


def layout(lengths, row_count):
    slot_ids = lax.iota(jnp.int32, lengths.shape[0])
    before = (slot_ids[:, None] <= slot_ids[None, :]).astype(jnp.int32)
    ends = jnp.sum(lengths[:, None] * before, axis=0)
    starts = ends - lengths
    places = lax.iota(jnp.int32, row_count)
    sequence_segment = jnp.sum((ends[None, :] <= places[:, None]).astype(jnp.int32), axis=1)
    first_row = jnp.sum(
        jnp.where(sequence_segment[:, None] == slot_ids[None, :], starts[None, :], 0), axis=1
    )
    return (sequence_segment, places - first_row, sequence_segment < lengths.shape[0])


def rotary(positions, head_size):
    half_size = head_size // 2
    frequency = rope_base ** (-(lax.iota(jnp.float32, half_size) * (2.0 / head_size)))
    angles = positions.astype(jnp.float32)[..., None] * frequency
    cosine_table = jnp.concatenate([jnp.cos(angles), jnp.cos(angles)], axis=-1)
    sine_table = jnp.concatenate([jnp.sin(angles), jnp.sin(angles)], axis=-1)
    return (cosine_table, sine_table)


def rotate_half(vector):
    half_size = vector.shape[-1] // 2
    return jnp.concatenate([-vector[..., half_size:], vector[..., :half_size]], axis=-1)


def rotate_back(vector):
    half_size = vector.shape[-1] // 2
    return jnp.concatenate([vector[..., half_size:], -vector[..., :half_size]], axis=-1)


def norm_statistics(values):
    average = jnp.mean(values, axis=-1, keepdims=True)
    centred = values - average
    inverse = lax.rsqrt(jnp.mean(centred * centred, axis=-1, keepdims=True) + norm_eps)
    return (centred * inverse, inverse)


def norm_backward_pass(grad_normed, gain_vec, normalized, inverse):
    scaled = grad_normed * gain_vec.astype(jnp.float32)
    return inverse * (
        scaled
        - jnp.mean(scaled, axis=-1, keepdims=True)
        - normalized * jnp.mean(scaled * normalized, axis=-1, keepdims=True)
    )


def attend(rotated_query, rotated_key, value_reduced_precision, sequence_segment):
    scores = batched("thd,shd->hts", rotated_query, rotated_key)
    allowed = sequence_segment[:, None] == sequence_segment[None, :]
    scores = jnp.where(allowed[None], scores, -jnp.inf)
    logarithm_totals = jax.nn.logsumexp(scores, axis=-1)
    weights = jnp.exp(scores - logarithm_totals[..., None]).astype(jnp.bfloat16)
    attended = batched("hts,shd->thd", weights, value_reduced_precision).astype(jnp.bfloat16)
    return (attended, logarithm_totals)


def attend_back(
    rotated_query,
    rotated_key,
    value_reduced_precision,
    sequence_segment,
    logarithm_totals,
    grad_attended,
):
    scores = batched("thd,shd->hts", rotated_query, rotated_key)
    allowed = sequence_segment[:, None] == sequence_segment[None, :]
    scores = jnp.where(allowed[None], scores, -jnp.inf)
    probs_full = jnp.exp(scores - logarithm_totals[..., None])
    weights = probs_full.astype(jnp.bfloat16)
    grad_value = batched("hts,thd->shd", weights, grad_attended)
    grad_probs = batched("thd,shd->hts", grad_attended, value_reduced_precision)
    row_delta = jnp.sum(probs_full * grad_probs, axis=-1, keepdims=True)
    grad_scores = (probs_full * (grad_probs - row_delta)).astype(jnp.bfloat16)
    grad_query = batched("hts,shd->thd", grad_scores, rotated_key)
    grad_key = batched("hts,thd->shd", grad_scores, rotated_query)
    return (grad_query, grad_key, grad_value)


def forward(
    tokens, lengths, attention_norm_gain, w_qkv, w_attn_out, feedforward_norm_gain, w_in, w_out
):
    groups, row_count, embedding_width = tokens.shape
    head_count = embedding_width // HEAD_DIM
    hidden_units = w_in.shape[1] // 2
    sequence_segment, positions, valid = jax.vmap(
        lambda row_lengths: layout(row_lengths, row_count)
    )(lengths)
    cosine_table, sine_table = rotary(positions, HEAD_DIM)
    cosine_table = cosine_table[:, :, None, :]
    sine_table = sine_table[:, :, None, :]
    residual_input = tokens.reshape(groups * row_count, embedding_width).astype(jnp.float32)
    attention_standardized, attention_inverse_norm = norm_statistics(residual_input)
    attention_normed_input = (
        attention_standardized * attention_norm_gain.astype(jnp.float32)
    ).astype(jnp.bfloat16)
    packed = matmul(attention_normed_input, w_qkv).reshape(
        groups, row_count, 3, head_count, HEAD_DIM
    )
    query_raw = packed[:, :, 0]
    key_raw = packed[:, :, 1]
    rotated_query = (
        (query_raw * cosine_table + rotate_half(query_raw) * sine_table) * HEAD_DIM ** (-0.5)
    ).astype(jnp.bfloat16)
    rotated_key = (key_raw * cosine_table + rotate_half(key_raw) * sine_table).astype(jnp.bfloat16)
    value_reduced_precision = packed[:, :, 2].astype(jnp.bfloat16)
    attended, logarithm_totals = jax.vmap(attend)(
        rotated_query, rotated_key, value_reduced_precision, sequence_segment
    )
    attention_rows_flat = attended.reshape(groups * row_count, embedding_width)
    hidden_residual = residual_input + matmul(attention_rows_flat, w_attn_out)
    feedforward_standardized, feedforward_inverse_norm = norm_statistics(hidden_residual)
    feedforward_normed_input = (
        feedforward_standardized * feedforward_norm_gain.astype(jnp.float32)
    ).astype(jnp.bfloat16)
    inner_proj = matmul(feedforward_normed_input, w_in)
    gate_projection = inner_proj[:, :hidden_units]
    up_projection = inner_proj[:, hidden_units:]
    activation_output = jax.nn.gelu(gate_projection, approximate=False)
    mixed_input = (activation_output * up_projection).astype(jnp.bfloat16)
    live_token_rows = valid.reshape(groups * row_count, 1)
    mlp_result = matmul_right_t(mixed_input, w_out)
    output = jnp.where(live_token_rows, hidden_residual + mlp_result, 0.0).astype(jnp.bfloat16)
    saved_residuals = (
        sequence_segment,
        live_token_rows,
        cosine_table,
        sine_table,
        attention_standardized,
        attention_inverse_norm,
        attention_normed_input,
        rotated_query,
        rotated_key,
        value_reduced_precision,
        logarithm_totals,
        attention_rows_flat,
        feedforward_standardized,
        feedforward_inverse_norm,
        feedforward_normed_input,
        gate_projection,
        up_projection,
        activation_output,
        mixed_input,
    )
    return (output, saved_residuals)


def backward(
    saved_residuals,
    cotangent,
    attention_norm_gain,
    w_qkv,
    w_attn_out,
    feedforward_norm_gain,
    w_in,
    w_out,
):
    (
        sequence_segment,
        live_token_rows,
        cosine_table,
        sine_table,
        attention_standardized,
        attention_inverse_norm,
        attention_normed_input,
        rotated_query,
        rotated_key,
        value_reduced_precision,
        logarithm_totals,
        attention_rows_flat,
        feedforward_standardized,
        feedforward_inverse_norm,
        feedforward_normed_input,
        gate_projection,
        up_projection,
        activation_output,
        mixed_input,
    ) = saved_residuals
    groups, row_count = sequence_segment.shape
    embedding_width = attention_standardized.shape[1]
    head_count = embedding_width // HEAD_DIM
    flat_cot = cotangent.reshape(groups * row_count, embedding_width)
    output_gradient = jnp.where(live_token_rows, flat_cot, jnp.zeros((), flat_cot.dtype))
    grad_mixed = matmul(output_gradient, w_out)
    slope = (
        0.5 * (1.0 + lax.erf(gate_projection * 0.7071067811865476))
        + gate_projection * jnp.exp(-0.5 * gate_projection * gate_projection) * 0.3989422804014327
    )
    grad_inner = jnp.concatenate(
        [grad_mixed * up_projection * slope, grad_mixed * activation_output], axis=1
    ).astype(jnp.bfloat16)
    feedforward_normed_gradient = matmul_right_t(grad_inner, w_in)
    hidden_gradient = output_gradient.astype(jnp.float32) + norm_backward_pass(
        feedforward_normed_gradient,
        feedforward_norm_gain,
        feedforward_standardized,
        feedforward_inverse_norm,
    )
    grad_hidden_low = hidden_gradient.astype(jnp.bfloat16)
    grad_attended = matmul_right_t(grad_hidden_low, w_attn_out).astype(jnp.bfloat16)
    grad_attended = grad_attended.reshape(groups, row_count, head_count, HEAD_DIM)
    grad_query, grad_key, grad_value = jax.vmap(attend_back)(
        rotated_query,
        rotated_key,
        value_reduced_precision,
        sequence_segment,
        logarithm_totals,
        grad_attended,
    )
    grad_query = grad_query * HEAD_DIM ** (-0.5)
    grad_query = grad_query * cosine_table + rotate_back(grad_query * sine_table)
    grad_key = grad_key * cosine_table + rotate_back(grad_key * sine_table)
    grad_packed = jnp.stack([grad_query, grad_key, grad_value], axis=2)
    grad_packed = grad_packed.reshape(groups * row_count, 3 * embedding_width).astype(jnp.bfloat16)
    attention_normed_gradient = matmul_right_t(grad_packed, w_qkv)
    block_input_gradient = hidden_gradient + norm_backward_pass(
        attention_normed_gradient,
        attention_norm_gain,
        attention_standardized,
        attention_inverse_norm,
    )
    factors = (
        attention_normed_input,
        grad_packed,
        attention_rows_flat,
        grad_hidden_low,
        feedforward_normed_input,
        grad_inner,
        output_gradient,
        mixed_input,
        attention_normed_gradient,
        attention_standardized,
        feedforward_normed_gradient,
        feedforward_standardized,
    )
    return (block_input_gradient, factors)


def local_plain(
    tokens,
    seq_lengths,
    cotangent,
    attention_norm_gain,
    w_qkv,
    w_attn_out,
    feedforward_norm_gain,
    w_in,
    w_out,
):
    row_count, embedding_width = tokens.shape
    gathered = (
        lax.all_gather(attention_norm_gain, ("fsdp", "rep"), axis=0, tiled=True),
        lax.all_gather(w_qkv, ("fsdp", "rep"), axis=0, tiled=True),
        lax.all_gather(w_attn_out, ("fsdp", "rep"), axis=0, tiled=True),
        lax.all_gather(feedforward_norm_gain, ("fsdp", "rep"), axis=0, tiled=True),
        lax.all_gather(w_in, ("fsdp", "rep"), axis=0, tiled=True),
        lax.all_gather(w_out, ("fsdp", "rep"), axis=0, tiled=True),
    )
    output, saved_residuals = forward(
        tokens.reshape(1, row_count, embedding_width),
        seq_lengths,
        gathered[0],
        gathered[1],
        gathered[2],
        gathered[3],
        gathered[4],
        gathered[5],
    )
    second_copy = (
        lax.all_gather(attention_norm_gain, ("fsdp", "rep"), axis=0, tiled=True),
        lax.all_gather(w_qkv, ("fsdp", "rep"), axis=0, tiled=True),
        lax.all_gather(w_attn_out, ("fsdp", "rep"), axis=0, tiled=True),
        lax.all_gather(feedforward_norm_gain, ("fsdp", "rep"), axis=0, tiled=True),
        lax.all_gather(w_in, ("fsdp", "rep"), axis=0, tiled=True),
        lax.all_gather(w_out, ("fsdp", "rep"), axis=0, tiled=True),
    )
    block_input_gradient, factors = backward(
        saved_residuals,
        cotangent.reshape(1, row_count, embedding_width),
        second_copy[0],
        second_copy[1],
        second_copy[2],
        second_copy[3],
        second_copy[4],
        second_copy[5],
    )
    (
        normed_attn,
        grad_packed,
        attended_rows,
        grad_hidden_low,
        normed_mlp,
        grad_inner,
        grad_out,
        mixed_input,
        grad_normed_attn,
        standard_attn,
        grad_normed_mlp,
        standard_mlp,
    ) = factors
    qkv_width = w_qkv.shape[1]
    attn_width = w_attn_out.shape[1]
    inner_width = w_in.shape[1]
    outer_width = w_out.shape[1]
    qkv_term = matmul_left_t(normed_attn, grad_packed)
    attn_term = matmul_left_t(attended_rows, grad_hidden_low)
    inner_term = matmul_left_t(normed_mlp, grad_inner)
    outer_term = matmul_left_t(grad_out, mixed_input)
    attn_gain_term = jnp.sum(grad_normed_attn * standard_attn, axis=0)
    mlp_gain_term = jnp.sum(grad_normed_mlp * standard_mlp, axis=0)
    summed = lax.psum_scatter(
        jnp.concatenate(
            [
                qkv_term,
                attn_term,
                inner_term,
                outer_term,
                attn_gain_term[:, None],
                mlp_gain_term[:, None],
            ],
            axis=1,
        ),
        ("fsdp", "rep"),
        scatter_dimension=0,
        tiled=True,
    )
    edge_two = qkv_width + attn_width
    edge_three = edge_two + inner_width
    edge_four = edge_three + outer_width
    return (
        output,
        block_input_gradient,
        summed[:, edge_four],
        summed[:, :qkv_width],
        summed[:, qkv_width:edge_two],
        summed[:, edge_four + 1],
        summed[:, edge_two:edge_three],
        summed[:, edge_three:edge_four],
    )


AXES = ("fsdp", "rep")
LANES = 128
HALF = HEAD_DIM // 2


def tie(*values):
    return lax.optimization_barrier(values)


def wide(value):
    return value.astype(jnp.float32)


def low(value):
    return value.astype(jnp.bfloat16)


def split_columns(value, count):
    width = value.shape[1] // count
    return [value[:, k * width : (k + 1) * width] for k in range(count)]


def split_rows(value, count):
    width = value.shape[0] // count
    return [value[k * width : (k + 1) * width] for k in range(count)]


def columns(blocks):
    return jnp.concatenate(blocks, axis=1)


def rows(blocks):
    return jnp.concatenate(blocks, axis=0)


def swap(value, distance):
    return lax.ppermute(value, "rep", [(k, k ^ distance) for k in range(4)])


def rep_exchange(value):
    blocks = value.reshape(4, value.shape[0] // 4, value.shape[1])
    return lax.all_to_all(blocks, "rep", 0, 0, tiled=True).reshape(value.shape)


def up(value):
    return lax.ppermute(value, "fsdp", [(k, (k + 2) % 8) for k in range(8)])


def down(value):
    return lax.ppermute(value, "fsdp", [(k, (k - 2) % 8) for k in range(8)])


def over(value):
    return lax.ppermute(value, "fsdp", [(k, k ^ 1) for k in range(8)])


def relative(value, z, x):
    blocks = split_columns(value, 8)
    blocks = [jnp.where(x == 1, blocks[k ^ 1], blocks[k]) for k in range(8)]
    for bit in (1, 2):
        turn = (z & bit) != 0
        blocks = [jnp.where(turn, blocks[(k + 2 * bit) % 8], blocks[k]) for k in range(8)]
    return columns([blocks[2 * ((p + 1) % 4) + i] for i in range(2) for p in range(4)])


def absolute(value, z, x):
    blocks = split_columns(value, 8)
    blocks = [blocks[4 * i + (j - 1) % 4] for j in range(4) for i in range(2)]
    blocks = [jnp.where(x == 1, blocks[k ^ 1], blocks[k]) for k in range(8)]
    for bit in (1, 2):
        turn = (z & bit) != 0
        blocks = [jnp.where(turn, blocks[(k - 2 * bit) % 8], blocks[k]) for k in range(8)]
    return columns(blocks)


def place_of(place, step, side):
    z, x = place[0], place[1]
    return 2 * lax.rem(z + step + 1, 4) + (x if side == 0 else 1 - x)


def block_of(place, z_at, side):
    z, x = place[0], place[1]
    return 4 * (x if side == 0 else 1 - x) + lax.rem(z_at - z + 7, 4)


def turned(value):
    width = value.shape[1]
    lane = lax.broadcasted_iota(jnp.int32, value.shape, 1)
    return jnp.where(
        lane % HEAD_DIM < HALF,
        pltpu.roll(value, width - HALF, 1),
        pltpu.roll(value, HALF, 1),
    )


def head_masks(row_count):
    lane = lax.broadcasted_iota(jnp.int32, (row_count, LANES), 1)
    return [low(wide(lane < HEAD_DIM)), low(wide(lane >= HEAD_DIM))], lane < HEAD_DIM


def token_rows(mine, across, beside, first, step):
    count = 128
    return [
        mine[first : first + count],
        beside[first : first + count],
        across[first : first + count],
        beside[step + first : step + first + count],
    ]


def attention_forward(
    place, seg_col, seg_row, cosine, sine, mine, across, beside,
    first, second, third, own, others, other_second, other,
    normed, qkv, attn, query, key, value, probs, attended, send, keep,
):
    size = own.shape[0]
    blocks = [
        (first, 0), (second, 0), (third, 0), (own, 0),
        (others, 0), (other_second, 0), (others, size), (other, 0),
    ]
    part = size // 4
    for at, (ref, row) in enumerate(blocks):
        qkv[size * at : size * (at + 1), :] = ref[row : row + size, :768]
        target = pl.multiple_of(place_of(place, at % 4, at // 4) * part, part)
        for z_at in range(4):
            for side in range(2):
                lanes = pl.multiple_of(block_of(place, z_at, side) * LANES, LANES)
                attn[pl.ds(target, part), pl.ds(lanes, LANES)] = ref[
                    row + part * z_at : row + part * (z_at + 1),
                    768 + LANES * side : 768 + LANES * (side + 1),
                ]
    count = 128
    for at, ref in enumerate(token_rows(mine, across, beside, 0, mine.shape[0])):
        values = wide(ref)
        centred = values - jnp.mean(values, axis=1, keepdims=True)
        inverse = lax.rsqrt(jnp.mean(centred * centred, axis=1, keepdims=True) + norm_eps)
        normed[count * at : count * (at + 1), :] = low(centred * inverse)
    packed = matmul(normed[...], qkv[...])
    cos_all, sin_all = columns([cosine[...]] * 2), columns([sine[...]] * 2)
    raw = packed[:, :256]
    query[...] = low((raw * cos_all + turned(raw) * sin_all) * HEAD_DIM ** (-0.5))
    raw = packed[:, 256:512]
    key[...] = low(raw * cos_all + turned(raw) * sin_all)
    value[...] = low(packed[:, 512:])
    masks, is_first = head_masks(count)
    for at in range(4):
        here = slice(count * at, count * (at + 1))
        allowed = seg_col[here, :] == seg_row[at : at + 1, :]
        for pair in range(2):
            lanes = slice(LANES * pair, LANES * (pair + 1))
            made = []
            for head in range(2):
                scores = matmul_right_t(query[here, lanes] * masks[head], key[here, lanes])
                scores = jnp.where(allowed, scores, -jnp.inf)
                powers = jnp.exp(scores - jnp.max(scores, axis=1, keepdims=True))
                weights = powers / jnp.sum(powers, axis=1, keepdims=True)
                slot = count * (4 * at + 2 * pair + head)
                probs[slot : slot + count, :] = weights
                made.append(matmul(low(weights), value[here, lanes]))
            attended[here, lanes] = low(jnp.where(is_first, made[0], made[1]))
    total = low(matmul(attended[...], attn[...]))
    keep[:count, :], send[:count, :] = total[:count], total[count : 2 * count]
    keep[count:, :], send[count:, :] = total[2 * count : 3 * count], total[3 * count :]


def mlp(
    seg_col, norm_own, norm_across, norm_beside, mine, across, beside,
    first, second, third, own, other_first, other_second, other_third, other,
    normed, grad_out, mixed, grad_inner, send, keep, w_down,
    w_up, inner, grad_mixed,
):
    size, count, edge = own.shape[0], 128, w_up.shape[1]
    blocks = (first, second, third, own, other_first, other_second, other_third, other)
    for at, ref in enumerate(blocks):
        w_up[size * at : size * (at + 1), :] = ref[:, :edge]
        w_down[size * at : size * (at + 1), :] = ref[:, edge:]
    for at, ref in enumerate(
        (norm_own[...], norm_beside[:count, :], norm_across[...], norm_beside[count:, :])
    ):
        normed[count * at : count * (at + 1), :] = ref
    for at, ref in enumerate(token_rows(mine, across, beside, count, mine.shape[0])):
        live = wide(seg_col[count * at : count * (at + 1), :] < 8)
        grad_out[count * at : count * (at + 1), :] = low(wide(ref) * live)
    inner[...] = matmul(normed[...], w_up[...])
    grad_mixed[...] = matmul(grad_out[...], w_down[...])
    main = (w_down.shape[1] // LANES - 1) * LANES
    rest = 16

    def parts(gate):
        phi = 0.5 * (1.0 + lax.erf(gate * 0.7071067811865476))
        slope = phi + gate * jnp.exp(-0.5 * gate * gate) * 0.3989422804014327
        return gate * phi, slope

    @pl.loop(0, 8)
    def _(step):
        here = pl.ds(pl.multiple_of(step * 64, 64), 64)
        gate, up_part = inner[here, :main], inner[here, main : 2 * main]
        grad = grad_mixed[here, :main]
        activation, slope = parts(gate)
        mixed[here, :main] = low(activation * up_part)
        grad_inner[here, :main] = low(grad * up_part * slope)
        grad_inner[here, main : 2 * main] = low(grad * activation)
        tail = inner[here, 2 * main :]
        grad = grad_mixed[here, main:]
        activation, slope = parts(tail)
        tail_up = pltpu.roll(tail, LANES - rest, 1)
        mixed[here, main:] = low(activation * tail_up)
        grad_inner[here, 2 * main :] = low(
            grad * tail_up * slope + pltpu.roll(grad * activation, rest, 1)
        )

    total = low(matmul_right_t(grad_inner[...], w_up[...]))
    keep[:count, :], send[:count, :] = total[:count], total[count : 2 * count]
    keep[count:, :], send[count:, :] = total[2 * count : 3 * count], total[3 * count :]


def mlp_terms(
    normed, grad_inner, grad_out, mixed,
    in_keep, in_early, in_late, out_first, out_second, out_third, out_own,
):
    term = low(matmul_left_t(normed[...], grad_inner[...]))
    half, quarter = term.shape[0] // 2, term.shape[0] // 4
    in_keep[...] = term[:half]
    in_early[...] = term[half : half + quarter]
    in_late[...] = term[half + quarter :]
    term = low(matmul_left_t(grad_out[...], mixed[...]))
    size = term.shape[0] // 8
    for at, ref in enumerate((out_first, out_second, out_third, out_own)):
        ref[:size, :] = term[size * at : size * (at + 1)]
        ref[size:, :] = term[size * (at + 4) : size * (at + 5)]


def attention_backward(
    place, cosine, sine, low_own, low_across, low_beside, attn, query, key, value, probs,
    attended, normed,
    grad_packed, g_keep, g_send, grad_low, grad_attended, term_attn,
):
    count = 128
    for at, ref in enumerate(
        (low_own[...], low_beside[:count, :], low_across[...], low_beside[count:, :])
    ):
        grad_low[count * at : count * (at + 1), :] = ref
    grad_attended[...] = low(matmul_right_t(grad_low[...], attn[...]))
    masks, is_first = head_masks(count)
    for at in range(4):
        here = slice(count * at, count * (at + 1))
        cos, sin = cosine[here, :], sine[here, :]
        for pair in range(2):
            lanes = slice(LANES * pair, LANES * (pair + 1))
            q, k, v = query[here, lanes], key[here, lanes], value[here, lanes]
            grad = grad_attended[here, lanes]
            made = []
            for head in range(2):
                slot = count * (4 * at + 2 * pair + head)
                weights = probs[slot : slot + count, :]
                grad_value = matmul_left_t(low(weights), grad)
                grad_probs = matmul_right_t(grad * masks[head], v)
                delta = jnp.sum(weights * grad_probs, axis=1, keepdims=True)
                grad_scores = low(weights * (grad_probs - delta))
                made.append((matmul(grad_scores, k), matmul_left_t(grad_scores, q), grad_value))
            grad_q, grad_k, grad_v = (jnp.where(is_first, *both) for both in zip(*made))
            grad_q = grad_q * HEAD_DIM ** (-0.5)
            grad_packed[here, lanes] = low(grad_q * cos - turned(grad_q) * sin)
            lanes = slice(256 + LANES * pair, 256 + LANES * (pair + 1))
            grad_packed[here, lanes] = low(grad_k * cos - turned(grad_k) * sin)
            lanes = slice(512 + LANES * pair, 512 + LANES * (pair + 1))
            grad_packed[here, lanes] = low(grad_v)
    term = low(matmul_left_t(normed[...], grad_packed[...]))
    half = term.shape[0] // 2
    g_keep[:, :768] = term[:half]
    g_send[:, :768] = term[half:]
    term_attn[...] = low(matmul_left_t(attended[...], grad_low[...]))
    size = term.shape[0] // 8
    part = size // 4
    targets = [(ref, size * p) for ref in (g_keep, g_send) for p in range(4)]
    for at, (ref, row) in enumerate(targets):
        source = pl.multiple_of(place_of(place, at % 4, at // 4) * part, part)
        for z_at in range(4):
            for side in range(2):
                lanes = pl.multiple_of(block_of(place, z_at, side) * LANES, LANES)
                ref[
                    row + part * z_at : row + part * (z_at + 1),
                    768 + LANES * side : 768 + LANES * (side + 1),
                ] = term_attn[pl.ds(source, part), pl.ds(lanes, LANES)]


def projections(grad_packed, qkv, mixed, w_down, send, keep):
    count = 128
    for row, total in (
        (0, low(matmul_right_t(grad_packed[...], qkv[...]))),
        (count, low(matmul_right_t(mixed[...], w_down[...]))),
    ):
        keep[row : row + count, :] = total[:count]
        send[row : row + count, :] = total[count : 2 * count]
        keep[2 * count + row : 3 * count + row, :] = total[2 * count : 3 * count]
        send[2 * count + row : 3 * count + row, :] = total[3 * count :]


def kernel(body, outs, cost, *args, scratch=(), scalars=0):
    flops, transcendentals = cost
    shapes = [jax.ShapeDtypeStruct(shape, kind) for shape, kind in outs]
    moved = sum(arg.size * arg.dtype.itemsize for arg in (*args, *shapes))
    return pl.pallas_call(
        body,
        out_shape=shapes,
        in_specs=[
            pl.BlockSpec(memory_space=pltpu.SMEM if k < scalars else pltpu.VMEM)
            for k in range(len(args))
        ],
        out_specs=[pl.BlockSpec(memory_space=pltpu.VMEM)] * len(shapes),
        scratch_shapes=[pltpu.VMEM(shape, kind) for shape, kind in scratch],
        compiler_params=pltpu.CompilerParams(vmem_limit_bytes=48 * 2**20),
        cost_estimate=pl.CostEstimate(
            flops=flops, bytes_accessed=moved, transcendentals=transcendentals
        ),
        name=body.__name__,
    )(*args)


def scatter_last(send, keep):
    beside = split_rows(swap(send, 1), 2)
    kept = split_rows(keep, 2)
    sent = low(wide(kept[1]) + wide(beside[1]))
    return wide(kept[0]) + wide(beside[0]), sent


def local_ring(
    tokens,
    seq_lengths,
    cotangent,
    attention_norm_gain,
    w_qkv,
    w_attn_out,
    feedforward_norm_gain,
    w_in,
    w_out,
):
    count, width = tokens.shape
    index = lax.axis_index("fsdp")
    z, x = index // 2, index % 2
    place = jnp.stack([z, x]).astype(jnp.int32)
    hidden = w_in.shape[1] // 2
    part = hidden // 4
    main = part // LANES * LANES
    in_width, out_width = 2 * main + LANES, main + LANES
    f32, b16 = jnp.float32, jnp.bfloat16
    group = 4 * count

    gain_attn = wide(attention_norm_gain)[:, None]
    gain_mlp = wide(feedforward_norm_gain)[:, None]
    order = [(k, (k % 8) * 4 + k // 8) for k in range(32)]
    attn_own = lax.ppermute(w_attn_out, AXES, order)
    qkv_parts = split_columns(low(wide(w_qkv) * gain_attn), 12)
    size = w_qkv.shape[0]
    slots = seq_lengths.shape[1]
    lengths_low = jnp.pad(low(wide(seq_lengths)), ((0, size - 1), (0, LANES - slots)))
    exchanged = rep_exchange(rows([columns([*qkv_parts[k::4], lengths_low]) for k in range(4)]))
    first_own = columns([exchanged[:, :768], rows(split_columns(attn_own, 4))])
    lengths = rows([exchanged[size * k : size * k + 1, 768 : 768 + slots] for k in range(4)])
    lengths = wide(lengths).astype(jnp.int32)
    for bit in (1, 2):
        turned_rows = rows([lengths[k ^ bit : (k ^ bit) + 1] for k in range(4)])
        lengths = jnp.where((lax.axis_index("rep") & bit) != 0, turned_rows, lengths)

    scaled_in = low(wide(w_in) * gain_mlp)
    pieces = []
    for k in range(4):
        gate = scaled_in[:, part * k : part * (k + 1)]
        up_part = scaled_in[:, hidden + part * k : hidden + part * (k + 1)]
        out_part = w_out[:, part * k : part * (k + 1)]
        fill = [jnp.zeros((w_in.shape[0], n), b16) for n in (in_width - 2 * part, out_width - part)]
        pieces.append(
            columns(
                [gate[:, :main], up_part[:, :main], gate[:, main:], up_part[:, main:], fill[0]]
                + [out_part, fill[1]]
            )
        )
    mine = rows([relative(tokens, z, x), relative(cotangent, z, x)])
    first_own, rest, mine = tie(first_own, rows(pieces), mine)
    rest = rep_exchange(rest)

    third, first, other = up(first_own), down(first_own), over(first_own)
    third, first, other, mine, rest = tie(third, first, other, mine, rest)
    across = swap(mine, 2)
    second, others = up(third), over(rows([first, third]))
    second, others, across, rest = tie(second, others, across, rest)
    other_second = over(second)
    rest_third, rest_first = up(rest), down(rest)
    beside = swap(rows([mine, across]), 1)
    rest_other = over(tie(rest, other_second, beside)[0])

    step = mine.shape[0]
    segment, positions, _ = jax.vmap(lambda row: layout(row, count))(lengths)
    frequency = rope_base ** (-(lax.iota(f32, HALF) * (2.0 / HEAD_DIM)))
    angles = positions.reshape(group, 1).astype(f32) * frequency
    cosine, sine = jnp.cos(angles), jnp.sin(angles)
    cosine, sine = columns([cosine] * 4), columns([-sine, sine] * 2)
    seg_col = segment.reshape(group, 1)

    normed, qkv, attn, query, key, value, probs, attended, send, keep = kernel(
        attention_forward,
        [((group, width), b16), ((width, 768), b16), ((256, width), b16)]
        + [((group, 256), b16)] * 3
        + [((16 * count, count), f32), ((group, 256), b16)]
        + [((2 * count, width), b16)] * 2,
        (2 * group * width * (768 + 256) + 4 * 16 * count * count * LANES, 16 * count * count),
        place, seg_col, segment, cosine, sine, mine, across, beside,
        first, second, third, first_own, others, other_second, other,
        scalars=1,
    )
    rest_third, rest_first, rest_other, send = tie(rest_third, rest_first, rest_other, send)
    rest_second, rest_other_third = up(rest_third), over(rest_third)
    x_own = wide(mine[:count])
    kept, sent = scatter_last(send, keep)
    rest_other_first = over(tie(rest_first, rest_other_third)[0])
    hidden_sum = x_own + kept + wide(swap(sent, 2))
    standard_mlp, inverse_mlp = norm_statistics(hidden_sum)
    norm_own = low(standard_mlp)
    norm_across = swap(norm_own, 2)
    rest_second, rest_other_third, _ = tie(rest_second, rest_other_third, norm_own)
    rest_other_second = up(rest_other_third)
    norm_beside = swap(rows([norm_own, norm_across]), 1)

    normed_mlp, grad_out, mixed, grad_inner, send, keep, w_down = kernel(
        mlp,
        [((group, width), b16)] * 2
        + [((group, out_width), b16), ((group, in_width), b16)]
        + [((2 * count, width), b16)] * 2
        + [((width, out_width), b16)],
        (2 * group * width * (2 * in_width + out_width), 3 * group * part),
        seg_col, norm_own, norm_across, norm_beside, mine, across, beside,
        rest_first, rest_second, rest_third, rest,
        rest_other_first, rest_other_second, rest_other_third, rest_other,
        scratch=[
            ((width, in_width), b16),
            ((group, in_width), f32),
            ((group, out_width), f32),
        ],
    )
    in_keep, in_early, in_late, *out_terms = kernel(
        mlp_terms,
        [((width // 2, in_width), b16)]
        + [((width // 4, in_width), b16)] * 2
        + [((width // 4, out_width), b16)] * 4,
        (2 * group * width * (in_width + out_width), 0),
        normed_mlp, grad_inner, grad_out, mixed,
    )
    out_up, out_down = up(out_terms[1]), down(out_terms[2])
    in_early = over(in_early)
    kept, sent = scatter_last(send, keep)
    scaled_mlp = kept + wide(swap(sent, 2))
    grad_hidden = wide(grad_out[:count]) + norm_backward_pass(
        scaled_mlp, jnp.ones((), f32), standard_mlp, inverse_mlp
    )
    low_own = low(grad_hidden)
    low_across = swap(low_own, 2)
    in_early, low_across, out_up = tie(in_early, low_across, out_up)
    in_late = over(tie(in_late, in_early)[0])
    low_beside = swap(rows([low_own, low_across]), 1)
    in_kept, in_first_two = split_rows(in_keep, 4), split_rows(in_early, 2)
    in_up = up(low(wide(in_kept[1]) + wide(in_first_two[1])))
    out_turned = up(low(wide(out_terms[0]) + wide(out_up)))

    grad_packed, g_keep, g_send = kernel(
        attention_backward,
        [((group, 768), b16)] + [((width // 2, width), b16)] * 2,
        (2 * group * width * (768 + 512) + 10 * 16 * count * count * LANES, 0),
        place, cosine, sine, low_own, low_across, low_beside, attn, query, key, value, probs,
        attended, normed,
        scratch=[((group, width), b16), ((group, 256), b16), ((256, width), b16)],
        scalars=1,
    )
    g_over = over(g_send)
    in_late, in_up, out_turned, out_down, _ = tie(in_late, in_up, out_turned, out_down, g_keep)
    in_last_two = split_rows(in_late, 2)
    in_turned = up(low(wide(in_kept[0]) + wide(in_first_two[0]) + wide(in_up)))
    in_down = down(low(wide(in_kept[2]) + wide(in_last_two[0])))
    out_sums = split_rows(wide(out_terms[3]) + wide(out_turned) + wide(out_down), 2)
    send, keep = kernel(
        projections,
        [((4 * count, width), b16)] * 2,
        (2 * group * width * (768 + out_width), 0),
        grad_packed, qkv, mixed, w_down,
    )
    g_over, send, in_turned, in_down = tie(g_over, send, in_turned, in_down)
    g_sums = [wide(a) + wide(b) for a, b in zip(split_rows(g_keep, 4), split_rows(g_over, 4))]
    g_up, g_down = up(low(g_sums[1])), down(low(g_sums[2]))
    kept, sent = scatter_last(send, keep)
    out_over = over(tie(low(out_sums[1]), g_over)[0])
    g_up, g_down, sent = tie(g_up, g_down, sent)
    last_across = swap(sent, 2)
    g_turned = up(low(g_sums[0] + wide(g_up)))
    out_over, _ = tie(out_over, g_up)
    sum_in = wide(in_kept[3]) + wide(in_last_two[1]) + wide(in_turned) + wide(in_down)
    sum_out = out_sums[0] + wide(out_over)
    back = rep_exchange(columns([low(sum_in), low(sum_out)]))
    g_turned, g_down, last_across = tie(g_turned, g_down, last_across)
    last = kept + wide(last_across)
    sum_g = low(g_sums[3] + wide(g_turned) + wide(g_down))
    back_qkv = rep_exchange(sum_g[:, :768])
    grad_w_attn_out = wide(
        lax.ppermute(
            columns(split_rows(sum_g[:, 768:], 4)), AXES, [(there, here) for here, there in order]
        )
    )

    standard, inverse = norm_statistics(x_own)
    block_input_gradient = grad_hidden + norm_backward_pass(
        last[:count], jnp.ones((), f32), standard, inverse
    )
    output = low(jnp.where(seg_col[:count] < 8, hidden_sum + last[count:], 0.0))
    back = split_rows(back, 4)
    back_qkv = [split_columns(piece, 3) for piece in split_rows(back_qkv, 4)]
    unit_qkv = wide(columns([piece[k] for k in range(3) for piece in back_qkv]))
    rest_width = part - main
    unit_in = wide(
        columns(
            [
                value
                for k in range(2)
                for piece in back
                for value in (
                    piece[:, main * k : main * (k + 1)],
                    piece[:, 2 * main + rest_width * k : 2 * main + rest_width * (k + 1)],
                )
            ]
        )
    )
    grad_w_out = wide(columns([piece[:, in_width : in_width + part] for piece in back]))
    return (
        absolute(output, z, x),
        absolute(block_input_gradient, z, x),
        jnp.sum(unit_qkv * wide(w_qkv), axis=1),
        unit_qkv * gain_attn,
        grad_w_attn_out,
        jnp.sum(unit_in * wide(w_in), axis=1),
        unit_in * gain_mlp,
        grad_w_out,
    )


def solution(mesh):
    ringed = dict(mesh.shape) == {"fsdp": 8, "rep": 4}
    return jax.shard_map(
        local_ring if ringed else local_plain,
        mesh=mesh,
        in_specs=(
            P(AXES, None),
            P(AXES, None),
            P(AXES, None),
            P(AXES),
            P(AXES, None),
            P(AXES, None),
            P(AXES),
            P(AXES, None),
            P(AXES, None),
        ),
        out_specs=(
            P(AXES, None),
            P(AXES, None),
            P(AXES),
            P(AXES, None),
            P(AXES, None),
            P(AXES),
            P(AXES, None),
            P(AXES, None),
        ),
        check_vma=False,
    )
```

```python
import jax
import jax.numpy as jnp
from jax import lax
from jax.experimental import pallas as pl
from jax.experimental.pallas import tpu as pltpu
from jax.sharding import PartitionSpec as P

HEAD_DIM = 64


norm_eps = 1e-05
rope_base = 160000.0


def matmul(left_side, right_side):
    return jnp.dot(left_side, right_side, preferred_element_type=jnp.float32)


def matmul_right_t(left_side, right_side):
    return lax.dot_general(
        left_side, right_side, (((1,), (1,)), ((), ())), preferred_element_type=jnp.float32
    )


def matmul_left_t(left_side, right_side):
    return lax.dot_general(
        left_side, right_side, (((0,), (0,)), ((), ())), preferred_element_type=jnp.float32
    )


def batched(form, left_side, right_side):
    return jnp.einsum(form, left_side, right_side, preferred_element_type=jnp.float32)


def layout(lengths, row_count):
    slot_ids = lax.iota(jnp.int32, lengths.shape[0])
    before = (slot_ids[:, None] <= slot_ids[None, :]).astype(jnp.int32)
    ends = jnp.sum(lengths[:, None] * before, axis=0)
    starts = ends - lengths
    places = lax.iota(jnp.int32, row_count)
    sequence_segment = jnp.sum((ends[None, :] <= places[:, None]).astype(jnp.int32), axis=1)
    first_row = jnp.sum(
        jnp.where(sequence_segment[:, None] == slot_ids[None, :], starts[None, :], 0), axis=1
    )
    return (sequence_segment, places - first_row, sequence_segment < lengths.shape[0])


def rotary(positions, head_size):
    half_size = head_size // 2
    frequency = rope_base ** (-(lax.iota(jnp.float32, half_size) * (2.0 / head_size)))
    angles = positions.astype(jnp.float32)[..., None] * frequency
    cosine_table = jnp.concatenate([jnp.cos(angles), jnp.cos(angles)], axis=-1)
    sine_table = jnp.concatenate([jnp.sin(angles), jnp.sin(angles)], axis=-1)
    return (cosine_table, sine_table)


def rotate_half(vector):
    half_size = vector.shape[-1] // 2
    return jnp.concatenate([-vector[..., half_size:], vector[..., :half_size]], axis=-1)


def rotate_back(vector):
    half_size = vector.shape[-1] // 2
    return jnp.concatenate([vector[..., half_size:], -vector[..., :half_size]], axis=-1)


def norm_statistics(values):
    average = jnp.mean(values, axis=-1, keepdims=True)
    centred = values - average
    inverse = lax.rsqrt(jnp.mean(centred * centred, axis=-1, keepdims=True) + norm_eps)
    return (centred * inverse, inverse)


def norm_backward_pass(grad_normed, gain_vec, normalized, inverse):
    scaled = grad_normed * gain_vec.astype(jnp.float32)
    return inverse * (
        scaled
        - jnp.mean(scaled, axis=-1, keepdims=True)
        - normalized * jnp.mean(scaled * normalized, axis=-1, keepdims=True)
    )


def attend(rotated_query, rotated_key, value_reduced_precision, sequence_segment):
    scores = batched("thd,shd->hts", rotated_query, rotated_key)
    allowed = sequence_segment[:, None] == sequence_segment[None, :]
    scores = jnp.where(allowed[None], scores, -jnp.inf)
    logarithm_totals = jax.nn.logsumexp(scores, axis=-1)
    weights = jnp.exp(scores - logarithm_totals[..., None]).astype(jnp.bfloat16)
    attended = batched("hts,shd->thd", weights, value_reduced_precision).astype(jnp.bfloat16)
    return (attended, logarithm_totals)


def attend_back(
    rotated_query,
    rotated_key,
    value_reduced_precision,
    sequence_segment,
    logarithm_totals,
    grad_attended,
):
    scores = batched("thd,shd->hts", rotated_query, rotated_key)
    allowed = sequence_segment[:, None] == sequence_segment[None, :]
    scores = jnp.where(allowed[None], scores, -jnp.inf)
    probs_full = jnp.exp(scores - logarithm_totals[..., None])
    weights = probs_full.astype(jnp.bfloat16)
    grad_value = batched("hts,thd->shd", weights, grad_attended)
    grad_probs = batched("thd,shd->hts", grad_attended, value_reduced_precision)
    row_delta = jnp.sum(probs_full * grad_probs, axis=-1, keepdims=True)
    grad_scores = (probs_full * (grad_probs - row_delta)).astype(jnp.bfloat16)
    grad_query = batched("hts,shd->thd", grad_scores, rotated_key)
    grad_key = batched("hts,thd->shd", grad_scores, rotated_query)
    return (grad_query, grad_key, grad_value)


def forward(
    tokens, lengths, attention_norm_gain, w_qkv, w_attn_out, feedforward_norm_gain, w_in, w_out
):
    groups, row_count, embedding_width = tokens.shape
    head_count = embedding_width // HEAD_DIM
    hidden_units = w_in.shape[1] // 2
    sequence_segment, positions, valid = jax.vmap(
        lambda row_lengths: layout(row_lengths, row_count)
    )(lengths)
    cosine_table, sine_table = rotary(positions, HEAD_DIM)
    cosine_table = cosine_table[:, :, None, :]
    sine_table = sine_table[:, :, None, :]
    residual_input = tokens.reshape(groups * row_count, embedding_width).astype(jnp.float32)
    attention_standardized, attention_inverse_norm = norm_statistics(residual_input)
    attention_normed_input = (
        attention_standardized * attention_norm_gain.astype(jnp.float32)
    ).astype(jnp.bfloat16)
    packed = matmul(attention_normed_input, w_qkv).reshape(
        groups, row_count, 3, head_count, HEAD_DIM
    )
    query_raw = packed[:, :, 0]
    key_raw = packed[:, :, 1]
    rotated_query = (
        (query_raw * cosine_table + rotate_half(query_raw) * sine_table) * HEAD_DIM ** (-0.5)
    ).astype(jnp.bfloat16)
    rotated_key = (key_raw * cosine_table + rotate_half(key_raw) * sine_table).astype(jnp.bfloat16)
    value_reduced_precision = packed[:, :, 2].astype(jnp.bfloat16)
    attended, logarithm_totals = jax.vmap(attend)(
        rotated_query, rotated_key, value_reduced_precision, sequence_segment
    )
    attention_rows_flat = attended.reshape(groups * row_count, embedding_width)
    hidden_residual = residual_input + matmul(attention_rows_flat, w_attn_out)
    feedforward_standardized, feedforward_inverse_norm = norm_statistics(hidden_residual)
    feedforward_normed_input = (
        feedforward_standardized * feedforward_norm_gain.astype(jnp.float32)
    ).astype(jnp.bfloat16)
    inner_proj = matmul(feedforward_normed_input, w_in)
    gate_projection = inner_proj[:, :hidden_units]
    up_projection = inner_proj[:, hidden_units:]
    activation_output = jax.nn.gelu(gate_projection, approximate=False)
    mixed_input = (activation_output * up_projection).astype(jnp.bfloat16)
    live_token_rows = valid.reshape(groups * row_count, 1)
    mlp_result = matmul_right_t(mixed_input, w_out)
    output = jnp.where(live_token_rows, hidden_residual + mlp_result, 0.0).astype(jnp.bfloat16)
    saved_residuals = (
        sequence_segment,
        live_token_rows,
        cosine_table,
        sine_table,
        attention_standardized,
        attention_inverse_norm,
        attention_normed_input,
        rotated_query,
        rotated_key,
        value_reduced_precision,
        logarithm_totals,
        attention_rows_flat,
        feedforward_standardized,
        feedforward_inverse_norm,
        feedforward_normed_input,
        gate_projection,
        up_projection,
        activation_output,
        mixed_input,
    )
    return (output, saved_residuals)


def backward(
    saved_residuals,
    cotangent,
    attention_norm_gain,
    w_qkv,
    w_attn_out,
    feedforward_norm_gain,
    w_in,
    w_out,
):
    (
        sequence_segment,
        live_token_rows,
        cosine_table,
        sine_table,
        attention_standardized,
        attention_inverse_norm,
        attention_normed_input,
        rotated_query,
        rotated_key,
        value_reduced_precision,
        logarithm_totals,
        attention_rows_flat,
        feedforward_standardized,
        feedforward_inverse_norm,
        feedforward_normed_input,
        gate_projection,
        up_projection,
        activation_output,
        mixed_input,
    ) = saved_residuals
    groups, row_count = sequence_segment.shape
    embedding_width = attention_standardized.shape[1]
    head_count = embedding_width // HEAD_DIM
    flat_cot = cotangent.reshape(groups * row_count, embedding_width)
    output_gradient = jnp.where(live_token_rows, flat_cot, jnp.zeros((), flat_cot.dtype))
    grad_mixed = matmul(output_gradient, w_out)
    slope = (
        0.5 * (1.0 + lax.erf(gate_projection * 0.7071067811865476))
        + gate_projection * jnp.exp(-0.5 * gate_projection * gate_projection) * 0.3989422804014327
    )
    grad_inner = jnp.concatenate(
        [grad_mixed * up_projection * slope, grad_mixed * activation_output], axis=1
    ).astype(jnp.bfloat16)
    feedforward_normed_gradient = matmul_right_t(grad_inner, w_in)
    hidden_gradient = output_gradient.astype(jnp.float32) + norm_backward_pass(
        feedforward_normed_gradient,
        feedforward_norm_gain,
        feedforward_standardized,
        feedforward_inverse_norm,
    )
    grad_hidden_low = hidden_gradient.astype(jnp.bfloat16)
    grad_attended = matmul_right_t(grad_hidden_low, w_attn_out).astype(jnp.bfloat16)
    grad_attended = grad_attended.reshape(groups, row_count, head_count, HEAD_DIM)
    grad_query, grad_key, grad_value = jax.vmap(attend_back)(
        rotated_query,
        rotated_key,
        value_reduced_precision,
        sequence_segment,
        logarithm_totals,
        grad_attended,
    )
    grad_query = grad_query * HEAD_DIM ** (-0.5)
    grad_query = grad_query * cosine_table + rotate_back(grad_query * sine_table)
    grad_key = grad_key * cosine_table + rotate_back(grad_key * sine_table)
    grad_packed = jnp.stack([grad_query, grad_key, grad_value], axis=2)
    grad_packed = grad_packed.reshape(groups * row_count, 3 * embedding_width).astype(jnp.bfloat16)
    attention_normed_gradient = matmul_right_t(grad_packed, w_qkv)
    block_input_gradient = hidden_gradient + norm_backward_pass(
        attention_normed_gradient,
        attention_norm_gain,
        attention_standardized,
        attention_inverse_norm,
    )
    factors = (
        attention_normed_input,
        grad_packed,
        attention_rows_flat,
        grad_hidden_low,
        feedforward_normed_input,
        grad_inner,
        output_gradient,
        mixed_input,
        attention_normed_gradient,
        attention_standardized,
        feedforward_normed_gradient,
        feedforward_standardized,
    )
    return (block_input_gradient, factors)


def local_plain(
    tokens,
    seq_lengths,
    cotangent,
    attention_norm_gain,
    w_qkv,
    w_attn_out,
    feedforward_norm_gain,
    w_in,
    w_out,
):
    row_count, embedding_width = tokens.shape
    gathered = (
        lax.all_gather(attention_norm_gain, ("fsdp", "rep"), axis=0, tiled=True),
        lax.all_gather(w_qkv, ("fsdp", "rep"), axis=0, tiled=True),
        lax.all_gather(w_attn_out, ("fsdp", "rep"), axis=0, tiled=True),
        lax.all_gather(feedforward_norm_gain, ("fsdp", "rep"), axis=0, tiled=True),
        lax.all_gather(w_in, ("fsdp", "rep"), axis=0, tiled=True),
        lax.all_gather(w_out, ("fsdp", "rep"), axis=0, tiled=True),
    )
    output, saved_residuals = forward(
        tokens.reshape(1, row_count, embedding_width),
        seq_lengths,
        gathered[0],
        gathered[1],
        gathered[2],
        gathered[3],
        gathered[4],
        gathered[5],
    )
    second_copy = (
        lax.all_gather(attention_norm_gain, ("fsdp", "rep"), axis=0, tiled=True),
        lax.all_gather(w_qkv, ("fsdp", "rep"), axis=0, tiled=True),
        lax.all_gather(w_attn_out, ("fsdp", "rep"), axis=0, tiled=True),
        lax.all_gather(feedforward_norm_gain, ("fsdp", "rep"), axis=0, tiled=True),
        lax.all_gather(w_in, ("fsdp", "rep"), axis=0, tiled=True),
        lax.all_gather(w_out, ("fsdp", "rep"), axis=0, tiled=True),
    )
    block_input_gradient, factors = backward(
        saved_residuals,
        cotangent.reshape(1, row_count, embedding_width),
        second_copy[0],
        second_copy[1],
        second_copy[2],
        second_copy[3],
        second_copy[4],
        second_copy[5],
    )
    (
        normed_attn,
        grad_packed,
        attended_rows,
        grad_hidden_low,
        normed_mlp,
        grad_inner,
        grad_out,
        mixed_input,
        grad_normed_attn,
        standard_attn,
        grad_normed_mlp,
        standard_mlp,
    ) = factors
    qkv_width = w_qkv.shape[1]
    attn_width = w_attn_out.shape[1]
    inner_width = w_in.shape[1]
    outer_width = w_out.shape[1]
    qkv_term = matmul_left_t(normed_attn, grad_packed)
    attn_term = matmul_left_t(attended_rows, grad_hidden_low)
    inner_term = matmul_left_t(normed_mlp, grad_inner)
    outer_term = matmul_left_t(grad_out, mixed_input)
    attn_gain_term = jnp.sum(grad_normed_attn * standard_attn, axis=0)
    mlp_gain_term = jnp.sum(grad_normed_mlp * standard_mlp, axis=0)
    summed = lax.psum_scatter(
        jnp.concatenate(
            [
                qkv_term,
                attn_term,
                inner_term,
                outer_term,
                attn_gain_term[:, None],
                mlp_gain_term[:, None],
            ],
            axis=1,
        ),
        ("fsdp", "rep"),
        scatter_dimension=0,
        tiled=True,
    )
    edge_two = qkv_width + attn_width
    edge_three = edge_two + inner_width
    edge_four = edge_three + outer_width
    return (
        output,
        block_input_gradient,
        summed[:, edge_four],
        summed[:, :qkv_width],
        summed[:, qkv_width:edge_two],
        summed[:, edge_four + 1],
        summed[:, edge_two:edge_three],
        summed[:, edge_three:edge_four],
    )


AXES = ("fsdp", "rep")
LANES = 128
HALF = HEAD_DIM // 2


def tie(*values):
    return lax.optimization_barrier(values)


def wide(value):
    return value.astype(jnp.float32)


def low(value):
    return value.astype(jnp.bfloat16)


def split_columns(value, count):
    width = value.shape[1] // count
    return [value[:, k * width : (k + 1) * width] for k in range(count)]


def split_rows(value, count):
    width = value.shape[0] // count
    return [value[k * width : (k + 1) * width] for k in range(count)]


def columns(blocks):
    return jnp.concatenate(blocks, axis=1)


def rows(blocks):
    return jnp.concatenate(blocks, axis=0)


def swap(value, distance):
    return lax.ppermute(value, "rep", [(k, k ^ distance) for k in range(4)])


def rep_exchange(value):
    blocks = value.reshape(4, value.shape[0] // 4, value.shape[1])
    return lax.all_to_all(blocks, "rep", 0, 0, tiled=True).reshape(value.shape)


def up(value):
    return lax.ppermute(value, "fsdp", [(k, (k + 2) % 8) for k in range(8)])


def down(value):
    return lax.ppermute(value, "fsdp", [(k, (k - 2) % 8) for k in range(8)])


def over(value):
    return lax.ppermute(value, "fsdp", [(k, k ^ 1) for k in range(8)])


def relative(value, z, x):
    blocks = split_columns(value, 8)
    blocks = [jnp.where(x == 1, blocks[k ^ 1], blocks[k]) for k in range(8)]
    for bit in (1, 2):
        turn = (z & bit) != 0
        blocks = [jnp.where(turn, blocks[(k + 2 * bit) % 8], blocks[k]) for k in range(8)]
    return columns([blocks[2 * ((p + 1) % 4) + i] for i in range(2) for p in range(4)])


def absolute(value, z, x):
    blocks = split_columns(value, 8)
    blocks = [blocks[4 * i + (j - 1) % 4] for j in range(4) for i in range(2)]
    blocks = [jnp.where(x == 1, blocks[k ^ 1], blocks[k]) for k in range(8)]
    for bit in (1, 2):
        turn = (z & bit) != 0
        blocks = [jnp.where(turn, blocks[(k - 2 * bit) % 8], blocks[k]) for k in range(8)]
    return columns(blocks)


def place_of(place, step, side):
    z, x = place[0], place[1]
    return 2 * lax.rem(z + step + 1, 4) + (x if side == 0 else 1 - x)


def block_of(place, z_at, side):
    z, x = place[0], place[1]
    return 4 * (x if side == 0 else 1 - x) + lax.rem(z_at - z + 7, 4)


def turned(value):
    width = value.shape[1]
    lane = lax.broadcasted_iota(jnp.int32, value.shape, 1)
    return jnp.where(
        lane % HEAD_DIM < HALF,
        pltpu.roll(value, width - HALF, 1),
        pltpu.roll(value, HALF, 1),
    )


def head_masks(row_count):
    lane = lax.broadcasted_iota(jnp.int32, (row_count, LANES), 1)
    return [low(wide(lane < HEAD_DIM)), low(wide(lane >= HEAD_DIM))], lane < HEAD_DIM


def token_rows(mine, across, beside, first, step):
    count = 128
    return [
        mine[first : first + count],
        beside[first : first + count],
        across[first : first + count],
        beside[step + first : step + first + count],
    ]


def attention_forward(
    place, seg_col, seg_row, cosine, sine, mine, across, beside,
    first, second, third, own, others, other_second, other,
    normed, qkv, attn, query, key, value, probs, attended, send, keep,
):
    size = own.shape[0]
    blocks = [
        (first, 0), (second, 0), (third, 0), (own, 0),
        (others, 0), (other_second, 0), (others, size), (other, 0),
    ]
    part = size // 4
    for at, (ref, row) in enumerate(blocks):
        qkv[size * at : size * (at + 1), :] = ref[row : row + size, :768]
        target = pl.multiple_of(place_of(place, at % 4, at // 4) * part, part)
        for z_at in range(4):
            for side in range(2):
                lanes = pl.multiple_of(block_of(place, z_at, side) * LANES, LANES)
                attn[pl.ds(target, part), pl.ds(lanes, LANES)] = ref[
                    row + part * z_at : row + part * (z_at + 1),
                    768 + LANES * side : 768 + LANES * (side + 1),
                ]
    count = 128
    for at, ref in enumerate(token_rows(mine, across, beside, 0, mine.shape[0])):
        values = wide(ref)
        centred = values - jnp.mean(values, axis=1, keepdims=True)
        inverse = lax.rsqrt(jnp.mean(centred * centred, axis=1, keepdims=True) + norm_eps)
        normed[count * at : count * (at + 1), :] = low(centred * inverse)
    packed = matmul(normed[...], qkv[...])
    cos_all, sin_all = columns([cosine[...]] * 2), columns([sine[...]] * 2)
    raw = packed[:, :256]
    query[...] = low((raw * cos_all + turned(raw) * sin_all) * HEAD_DIM ** (-0.5))
    raw = packed[:, 256:512]
    key[...] = low(raw * cos_all + turned(raw) * sin_all)
    value[...] = low(packed[:, 512:])
    masks, is_first = head_masks(count)
    for at in range(4):
        here = slice(count * at, count * (at + 1))
        allowed = seg_col[here, :] == seg_row[at : at + 1, :]
        for pair in range(2):
            lanes = slice(LANES * pair, LANES * (pair + 1))
            made = []
            for head in range(2):
                scores = matmul_right_t(query[here, lanes] * masks[head], key[here, lanes])
                scores = jnp.where(allowed, scores, -jnp.inf)
                powers = jnp.exp(scores - jnp.max(scores, axis=1, keepdims=True))
                weights = powers / jnp.sum(powers, axis=1, keepdims=True)
                slot = count * (4 * at + 2 * pair + head)
                probs[slot : slot + count, :] = weights
                made.append(matmul(low(weights), value[here, lanes]))
            attended[here, lanes] = low(jnp.where(is_first, made[0], made[1]))
    total = low(matmul(attended[...], attn[...]))
    keep[:count, :], send[:count, :] = total[:count], total[count : 2 * count]
    keep[count:, :], send[count:, :] = total[2 * count : 3 * count], total[3 * count :]


def mlp(
    seg_col, norm_own, norm_across, norm_beside, mine, across, beside,
    first, second, third, own, other_first, other_second, other_third, other,
    normed, grad_out, mixed, grad_inner, send, keep, w_down,
    w_up, inner, grad_mixed,
):
    size, count, edge = own.shape[0], 128, w_up.shape[1]
    blocks = (first, second, third, own, other_first, other_second, other_third, other)
    for at, ref in enumerate(blocks):
        w_up[size * at : size * (at + 1), :] = ref[:, :edge]
        w_down[size * at : size * (at + 1), :] = ref[:, edge:]
    for at, ref in enumerate(
        (norm_own[...], norm_beside[:count, :], norm_across[...], norm_beside[count:, :])
    ):
        normed[count * at : count * (at + 1), :] = ref
    for at, ref in enumerate(token_rows(mine, across, beside, count, mine.shape[0])):
        live = wide(seg_col[count * at : count * (at + 1), :] < 8)
        grad_out[count * at : count * (at + 1), :] = low(wide(ref) * live)
    inner[...] = matmul(normed[...], w_up[...])
    grad_mixed[...] = matmul(grad_out[...], w_down[...])
    main = (w_down.shape[1] // LANES - 1) * LANES
    rest = 16

    def parts(gate):
        phi = 0.5 * (1.0 + lax.erf(gate * 0.7071067811865476))
        slope = phi + gate * jnp.exp(-0.5 * gate * gate) * 0.3989422804014327
        return gate * phi, slope

    @pl.loop(0, 8)
    def _(step):
        here = pl.ds(pl.multiple_of(step * 64, 64), 64)
        gate, up_part = inner[here, :main], inner[here, main : 2 * main]
        grad = grad_mixed[here, :main]
        activation, slope = parts(gate)
        mixed[here, :main] = low(activation * up_part)
        grad_inner[here, :main] = low(grad * up_part * slope)
        grad_inner[here, main : 2 * main] = low(grad * activation)
        tail = inner[here, 2 * main :]
        grad = grad_mixed[here, main:]
        activation, slope = parts(tail)
        tail_up = pltpu.roll(tail, LANES - rest, 1)
        mixed[here, main:] = low(activation * tail_up)
        grad_inner[here, 2 * main :] = low(
            grad * tail_up * slope + pltpu.roll(grad * activation, rest, 1)
        )

    total = low(matmul_right_t(grad_inner[...], w_up[...]))
    keep[:count, :], send[:count, :] = total[:count], total[count : 2 * count]
    keep[count:, :], send[count:, :] = total[2 * count : 3 * count], total[3 * count :]


def place_term(term, keep, pair, near, far, lanes):
    size = term.shape[0] // 8
    for at, (ref, row) in enumerate(
        [(keep, 0), (pair, 0), (keep, 1), (keep, 2), (near, 0), (pair, 1), (far, 0), (far, 1)]
    ):
        ref[size * row : size * (row + 1), lanes] = term[size * at : size * (at + 1)]


def mlp_terms(normed, grad_inner, grad_out, mixed, keep, pair, near, far):
    edge = grad_inner.shape[1]
    term = low(matmul_left_t(normed[...], grad_inner[...]))
    place_term(term, keep, pair, near, far, slice(0, edge))
    term = low(matmul_left_t(grad_out[...], mixed[...]))
    place_term(term, keep, pair, near, far, slice(edge, edge + mixed.shape[1]))


def attention_backward(
    place, cosine, sine, low_own, low_across, low_beside, attn, query, key, value, probs,
    attended, normed,
    grad_packed, keep, pair, near, far, grad_low, grad_attended, term_attn,
):
    count = 128
    for at, ref in enumerate(
        (low_own[...], low_beside[:count, :], low_across[...], low_beside[count:, :])
    ):
        grad_low[count * at : count * (at + 1), :] = ref
    grad_attended[...] = low(matmul_right_t(grad_low[...], attn[...]))
    masks, is_first = head_masks(count)
    for at in range(4):
        here = slice(count * at, count * (at + 1))
        cos, sin = cosine[here, :], sine[here, :]
        for half in range(2):
            lanes = slice(LANES * half, LANES * (half + 1))
            q, k, v = query[here, lanes], key[here, lanes], value[here, lanes]
            grad = grad_attended[here, lanes]
            made = []
            for head in range(2):
                slot = count * (4 * at + 2 * half + head)
                weights = probs[slot : slot + count, :]
                grad_value = matmul_left_t(low(weights), grad)
                grad_probs = matmul_right_t(grad * masks[head], v)
                delta = jnp.sum(weights * grad_probs, axis=1, keepdims=True)
                grad_scores = low(weights * (grad_probs - delta))
                made.append((matmul(grad_scores, k), matmul_left_t(grad_scores, q), grad_value))
            grad_q, grad_k, grad_v = (jnp.where(is_first, *both) for both in zip(*made))
            grad_q = grad_q * HEAD_DIM ** (-0.5)
            grad_packed[here, lanes] = low(grad_q * cos - turned(grad_q) * sin)
            lanes = slice(256 + LANES * half, 256 + LANES * (half + 1))
            grad_packed[here, lanes] = low(grad_k * cos - turned(grad_k) * sin)
            lanes = slice(512 + LANES * half, 512 + LANES * (half + 1))
            grad_packed[here, lanes] = low(grad_v)
    term = low(matmul_left_t(normed[...], grad_packed[...]))
    place_term(term, keep, pair, near, far, slice(0, 768))
    term_attn[...] = low(matmul_left_t(attended[...], grad_low[...]))
    size = term.shape[0] // 8
    part = size // 4
    targets = [
        (keep, 0), (pair, 0), (keep, size), (keep, 2 * size),
        (near, 0), (pair, size), (far, 0), (far, size),
    ]
    for at, (ref, row) in enumerate(targets):
        source = pl.multiple_of(place_of(place, at % 4, at // 4) * part, part)
        for z_at in range(4):
            for side in range(2):
                lanes = pl.multiple_of(block_of(place, z_at, side) * LANES, LANES)
                ref[
                    row + part * z_at : row + part * (z_at + 1),
                    768 + LANES * side : 768 + LANES * (side + 1),
                ] = term_attn[pl.ds(source, part), pl.ds(lanes, LANES)]


def projections(grad_packed, qkv, mixed, w_down, send, keep):
    count = 128
    for row, total in (
        (0, low(matmul_right_t(grad_packed[...], qkv[...]))),
        (count, low(matmul_right_t(mixed[...], w_down[...]))),
    ):
        keep[row : row + count, :] = total[:count]
        send[row : row + count, :] = total[count : 2 * count]
        keep[2 * count + row : 3 * count + row, :] = total[2 * count : 3 * count]
        send[2 * count + row : 3 * count + row, :] = total[3 * count :]


def kernel(body, outs, cost, *args, scratch=(), scalars=0):
    flops, transcendentals = cost
    shapes = [jax.ShapeDtypeStruct(shape, kind) for shape, kind in outs]
    moved = sum(arg.size * arg.dtype.itemsize for arg in (*args, *shapes))
    return pl.pallas_call(
        body,
        out_shape=shapes,
        in_specs=[
            pl.BlockSpec(memory_space=pltpu.SMEM if k < scalars else pltpu.VMEM)
            for k in range(len(args))
        ],
        out_specs=[pl.BlockSpec(memory_space=pltpu.VMEM)] * len(shapes),
        scratch_shapes=[pltpu.VMEM(shape, kind) for shape, kind in scratch],
        compiler_params=pltpu.CompilerParams(vmem_limit_bytes=48 * 2**20),
        cost_estimate=pl.CostEstimate(
            flops=flops, bytes_accessed=moved, transcendentals=transcendentals
        ),
        name=body.__name__,
    )(*args)


def scatter_last(send, keep):
    beside = split_rows(swap(send, 1), 2)
    kept = split_rows(keep, 2)
    sent = low(wide(kept[1]) + wide(beside[1]))
    return wide(kept[0]) + wide(beside[0]), sent


def local_ring(
    tokens,
    seq_lengths,
    cotangent,
    attention_norm_gain,
    w_qkv,
    w_attn_out,
    feedforward_norm_gain,
    w_in,
    w_out,
):
    count, width = tokens.shape
    index = lax.axis_index("fsdp")
    z, x = index // 2, index % 2
    place = jnp.stack([z, x]).astype(jnp.int32)
    hidden = w_in.shape[1] // 2
    part = hidden // 4
    main = part // LANES * LANES
    in_width, out_width = 2 * main + LANES, main + LANES
    f32, b16 = jnp.float32, jnp.bfloat16
    group = 4 * count

    gain_attn = wide(attention_norm_gain)[:, None]
    gain_mlp = wide(feedforward_norm_gain)[:, None]
    order = [(k, (k % 8) * 4 + k // 8) for k in range(32)]
    attn_own = lax.ppermute(w_attn_out, AXES, order)
    qkv_parts = split_columns(low(wide(w_qkv) * gain_attn), 12)
    size = w_qkv.shape[0]
    slots = seq_lengths.shape[1]
    lengths_low = jnp.pad(low(wide(seq_lengths)), ((0, size - 1), (0, LANES - slots)))
    exchanged = rep_exchange(rows([columns([*qkv_parts[k::4], lengths_low]) for k in range(4)]))
    first_own = columns([exchanged[:, :768], rows(split_columns(attn_own, 4))])
    lengths = rows([exchanged[size * k : size * k + 1, 768 : 768 + slots] for k in range(4)])
    lengths = wide(lengths).astype(jnp.int32)
    for bit in (1, 2):
        turned_rows = rows([lengths[k ^ bit : (k ^ bit) + 1] for k in range(4)])
        lengths = jnp.where((lax.axis_index("rep") & bit) != 0, turned_rows, lengths)

    scaled_in = low(wide(w_in) * gain_mlp)
    pieces = []
    for k in range(4):
        gate = scaled_in[:, part * k : part * (k + 1)]
        up_part = scaled_in[:, hidden + part * k : hidden + part * (k + 1)]
        out_part = w_out[:, part * k : part * (k + 1)]
        fill = [jnp.zeros((w_in.shape[0], n), b16) for n in (in_width - 2 * part, out_width - part)]
        pieces.append(
            columns(
                [gate[:, :main], up_part[:, :main], gate[:, main:], up_part[:, main:], fill[0]]
                + [out_part, fill[1]]
            )
        )
    mine = rows([relative(tokens, z, x), relative(cotangent, z, x)])
    first_own, rest, mine = tie(first_own, rows(pieces), mine)
    rest = rep_exchange(rest)

    third, first, other = up(first_own), down(first_own), over(first_own)
    third, first, other, mine, rest = tie(third, first, other, mine, rest)
    across = swap(mine, 2)
    second, others = up(third), over(rows([first, third]))
    second, others, across, rest = tie(second, others, across, rest)
    other_second = over(second)
    rest_third, rest_first = up(rest), down(rest)
    beside = swap(rows([mine, across]), 1)
    rest_other = over(tie(rest, other_second, beside)[0])

    step = mine.shape[0]
    segment, positions, _ = jax.vmap(lambda row: layout(row, count))(lengths)
    frequency = rope_base ** (-(lax.iota(f32, HALF) * (2.0 / HEAD_DIM)))
    angles = positions.reshape(group, 1).astype(f32) * frequency
    cosine, sine = jnp.cos(angles), jnp.sin(angles)
    cosine, sine = columns([cosine] * 4), columns([-sine, sine] * 2)
    seg_col = segment.reshape(group, 1)

    normed, qkv, attn, query, key, value, probs, attended, send, keep = kernel(
        attention_forward,
        [((group, width), b16), ((width, 768), b16), ((256, width), b16)]
        + [((group, 256), b16)] * 3
        + [((16 * count, count), f32), ((group, 256), b16)]
        + [((2 * count, width), b16)] * 2,
        (2 * group * width * (768 + 256) + 4 * 16 * count * count * LANES, 16 * count * count),
        place, seg_col, segment, cosine, sine, mine, across, beside,
        first, second, third, first_own, others, other_second, other,
        scalars=1,
    )
    rest_third, rest_first, rest_other, send = tie(rest_third, rest_first, rest_other, send)
    rest_second, rest_other_third = up(rest_third), over(rest_third)
    x_own = wide(mine[:count])
    kept, sent = scatter_last(send, keep)
    rest_other_first = over(tie(rest_first, rest_other_third)[0])
    hidden_sum = x_own + kept + wide(swap(sent, 2))
    standard_mlp, inverse_mlp = norm_statistics(hidden_sum)
    norm_own = low(standard_mlp)
    norm_across = swap(norm_own, 2)
    rest_second, rest_other_third, _ = tie(rest_second, rest_other_third, norm_own)
    rest_other_second = up(rest_other_third)
    norm_beside = swap(rows([norm_own, norm_across]), 1)

    normed_mlp, grad_out, mixed, grad_inner, send, keep, w_down = kernel(
        mlp,
        [((group, width), b16)] * 2
        + [((group, out_width), b16), ((group, in_width), b16)]
        + [((2 * count, width), b16)] * 2
        + [((width, out_width), b16)],
        (2 * group * width * (2 * in_width + out_width), 3 * group * part),
        seg_col, norm_own, norm_across, norm_beside, mine, across, beside,
        rest_first, rest_second, rest_third, rest,
        rest_other_first, rest_other_second, rest_other_third, rest_other,
        scratch=[
            ((width, in_width), b16),
            ((group, in_width), f32),
            ((group, out_width), f32),
        ],
    )
    all_width = in_width + out_width
    size = width // 8
    io_keep, io_pair, io_near, io_far = kernel(
        mlp_terms,
        [((size * n, all_width), b16) for n in (3, 2, 1, 2)],
        (2 * group * width * all_width, 0),
        normed_mlp, grad_inner, grad_out, mixed,
    )
    io_pair, io_far = up(io_pair), over(io_far)
    kept, sent = scatter_last(send, keep)
    scaled_mlp = kept + wide(swap(sent, 2))
    grad_hidden = wide(grad_out[:count]) + norm_backward_pass(
        scaled_mlp, jnp.ones((), f32), standard_mlp, inverse_mlp
    )
    low_own = low(grad_hidden)
    low_across = swap(low_own, 2)
    low_beside = swap(rows([low_own, low_across]), 1)

    grad_packed, g_keep, g_pair, g_near, g_far = kernel(
        attention_backward,
        [((group, 768), b16)] + [((size * n, width), b16) for n in (3, 2, 1, 2)],
        (2 * group * width * (768 + 512) + 10 * 16 * count * count * LANES, 0),
        place, cosine, sine, low_own, low_across, low_beside, attn, query, key, value, probs,
        attended, normed,
        scratch=[((group, width), b16), ((group, 256), b16), ((256, width), b16)],
        scalars=1,
    )
    g_pair, g_far = up(g_pair), over(g_far)
    io_pair, io_far, _ = tie(io_pair, io_far, g_near)
    io_kept, io_pair, io_far = split_rows(io_keep, 3), split_rows(io_pair, 2), split_rows(io_far, 2)
    io_near = over(low(wide(io_near) + wide(io_pair[1])))
    io_down = down(low(wide(io_kept[1]) + wide(io_far[0])))
    send, keep = kernel(
        projections,
        [((4 * count, width), b16)] * 2,
        (2 * group * width * (768 + out_width), 0),
        grad_packed, qkv, mixed, w_down,
    )
    io_near, io_down, g_pair, g_far, send = tie(io_near, io_down, g_pair, g_far, send)
    g_kept, g_pair, g_far = split_rows(g_keep, 3), split_rows(g_pair, 2), split_rows(g_far, 2)
    g_near = over(low(wide(g_near) + wide(g_pair[1])))
    g_down = down(low(wide(g_kept[1]) + wide(g_far[0])))
    kept, sent = scatter_last(send, keep)
    io_up = up(low(wide(io_kept[0]) + wide(io_pair[0]) + wide(io_near)))
    io_up, g_near, g_down, sent = tie(io_up, g_near, g_down, sent)
    g_up = up(low(wide(g_kept[0]) + wide(g_pair[0]) + wide(g_near)))
    last_across = swap(sent, 2)
    back = rep_exchange(
        low(wide(io_kept[2]) + wide(io_far[1]) + wide(io_down) + wide(io_up))
    )
    g_up, g_down, last_across = tie(g_up, g_down, last_across)
    last = kept + wide(last_across)
    sum_g = low(wide(g_kept[2]) + wide(g_far[1]) + wide(g_down) + wide(g_up))
    back_qkv = rep_exchange(sum_g[:, :768])
    grad_w_attn_out = wide(
        lax.ppermute(
            columns(split_rows(sum_g[:, 768:], 4)), AXES, [(there, here) for here, there in order]
        )
    )

    standard, inverse = norm_statistics(x_own)
    block_input_gradient = grad_hidden + norm_backward_pass(
        last[:count], jnp.ones((), f32), standard, inverse
    )
    output = low(jnp.where(seg_col[:count] < 8, hidden_sum + last[count:], 0.0))
    back = split_rows(back, 4)
    back_qkv = [split_columns(piece, 3) for piece in split_rows(back_qkv, 4)]
    unit_qkv = wide(columns([piece[k] for k in range(3) for piece in back_qkv]))
    rest_width = part - main
    unit_in = wide(
        columns(
            [
                value
                for k in range(2)
                for piece in back
                for value in (
                    piece[:, main * k : main * (k + 1)],
                    piece[:, 2 * main + rest_width * k : 2 * main + rest_width * (k + 1)],
                )
            ]
        )
    )
    grad_w_out = wide(columns([piece[:, in_width : in_width + part] for piece in back]))
    return (
        absolute(output, z, x),
        absolute(block_input_gradient, z, x),
        jnp.sum(unit_qkv * wide(w_qkv), axis=1),
        unit_qkv * gain_attn,
        grad_w_attn_out,
        jnp.sum(unit_in * wide(w_in), axis=1),
        unit_in * gain_mlp,
        grad_w_out,
    )


def solution(mesh):
    ringed = dict(mesh.shape) == {"fsdp": 8, "rep": 4}
    return jax.shard_map(
        local_ring if ringed else local_plain,
        mesh=mesh,
        in_specs=(
            P(AXES, None),
            P(AXES, None),
            P(AXES, None),
            P(AXES),
            P(AXES, None),
            P(AXES, None),
            P(AXES),
            P(AXES, None),
            P(AXES, None),
        ),
        out_specs=(
            P(AXES, None),
            P(AXES, None),
            P(AXES),
            P(AXES, None),
            P(AXES, None),
            P(AXES),
            P(AXES, None),
            P(AXES, None),
        ),
        check_vma=False,
    )
```

```python
import jax
import jax.numpy as jnp
from jax import lax
from jax.experimental import pallas as pl
from jax.experimental.pallas import tpu as pltpu
from jax.sharding import PartitionSpec as P

HEAD_DIM = 64


norm_eps = 1e-05
rope_base = 160000.0


def matmul(left_side, right_side):
    return jnp.dot(left_side, right_side, preferred_element_type=jnp.float32)


def matmul_right_t(left_side, right_side):
    return lax.dot_general(
        left_side, right_side, (((1,), (1,)), ((), ())), preferred_element_type=jnp.float32
    )


def matmul_left_t(left_side, right_side):
    return lax.dot_general(
        left_side, right_side, (((0,), (0,)), ((), ())), preferred_element_type=jnp.float32
    )


def batched(form, left_side, right_side):
    return jnp.einsum(form, left_side, right_side, preferred_element_type=jnp.float32)


def layout(lengths, row_count):
    slot_ids = lax.iota(jnp.int32, lengths.shape[0])
    before = (slot_ids[:, None] <= slot_ids[None, :]).astype(jnp.int32)
    ends = jnp.sum(lengths[:, None] * before, axis=0)
    starts = ends - lengths
    places = lax.iota(jnp.int32, row_count)
    sequence_segment = jnp.sum((ends[None, :] <= places[:, None]).astype(jnp.int32), axis=1)
    first_row = jnp.sum(
        jnp.where(sequence_segment[:, None] == slot_ids[None, :], starts[None, :], 0), axis=1
    )
    return (sequence_segment, places - first_row, sequence_segment < lengths.shape[0])


def rotary(positions, head_size):
    half_size = head_size // 2
    frequency = rope_base ** (-(lax.iota(jnp.float32, half_size) * (2.0 / head_size)))
    angles = positions.astype(jnp.float32)[..., None] * frequency
    cosine_table = jnp.concatenate([jnp.cos(angles), jnp.cos(angles)], axis=-1)
    sine_table = jnp.concatenate([jnp.sin(angles), jnp.sin(angles)], axis=-1)
    return (cosine_table, sine_table)


def rotate_half(vector):
    half_size = vector.shape[-1] // 2
    return jnp.concatenate([-vector[..., half_size:], vector[..., :half_size]], axis=-1)


def rotate_back(vector):
    half_size = vector.shape[-1] // 2
    return jnp.concatenate([vector[..., half_size:], -vector[..., :half_size]], axis=-1)


def norm_statistics(values):
    average = jnp.mean(values, axis=-1, keepdims=True)
    centred = values - average
    inverse = lax.rsqrt(jnp.mean(centred * centred, axis=-1, keepdims=True) + norm_eps)
    return (centred * inverse, inverse)


def norm_backward_pass(grad_normed, gain_vec, normalized, inverse):
    scaled = grad_normed * gain_vec.astype(jnp.float32)
    return inverse * (
        scaled
        - jnp.mean(scaled, axis=-1, keepdims=True)
        - normalized * jnp.mean(scaled * normalized, axis=-1, keepdims=True)
    )


def attend(rotated_query, rotated_key, value_reduced_precision, sequence_segment):
    scores = batched("thd,shd->hts", rotated_query, rotated_key)
    allowed = sequence_segment[:, None] == sequence_segment[None, :]
    scores = jnp.where(allowed[None], scores, -jnp.inf)
    logarithm_totals = jax.nn.logsumexp(scores, axis=-1)
    weights = jnp.exp(scores - logarithm_totals[..., None]).astype(jnp.bfloat16)
    attended = batched("hts,shd->thd", weights, value_reduced_precision).astype(jnp.bfloat16)
    return (attended, logarithm_totals)


def attend_back(
    rotated_query,
    rotated_key,
    value_reduced_precision,
    sequence_segment,
    logarithm_totals,
    grad_attended,
):
    scores = batched("thd,shd->hts", rotated_query, rotated_key)
    allowed = sequence_segment[:, None] == sequence_segment[None, :]
    scores = jnp.where(allowed[None], scores, -jnp.inf)
    probs_full = jnp.exp(scores - logarithm_totals[..., None])
    weights = probs_full.astype(jnp.bfloat16)
    grad_value = batched("hts,thd->shd", weights, grad_attended)
    grad_probs = batched("thd,shd->hts", grad_attended, value_reduced_precision)
    row_delta = jnp.sum(probs_full * grad_probs, axis=-1, keepdims=True)
    grad_scores = (probs_full * (grad_probs - row_delta)).astype(jnp.bfloat16)
    grad_query = batched("hts,shd->thd", grad_scores, rotated_key)
    grad_key = batched("hts,thd->shd", grad_scores, rotated_query)
    return (grad_query, grad_key, grad_value)


def forward(
    tokens, lengths, attention_norm_gain, w_qkv, w_attn_out, feedforward_norm_gain, w_in, w_out
):
    groups, row_count, embedding_width = tokens.shape
    head_count = embedding_width // HEAD_DIM
    hidden_units = w_in.shape[1] // 2
    sequence_segment, positions, valid = jax.vmap(
        lambda row_lengths: layout(row_lengths, row_count)
    )(lengths)
    cosine_table, sine_table = rotary(positions, HEAD_DIM)
    cosine_table = cosine_table[:, :, None, :]
    sine_table = sine_table[:, :, None, :]
    residual_input = tokens.reshape(groups * row_count, embedding_width).astype(jnp.float32)
    attention_standardized, attention_inverse_norm = norm_statistics(residual_input)
    attention_normed_input = (
        attention_standardized * attention_norm_gain.astype(jnp.float32)
    ).astype(jnp.bfloat16)
    packed = matmul(attention_normed_input, w_qkv).reshape(
        groups, row_count, 3, head_count, HEAD_DIM
    )
    query_raw = packed[:, :, 0]
    key_raw = packed[:, :, 1]
    rotated_query = (
        (query_raw * cosine_table + rotate_half(query_raw) * sine_table) * HEAD_DIM ** (-0.5)
    ).astype(jnp.bfloat16)
    rotated_key = (key_raw * cosine_table + rotate_half(key_raw) * sine_table).astype(jnp.bfloat16)
    value_reduced_precision = packed[:, :, 2].astype(jnp.bfloat16)
    attended, logarithm_totals = jax.vmap(attend)(
        rotated_query, rotated_key, value_reduced_precision, sequence_segment
    )
    attention_rows_flat = attended.reshape(groups * row_count, embedding_width)
    hidden_residual = residual_input + matmul(attention_rows_flat, w_attn_out)
    feedforward_standardized, feedforward_inverse_norm = norm_statistics(hidden_residual)
    feedforward_normed_input = (
        feedforward_standardized * feedforward_norm_gain.astype(jnp.float32)
    ).astype(jnp.bfloat16)
    inner_proj = matmul(feedforward_normed_input, w_in)
    gate_projection = inner_proj[:, :hidden_units]
    up_projection = inner_proj[:, hidden_units:]
    activation_output = jax.nn.gelu(gate_projection, approximate=False)
    mixed_input = (activation_output * up_projection).astype(jnp.bfloat16)
    live_token_rows = valid.reshape(groups * row_count, 1)
    mlp_result = matmul_right_t(mixed_input, w_out)
    output = jnp.where(live_token_rows, hidden_residual + mlp_result, 0.0).astype(jnp.bfloat16)
    saved_residuals = (
        sequence_segment,
        live_token_rows,
        cosine_table,
        sine_table,
        attention_standardized,
        attention_inverse_norm,
        attention_normed_input,
        rotated_query,
        rotated_key,
        value_reduced_precision,
        logarithm_totals,
        attention_rows_flat,
        feedforward_standardized,
        feedforward_inverse_norm,
        feedforward_normed_input,
        gate_projection,
        up_projection,
        activation_output,
        mixed_input,
    )
    return (output, saved_residuals)


def backward(
    saved_residuals,
    cotangent,
    attention_norm_gain,
    w_qkv,
    w_attn_out,
    feedforward_norm_gain,
    w_in,
    w_out,
):
    (
        sequence_segment,
        live_token_rows,
        cosine_table,
        sine_table,
        attention_standardized,
        attention_inverse_norm,
        attention_normed_input,
        rotated_query,
        rotated_key,
        value_reduced_precision,
        logarithm_totals,
        attention_rows_flat,
        feedforward_standardized,
        feedforward_inverse_norm,
        feedforward_normed_input,
        gate_projection,
        up_projection,
        activation_output,
        mixed_input,
    ) = saved_residuals
    groups, row_count = sequence_segment.shape
    embedding_width = attention_standardized.shape[1]
    head_count = embedding_width // HEAD_DIM
    flat_cot = cotangent.reshape(groups * row_count, embedding_width)
    output_gradient = jnp.where(live_token_rows, flat_cot, jnp.zeros((), flat_cot.dtype))
    grad_mixed = matmul(output_gradient, w_out)
    slope = (
        0.5 * (1.0 + lax.erf(gate_projection * 0.7071067811865476))
        + gate_projection * jnp.exp(-0.5 * gate_projection * gate_projection) * 0.3989422804014327
    )
    grad_inner = jnp.concatenate(
        [grad_mixed * up_projection * slope, grad_mixed * activation_output], axis=1
    ).astype(jnp.bfloat16)
    feedforward_normed_gradient = matmul_right_t(grad_inner, w_in)
    hidden_gradient = output_gradient.astype(jnp.float32) + norm_backward_pass(
        feedforward_normed_gradient,
        feedforward_norm_gain,
        feedforward_standardized,
        feedforward_inverse_norm,
    )
    grad_hidden_low = hidden_gradient.astype(jnp.bfloat16)
    grad_attended = matmul_right_t(grad_hidden_low, w_attn_out).astype(jnp.bfloat16)
    grad_attended = grad_attended.reshape(groups, row_count, head_count, HEAD_DIM)
    grad_query, grad_key, grad_value = jax.vmap(attend_back)(
        rotated_query,
        rotated_key,
        value_reduced_precision,
        sequence_segment,
        logarithm_totals,
        grad_attended,
    )
    grad_query = grad_query * HEAD_DIM ** (-0.5)
    grad_query = grad_query * cosine_table + rotate_back(grad_query * sine_table)
    grad_key = grad_key * cosine_table + rotate_back(grad_key * sine_table)
    grad_packed = jnp.stack([grad_query, grad_key, grad_value], axis=2)
    grad_packed = grad_packed.reshape(groups * row_count, 3 * embedding_width).astype(jnp.bfloat16)
    attention_normed_gradient = matmul_right_t(grad_packed, w_qkv)
    block_input_gradient = hidden_gradient + norm_backward_pass(
        attention_normed_gradient,
        attention_norm_gain,
        attention_standardized,
        attention_inverse_norm,
    )
    factors = (
        attention_normed_input,
        grad_packed,
        attention_rows_flat,
        grad_hidden_low,
        feedforward_normed_input,
        grad_inner,
        output_gradient,
        mixed_input,
        attention_normed_gradient,
        attention_standardized,
        feedforward_normed_gradient,
        feedforward_standardized,
    )
    return (block_input_gradient, factors)


def local_plain(
    tokens,
    seq_lengths,
    cotangent,
    attention_norm_gain,
    w_qkv,
    w_attn_out,
    feedforward_norm_gain,
    w_in,
    w_out,
):
    row_count, embedding_width = tokens.shape
    gathered = (
        lax.all_gather(attention_norm_gain, ("fsdp", "rep"), axis=0, tiled=True),
        lax.all_gather(w_qkv, ("fsdp", "rep"), axis=0, tiled=True),
        lax.all_gather(w_attn_out, ("fsdp", "rep"), axis=0, tiled=True),
        lax.all_gather(feedforward_norm_gain, ("fsdp", "rep"), axis=0, tiled=True),
        lax.all_gather(w_in, ("fsdp", "rep"), axis=0, tiled=True),
        lax.all_gather(w_out, ("fsdp", "rep"), axis=0, tiled=True),
    )
    output, saved_residuals = forward(
        tokens.reshape(1, row_count, embedding_width),
        seq_lengths,
        gathered[0],
        gathered[1],
        gathered[2],
        gathered[3],
        gathered[4],
        gathered[5],
    )
    second_copy = (
        lax.all_gather(attention_norm_gain, ("fsdp", "rep"), axis=0, tiled=True),
        lax.all_gather(w_qkv, ("fsdp", "rep"), axis=0, tiled=True),
        lax.all_gather(w_attn_out, ("fsdp", "rep"), axis=0, tiled=True),
        lax.all_gather(feedforward_norm_gain, ("fsdp", "rep"), axis=0, tiled=True),
        lax.all_gather(w_in, ("fsdp", "rep"), axis=0, tiled=True),
        lax.all_gather(w_out, ("fsdp", "rep"), axis=0, tiled=True),
    )
    block_input_gradient, factors = backward(
        saved_residuals,
        cotangent.reshape(1, row_count, embedding_width),
        second_copy[0],
        second_copy[1],
        second_copy[2],
        second_copy[3],
        second_copy[4],
        second_copy[5],
    )
    (
        normed_attn,
        grad_packed,
        attended_rows,
        grad_hidden_low,
        normed_mlp,
        grad_inner,
        grad_out,
        mixed_input,
        grad_normed_attn,
        standard_attn,
        grad_normed_mlp,
        standard_mlp,
    ) = factors
    qkv_width = w_qkv.shape[1]
    attn_width = w_attn_out.shape[1]
    inner_width = w_in.shape[1]
    outer_width = w_out.shape[1]
    qkv_term = matmul_left_t(normed_attn, grad_packed)
    attn_term = matmul_left_t(attended_rows, grad_hidden_low)
    inner_term = matmul_left_t(normed_mlp, grad_inner)
    outer_term = matmul_left_t(grad_out, mixed_input)
    attn_gain_term = jnp.sum(grad_normed_attn * standard_attn, axis=0)
    mlp_gain_term = jnp.sum(grad_normed_mlp * standard_mlp, axis=0)
    summed = lax.psum_scatter(
        jnp.concatenate(
            [
                qkv_term,
                attn_term,
                inner_term,
                outer_term,
                attn_gain_term[:, None],
                mlp_gain_term[:, None],
            ],
            axis=1,
        ),
        ("fsdp", "rep"),
        scatter_dimension=0,
        tiled=True,
    )
    edge_two = qkv_width + attn_width
    edge_three = edge_two + inner_width
    edge_four = edge_three + outer_width
    return (
        output,
        block_input_gradient,
        summed[:, edge_four],
        summed[:, :qkv_width],
        summed[:, qkv_width:edge_two],
        summed[:, edge_four + 1],
        summed[:, edge_two:edge_three],
        summed[:, edge_three:edge_four],
    )


AXES = ("fsdp", "rep")
LANES = 128
HALF = HEAD_DIM // 2


def tie(*values):
    return lax.optimization_barrier(values)


def wide(value):
    return value.astype(jnp.float32)


def low(value):
    return value.astype(jnp.bfloat16)


def split_columns(value, count):
    width = value.shape[1] // count
    return [value[:, k * width : (k + 1) * width] for k in range(count)]


def split_rows(value, count):
    width = value.shape[0] // count
    return [value[k * width : (k + 1) * width] for k in range(count)]


def columns(blocks):
    return jnp.concatenate(blocks, axis=1)


def rows(blocks):
    return jnp.concatenate(blocks, axis=0)


def swap(value, distance):
    return lax.ppermute(value, "rep", [(k, k ^ distance) for k in range(4)])


def rep_exchange(value):
    blocks = value.reshape(4, value.shape[0] // 4, value.shape[1])
    return lax.all_to_all(blocks, "rep", 0, 0, tiled=True).reshape(value.shape)


def up(value):
    return lax.ppermute(value, "fsdp", [(k, (k + 2) % 8) for k in range(8)])


def down(value):
    return lax.ppermute(value, "fsdp", [(k, (k - 2) % 8) for k in range(8)])


def over(value):
    return lax.ppermute(value, "fsdp", [(k, k ^ 1) for k in range(8)])


def relative(value, z, x):
    blocks = split_columns(value, 8)
    blocks = [jnp.where(x == 1, blocks[k ^ 1], blocks[k]) for k in range(8)]
    for bit in (1, 2):
        turn = (z & bit) != 0
        blocks = [jnp.where(turn, blocks[(k + 2 * bit) % 8], blocks[k]) for k in range(8)]
    return columns([blocks[2 * ((p + 1) % 4) + i] for i in range(2) for p in range(4)])


def absolute(value, z, x):
    blocks = split_columns(value, 8)
    blocks = [blocks[4 * i + (j - 1) % 4] for j in range(4) for i in range(2)]
    blocks = [jnp.where(x == 1, blocks[k ^ 1], blocks[k]) for k in range(8)]
    for bit in (1, 2):
        turn = (z & bit) != 0
        blocks = [jnp.where(turn, blocks[(k - 2 * bit) % 8], blocks[k]) for k in range(8)]
    return columns(blocks)


def place_of(place, step, side):
    z, x = place[0], place[1]
    return 2 * lax.rem(z + step + 1, 4) + (x if side == 0 else 1 - x)


def block_of(place, z_at, side):
    z, x = place[0], place[1]
    return 4 * (x if side == 0 else 1 - x) + lax.rem(z_at - z + 7, 4)


def turned(value):
    width = value.shape[1]
    lane = lax.broadcasted_iota(jnp.int32, value.shape, 1)
    return jnp.where(
        lane % HEAD_DIM < HALF,
        pltpu.roll(value, width - HALF, 1),
        pltpu.roll(value, HALF, 1),
    )


def head_masks(row_count):
    lane = lax.broadcasted_iota(jnp.int32, (row_count, LANES), 1)
    return [low(wide(lane < HEAD_DIM)), low(wide(lane >= HEAD_DIM))], lane < HEAD_DIM


def token_rows(mine, across, beside, first, step):
    count = 128
    return [
        mine[first : first + count],
        beside[first : first + count],
        across[first : first + count],
        beside[step + first : step + first + count],
    ]


def attention_forward(
    place, seg_col, seg_row, cosine, sine, mine, across, beside,
    first, second, third, own, others, other_second, other,
    normed, qkv, attn, query, key, value, probs, attended, send, keep,
):
    size = own.shape[0]
    blocks = [
        (first, 0), (second, 0), (third, 0), (own, 0),
        (others, 0), (other_second, 0), (others, size), (other, 0),
    ]
    part = size // 4
    for at, (ref, row) in enumerate(blocks):
        qkv[size * at : size * (at + 1), :] = ref[row : row + size, :768]
        target = pl.multiple_of(place_of(place, at % 4, at // 4) * part, part)
        for z_at in range(4):
            for side in range(2):
                lanes = pl.multiple_of(block_of(place, z_at, side) * LANES, LANES)
                attn[pl.ds(target, part), pl.ds(lanes, LANES)] = ref[
                    row + part * z_at : row + part * (z_at + 1),
                    768 + LANES * side : 768 + LANES * (side + 1),
                ]
    count = 128
    for at, ref in enumerate(token_rows(mine, across, beside, 0, mine.shape[0])):
        values = wide(ref)
        centred = values - jnp.mean(values, axis=1, keepdims=True)
        inverse = lax.rsqrt(jnp.mean(centred * centred, axis=1, keepdims=True) + norm_eps)
        normed[count * at : count * (at + 1), :] = low(centred * inverse)
    packed = matmul(normed[...], qkv[...])
    cos_all, sin_all = columns([cosine[...]] * 2), columns([sine[...]] * 2)
    raw = packed[:, :256]
    query[...] = low((raw * cos_all + turned(raw) * sin_all) * HEAD_DIM ** (-0.5))
    raw = packed[:, 256:512]
    key[...] = low(raw * cos_all + turned(raw) * sin_all)
    value[...] = low(packed[:, 512:])
    masks, is_first = head_masks(count)
    for at in range(4):
        here = slice(count * at, count * (at + 1))
        allowed = seg_col[here, :] == seg_row[at : at + 1, :]
        for pair in range(2):
            lanes = slice(LANES * pair, LANES * (pair + 1))
            made = []
            for head in range(2):
                scores = matmul_right_t(query[here, lanes] * masks[head], key[here, lanes])
                scores = jnp.where(allowed, scores, -jnp.inf)
                powers = jnp.exp(scores - jnp.max(scores, axis=1, keepdims=True))
                weights = powers / jnp.sum(powers, axis=1, keepdims=True)
                slot = count * (4 * at + 2 * pair + head)
                probs[slot : slot + count, :] = weights
                made.append(matmul(low(weights), value[here, lanes]))
            attended[here, lanes] = low(jnp.where(is_first, made[0], made[1]))
    total = low(matmul(attended[...], attn[...]))
    keep[:count, :], send[:count, :] = total[:count], total[count : 2 * count]
    keep[count:, :], send[count:, :] = total[2 * count : 3 * count], total[3 * count :]


def mlp(
    seg_col, norm_own, norm_across, norm_beside, mine, across, beside,
    first, second, third, own, other_first, other_second, other_third, other,
    normed, grad_out, mixed, grad_inner, send, keep, w_down,
    w_up, inner, grad_mixed,
):
    size, count, edge = own.shape[0], 128, w_up.shape[1]
    blocks = (first, second, third, own, other_first, other_second, other_third, other)
    for at, ref in enumerate(blocks):
        w_up[size * at : size * (at + 1), :] = ref[:, :edge]
        w_down[size * at : size * (at + 1), :] = ref[:, edge:]
    for at, ref in enumerate(
        (norm_own[...], norm_beside[:count, :], norm_across[...], norm_beside[count:, :])
    ):
        normed[count * at : count * (at + 1), :] = ref
    for at, ref in enumerate(token_rows(mine, across, beside, count, mine.shape[0])):
        live = wide(seg_col[count * at : count * (at + 1), :] < 8)
        grad_out[count * at : count * (at + 1), :] = low(wide(ref) * live)
    inner[...] = matmul(normed[...], w_up[...])
    grad_mixed[...] = matmul(grad_out[...], w_down[...])
    main = (w_down.shape[1] // LANES - 1) * LANES
    rest = 16

    def parts(gate):
        phi = 0.5 * (1.0 + lax.erf(gate * 0.7071067811865476))
        slope = phi + gate * jnp.exp(-0.5 * gate * gate) * 0.3989422804014327
        return gate * phi, slope

    @pl.loop(0, 8)
    def _(step):
        here = pl.ds(pl.multiple_of(step * 64, 64), 64)
        gate, up_part = inner[here, :main], inner[here, main : 2 * main]
        grad = grad_mixed[here, :main]
        activation, slope = parts(gate)
        mixed[here, :main] = low(activation * up_part)
        grad_inner[here, :main] = low(grad * up_part * slope)
        grad_inner[here, main : 2 * main] = low(grad * activation)
        tail = inner[here, 2 * main :]
        grad = grad_mixed[here, main:]
        activation, slope = parts(tail)
        tail_up = pltpu.roll(tail, LANES - rest, 1)
        mixed[here, main:] = low(activation * tail_up)
        grad_inner[here, 2 * main :] = low(
            grad * tail_up * slope + pltpu.roll(grad * activation, rest, 1)
        )

    total = low(matmul_right_t(grad_inner[...], w_up[...]))
    keep[:count, :], send[:count, :] = total[:count], total[count : 2 * count]
    keep[count:, :], send[count:, :] = total[2 * count : 3 * count], total[3 * count :]


def place_term(term, keep, pair, near, far, lanes):
    size = term.shape[0] // 8
    for at, (ref, row) in enumerate(
        [(keep, 0), (pair, 0), (keep, 1), (keep, 2), (near, 0), (pair, 1), (far, 0), (far, 1)]
    ):
        ref[size * row : size * (row + 1), lanes] = term[size * at : size * (at + 1)]


def mlp_terms(normed, grad_inner, grad_out, mixed, keep, pair, near, far):
    edge = grad_inner.shape[1]
    term = low(matmul_left_t(normed[...], grad_inner[...]))
    place_term(term, keep, pair, near, far, slice(0, edge))
    term = low(matmul_left_t(grad_out[...], mixed[...]))
    place_term(term, keep, pair, near, far, slice(edge, edge + mixed.shape[1]))


def attention_backward(
    place, cosine, sine, low_own, low_across, low_beside, attn, query, key, value, probs,
    attended, normed,
    grad_packed, keep, pair, near, far, grad_low, grad_attended, term_attn,
):
    count = 128
    for at, ref in enumerate(
        (low_own[...], low_beside[:count, :], low_across[...], low_beside[count:, :])
    ):
        grad_low[count * at : count * (at + 1), :] = ref
    grad_attended[...] = low(matmul_right_t(grad_low[...], attn[...]))
    masks, is_first = head_masks(count)
    for at in range(4):
        here = slice(count * at, count * (at + 1))
        cos, sin = cosine[here, :], sine[here, :]
        for half in range(2):
            lanes = slice(LANES * half, LANES * (half + 1))
            q, k, v = query[here, lanes], key[here, lanes], value[here, lanes]
            grad = grad_attended[here, lanes]
            made = []
            for head in range(2):
                slot = count * (4 * at + 2 * half + head)
                weights = probs[slot : slot + count, :]
                grad_value = matmul_left_t(low(weights), grad)
                grad_probs = matmul_right_t(grad * masks[head], v)
                delta = jnp.sum(weights * grad_probs, axis=1, keepdims=True)
                grad_scores = low(weights * (grad_probs - delta))
                made.append((matmul(grad_scores, k), matmul_left_t(grad_scores, q), grad_value))
            grad_q, grad_k, grad_v = (jnp.where(is_first, *both) for both in zip(*made))
            grad_q = grad_q * HEAD_DIM ** (-0.5)
            grad_packed[here, lanes] = low(grad_q * cos - turned(grad_q) * sin)
            lanes = slice(256 + LANES * half, 256 + LANES * (half + 1))
            grad_packed[here, lanes] = low(grad_k * cos - turned(grad_k) * sin)
            lanes = slice(512 + LANES * half, 512 + LANES * (half + 1))
            grad_packed[here, lanes] = low(grad_v)
    term = low(matmul_left_t(normed[...], grad_packed[...]))
    place_term(term, keep, pair, near, far, slice(0, 768))
    term_attn[...] = low(matmul_left_t(attended[...], grad_low[...]))
    size = term.shape[0] // 8
    part = size // 4
    targets = [
        (keep, 0), (pair, 0), (keep, size), (keep, 2 * size),
        (near, 0), (pair, size), (far, 0), (far, size),
    ]
    for at, (ref, row) in enumerate(targets):
        source = pl.multiple_of(place_of(place, at % 4, at // 4) * part, part)
        for z_at in range(4):
            for side in range(2):
                lanes = pl.multiple_of(block_of(place, z_at, side) * LANES, LANES)
                ref[
                    row + part * z_at : row + part * (z_at + 1),
                    768 + LANES * side : 768 + LANES * (side + 1),
                ] = term_attn[pl.ds(source, part), pl.ds(lanes, LANES)]


def projections(grad_packed, qkv, mixed, w_down, send, keep):
    count = 128
    for row, total in (
        (0, low(matmul_right_t(grad_packed[...], qkv[...]))),
        (count, low(matmul_right_t(mixed[...], w_down[...]))),
    ):
        keep[row : row + count, :] = total[:count]
        send[row : row + count, :] = total[count : 2 * count]
        keep[2 * count + row : 3 * count + row, :] = total[2 * count : 3 * count]
        send[2 * count + row : 3 * count + row, :] = total[3 * count :]


def unpack_rest(back, w_in, gain, grad_in, gain_grad, grad_out):
    size, hidden, part = w_in.shape[0], w_in.shape[1] // 2, w_in.shape[1] // 8
    main = part // LANES * LANES
    rest, edge = part - main, 2 * main + LANES
    total = jnp.zeros(gain_grad.shape, jnp.float32)
    for k in range(4):
        here = slice(size * k, size * (k + 1))
        for half in range(2):
            base = hidden * half + part * k
            for source, target, count in (
                (main * half, base, main),
                (2 * main + rest * half, base + main, rest),
            ):
                piece = wide(back[here, source : source + count])
                grad_in[:, target : target + count] = piece * gain[...]
                weights = wide(w_in[:, target : target + count])
                total += jnp.sum(piece * weights, axis=1, keepdims=True)
        grad_out[:, part * k : part * (k + 1)] = wide(back[here, edge : edge + part])
    gain_grad[...] = total


def unpack_qkv(back, w_qkv, gain, grad, gain_grad):
    size, part = w_qkv.shape[0], 256
    total = jnp.zeros(gain_grad.shape, jnp.float32)
    for k in range(4):
        for third in range(3):
            piece = wide(back[size * k : size * (k + 1), part * third : part * (third + 1)])
            lanes = slice(part * (4 * third + k), part * (4 * third + k + 1))
            grad[:, lanes] = piece * gain[...]
            total += jnp.sum(piece * wide(w_qkv[:, lanes]), axis=1, keepdims=True)
    gain_grad[...] = total


def kernel(body, outs, cost, *args, scratch=(), scalars=0):
    flops, transcendentals = cost
    shapes = [jax.ShapeDtypeStruct(shape, kind) for shape, kind in outs]
    moved = sum(arg.size * arg.dtype.itemsize for arg in (*args, *shapes))
    return pl.pallas_call(
        body,
        out_shape=shapes,
        in_specs=[
            pl.BlockSpec(memory_space=pltpu.SMEM if k < scalars else pltpu.VMEM)
            for k in range(len(args))
        ],
        out_specs=[pl.BlockSpec(memory_space=pltpu.VMEM)] * len(shapes),
        scratch_shapes=[pltpu.VMEM(shape, kind) for shape, kind in scratch],
        compiler_params=pltpu.CompilerParams(vmem_limit_bytes=28 * 2**20),
        cost_estimate=pl.CostEstimate(
            flops=flops, bytes_accessed=moved, transcendentals=transcendentals
        ),
        name=body.__name__,
    )(*args)


def scatter_last(send, keep):
    beside = split_rows(swap(send, 1), 2)
    kept = split_rows(keep, 2)
    sent = low(wide(kept[1]) + wide(beside[1]))
    return wide(kept[0]) + wide(beside[0]), sent


def local_ring(
    tokens,
    seq_lengths,
    cotangent,
    attention_norm_gain,
    w_qkv,
    w_attn_out,
    feedforward_norm_gain,
    w_in,
    w_out,
):
    count, width = tokens.shape
    index = lax.axis_index("fsdp")
    z, x = index // 2, index % 2
    place = jnp.stack([z, x]).astype(jnp.int32)
    hidden = w_in.shape[1] // 2
    part = hidden // 4
    main = part // LANES * LANES
    in_width, out_width = 2 * main + LANES, main + LANES
    f32, b16 = jnp.float32, jnp.bfloat16
    group = 4 * count

    gain_attn = wide(attention_norm_gain)[:, None]
    gain_mlp = wide(feedforward_norm_gain)[:, None]
    order = [(k, (k % 8) * 4 + k // 8) for k in range(32)]
    attn_own = lax.ppermute(w_attn_out, AXES, order)
    qkv_parts = split_columns(low(wide(w_qkv) * gain_attn), 12)
    size = w_qkv.shape[0]
    slots = seq_lengths.shape[1]
    lengths_low = jnp.pad(low(wide(seq_lengths)), ((0, size - 1), (0, LANES - slots)))
    exchanged = rep_exchange(rows([columns([*qkv_parts[k::4], lengths_low]) for k in range(4)]))
    first_own = columns([exchanged[:, :768], rows(split_columns(attn_own, 4))])
    lengths = rows([exchanged[size * k : size * k + 1, 768 : 768 + slots] for k in range(4)])
    lengths = wide(lengths).astype(jnp.int32)
    for bit in (1, 2):
        turned_rows = rows([lengths[k ^ bit : (k ^ bit) + 1] for k in range(4)])
        lengths = jnp.where((lax.axis_index("rep") & bit) != 0, turned_rows, lengths)

    scaled_in = low(wide(w_in) * gain_mlp)
    pieces = []
    for k in range(4):
        gate = scaled_in[:, part * k : part * (k + 1)]
        up_part = scaled_in[:, hidden + part * k : hidden + part * (k + 1)]
        out_part = w_out[:, part * k : part * (k + 1)]
        fill = [jnp.zeros((w_in.shape[0], n), b16) for n in (in_width - 2 * part, out_width - part)]
        pieces.append(
            columns(
                [gate[:, :main], up_part[:, :main], gate[:, main:], up_part[:, main:], fill[0]]
                + [out_part, fill[1]]
            )
        )
    mine = rows([relative(tokens, z, x), relative(cotangent, z, x)])
    first_own, rest, mine = tie(first_own, rows(pieces), mine)
    rest = rep_exchange(rest)

    third, first, other = up(first_own), down(first_own), over(first_own)
    third, first, other, mine, rest = tie(third, first, other, mine, rest)
    across = swap(mine, 2)
    second, others = up(third), over(rows([first, third]))
    second, others, across, rest = tie(second, others, across, rest)
    other_second = over(second)
    rest_third, rest_first = up(rest), down(rest)
    beside = swap(rows([mine, across]), 1)
    rest_other = over(tie(rest, other_second, beside)[0])

    step = mine.shape[0]
    segment, positions, _ = jax.vmap(lambda row: layout(row, count))(lengths)
    frequency = rope_base ** (-(lax.iota(f32, HALF) * (2.0 / HEAD_DIM)))
    angles = positions.reshape(group, 1).astype(f32) * frequency
    cosine, sine = jnp.cos(angles), jnp.sin(angles)
    cosine, sine = columns([cosine] * 4), columns([-sine, sine] * 2)
    seg_col = segment.reshape(group, 1)

    normed, qkv, attn, query, key, value, probs, attended, send, keep = kernel(
        attention_forward,
        [((group, width), b16), ((width, 768), b16), ((256, width), b16)]
        + [((group, 256), b16)] * 3
        + [((16 * count, count), f32), ((group, 256), b16)]
        + [((2 * count, width), b16)] * 2,
        (2 * group * width * (768 + 256) + 4 * 16 * count * count * LANES, 16 * count * count),
        place, seg_col, segment, cosine, sine, mine, across, beside,
        first, second, third, first_own, others, other_second, other,
        scalars=1,
    )
    rest_third, rest_first, rest_other, send = tie(rest_third, rest_first, rest_other, send)
    rest_second, rest_other_third = up(rest_third), over(rest_third)
    x_own = wide(mine[:count])
    kept, sent = scatter_last(send, keep)
    rest_other_first = over(tie(rest_first, rest_other_third)[0])
    hidden_sum = x_own + kept + wide(swap(sent, 2))
    standard_mlp, inverse_mlp = norm_statistics(hidden_sum)
    norm_own = low(standard_mlp)
    norm_across = swap(norm_own, 2)
    rest_second, rest_other_third, _ = tie(rest_second, rest_other_third, norm_own)
    rest_other_second = up(rest_other_third)
    norm_beside = swap(rows([norm_own, norm_across]), 1)

    normed_mlp, grad_out, mixed, grad_inner, send, keep, w_down = kernel(
        mlp,
        [((group, width), b16)] * 2
        + [((group, out_width), b16), ((group, in_width), b16)]
        + [((2 * count, width), b16)] * 2
        + [((width, out_width), b16)],
        (2 * group * width * (2 * in_width + out_width), 3 * group * part),
        seg_col, norm_own, norm_across, norm_beside, mine, across, beside,
        rest_first, rest_second, rest_third, rest,
        rest_other_first, rest_other_second, rest_other_third, rest_other,
        scratch=[
            ((width, in_width), b16),
            ((group, in_width), f32),
            ((group, out_width), f32),
        ],
    )
    all_width = in_width + out_width
    size = width // 8
    io_keep, io_pair, io_near, io_far = kernel(
        mlp_terms,
        [((size * n, all_width), b16) for n in (3, 2, 1, 2)],
        (2 * group * width * all_width, 0),
        normed_mlp, grad_inner, grad_out, mixed,
    )
    io_pair, io_far = up(io_pair), over(io_far)
    kept, sent = scatter_last(send, keep)
    scaled_mlp = kept + wide(swap(sent, 2))
    grad_hidden = wide(grad_out[:count]) + norm_backward_pass(
        scaled_mlp, jnp.ones((), f32), standard_mlp, inverse_mlp
    )
    low_own = low(grad_hidden)
    low_across = swap(low_own, 2)
    low_beside = swap(rows([low_own, low_across]), 1)

    grad_packed, g_keep, g_pair, g_near, g_far = kernel(
        attention_backward,
        [((group, 768), b16)] + [((size * n, width), b16) for n in (3, 2, 1, 2)],
        (2 * group * width * (768 + 512) + 10 * 16 * count * count * LANES, 0),
        place, cosine, sine, low_own, low_across, low_beside, attn, query, key, value, probs,
        attended, normed,
        scratch=[((group, width), b16), ((group, 256), b16), ((256, width), b16)],
        scalars=1,
    )
    g_pair, g_far = up(g_pair), over(g_far)
    io_pair, io_far, _ = tie(io_pair, io_far, g_near)
    io_kept, io_pair, io_far = split_rows(io_keep, 3), split_rows(io_pair, 2), split_rows(io_far, 2)
    io_near = over(low(wide(io_near) + wide(io_pair[1])))
    io_down = down(low(wide(io_kept[1]) + wide(io_far[0])))
    send, keep = kernel(
        projections,
        [((4 * count, width), b16)] * 2,
        (2 * group * width * (768 + out_width), 0),
        grad_packed, qkv, mixed, w_down,
    )
    io_near, io_down, g_pair, g_far, send = tie(io_near, io_down, g_pair, g_far, send)
    g_kept, g_pair, g_far = split_rows(g_keep, 3), split_rows(g_pair, 2), split_rows(g_far, 2)
    g_near = over(low(wide(g_near) + wide(g_pair[1])))
    g_down = down(low(wide(g_kept[1]) + wide(g_far[0])))
    kept, sent = scatter_last(send, keep)
    io_up = up(low(wide(io_kept[0]) + wide(io_pair[0]) + wide(io_near)))
    io_up, g_near, g_down, sent = tie(io_up, g_near, g_down, sent)
    g_up = up(low(wide(g_kept[0]) + wide(g_pair[0]) + wide(g_near)))
    last_across = swap(sent, 2)
    back = rep_exchange(
        low(wide(io_kept[2]) + wide(io_far[1]) + wide(io_down) + wide(io_up))
    )
    back, g_up = tie(back, g_up)
    sum_g = low(wide(g_kept[2]) + wide(g_far[1]) + wide(g_down) + wide(g_up))
    back_qkv = rep_exchange(sum_g[:, :768])
    grad_w_attn_out = wide(
        lax.ppermute(
            columns(split_rows(sum_g[:, 768:], 4)), AXES, [(there, here) for here, there in order]
        )
    )
    grad_w_in, gain_in, grad_w_out = kernel(
        unpack_rest,
        [(w_in.shape, f32), (gain_mlp.shape, f32), (w_out.shape, f32)],
        (4 * w_in.size, 0),
        back, w_in, gain_mlp,
    )
    grad_w_qkv, gain_qkv = kernel(
        unpack_qkv,
        [(w_qkv.shape, f32), (gain_attn.shape, f32)],
        (4 * w_qkv.size, 0),
        back_qkv, w_qkv, gain_attn,
    )
    last = kept + wide(last_across)

    standard, inverse = norm_statistics(x_own)
    block_input_gradient = grad_hidden + norm_backward_pass(
        last[:count], jnp.ones((), f32), standard, inverse
    )
    output = low(jnp.where(seg_col[:count] < 8, hidden_sum + last[count:], 0.0))
    return (
        absolute(output, z, x),
        absolute(block_input_gradient, z, x),
        gain_qkv.reshape(-1),
        grad_w_qkv,
        grad_w_attn_out,
        gain_in.reshape(-1),
        grad_w_in,
        grad_w_out,
    )


def solution(mesh):
    ringed = dict(mesh.shape) == {"fsdp": 8, "rep": 4}
    return jax.shard_map(
        local_ring if ringed else local_plain,
        mesh=mesh,
        in_specs=(
            P(AXES, None),
            P(AXES, None),
            P(AXES, None),
            P(AXES),
            P(AXES, None),
            P(AXES, None),
            P(AXES),
            P(AXES, None),
            P(AXES, None),
        ),
        out_specs=(
            P(AXES, None),
            P(AXES, None),
            P(AXES),
            P(AXES, None),
            P(AXES, None),
            P(AXES),
            P(AXES, None),
            P(AXES, None),
        ),
        check_vma=False,
    )
```

```python
import jax
import jax.numpy as jnp
from jax import lax
from jax.experimental import pallas as pl
from jax.experimental.pallas import tpu as pltpu
from jax.sharding import PartitionSpec as P

HEAD_DIM = 64


norm_eps = 1e-05
rope_base = 160000.0


def matmul(left_side, right_side):
    return jnp.dot(left_side, right_side, preferred_element_type=jnp.float32)


def matmul_right_t(left_side, right_side):
    return lax.dot_general(
        left_side, right_side, (((1,), (1,)), ((), ())), preferred_element_type=jnp.float32
    )


def matmul_left_t(left_side, right_side):
    return lax.dot_general(
        left_side, right_side, (((0,), (0,)), ((), ())), preferred_element_type=jnp.float32
    )


def batched(form, left_side, right_side):
    return jnp.einsum(form, left_side, right_side, preferred_element_type=jnp.float32)


def layout(lengths, row_count):
    slot_ids = lax.iota(jnp.int32, lengths.shape[0])
    before = (slot_ids[:, None] <= slot_ids[None, :]).astype(jnp.int32)
    ends = jnp.sum(lengths[:, None] * before, axis=0)
    starts = ends - lengths
    places = lax.iota(jnp.int32, row_count)
    sequence_segment = jnp.sum((ends[None, :] <= places[:, None]).astype(jnp.int32), axis=1)
    first_row = jnp.sum(
        jnp.where(sequence_segment[:, None] == slot_ids[None, :], starts[None, :], 0), axis=1
    )
    return (sequence_segment, places - first_row, sequence_segment < lengths.shape[0])


def rotary(positions, head_size):
    half_size = head_size // 2
    frequency = rope_base ** (-(lax.iota(jnp.float32, half_size) * (2.0 / head_size)))
    angles = positions.astype(jnp.float32)[..., None] * frequency
    cosine_table = jnp.concatenate([jnp.cos(angles), jnp.cos(angles)], axis=-1)
    sine_table = jnp.concatenate([jnp.sin(angles), jnp.sin(angles)], axis=-1)
    return (cosine_table, sine_table)


def rotate_half(vector):
    half_size = vector.shape[-1] // 2
    return jnp.concatenate([-vector[..., half_size:], vector[..., :half_size]], axis=-1)


def rotate_back(vector):
    half_size = vector.shape[-1] // 2
    return jnp.concatenate([vector[..., half_size:], -vector[..., :half_size]], axis=-1)


def norm_statistics(values):
    average = jnp.mean(values, axis=-1, keepdims=True)
    centred = values - average
    inverse = lax.rsqrt(jnp.mean(centred * centred, axis=-1, keepdims=True) + norm_eps)
    return (centred * inverse, inverse)


def norm_backward_pass(grad_normed, gain_vec, normalized, inverse):
    scaled = grad_normed * gain_vec.astype(jnp.float32)
    return inverse * (
        scaled
        - jnp.mean(scaled, axis=-1, keepdims=True)
        - normalized * jnp.mean(scaled * normalized, axis=-1, keepdims=True)
    )


def attend(rotated_query, rotated_key, value_reduced_precision, sequence_segment):
    scores = batched("thd,shd->hts", rotated_query, rotated_key)
    allowed = sequence_segment[:, None] == sequence_segment[None, :]
    scores = jnp.where(allowed[None], scores, -jnp.inf)
    logarithm_totals = jax.nn.logsumexp(scores, axis=-1)
    weights = jnp.exp(scores - logarithm_totals[..., None]).astype(jnp.bfloat16)
    attended = batched("hts,shd->thd", weights, value_reduced_precision).astype(jnp.bfloat16)
    return (attended, logarithm_totals)


def attend_back(
    rotated_query,
    rotated_key,
    value_reduced_precision,
    sequence_segment,
    logarithm_totals,
    grad_attended,
):
    scores = batched("thd,shd->hts", rotated_query, rotated_key)
    allowed = sequence_segment[:, None] == sequence_segment[None, :]
    scores = jnp.where(allowed[None], scores, -jnp.inf)
    probs_full = jnp.exp(scores - logarithm_totals[..., None])
    weights = probs_full.astype(jnp.bfloat16)
    grad_value = batched("hts,thd->shd", weights, grad_attended)
    grad_probs = batched("thd,shd->hts", grad_attended, value_reduced_precision)
    row_delta = jnp.sum(probs_full * grad_probs, axis=-1, keepdims=True)
    grad_scores = (probs_full * (grad_probs - row_delta)).astype(jnp.bfloat16)
    grad_query = batched("hts,shd->thd", grad_scores, rotated_key)
    grad_key = batched("hts,thd->shd", grad_scores, rotated_query)
    return (grad_query, grad_key, grad_value)


def forward(
    tokens, lengths, attention_norm_gain, w_qkv, w_attn_out, feedforward_norm_gain, w_in, w_out
):
    groups, row_count, embedding_width = tokens.shape
    head_count = embedding_width // HEAD_DIM
    hidden_units = w_in.shape[1] // 2
    sequence_segment, positions, valid = jax.vmap(
        lambda row_lengths: layout(row_lengths, row_count)
    )(lengths)
    cosine_table, sine_table = rotary(positions, HEAD_DIM)
    cosine_table = cosine_table[:, :, None, :]
    sine_table = sine_table[:, :, None, :]
    residual_input = tokens.reshape(groups * row_count, embedding_width).astype(jnp.float32)
    attention_standardized, attention_inverse_norm = norm_statistics(residual_input)
    attention_normed_input = (
        attention_standardized * attention_norm_gain.astype(jnp.float32)
    ).astype(jnp.bfloat16)
    packed = matmul(attention_normed_input, w_qkv).reshape(
        groups, row_count, 3, head_count, HEAD_DIM
    )
    query_raw = packed[:, :, 0]
    key_raw = packed[:, :, 1]
    rotated_query = (
        (query_raw * cosine_table + rotate_half(query_raw) * sine_table) * HEAD_DIM ** (-0.5)
    ).astype(jnp.bfloat16)
    rotated_key = (key_raw * cosine_table + rotate_half(key_raw) * sine_table).astype(jnp.bfloat16)
    value_reduced_precision = packed[:, :, 2].astype(jnp.bfloat16)
    attended, logarithm_totals = jax.vmap(attend)(
        rotated_query, rotated_key, value_reduced_precision, sequence_segment
    )
    attention_rows_flat = attended.reshape(groups * row_count, embedding_width)
    hidden_residual = residual_input + matmul(attention_rows_flat, w_attn_out)
    feedforward_standardized, feedforward_inverse_norm = norm_statistics(hidden_residual)
    feedforward_normed_input = (
        feedforward_standardized * feedforward_norm_gain.astype(jnp.float32)
    ).astype(jnp.bfloat16)
    inner_proj = matmul(feedforward_normed_input, w_in)
    gate_projection = inner_proj[:, :hidden_units]
    up_projection = inner_proj[:, hidden_units:]
    activation_output = jax.nn.gelu(gate_projection, approximate=False)
    mixed_input = (activation_output * up_projection).astype(jnp.bfloat16)
    live_token_rows = valid.reshape(groups * row_count, 1)
    mlp_result = matmul_right_t(mixed_input, w_out)
    output = jnp.where(live_token_rows, hidden_residual + mlp_result, 0.0).astype(jnp.bfloat16)
    saved_residuals = (
        sequence_segment,
        live_token_rows,
        cosine_table,
        sine_table,
        attention_standardized,
        attention_inverse_norm,
        attention_normed_input,
        rotated_query,
        rotated_key,
        value_reduced_precision,
        logarithm_totals,
        attention_rows_flat,
        feedforward_standardized,
        feedforward_inverse_norm,
        feedforward_normed_input,
        gate_projection,
        up_projection,
        activation_output,
        mixed_input,
    )
    return (output, saved_residuals)


def backward(
    saved_residuals,
    cotangent,
    attention_norm_gain,
    w_qkv,
    w_attn_out,
    feedforward_norm_gain,
    w_in,
    w_out,
):
    (
        sequence_segment,
        live_token_rows,
        cosine_table,
        sine_table,
        attention_standardized,
        attention_inverse_norm,
        attention_normed_input,
        rotated_query,
        rotated_key,
        value_reduced_precision,
        logarithm_totals,
        attention_rows_flat,
        feedforward_standardized,
        feedforward_inverse_norm,
        feedforward_normed_input,
        gate_projection,
        up_projection,
        activation_output,
        mixed_input,
    ) = saved_residuals
    groups, row_count = sequence_segment.shape
    embedding_width = attention_standardized.shape[1]
    head_count = embedding_width // HEAD_DIM
    flat_cot = cotangent.reshape(groups * row_count, embedding_width)
    output_gradient = jnp.where(live_token_rows, flat_cot, jnp.zeros((), flat_cot.dtype))
    grad_mixed = matmul(output_gradient, w_out)
    slope = (
        0.5 * (1.0 + lax.erf(gate_projection * 0.7071067811865476))
        + gate_projection * jnp.exp(-0.5 * gate_projection * gate_projection) * 0.3989422804014327
    )
    grad_inner = jnp.concatenate(
        [grad_mixed * up_projection * slope, grad_mixed * activation_output], axis=1
    ).astype(jnp.bfloat16)
    feedforward_normed_gradient = matmul_right_t(grad_inner, w_in)
    hidden_gradient = output_gradient.astype(jnp.float32) + norm_backward_pass(
        feedforward_normed_gradient,
        feedforward_norm_gain,
        feedforward_standardized,
        feedforward_inverse_norm,
    )
    grad_hidden_low = hidden_gradient.astype(jnp.bfloat16)
    grad_attended = matmul_right_t(grad_hidden_low, w_attn_out).astype(jnp.bfloat16)
    grad_attended = grad_attended.reshape(groups, row_count, head_count, HEAD_DIM)
    grad_query, grad_key, grad_value = jax.vmap(attend_back)(
        rotated_query,
        rotated_key,
        value_reduced_precision,
        sequence_segment,
        logarithm_totals,
        grad_attended,
    )
    grad_query = grad_query * HEAD_DIM ** (-0.5)
    grad_query = grad_query * cosine_table + rotate_back(grad_query * sine_table)
    grad_key = grad_key * cosine_table + rotate_back(grad_key * sine_table)
    grad_packed = jnp.stack([grad_query, grad_key, grad_value], axis=2)
    grad_packed = grad_packed.reshape(groups * row_count, 3 * embedding_width).astype(jnp.bfloat16)
    attention_normed_gradient = matmul_right_t(grad_packed, w_qkv)
    block_input_gradient = hidden_gradient + norm_backward_pass(
        attention_normed_gradient,
        attention_norm_gain,
        attention_standardized,
        attention_inverse_norm,
    )
    factors = (
        attention_normed_input,
        grad_packed,
        attention_rows_flat,
        grad_hidden_low,
        feedforward_normed_input,
        grad_inner,
        output_gradient,
        mixed_input,
        attention_normed_gradient,
        attention_standardized,
        feedforward_normed_gradient,
        feedforward_standardized,
    )
    return (block_input_gradient, factors)


def local_plain(
    tokens,
    seq_lengths,
    cotangent,
    attention_norm_gain,
    w_qkv,
    w_attn_out,
    feedforward_norm_gain,
    w_in,
    w_out,
):
    row_count, embedding_width = tokens.shape
    gathered = (
        lax.all_gather(attention_norm_gain, ("fsdp", "rep"), axis=0, tiled=True),
        lax.all_gather(w_qkv, ("fsdp", "rep"), axis=0, tiled=True),
        lax.all_gather(w_attn_out, ("fsdp", "rep"), axis=0, tiled=True),
        lax.all_gather(feedforward_norm_gain, ("fsdp", "rep"), axis=0, tiled=True),
        lax.all_gather(w_in, ("fsdp", "rep"), axis=0, tiled=True),
        lax.all_gather(w_out, ("fsdp", "rep"), axis=0, tiled=True),
    )
    output, saved_residuals = forward(
        tokens.reshape(1, row_count, embedding_width),
        seq_lengths,
        gathered[0],
        gathered[1],
        gathered[2],
        gathered[3],
        gathered[4],
        gathered[5],
    )
    second_copy = (
        lax.all_gather(attention_norm_gain, ("fsdp", "rep"), axis=0, tiled=True),
        lax.all_gather(w_qkv, ("fsdp", "rep"), axis=0, tiled=True),
        lax.all_gather(w_attn_out, ("fsdp", "rep"), axis=0, tiled=True),
        lax.all_gather(feedforward_norm_gain, ("fsdp", "rep"), axis=0, tiled=True),
        lax.all_gather(w_in, ("fsdp", "rep"), axis=0, tiled=True),
        lax.all_gather(w_out, ("fsdp", "rep"), axis=0, tiled=True),
    )
    block_input_gradient, factors = backward(
        saved_residuals,
        cotangent.reshape(1, row_count, embedding_width),
        second_copy[0],
        second_copy[1],
        second_copy[2],
        second_copy[3],
        second_copy[4],
        second_copy[5],
    )
    (
        normed_attn,
        grad_packed,
        attended_rows,
        grad_hidden_low,
        normed_mlp,
        grad_inner,
        grad_out,
        mixed_input,
        grad_normed_attn,
        standard_attn,
        grad_normed_mlp,
        standard_mlp,
    ) = factors
    qkv_width = w_qkv.shape[1]
    attn_width = w_attn_out.shape[1]
    inner_width = w_in.shape[1]
    outer_width = w_out.shape[1]
    qkv_term = matmul_left_t(normed_attn, grad_packed)
    attn_term = matmul_left_t(attended_rows, grad_hidden_low)
    inner_term = matmul_left_t(normed_mlp, grad_inner)
    outer_term = matmul_left_t(grad_out, mixed_input)
    attn_gain_term = jnp.sum(grad_normed_attn * standard_attn, axis=0)
    mlp_gain_term = jnp.sum(grad_normed_mlp * standard_mlp, axis=0)
    summed = lax.psum_scatter(
        jnp.concatenate(
            [
                qkv_term,
                attn_term,
                inner_term,
                outer_term,
                attn_gain_term[:, None],
                mlp_gain_term[:, None],
            ],
            axis=1,
        ),
        ("fsdp", "rep"),
        scatter_dimension=0,
        tiled=True,
    )
    edge_two = qkv_width + attn_width
    edge_three = edge_two + inner_width
    edge_four = edge_three + outer_width
    return (
        output,
        block_input_gradient,
        summed[:, edge_four],
        summed[:, :qkv_width],
        summed[:, qkv_width:edge_two],
        summed[:, edge_four + 1],
        summed[:, edge_two:edge_three],
        summed[:, edge_three:edge_four],
    )


AXES = ("fsdp", "rep")
LANES = 128
HALF = HEAD_DIM // 2


def tie(*values):
    return lax.optimization_barrier(values)


def wide(value):
    return value.astype(jnp.float32)


def low(value):
    return value.astype(jnp.bfloat16)


def split_columns(value, count):
    width = value.shape[1] // count
    return [value[:, k * width : (k + 1) * width] for k in range(count)]


def split_rows(value, count):
    width = value.shape[0] // count
    return [value[k * width : (k + 1) * width] for k in range(count)]


def columns(blocks):
    return jnp.concatenate(blocks, axis=1)


def rows(blocks):
    return jnp.concatenate(blocks, axis=0)


def swap(value, distance):
    return lax.ppermute(value, "rep", [(k, k ^ distance) for k in range(4)])


def rep_exchange(value):
    blocks = value.reshape(4, value.shape[0] // 4, value.shape[1])
    return lax.all_to_all(blocks, "rep", 0, 0, tiled=True).reshape(value.shape)


def up(value):
    return lax.ppermute(value, "fsdp", [(k, (k + 2) % 8) for k in range(8)])


def down(value):
    return lax.ppermute(value, "fsdp", [(k, (k - 2) % 8) for k in range(8)])


def over(value):
    return lax.ppermute(value, "fsdp", [(k, k ^ 1) for k in range(8)])


def relative(value, z, x):
    blocks = split_columns(value, 8)
    blocks = [jnp.where(x == 1, blocks[k ^ 1], blocks[k]) for k in range(8)]
    for bit in (1, 2):
        turn = (z & bit) != 0
        blocks = [jnp.where(turn, blocks[(k + 2 * bit) % 8], blocks[k]) for k in range(8)]
    return columns([blocks[2 * ((p + 1) % 4) + i] for i in range(2) for p in range(4)])


def absolute(value, z, x):
    blocks = split_columns(value, 8)
    blocks = [blocks[4 * i + (j - 1) % 4] for j in range(4) for i in range(2)]
    blocks = [jnp.where(x == 1, blocks[k ^ 1], blocks[k]) for k in range(8)]
    for bit in (1, 2):
        turn = (z & bit) != 0
        blocks = [jnp.where(turn, blocks[(k - 2 * bit) % 8], blocks[k]) for k in range(8)]
    return columns(blocks)


def place_of(place, step, side):
    z, x = place[0], place[1]
    return 2 * lax.rem(z + step + 1, 4) + (x if side == 0 else 1 - x)


def block_of(place, z_at, side):
    z, x = place[0], place[1]
    return 4 * (x if side == 0 else 1 - x) + lax.rem(z_at - z + 7, 4)


def turned(value):
    width = value.shape[1]
    lane = lax.broadcasted_iota(jnp.int32, value.shape, 1)
    return jnp.where(
        lane % HEAD_DIM < HALF,
        pltpu.roll(value, width - HALF, 1),
        pltpu.roll(value, HALF, 1),
    )


def head_masks(row_count):
    lane = lax.broadcasted_iota(jnp.int32, (row_count, LANES), 1)
    return [low(wide(lane < HEAD_DIM)), low(wide(lane >= HEAD_DIM))], lane < HEAD_DIM


def token_rows(mine, across, beside, first, step):
    count = 128
    return [
        mine[first : first + count],
        beside[first : first + count],
        across[first : first + count],
        beside[step + first : step + first + count],
    ]


def attention_forward(
    place, seg_col, seg_row, cosine, sine, mine, across, beside,
    first, second, third, own, others, other_second, other,
    normed, qkv, attn, query, key, value, probs, attended, send, keep,
):
    size = own.shape[0]
    blocks = [
        (first, 0), (second, 0), (third, 0), (own, 0),
        (others, 0), (other_second, 0), (others, size), (other, 0),
    ]
    part = size // 4
    for at, (ref, row) in enumerate(blocks):
        qkv[size * at : size * (at + 1), :] = ref[row : row + size, :768]
        target = pl.multiple_of(place_of(place, at % 4, at // 4) * part, part)
        for z_at in range(4):
            for side in range(2):
                lanes = pl.multiple_of(block_of(place, z_at, side) * LANES, LANES)
                attn[pl.ds(target, part), pl.ds(lanes, LANES)] = ref[
                    row + part * z_at : row + part * (z_at + 1),
                    768 + LANES * side : 768 + LANES * (side + 1),
                ]
    count = 128
    for at, ref in enumerate(token_rows(mine, across, beside, 0, mine.shape[0])):
        values = wide(ref)
        centred = values - jnp.mean(values, axis=1, keepdims=True)
        inverse = lax.rsqrt(jnp.mean(centred * centred, axis=1, keepdims=True) + norm_eps)
        normed[count * at : count * (at + 1), :] = low(centred * inverse)
    packed = matmul(normed[...], qkv[...])
    cos_all, sin_all = columns([cosine[...]] * 2), columns([sine[...]] * 2)
    raw = packed[:, :256]
    query[...] = low((raw * cos_all + turned(raw) * sin_all) * HEAD_DIM ** (-0.5))
    raw = packed[:, 256:512]
    key[...] = low(raw * cos_all + turned(raw) * sin_all)
    value[...] = low(packed[:, 512:])
    masks, is_first = head_masks(count)
    for at in range(4):
        here = slice(count * at, count * (at + 1))
        allowed = seg_col[here, :] == seg_row[at : at + 1, :]
        for pair in range(2):
            lanes = slice(LANES * pair, LANES * (pair + 1))
            made = []
            for head in range(2):
                scores = matmul_right_t(query[here, lanes] * masks[head], key[here, lanes])
                scores = jnp.where(allowed, scores, -jnp.inf)
                powers = jnp.exp(scores - jnp.max(scores, axis=1, keepdims=True))
                weights = powers / jnp.sum(powers, axis=1, keepdims=True)
                slot = count * (4 * at + 2 * pair + head)
                probs[slot : slot + count, :] = weights
                made.append(matmul(low(weights), value[here, lanes]))
            attended[here, lanes] = low(jnp.where(is_first, made[0], made[1]))
    total = low(matmul(attended[...], attn[...]))
    keep[:count, :], send[:count, :] = total[:count], total[count : 2 * count]
    keep[count:, :], send[count:, :] = total[2 * count : 3 * count], total[3 * count :]


def mlp(
    seg_col, norm_own, norm_across, norm_beside, mine, across, beside,
    first, second, third, own, other_first, other_second, other_third, other,
    normed, grad_out, mixed, grad_inner, send, keep, w_down,
    w_up, inner, grad_mixed,
):
    size, count, edge = own.shape[0], 128, w_up.shape[1]
    blocks = (first, second, third, own, other_first, other_second, other_third, other)
    for at, ref in enumerate(blocks):
        w_up[size * at : size * (at + 1), :] = ref[:, :edge]
        w_down[size * at : size * (at + 1), :] = ref[:, edge:]
    for at, ref in enumerate(
        (norm_own[...], norm_beside[:count, :], norm_across[...], norm_beside[count:, :])
    ):
        normed[count * at : count * (at + 1), :] = ref
    for at, ref in enumerate(token_rows(mine, across, beside, count, mine.shape[0])):
        live = wide(seg_col[count * at : count * (at + 1), :] < 8)
        grad_out[count * at : count * (at + 1), :] = low(wide(ref) * live)
    inner[...] = matmul(normed[...], w_up[...])
    grad_mixed[...] = matmul(grad_out[...], w_down[...])
    main = (w_down.shape[1] // LANES - 1) * LANES
    rest = 16

    def parts(gate):
        phi = 0.5 * (1.0 + lax.erf(gate * 0.7071067811865476))
        slope = phi + gate * jnp.exp(-0.5 * gate * gate) * 0.3989422804014327
        return gate * phi, slope

    @pl.loop(0, 8)
    def _(step):
        here = pl.ds(pl.multiple_of(step * 64, 64), 64)
        gate, up_part = inner[here, :main], inner[here, main : 2 * main]
        grad = grad_mixed[here, :main]
        activation, slope = parts(gate)
        mixed[here, :main] = low(activation * up_part)
        grad_inner[here, :main] = low(grad * up_part * slope)
        grad_inner[here, main : 2 * main] = low(grad * activation)
        tail = inner[here, 2 * main :]
        grad = grad_mixed[here, main:]
        activation, slope = parts(tail)
        tail_up = pltpu.roll(tail, LANES - rest, 1)
        mixed[here, main:] = low(activation * tail_up)
        grad_inner[here, 2 * main :] = low(
            grad * tail_up * slope + pltpu.roll(grad * activation, rest, 1)
        )

    total = low(matmul_right_t(grad_inner[...], w_up[...]))
    keep[:count, :], send[:count, :] = total[:count], total[count : 2 * count]
    keep[count:, :], send[count:, :] = total[2 * count : 3 * count], total[3 * count :]


def place_term(term, keep, pair, near, far, lanes):
    size = term.shape[0] // 8
    for at, (ref, row) in enumerate(
        [(keep, 0), (pair, 0), (keep, 1), (keep, 2), (near, 0), (pair, 1), (far, 0), (far, 1)]
    ):
        ref[size * row : size * (row + 1), lanes] = term[size * at : size * (at + 1)]


def mlp_terms(normed, grad_inner, grad_out, mixed, keep, pair, near, far):
    edge = grad_inner.shape[1]
    term = low(matmul_left_t(normed[...], grad_inner[...]))
    place_term(term, keep, pair, near, far, slice(0, edge))
    term = low(matmul_left_t(grad_out[...], mixed[...]))
    place_term(term, keep, pair, near, far, slice(edge, edge + mixed.shape[1]))


def attention_backward(
    place, cosine, sine, low_own, low_across, low_beside, attn, query, key, value, probs,
    attended, normed,
    grad_packed, keep, pair, near, far, grad_low, grad_attended, term_attn,
):
    count = 128
    for at, ref in enumerate(
        (low_own[...], low_beside[:count, :], low_across[...], low_beside[count:, :])
    ):
        grad_low[count * at : count * (at + 1), :] = ref
    grad_attended[...] = low(matmul_right_t(grad_low[...], attn[...]))
    masks, is_first = head_masks(count)
    for at in range(4):
        here = slice(count * at, count * (at + 1))
        cos, sin = cosine[here, :], sine[here, :]
        for half in range(2):
            lanes = slice(LANES * half, LANES * (half + 1))
            q, k, v = query[here, lanes], key[here, lanes], value[here, lanes]
            grad = grad_attended[here, lanes]
            made = []
            for head in range(2):
                slot = count * (4 * at + 2 * half + head)
                weights = probs[slot : slot + count, :]
                grad_value = matmul_left_t(low(weights), grad)
                grad_probs = matmul_right_t(grad * masks[head], v)
                delta = jnp.sum(weights * grad_probs, axis=1, keepdims=True)
                grad_scores = low(weights * (grad_probs - delta))
                made.append((matmul(grad_scores, k), matmul_left_t(grad_scores, q), grad_value))
            grad_q, grad_k, grad_v = (jnp.where(is_first, *both) for both in zip(*made))
            grad_q = grad_q * HEAD_DIM ** (-0.5)
            grad_packed[here, lanes] = low(grad_q * cos - turned(grad_q) * sin)
            lanes = slice(256 + LANES * half, 256 + LANES * (half + 1))
            grad_packed[here, lanes] = low(grad_k * cos - turned(grad_k) * sin)
            lanes = slice(512 + LANES * half, 512 + LANES * (half + 1))
            grad_packed[here, lanes] = low(grad_v)
    term = low(matmul_left_t(normed[...], grad_packed[...]))
    place_term(term, keep, pair, near, far, slice(0, 768))
    term_attn[...] = low(matmul_left_t(attended[...], grad_low[...]))
    size = term.shape[0] // 8
    part = size // 4
    targets = [
        (keep, 0), (pair, 0), (keep, size), (keep, 2 * size),
        (near, 0), (pair, size), (far, 0), (far, size),
    ]
    for at, (ref, row) in enumerate(targets):
        source = pl.multiple_of(place_of(place, at % 4, at // 4) * part, part)
        for z_at in range(4):
            for side in range(2):
                lanes = pl.multiple_of(block_of(place, z_at, side) * LANES, LANES)
                ref[
                    row + part * z_at : row + part * (z_at + 1),
                    768 + LANES * side : 768 + LANES * (side + 1),
                ] = term_attn[pl.ds(source, part), pl.ds(lanes, LANES)]


def projections(grad_packed, qkv, mixed, w_down, send, keep):
    count = 128
    for row, total in (
        (0, low(matmul_right_t(grad_packed[...], qkv[...]))),
        (count, low(matmul_right_t(mixed[...], w_down[...]))),
    ):
        keep[row : row + count, :] = total[:count]
        send[row : row + count, :] = total[count : 2 * count]
        keep[2 * count + row : 3 * count + row, :] = total[2 * count : 3 * count]
        send[2 * count + row : 3 * count + row, :] = total[3 * count :]


def unpack_rest(back, w_in, gain, grad_in, gain_grad, grad_out):
    size, hidden, part = w_in.shape[0], w_in.shape[1] // 2, w_in.shape[1] // 8
    main = part // LANES * LANES
    rest, edge = part - main, 2 * main + LANES
    total = jnp.zeros(gain_grad.shape, jnp.float32)
    for k in range(4):
        here = slice(size * k, size * (k + 1))
        for half in range(2):
            base = hidden * half + part * k
            for source, target, count in (
                (main * half, base, main),
                (2 * main + rest * half, base + main, rest),
            ):
                piece = wide(back[here, source : source + count])
                grad_in[:, target : target + count] = piece * gain[...]
                weights = wide(w_in[:, target : target + count])
                total += jnp.sum(piece * weights, axis=1, keepdims=True)
        grad_out[:, part * k : part * (k + 1)] = wide(back[here, edge : edge + part])
    gain_grad[...] = total


def unpack_qkv(back, w_qkv, gain, grad, gain_grad):
    size, part = w_qkv.shape[0], 256
    total = jnp.zeros(gain_grad.shape, jnp.float32)
    for k in range(4):
        for third in range(3):
            piece = wide(back[size * k : size * (k + 1), part * third : part * (third + 1)])
            lanes = slice(part * (4 * third + k), part * (4 * third + k + 1))
            grad[:, lanes] = piece * gain[...]
            total += jnp.sum(piece * wide(w_qkv[:, lanes]), axis=1, keepdims=True)
    gain_grad[...] = total


def kernel(body, outs, cost, *args, scratch=(), scalars=0):
    flops, transcendentals = cost
    shapes = [jax.ShapeDtypeStruct(shape, kind) for shape, kind in outs]
    moved = sum(arg.size * arg.dtype.itemsize for arg in (*args, *shapes))
    return pl.pallas_call(
        body,
        out_shape=shapes,
        in_specs=[
            pl.BlockSpec(memory_space=pltpu.SMEM if k < scalars else pltpu.VMEM)
            for k in range(len(args))
        ],
        out_specs=[pl.BlockSpec(memory_space=pltpu.VMEM)] * len(shapes),
        scratch_shapes=[pltpu.VMEM(shape, kind) for shape, kind in scratch],
        compiler_params=pltpu.CompilerParams(vmem_limit_bytes=28 * 2**20),
        cost_estimate=pl.CostEstimate(
            flops=flops, bytes_accessed=moved, transcendentals=transcendentals
        ),
        name=body.__name__,
    )(*args)


def scatter_last(send, keep):
    beside = split_rows(swap(send, 1), 2)
    kept = split_rows(keep, 2)
    sent = low(wide(kept[1]) + wide(beside[1]))
    return wide(kept[0]) + wide(beside[0]), sent


def local_ring(
    tokens,
    seq_lengths,
    cotangent,
    attention_norm_gain,
    w_qkv,
    w_attn_out,
    feedforward_norm_gain,
    w_in,
    w_out,
):
    count, width = tokens.shape
    index = lax.axis_index("fsdp")
    z, x = index // 2, index % 2
    place = jnp.stack([z, x]).astype(jnp.int32)
    hidden = w_in.shape[1] // 2
    part = hidden // 4
    main = part // LANES * LANES
    in_width, out_width = 2 * main + LANES, main + LANES
    f32, b16 = jnp.float32, jnp.bfloat16
    group = 4 * count

    gain_attn = wide(attention_norm_gain)[:, None]
    gain_mlp = wide(feedforward_norm_gain)[:, None]
    order = [(k, (k % 8) * 4 + k // 8) for k in range(32)]
    attn_own = lax.ppermute(w_attn_out, AXES, order)
    qkv_parts = split_columns(low(wide(w_qkv) * gain_attn), 12)
    size = w_qkv.shape[0]
    slots = seq_lengths.shape[1]
    lengths_low = jnp.pad(low(wide(seq_lengths)), ((0, size - 1), (0, LANES - slots)))
    exchanged = rep_exchange(rows([columns([*qkv_parts[k::4], lengths_low]) for k in range(4)]))
    first_own = columns([exchanged[:, :768], rows(split_columns(attn_own, 4))])
    lengths = rows([exchanged[size * k : size * k + 1, 768 : 768 + slots] for k in range(4)])
    lengths = wide(lengths).astype(jnp.int32)
    for bit in (1, 2):
        turned_rows = rows([lengths[k ^ bit : (k ^ bit) + 1] for k in range(4)])
        lengths = jnp.where((lax.axis_index("rep") & bit) != 0, turned_rows, lengths)

    scaled_in = low(wide(w_in) * gain_mlp)
    pieces = []
    for k in range(4):
        gate = scaled_in[:, part * k : part * (k + 1)]
        up_part = scaled_in[:, hidden + part * k : hidden + part * (k + 1)]
        out_part = w_out[:, part * k : part * (k + 1)]
        fill = [jnp.zeros((w_in.shape[0], n), b16) for n in (in_width - 2 * part, out_width - part)]
        pieces.append(
            columns(
                [gate[:, :main], up_part[:, :main], gate[:, main:], up_part[:, main:], fill[0]]
                + [out_part, fill[1]]
            )
        )
    mine = rows([relative(tokens, z, x), relative(cotangent, z, x)])
    first_own, rest, mine = tie(first_own, rows(pieces), mine)
    rest = rep_exchange(rest)

    third, first, other = up(first_own), down(first_own), over(first_own)
    third, first, other, mine, rest = tie(third, first, other, mine, rest)
    across = swap(mine, 2)
    second, others, rest_third = up(third), over(rows([first, third])), up(rest)
    second, others, across, rest_third, rest = tie(second, others, across, rest_third, rest)
    other_second = over(second)
    rest_first = down(rest)
    beside = swap(rows([mine, across]), 1)
    rest_other = over(tie(rest, other_second, beside)[0])

    step = mine.shape[0]
    segment, positions, _ = jax.vmap(lambda row: layout(row, count))(lengths)
    frequency = rope_base ** (-(lax.iota(f32, HALF) * (2.0 / HEAD_DIM)))
    angles = positions.reshape(group, 1).astype(f32) * frequency
    cosine, sine = jnp.cos(angles), jnp.sin(angles)
    cosine, sine = columns([cosine] * 4), columns([-sine, sine] * 2)
    seg_col = segment.reshape(group, 1)

    normed, qkv, attn, query, key, value, probs, attended, send, keep = kernel(
        attention_forward,
        [((group, width), b16), ((width, 768), b16), ((256, width), b16)]
        + [((group, 256), b16)] * 3
        + [((16 * count, count), f32), ((group, 256), b16)]
        + [((2 * count, width), b16)] * 2,
        (2 * group * width * (768 + 256) + 4 * 16 * count * count * LANES, 16 * count * count),
        place, seg_col, segment, cosine, sine, mine, across, beside,
        first, second, third, first_own, others, other_second, other,
        scalars=1,
    )
    rest_third, rest_first, rest_other, send = tie(rest_third, rest_first, rest_other, send)
    rest_second, rest_other_third = up(rest_third), over(rest_third)
    x_own = wide(mine[:count])
    kept, sent = scatter_last(send, keep)
    rest_other_first = over(tie(rest_first, rest_other_third)[0])
    hidden_sum = x_own + kept + wide(swap(sent, 2))
    standard_mlp, inverse_mlp = norm_statistics(hidden_sum)
    norm_own = low(standard_mlp)
    norm_across = swap(norm_own, 2)
    rest_second, rest_other_third, _ = tie(rest_second, rest_other_third, norm_own)
    rest_other_second = up(rest_other_third)
    norm_beside = swap(rows([norm_own, norm_across]), 1)

    normed_mlp, grad_out, mixed, grad_inner, send, keep, w_down = kernel(
        mlp,
        [((group, width), b16)] * 2
        + [((group, out_width), b16), ((group, in_width), b16)]
        + [((2 * count, width), b16)] * 2
        + [((width, out_width), b16)],
        (2 * group * width * (2 * in_width + out_width), 3 * group * part),
        seg_col, norm_own, norm_across, norm_beside, mine, across, beside,
        rest_first, rest_second, rest_third, rest,
        rest_other_first, rest_other_second, rest_other_third, rest_other,
        scratch=[
            ((width, in_width), b16),
            ((group, in_width), f32),
            ((group, out_width), f32),
        ],
    )
    all_width = in_width + out_width
    size = width // 8
    io_keep, io_pair, io_near, io_far = kernel(
        mlp_terms,
        [((size * n, all_width), b16) for n in (3, 2, 1, 2)],
        (2 * group * width * all_width, 0),
        normed_mlp, grad_inner, grad_out, mixed,
    )
    io_pair, io_far = up(io_pair), over(io_far)
    kept, sent = scatter_last(send, keep)
    scaled_mlp = kept + wide(tie(swap(sent, 2), io_keep)[0])
    grad_hidden = wide(grad_out[:count]) + norm_backward_pass(
        scaled_mlp, jnp.ones((), f32), standard_mlp, inverse_mlp
    )
    low_own = low(grad_hidden)
    low_across = swap(low_own, 2)
    low_beside = swap(rows([low_own, low_across]), 1)

    grad_packed, g_keep, g_pair, g_near, g_far = kernel(
        attention_backward,
        [((group, 768), b16)] + [((size * n, width), b16) for n in (3, 2, 1, 2)],
        (2 * group * width * (768 + 512) + 10 * 16 * count * count * LANES, 0),
        place, cosine, sine, low_own, low_across, low_beside, attn, query, key, value, probs,
        attended, normed,
        scratch=[((group, width), b16), ((group, 256), b16), ((256, width), b16)],
        scalars=1,
    )
    g_pair, g_far = up(g_pair), over(g_far)
    io_pair, io_far, _ = tie(io_pair, io_far, g_near)
    io_kept, io_pair, io_far = split_rows(io_keep, 3), split_rows(io_pair, 2), split_rows(io_far, 2)
    io_near = over(low(wide(io_near) + wide(io_pair[1])))
    io_down = down(low(wide(io_kept[1]) + wide(io_far[0])))
    send, keep = kernel(
        projections,
        [((4 * count, width), b16)] * 2,
        (2 * group * width * (768 + out_width), 0),
        grad_packed, qkv, mixed, w_down,
    )
    io_near, io_down, g_pair, g_far, send = tie(io_near, io_down, g_pair, g_far, send)
    g_kept, g_pair, g_far = split_rows(g_keep, 3), split_rows(g_pair, 2), split_rows(g_far, 2)
    g_near = over(low(wide(g_near) + wide(g_pair[1])))
    g_down = down(low(wide(g_kept[1]) + wide(g_far[0])))
    kept, sent = scatter_last(send, keep)
    io_up = up(low(wide(io_kept[0]) + wide(io_pair[0]) + wide(io_near)))
    io_up, g_near, g_down, sent = tie(io_up, g_near, g_down, sent)
    sum_io, g_turned = tie(
        low(wide(io_kept[2]) + wide(io_far[1]) + wide(io_down) + wide(io_up)),
        low(wide(g_kept[0]) + wide(g_pair[0]) + wide(g_near)),
    )
    g_up = up(g_turned)
    last_across = swap(sent, 2)
    back = rep_exchange(sum_io)
    back, g_up = tie(back, g_up)
    sum_g = low(wide(g_kept[2]) + wide(g_far[1]) + wide(g_down) + wide(g_up))
    back_qkv = rep_exchange(sum_g[:, :768])
    grad_w_attn_out = wide(
        lax.ppermute(
            columns(split_rows(tie(sum_g, back)[0][:, 768:], 4)),
            AXES,
            [(there, here) for here, there in order],
        )
    )
    grad_w_in, gain_in, grad_w_out = kernel(
        unpack_rest,
        [(w_in.shape, f32), (gain_mlp.shape, f32), (w_out.shape, f32)],
        (4 * w_in.size, 0),
        back, w_in, gain_mlp,
    )
    grad_w_qkv, gain_qkv = kernel(
        unpack_qkv,
        [(w_qkv.shape, f32), (gain_attn.shape, f32)],
        (4 * w_qkv.size, 0),
        back_qkv, w_qkv, gain_attn,
    )
    last = kept + wide(last_across)

    standard, inverse = norm_statistics(x_own)
    block_input_gradient = grad_hidden + norm_backward_pass(
        last[:count], jnp.ones((), f32), standard, inverse
    )
    output = low(jnp.where(seg_col[:count] < 8, hidden_sum + last[count:], 0.0))
    return (
        absolute(output, z, x),
        absolute(block_input_gradient, z, x),
        gain_qkv.reshape(-1),
        grad_w_qkv,
        grad_w_attn_out,
        gain_in.reshape(-1),
        grad_w_in,
        grad_w_out,
    )


def solution(mesh):
    ringed = dict(mesh.shape) == {"fsdp": 8, "rep": 4}
    return jax.shard_map(
        local_ring if ringed else local_plain,
        mesh=mesh,
        in_specs=(
            P(AXES, None),
            P(AXES, None),
            P(AXES, None),
            P(AXES),
            P(AXES, None),
            P(AXES, None),
            P(AXES),
            P(AXES, None),
            P(AXES, None),
        ),
        out_specs=(
            P(AXES, None),
            P(AXES, None),
            P(AXES),
            P(AXES, None),
            P(AXES, None),
            P(AXES),
            P(AXES, None),
            P(AXES, None),
        ),
        check_vma=False,
    )
```

```python
import jax
import jax.numpy as jnp
from jax import lax
from jax.experimental import pallas as pl
from jax.experimental.pallas import tpu as pltpu
from jax.sharding import PartitionSpec as P

HEAD_DIM = 64


norm_eps = 1e-05
rope_base = 160000.0


def matmul(left_side, right_side):
    return jnp.dot(left_side, right_side, preferred_element_type=jnp.float32)


def matmul_right_t(left_side, right_side):
    return lax.dot_general(
        left_side, right_side, (((1,), (1,)), ((), ())), preferred_element_type=jnp.float32
    )


def matmul_left_t(left_side, right_side):
    return lax.dot_general(
        left_side, right_side, (((0,), (0,)), ((), ())), preferred_element_type=jnp.float32
    )


def batched(form, left_side, right_side):
    return jnp.einsum(form, left_side, right_side, preferred_element_type=jnp.float32)


def layout(lengths, row_count):
    slot_ids = lax.iota(jnp.int32, lengths.shape[0])
    before = (slot_ids[:, None] <= slot_ids[None, :]).astype(jnp.int32)
    ends = jnp.sum(lengths[:, None] * before, axis=0)
    starts = ends - lengths
    places = lax.iota(jnp.int32, row_count)
    sequence_segment = jnp.sum((ends[None, :] <= places[:, None]).astype(jnp.int32), axis=1)
    first_row = jnp.sum(
        jnp.where(sequence_segment[:, None] == slot_ids[None, :], starts[None, :], 0), axis=1
    )
    return (sequence_segment, places - first_row, sequence_segment < lengths.shape[0])


def rotary(positions, head_size):
    half_size = head_size // 2
    frequency = rope_base ** (-(lax.iota(jnp.float32, half_size) * (2.0 / head_size)))
    angles = positions.astype(jnp.float32)[..., None] * frequency
    cosine_table = jnp.concatenate([jnp.cos(angles), jnp.cos(angles)], axis=-1)
    sine_table = jnp.concatenate([jnp.sin(angles), jnp.sin(angles)], axis=-1)
    return (cosine_table, sine_table)


def rotate_half(vector):
    half_size = vector.shape[-1] // 2
    return jnp.concatenate([-vector[..., half_size:], vector[..., :half_size]], axis=-1)


def rotate_back(vector):
    half_size = vector.shape[-1] // 2
    return jnp.concatenate([vector[..., half_size:], -vector[..., :half_size]], axis=-1)


def norm_statistics(values):
    average = jnp.mean(values, axis=-1, keepdims=True)
    centred = values - average
    inverse = lax.rsqrt(jnp.mean(centred * centred, axis=-1, keepdims=True) + norm_eps)
    return (centred * inverse, inverse)


def norm_backward_pass(grad_normed, gain_vec, normalized, inverse):
    scaled = grad_normed * gain_vec.astype(jnp.float32)
    return inverse * (
        scaled
        - jnp.mean(scaled, axis=-1, keepdims=True)
        - normalized * jnp.mean(scaled * normalized, axis=-1, keepdims=True)
    )


def attend(rotated_query, rotated_key, value_reduced_precision, sequence_segment):
    scores = batched("thd,shd->hts", rotated_query, rotated_key)
    allowed = sequence_segment[:, None] == sequence_segment[None, :]
    scores = jnp.where(allowed[None], scores, -jnp.inf)
    logarithm_totals = jax.nn.logsumexp(scores, axis=-1)
    weights = jnp.exp(scores - logarithm_totals[..., None]).astype(jnp.bfloat16)
    attended = batched("hts,shd->thd", weights, value_reduced_precision).astype(jnp.bfloat16)
    return (attended, logarithm_totals)


def attend_back(
    rotated_query,
    rotated_key,
    value_reduced_precision,
    sequence_segment,
    logarithm_totals,
    grad_attended,
):
    scores = batched("thd,shd->hts", rotated_query, rotated_key)
    allowed = sequence_segment[:, None] == sequence_segment[None, :]
    scores = jnp.where(allowed[None], scores, -jnp.inf)
    probs_full = jnp.exp(scores - logarithm_totals[..., None])
    weights = probs_full.astype(jnp.bfloat16)
    grad_value = batched("hts,thd->shd", weights, grad_attended)
    grad_probs = batched("thd,shd->hts", grad_attended, value_reduced_precision)
    row_delta = jnp.sum(probs_full * grad_probs, axis=-1, keepdims=True)
    grad_scores = (probs_full * (grad_probs - row_delta)).astype(jnp.bfloat16)
    grad_query = batched("hts,shd->thd", grad_scores, rotated_key)
    grad_key = batched("hts,thd->shd", grad_scores, rotated_query)
    return (grad_query, grad_key, grad_value)


def forward(
    tokens, lengths, attention_norm_gain, w_qkv, w_attn_out, feedforward_norm_gain, w_in, w_out
):
    groups, row_count, embedding_width = tokens.shape
    head_count = embedding_width // HEAD_DIM
    hidden_units = w_in.shape[1] // 2
    sequence_segment, positions, valid = jax.vmap(
        lambda row_lengths: layout(row_lengths, row_count)
    )(lengths)
    cosine_table, sine_table = rotary(positions, HEAD_DIM)
    cosine_table = cosine_table[:, :, None, :]
    sine_table = sine_table[:, :, None, :]
    residual_input = tokens.reshape(groups * row_count, embedding_width).astype(jnp.float32)
    attention_standardized, attention_inverse_norm = norm_statistics(residual_input)
    attention_normed_input = (
        attention_standardized * attention_norm_gain.astype(jnp.float32)
    ).astype(jnp.bfloat16)
    packed = matmul(attention_normed_input, w_qkv).reshape(
        groups, row_count, 3, head_count, HEAD_DIM
    )
    query_raw = packed[:, :, 0]
    key_raw = packed[:, :, 1]
    rotated_query = (
        (query_raw * cosine_table + rotate_half(query_raw) * sine_table) * HEAD_DIM ** (-0.5)
    ).astype(jnp.bfloat16)
    rotated_key = (key_raw * cosine_table + rotate_half(key_raw) * sine_table).astype(jnp.bfloat16)
    value_reduced_precision = packed[:, :, 2].astype(jnp.bfloat16)
    attended, logarithm_totals = jax.vmap(attend)(
        rotated_query, rotated_key, value_reduced_precision, sequence_segment
    )
    attention_rows_flat = attended.reshape(groups * row_count, embedding_width)
    hidden_residual = residual_input + matmul(attention_rows_flat, w_attn_out)
    feedforward_standardized, feedforward_inverse_norm = norm_statistics(hidden_residual)
    feedforward_normed_input = (
        feedforward_standardized * feedforward_norm_gain.astype(jnp.float32)
    ).astype(jnp.bfloat16)
    inner_proj = matmul(feedforward_normed_input, w_in)
    gate_projection = inner_proj[:, :hidden_units]
    up_projection = inner_proj[:, hidden_units:]
    activation_output = jax.nn.gelu(gate_projection, approximate=False)
    mixed_input = (activation_output * up_projection).astype(jnp.bfloat16)
    live_token_rows = valid.reshape(groups * row_count, 1)
    mlp_result = matmul_right_t(mixed_input, w_out)
    output = jnp.where(live_token_rows, hidden_residual + mlp_result, 0.0).astype(jnp.bfloat16)
    saved_residuals = (
        sequence_segment,
        live_token_rows,
        cosine_table,
        sine_table,
        attention_standardized,
        attention_inverse_norm,
        attention_normed_input,
        rotated_query,
        rotated_key,
        value_reduced_precision,
        logarithm_totals,
        attention_rows_flat,
        feedforward_standardized,
        feedforward_inverse_norm,
        feedforward_normed_input,
        gate_projection,
        up_projection,
        activation_output,
        mixed_input,
    )
    return (output, saved_residuals)


def backward(
    saved_residuals,
    cotangent,
    attention_norm_gain,
    w_qkv,
    w_attn_out,
    feedforward_norm_gain,
    w_in,
    w_out,
):
    (
        sequence_segment,
        live_token_rows,
        cosine_table,
        sine_table,
        attention_standardized,
        attention_inverse_norm,
        attention_normed_input,
        rotated_query,
        rotated_key,
        value_reduced_precision,
        logarithm_totals,
        attention_rows_flat,
        feedforward_standardized,
        feedforward_inverse_norm,
        feedforward_normed_input,
        gate_projection,
        up_projection,
        activation_output,
        mixed_input,
    ) = saved_residuals
    groups, row_count = sequence_segment.shape
    embedding_width = attention_standardized.shape[1]
    head_count = embedding_width // HEAD_DIM
    flat_cot = cotangent.reshape(groups * row_count, embedding_width)
    output_gradient = jnp.where(live_token_rows, flat_cot, jnp.zeros((), flat_cot.dtype))
    grad_mixed = matmul(output_gradient, w_out)
    slope = (
        0.5 * (1.0 + lax.erf(gate_projection * 0.7071067811865476))
        + gate_projection * jnp.exp(-0.5 * gate_projection * gate_projection) * 0.3989422804014327
    )
    grad_inner = jnp.concatenate(
        [grad_mixed * up_projection * slope, grad_mixed * activation_output], axis=1
    ).astype(jnp.bfloat16)
    feedforward_normed_gradient = matmul_right_t(grad_inner, w_in)
    hidden_gradient = output_gradient.astype(jnp.float32) + norm_backward_pass(
        feedforward_normed_gradient,
        feedforward_norm_gain,
        feedforward_standardized,
        feedforward_inverse_norm,
    )
    grad_hidden_low = hidden_gradient.astype(jnp.bfloat16)
    grad_attended = matmul_right_t(grad_hidden_low, w_attn_out).astype(jnp.bfloat16)
    grad_attended = grad_attended.reshape(groups, row_count, head_count, HEAD_DIM)
    grad_query, grad_key, grad_value = jax.vmap(attend_back)(
        rotated_query,
        rotated_key,
        value_reduced_precision,
        sequence_segment,
        logarithm_totals,
        grad_attended,
    )
    grad_query = grad_query * HEAD_DIM ** (-0.5)
    grad_query = grad_query * cosine_table + rotate_back(grad_query * sine_table)
    grad_key = grad_key * cosine_table + rotate_back(grad_key * sine_table)
    grad_packed = jnp.stack([grad_query, grad_key, grad_value], axis=2)
    grad_packed = grad_packed.reshape(groups * row_count, 3 * embedding_width).astype(jnp.bfloat16)
    attention_normed_gradient = matmul_right_t(grad_packed, w_qkv)
    block_input_gradient = hidden_gradient + norm_backward_pass(
        attention_normed_gradient,
        attention_norm_gain,
        attention_standardized,
        attention_inverse_norm,
    )
    factors = (
        attention_normed_input,
        grad_packed,
        attention_rows_flat,
        grad_hidden_low,
        feedforward_normed_input,
        grad_inner,
        output_gradient,
        mixed_input,
        attention_normed_gradient,
        attention_standardized,
        feedforward_normed_gradient,
        feedforward_standardized,
    )
    return (block_input_gradient, factors)


def local_plain(
    tokens,
    seq_lengths,
    cotangent,
    attention_norm_gain,
    w_qkv,
    w_attn_out,
    feedforward_norm_gain,
    w_in,
    w_out,
):
    row_count, embedding_width = tokens.shape
    gathered = (
        lax.all_gather(attention_norm_gain, ("fsdp", "rep"), axis=0, tiled=True),
        lax.all_gather(w_qkv, ("fsdp", "rep"), axis=0, tiled=True),
        lax.all_gather(w_attn_out, ("fsdp", "rep"), axis=0, tiled=True),
        lax.all_gather(feedforward_norm_gain, ("fsdp", "rep"), axis=0, tiled=True),
        lax.all_gather(w_in, ("fsdp", "rep"), axis=0, tiled=True),
        lax.all_gather(w_out, ("fsdp", "rep"), axis=0, tiled=True),
    )
    output, saved_residuals = forward(
        tokens.reshape(1, row_count, embedding_width),
        seq_lengths,
        gathered[0],
        gathered[1],
        gathered[2],
        gathered[3],
        gathered[4],
        gathered[5],
    )
    second_copy = (
        lax.all_gather(attention_norm_gain, ("fsdp", "rep"), axis=0, tiled=True),
        lax.all_gather(w_qkv, ("fsdp", "rep"), axis=0, tiled=True),
        lax.all_gather(w_attn_out, ("fsdp", "rep"), axis=0, tiled=True),
        lax.all_gather(feedforward_norm_gain, ("fsdp", "rep"), axis=0, tiled=True),
        lax.all_gather(w_in, ("fsdp", "rep"), axis=0, tiled=True),
        lax.all_gather(w_out, ("fsdp", "rep"), axis=0, tiled=True),
    )
    block_input_gradient, factors = backward(
        saved_residuals,
        cotangent.reshape(1, row_count, embedding_width),
        second_copy[0],
        second_copy[1],
        second_copy[2],
        second_copy[3],
        second_copy[4],
        second_copy[5],
    )
    (
        normed_attn,
        grad_packed,
        attended_rows,
        grad_hidden_low,
        normed_mlp,
        grad_inner,
        grad_out,
        mixed_input,
        grad_normed_attn,
        standard_attn,
        grad_normed_mlp,
        standard_mlp,
    ) = factors
    qkv_width = w_qkv.shape[1]
    attn_width = w_attn_out.shape[1]
    inner_width = w_in.shape[1]
    outer_width = w_out.shape[1]
    qkv_term = matmul_left_t(normed_attn, grad_packed)
    attn_term = matmul_left_t(attended_rows, grad_hidden_low)
    inner_term = matmul_left_t(normed_mlp, grad_inner)
    outer_term = matmul_left_t(grad_out, mixed_input)
    attn_gain_term = jnp.sum(grad_normed_attn * standard_attn, axis=0)
    mlp_gain_term = jnp.sum(grad_normed_mlp * standard_mlp, axis=0)
    summed = lax.psum_scatter(
        jnp.concatenate(
            [
                qkv_term,
                attn_term,
                inner_term,
                outer_term,
                attn_gain_term[:, None],
                mlp_gain_term[:, None],
            ],
            axis=1,
        ),
        ("fsdp", "rep"),
        scatter_dimension=0,
        tiled=True,
    )
    edge_two = qkv_width + attn_width
    edge_three = edge_two + inner_width
    edge_four = edge_three + outer_width
    return (
        output,
        block_input_gradient,
        summed[:, edge_four],
        summed[:, :qkv_width],
        summed[:, qkv_width:edge_two],
        summed[:, edge_four + 1],
        summed[:, edge_two:edge_three],
        summed[:, edge_three:edge_four],
    )


AXES = ("fsdp", "rep")
LANES = 128
HALF = HEAD_DIM // 2


def tie(*values):
    return lax.optimization_barrier(values)


def wide(value):
    return value.astype(jnp.float32)


def low(value):
    return value.astype(jnp.bfloat16)


def split_columns(value, count):
    width = value.shape[1] // count
    return [value[:, k * width : (k + 1) * width] for k in range(count)]


def split_rows(value, count):
    width = value.shape[0] // count
    return [value[k * width : (k + 1) * width] for k in range(count)]


def columns(blocks):
    return jnp.concatenate(blocks, axis=1)


def rows(blocks):
    return jnp.concatenate(blocks, axis=0)


def swap(value, distance):
    return lax.ppermute(value, "rep", [(k, k ^ distance) for k in range(4)])


def rep_exchange(value):
    blocks = value.reshape(4, value.shape[0] // 4, value.shape[1])
    return lax.all_to_all(blocks, "rep", 0, 0, tiled=True).reshape(value.shape)


def up(value):
    return lax.ppermute(value, "fsdp", [(k, (k + 2) % 8) for k in range(8)])


def down(value):
    return lax.ppermute(value, "fsdp", [(k, (k - 2) % 8) for k in range(8)])


def over(value):
    return lax.ppermute(value, "fsdp", [(k, k ^ 1) for k in range(8)])


def relative(value, z, x):
    blocks = split_columns(value, 8)
    blocks = [jnp.where(x == 1, blocks[k ^ 1], blocks[k]) for k in range(8)]
    for bit in (1, 2):
        turn = (z & bit) != 0
        blocks = [jnp.where(turn, blocks[(k + 2 * bit) % 8], blocks[k]) for k in range(8)]
    return columns([blocks[2 * ((p + 1) % 4) + i] for i in range(2) for p in range(4)])


def absolute(value, z, x):
    blocks = split_columns(value, 8)
    blocks = [blocks[4 * i + (j - 1) % 4] for j in range(4) for i in range(2)]
    blocks = [jnp.where(x == 1, blocks[k ^ 1], blocks[k]) for k in range(8)]
    for bit in (1, 2):
        turn = (z & bit) != 0
        blocks = [jnp.where(turn, blocks[(k - 2 * bit) % 8], blocks[k]) for k in range(8)]
    return columns(blocks)


def place_of(place, step, side):
    z, x = place[0], place[1]
    return 2 * lax.rem(z + step + 1, 4) + (x if side == 0 else 1 - x)


def block_of(place, z_at, side):
    z, x = place[0], place[1]
    return 4 * (x if side == 0 else 1 - x) + lax.rem(z_at - z + 7, 4)


def turned(value):
    width = value.shape[1]
    lane = lax.broadcasted_iota(jnp.int32, value.shape, 1)
    return jnp.where(
        lane % HEAD_DIM < HALF,
        pltpu.roll(value, width - HALF, 1),
        pltpu.roll(value, HALF, 1),
    )


def head_masks(row_count):
    lane = lax.broadcasted_iota(jnp.int32, (row_count, LANES), 1)
    return [low(wide(lane < HEAD_DIM)), low(wide(lane >= HEAD_DIM))], lane < HEAD_DIM


def token_rows(mine, across, beside, first, step):
    count = 128
    return [
        mine[first : first + count],
        beside[first : first + count],
        across[first : first + count],
        beside[step + first : step + first + count],
    ]


def attention_forward(
    place, seg_col, seg_row, cosine, sine, mine, across, beside,
    first, second, third, own, others, other_second, other,
    normed, qkv, attn, query, key, value, probs, attended, send, keep,
):
    size = own.shape[0]
    blocks = [
        (first, 0), (second, 0), (third, 0), (own, 0),
        (others, 0), (other_second, 0), (others, size), (other, 0),
    ]
    part = size // 4
    for at, (ref, row) in enumerate(blocks):
        qkv[size * at : size * (at + 1), :] = ref[row : row + size, :768]
        target = pl.multiple_of(place_of(place, at % 4, at // 4) * part, part)
        for z_at in range(4):
            for side in range(2):
                lanes = pl.multiple_of(block_of(place, z_at, side) * LANES, LANES)
                attn[pl.ds(target, part), pl.ds(lanes, LANES)] = ref[
                    row + part * z_at : row + part * (z_at + 1),
                    768 + LANES * side : 768 + LANES * (side + 1),
                ]
    count = 128
    for at, ref in enumerate(token_rows(mine, across, beside, 0, mine.shape[0])):
        values = wide(ref)
        centred = values - jnp.mean(values, axis=1, keepdims=True)
        inverse = lax.rsqrt(jnp.mean(centred * centred, axis=1, keepdims=True) + norm_eps)
        normed[count * at : count * (at + 1), :] = low(centred * inverse)
    packed = matmul(normed[...], qkv[...])
    cos_all, sin_all = columns([cosine[...]] * 2), columns([sine[...]] * 2)
    raw = packed[:, :256]
    query[...] = low((raw * cos_all + turned(raw) * sin_all) * HEAD_DIM ** (-0.5))
    raw = packed[:, 256:512]
    key[...] = low(raw * cos_all + turned(raw) * sin_all)
    value[...] = low(packed[:, 512:])
    masks, is_first = head_masks(count)
    for at in range(4):
        here = slice(count * at, count * (at + 1))
        allowed = seg_col[here, :] == seg_row[at : at + 1, :]
        for pair in range(2):
            lanes = slice(LANES * pair, LANES * (pair + 1))
            made = []
            for head in range(2):
                scores = matmul_right_t(query[here, lanes] * masks[head], key[here, lanes])
                scores = jnp.where(allowed, scores, -jnp.inf)
                powers = jnp.exp(scores - jnp.max(scores, axis=1, keepdims=True))
                weights = powers / jnp.sum(powers, axis=1, keepdims=True)
                slot = count * (4 * at + 2 * pair + head)
                probs[slot : slot + count, :] = weights
                made.append(matmul(low(weights), value[here, lanes]))
            attended[here, lanes] = low(jnp.where(is_first, made[0], made[1]))
    total = low(matmul(attended[...], attn[...]))
    keep[:count, :], send[:count, :] = total[:count], total[count : 2 * count]
    keep[count:, :], send[count:, :] = total[2 * count : 3 * count], total[3 * count :]


def mlp(
    seg_col, norm_own, norm_across, norm_beside, mine, across, beside,
    first, second, third, own, other_first, other_second, other_third, other,
    normed, grad_out, mixed, grad_inner, send, keep, w_down,
    w_up, inner, grad_mixed,
):
    size, count, edge = own.shape[0], 128, w_up.shape[1]
    blocks = (first, second, third, own, other_first, other_second, other_third, other)
    for at, ref in enumerate(blocks):
        w_up[size * at : size * (at + 1), :] = ref[:, :edge]
        w_down[size * at : size * (at + 1), :] = ref[:, edge:]
    for at, ref in enumerate(
        (norm_own[...], norm_beside[:count, :], norm_across[...], norm_beside[count:, :])
    ):
        normed[count * at : count * (at + 1), :] = ref
    for at, ref in enumerate(token_rows(mine, across, beside, count, mine.shape[0])):
        live = wide(seg_col[count * at : count * (at + 1), :] < 8)
        grad_out[count * at : count * (at + 1), :] = low(wide(ref) * live)
    inner[...] = matmul(normed[...], w_up[...])
    grad_mixed[...] = matmul(grad_out[...], w_down[...])
    main = (w_down.shape[1] // LANES - 1) * LANES
    rest = 16

    def parts(gate):
        phi = 0.5 * (1.0 + lax.erf(gate * 0.7071067811865476))
        slope = phi + gate * jnp.exp(-0.5 * gate * gate) * 0.3989422804014327
        return gate * phi, slope

    @pl.loop(0, 8)
    def _(step):
        here = pl.ds(pl.multiple_of(step * 64, 64), 64)
        gate, up_part = inner[here, :main], inner[here, main : 2 * main]
        grad = grad_mixed[here, :main]
        activation, slope = parts(gate)
        mixed[here, :main] = low(activation * up_part)
        grad_inner[here, :main] = low(grad * up_part * slope)
        grad_inner[here, main : 2 * main] = low(grad * activation)
        tail = inner[here, 2 * main :]
        grad = grad_mixed[here, main:]
        activation, slope = parts(tail)
        tail_up = pltpu.roll(tail, LANES - rest, 1)
        mixed[here, main:] = low(activation * tail_up)
        grad_inner[here, 2 * main :] = low(
            grad * tail_up * slope + pltpu.roll(grad * activation, rest, 1)
        )

    total = low(matmul_right_t(grad_inner[...], w_up[...]))
    keep[:count, :], send[:count, :] = total[:count], total[count : 2 * count]
    keep[count:, :], send[count:, :] = total[2 * count : 3 * count], total[3 * count :]


def place_term(term, keep, pair, near, far, lanes):
    size = term.shape[0] // 8
    for at, (ref, row) in enumerate(
        [(keep, 0), (pair, 0), (keep, 1), (keep, 2), (near, 0), (pair, 1), (far, 0), (far, 1)]
    ):
        ref[size * row : size * (row + 1), lanes] = term[size * at : size * (at + 1)]


def mlp_terms(normed, grad_inner, grad_out, mixed, keep, pair, near, far):
    edge = grad_inner.shape[1]
    term = low(matmul_left_t(normed[...], grad_inner[...]))
    place_term(term, keep, pair, near, far, slice(0, edge))
    term = low(matmul_left_t(grad_out[...], mixed[...]))
    place_term(term, keep, pair, near, far, slice(edge, edge + mixed.shape[1]))


def attention_backward(
    place, cosine, sine, low_own, low_across, low_beside, attn, query, key, value, probs,
    attended, normed,
    grad_packed, keep, pair, near, far, grad_low, grad_attended, term_attn,
):
    count = 128
    for at, ref in enumerate(
        (low_own[...], low_beside[:count, :], low_across[...], low_beside[count:, :])
    ):
        grad_low[count * at : count * (at + 1), :] = ref
    grad_attended[...] = low(matmul_right_t(grad_low[...], attn[...]))
    masks, is_first = head_masks(count)
    for at in range(4):
        here = slice(count * at, count * (at + 1))
        cos, sin = cosine[here, :], sine[here, :]
        for half in range(2):
            lanes = slice(LANES * half, LANES * (half + 1))
            q, k, v = query[here, lanes], key[here, lanes], value[here, lanes]
            grad = grad_attended[here, lanes]
            made = []
            for head in range(2):
                slot = count * (4 * at + 2 * half + head)
                weights = probs[slot : slot + count, :]
                grad_value = matmul_left_t(low(weights), grad)
                grad_probs = matmul_right_t(grad * masks[head], v)
                delta = jnp.sum(weights * grad_probs, axis=1, keepdims=True)
                grad_scores = low(weights * (grad_probs - delta))
                made.append((matmul(grad_scores, k), matmul_left_t(grad_scores, q), grad_value))
            grad_q, grad_k, grad_v = (jnp.where(is_first, *both) for both in zip(*made))
            grad_q = grad_q * HEAD_DIM ** (-0.5)
            grad_packed[here, lanes] = low(grad_q * cos - turned(grad_q) * sin)
            lanes = slice(256 + LANES * half, 256 + LANES * (half + 1))
            grad_packed[here, lanes] = low(grad_k * cos - turned(grad_k) * sin)
            lanes = slice(512 + LANES * half, 512 + LANES * (half + 1))
            grad_packed[here, lanes] = low(grad_v)
    term = low(matmul_left_t(normed[...], grad_packed[...]))
    place_term(term, keep, pair, near, far, slice(0, 768))
    term_attn[...] = low(matmul_left_t(attended[...], grad_low[...]))
    size = term.shape[0] // 8
    part = size // 4
    targets = [
        (keep, 0), (pair, 0), (keep, size), (keep, 2 * size),
        (near, 0), (pair, size), (far, 0), (far, size),
    ]
    for at, (ref, row) in enumerate(targets):
        source = pl.multiple_of(place_of(place, at % 4, at // 4) * part, part)
        for z_at in range(4):
            for side in range(2):
                lanes = pl.multiple_of(block_of(place, z_at, side) * LANES, LANES)
                ref[
                    row + part * z_at : row + part * (z_at + 1),
                    768 + LANES * side : 768 + LANES * (side + 1),
                ] = term_attn[pl.ds(source, part), pl.ds(lanes, LANES)]


def projections(grad_packed, qkv, mixed, w_down, send, keep):
    count = 128
    for row, total in (
        (0, low(matmul_right_t(grad_packed[...], qkv[...]))),
        (count, low(matmul_right_t(mixed[...], w_down[...]))),
    ):
        keep[row : row + count, :] = total[:count]
        send[row : row + count, :] = total[count : 2 * count]
        keep[2 * count + row : 3 * count + row, :] = total[2 * count : 3 * count]
        send[2 * count + row : 3 * count + row, :] = total[3 * count :]


def unpack_rest(back, w_in, gain, grad_in, gain_grad, grad_out):
    size, hidden, part = w_in.shape[0], w_in.shape[1] // 2, w_in.shape[1] // 8
    main = part // LANES * LANES
    rest, edge = part - main, 2 * main + LANES
    total = jnp.zeros(gain_grad.shape, jnp.float32)
    for k in range(4):
        here = slice(size * k, size * (k + 1))
        for half in range(2):
            base = hidden * half + part * k
            for source, target, count in (
                (main * half, base, main),
                (2 * main + rest * half, base + main, rest),
            ):
                piece = wide(back[here, source : source + count])
                grad_in[:, target : target + count] = piece * gain[...]
                weights = wide(w_in[:, target : target + count])
                total += jnp.sum(piece * weights, axis=1, keepdims=True)
        grad_out[:, part * k : part * (k + 1)] = wide(back[here, edge : edge + part])
    gain_grad[...] = total


def unpack_qkv(back, w_qkv, gain, grad, gain_grad):
    size, part = w_qkv.shape[0], 256
    total = jnp.zeros(gain_grad.shape, jnp.float32)
    for k in range(4):
        for third in range(3):
            piece = wide(back[size * k : size * (k + 1), part * third : part * (third + 1)])
            lanes = slice(part * (4 * third + k), part * (4 * third + k + 1))
            grad[:, lanes] = piece * gain[...]
            total += jnp.sum(piece * wide(w_qkv[:, lanes]), axis=1, keepdims=True)
    gain_grad[...] = total


def kernel(body, outs, cost, *args, scratch=(), scalars=0):
    flops, transcendentals = cost
    shapes = [jax.ShapeDtypeStruct(shape, kind) for shape, kind in outs]
    moved = sum(arg.size * arg.dtype.itemsize for arg in (*args, *shapes))
    return pl.pallas_call(
        body,
        out_shape=shapes,
        in_specs=[
            pl.BlockSpec(memory_space=pltpu.SMEM if k < scalars else pltpu.VMEM)
            for k in range(len(args))
        ],
        out_specs=[pl.BlockSpec(memory_space=pltpu.VMEM)] * len(shapes),
        scratch_shapes=[pltpu.VMEM(shape, kind) for shape, kind in scratch],
        compiler_params=pltpu.CompilerParams(vmem_limit_bytes=28 * 2**20),
        cost_estimate=pl.CostEstimate(
            flops=flops, bytes_accessed=moved, transcendentals=transcendentals
        ),
        name=body.__name__,
    )(*args)


def scatter_last(send, keep):
    beside = split_rows(swap(send, 1), 2)
    kept = split_rows(keep, 2)
    sent = low(wide(kept[1]) + wide(beside[1]))
    return wide(kept[0]) + wide(beside[0]), sent


def local_ring(
    tokens,
    seq_lengths,
    cotangent,
    attention_norm_gain,
    w_qkv,
    w_attn_out,
    feedforward_norm_gain,
    w_in,
    w_out,
):
    count, width = tokens.shape
    index = lax.axis_index("fsdp")
    z, x = index // 2, index % 2
    place = jnp.stack([z, x]).astype(jnp.int32)
    hidden = w_in.shape[1] // 2
    part = hidden // 4
    main = part // LANES * LANES
    in_width, out_width = 2 * main + LANES, main + LANES
    f32, b16 = jnp.float32, jnp.bfloat16
    group = 4 * count

    gain_attn = wide(attention_norm_gain)[:, None]
    gain_mlp = wide(feedforward_norm_gain)[:, None]
    order = [(k, (k % 8) * 4 + k // 8) for k in range(32)]
    attn_own = lax.ppermute(w_attn_out, AXES, order)
    qkv_parts = split_columns(low(wide(w_qkv) * gain_attn), 12)
    size = w_qkv.shape[0]
    slots = seq_lengths.shape[1]
    lengths_low = jnp.pad(low(wide(seq_lengths)), ((0, size - 1), (0, LANES - slots)))
    exchanged = rep_exchange(rows([columns([*qkv_parts[k::4], lengths_low]) for k in range(4)]))
    first_own = columns([exchanged[:, :768], rows(split_columns(attn_own, 4))])
    lengths = rows([exchanged[size * k : size * k + 1, 768 : 768 + slots] for k in range(4)])
    lengths = wide(lengths).astype(jnp.int32)
    for bit in (1, 2):
        turned_rows = rows([lengths[k ^ bit : (k ^ bit) + 1] for k in range(4)])
        lengths = jnp.where((lax.axis_index("rep") & bit) != 0, turned_rows, lengths)

    scaled_in = low(wide(w_in) * gain_mlp)
    pieces = []
    for k in range(4):
        gate = scaled_in[:, part * k : part * (k + 1)]
        up_part = scaled_in[:, hidden + part * k : hidden + part * (k + 1)]
        out_part = w_out[:, part * k : part * (k + 1)]
        fill = [jnp.zeros((w_in.shape[0], n), b16) for n in (in_width - 2 * part, out_width - part)]
        pieces.append(
            columns(
                [gate[:, :main], up_part[:, :main], gate[:, main:], up_part[:, main:], fill[0]]
                + [out_part, fill[1]]
            )
        )
    mine = rows([relative(tokens, z, x), relative(cotangent, z, x)])
    first_own, rest, mine = tie(first_own, rows(pieces), mine)
    rest = rep_exchange(rest)

    third, first, other = up(first_own), down(first_own), over(first_own)
    third, first, other, mine, rest = tie(third, first, other, mine, rest)
    across = swap(mine, 2)
    second, others, rest_third = up(third), over(rows([first, third])), up(rest)
    second, others, across = tie(second, others, across)
    other_second = over(second)
    rest_first = down(tie(rest, rest_third)[0])
    beside = swap(rows([mine, across]), 1)
    rest_other = over(tie(rest, other_second)[0])

    step = mine.shape[0]
    segment, positions, _ = jax.vmap(lambda row: layout(row, count))(lengths)
    frequency = rope_base ** (-(lax.iota(f32, HALF) * (2.0 / HEAD_DIM)))
    angles = positions.reshape(group, 1).astype(f32) * frequency
    cosine, sine = jnp.cos(angles), jnp.sin(angles)
    cosine, sine = columns([cosine] * 4), columns([-sine, sine] * 2)
    seg_col = segment.reshape(group, 1)

    normed, qkv, attn, query, key, value, probs, attended, send, keep = kernel(
        attention_forward,
        [((group, width), b16), ((width, 768), b16), ((256, width), b16)]
        + [((group, 256), b16)] * 3
        + [((16 * count, count), f32), ((group, 256), b16)]
        + [((2 * count, width), b16)] * 2,
        (2 * group * width * (768 + 256) + 4 * 16 * count * count * LANES, 16 * count * count),
        place, seg_col, segment, cosine, sine, mine, across, beside,
        first, second, third, first_own, others, other_second, other,
        scalars=1,
    )
    rest_third, rest_first, rest_other, send = tie(rest_third, rest_first, rest_other, send)
    rest_second, rest_other_third = up(rest_third), over(rest_third)
    x_own = wide(mine[:count])
    kept, sent = scatter_last(send, keep)
    rest_other_first = over(tie(rest_first, rest_other_third)[0])
    hidden_sum = x_own + kept + wide(swap(sent, 2))
    standard_mlp, inverse_mlp = norm_statistics(hidden_sum)
    norm_own = low(standard_mlp)
    norm_across = swap(norm_own, 2)
    rest_second, rest_other_third, _ = tie(rest_second, rest_other_third, norm_own)
    rest_other_second = up(rest_other_third)
    norm_beside = swap(rows([norm_own, norm_across]), 1)

    normed_mlp, grad_out, mixed, grad_inner, send, keep, w_down = kernel(
        mlp,
        [((group, width), b16)] * 2
        + [((group, out_width), b16), ((group, in_width), b16)]
        + [((2 * count, width), b16)] * 2
        + [((width, out_width), b16)],
        (2 * group * width * (2 * in_width + out_width), 3 * group * part),
        seg_col, norm_own, norm_across, norm_beside, mine, across, beside,
        rest_first, rest_second, rest_third, rest,
        rest_other_first, rest_other_second, rest_other_third, rest_other,
        scratch=[
            ((width, in_width), b16),
            ((group, in_width), f32),
            ((group, out_width), f32),
        ],
    )
    all_width = in_width + out_width
    size = width // 8
    io_keep, io_pair, io_near, io_far = kernel(
        mlp_terms,
        [((size * n, all_width), b16) for n in (3, 2, 1, 2)],
        (2 * group * width * all_width, 0),
        normed_mlp, grad_inner, grad_out, mixed,
    )
    io_pair, io_far = up(io_pair), over(io_far)
    kept, sent = scatter_last(send, keep)
    scaled_mlp = kept + wide(tie(swap(sent, 2), io_keep)[0])
    grad_hidden = wide(grad_out[:count]) + norm_backward_pass(
        scaled_mlp, jnp.ones((), f32), standard_mlp, inverse_mlp
    )
    low_own = low(grad_hidden)
    low_across = swap(low_own, 2)
    low_beside = swap(rows([low_own, low_across]), 1)

    grad_packed, g_keep, g_pair, g_near, g_far = kernel(
        attention_backward,
        [((group, 768), b16)] + [((size * n, width), b16) for n in (3, 2, 1, 2)],
        (2 * group * width * (768 + 512) + 10 * 16 * count * count * LANES, 0),
        place, cosine, sine, low_own, low_across, low_beside, attn, query, key, value, probs,
        attended, normed,
        scratch=[((group, width), b16), ((group, 256), b16), ((256, width), b16)],
        scalars=1,
    )
    g_pair, g_far = up(g_pair), over(g_far)
    io_pair, io_far, _ = tie(io_pair, io_far, g_near)
    io_kept, io_pair, io_far = split_rows(io_keep, 3), split_rows(io_pair, 2), split_rows(io_far, 2)
    io_near = over(low(wide(io_near) + wide(io_pair[1])))
    io_down = down(low(wide(io_kept[1]) + wide(io_far[0])))
    send, keep = kernel(
        projections,
        [((4 * count, width), b16)] * 2,
        (2 * group * width * (768 + out_width), 0),
        grad_packed, qkv, mixed, w_down,
    )
    io_near, io_down, g_pair, g_far, send = tie(io_near, io_down, g_pair, g_far, send)
    g_kept, g_pair, g_far = split_rows(g_keep, 3), split_rows(g_pair, 2), split_rows(g_far, 2)
    g_near = over(low(wide(g_near) + wide(g_pair[1])))
    g_down = down(low(wide(g_kept[1]) + wide(g_far[0])))
    kept, sent = scatter_last(send, keep)
    io_up = up(low(wide(io_kept[0]) + wide(io_pair[0]) + wide(io_near)))
    io_up, g_near, g_down, sent = tie(io_up, g_near, g_down, sent)
    sum_io, g_turned = tie(
        low(wide(io_kept[2]) + wide(io_far[1]) + wide(io_down) + wide(io_up)),
        low(wide(g_kept[0]) + wide(g_pair[0]) + wide(g_near)),
    )
    g_up = up(g_turned)
    last_across = swap(sent, 2)
    back = rep_exchange(sum_io)
    back, g_up = tie(back, g_up)
    sum_g = low(wide(g_kept[2]) + wide(g_far[1]) + wide(g_down) + wide(g_up))
    back_qkv = rep_exchange(sum_g[:, :768])
    grad_w_attn_out = wide(
        lax.ppermute(
            columns(split_rows(tie(sum_g, back)[0][:, 768:], 4)),
            AXES,
            [(there, here) for here, there in order],
        )
    )
    grad_w_in, gain_in, grad_w_out = kernel(
        unpack_rest,
        [(w_in.shape, f32), (gain_mlp.shape, f32), (w_out.shape, f32)],
        (4 * w_in.size, 0),
        back, w_in, gain_mlp,
    )
    grad_w_qkv, gain_qkv = kernel(
        unpack_qkv,
        [(w_qkv.shape, f32), (gain_attn.shape, f32)],
        (4 * w_qkv.size, 0),
        back_qkv, w_qkv, gain_attn,
    )
    last = kept + wide(last_across)

    standard, inverse = norm_statistics(x_own)
    block_input_gradient = grad_hidden + norm_backward_pass(
        last[:count], jnp.ones((), f32), standard, inverse
    )
    output = low(jnp.where(seg_col[:count] < 8, hidden_sum + last[count:], 0.0))
    return (
        absolute(output, z, x),
        absolute(block_input_gradient, z, x),
        gain_qkv.reshape(-1),
        grad_w_qkv,
        grad_w_attn_out,
        gain_in.reshape(-1),
        grad_w_in,
        grad_w_out,
    )


def solution(mesh):
    ringed = dict(mesh.shape) == {"fsdp": 8, "rep": 4}
    return jax.shard_map(
        local_ring if ringed else local_plain,
        mesh=mesh,
        in_specs=(
            P(AXES, None),
            P(AXES, None),
            P(AXES, None),
            P(AXES),
            P(AXES, None),
            P(AXES, None),
            P(AXES),
            P(AXES, None),
            P(AXES, None),
        ),
        out_specs=(
            P(AXES, None),
            P(AXES, None),
            P(AXES),
            P(AXES, None),
            P(AXES, None),
            P(AXES),
            P(AXES, None),
            P(AXES, None),
        ),
        check_vma=False,
    )
```

```python
import jax
import jax.numpy as jnp
from jax import lax
from jax.experimental import pallas as pl
from jax.experimental.pallas import tpu as pltpu
from jax.sharding import PartitionSpec as P

HEAD_DIM = 64


norm_eps = 1e-05
rope_base = 160000.0


def matmul(left_side, right_side):
    return jnp.dot(left_side, right_side, preferred_element_type=jnp.float32)


def matmul_right_t(left_side, right_side):
    return lax.dot_general(
        left_side, right_side, (((1,), (1,)), ((), ())), preferred_element_type=jnp.float32
    )


def matmul_left_t(left_side, right_side):
    return lax.dot_general(
        left_side, right_side, (((0,), (0,)), ((), ())), preferred_element_type=jnp.float32
    )


def batched(form, left_side, right_side):
    return jnp.einsum(form, left_side, right_side, preferred_element_type=jnp.float32)


def layout(lengths, row_count):
    slot_ids = lax.iota(jnp.int32, lengths.shape[0])
    before = (slot_ids[:, None] <= slot_ids[None, :]).astype(jnp.int32)
    ends = jnp.sum(lengths[:, None] * before, axis=0)
    starts = ends - lengths
    places = lax.iota(jnp.int32, row_count)
    sequence_segment = jnp.sum((ends[None, :] <= places[:, None]).astype(jnp.int32), axis=1)
    first_row = jnp.sum(
        jnp.where(sequence_segment[:, None] == slot_ids[None, :], starts[None, :], 0), axis=1
    )
    return (sequence_segment, places - first_row, sequence_segment < lengths.shape[0])


def rotary(positions, head_size):
    half_size = head_size // 2
    frequency = rope_base ** (-(lax.iota(jnp.float32, half_size) * (2.0 / head_size)))
    angles = positions.astype(jnp.float32)[..., None] * frequency
    cosine_table = jnp.concatenate([jnp.cos(angles), jnp.cos(angles)], axis=-1)
    sine_table = jnp.concatenate([jnp.sin(angles), jnp.sin(angles)], axis=-1)
    return (cosine_table, sine_table)


def rotate_half(vector):
    half_size = vector.shape[-1] // 2
    return jnp.concatenate([-vector[..., half_size:], vector[..., :half_size]], axis=-1)


def rotate_back(vector):
    half_size = vector.shape[-1] // 2
    return jnp.concatenate([vector[..., half_size:], -vector[..., :half_size]], axis=-1)


def norm_statistics(values):
    average = jnp.mean(values, axis=-1, keepdims=True)
    centred = values - average
    inverse = lax.rsqrt(jnp.mean(centred * centred, axis=-1, keepdims=True) + norm_eps)
    return (centred * inverse, inverse)


def norm_backward_pass(grad_normed, gain_vec, normalized, inverse):
    scaled = grad_normed * gain_vec.astype(jnp.float32)
    return inverse * (
        scaled
        - jnp.mean(scaled, axis=-1, keepdims=True)
        - normalized * jnp.mean(scaled * normalized, axis=-1, keepdims=True)
    )


def attend(rotated_query, rotated_key, value_reduced_precision, sequence_segment):
    scores = batched("thd,shd->hts", rotated_query, rotated_key)
    allowed = sequence_segment[:, None] == sequence_segment[None, :]
    scores = jnp.where(allowed[None], scores, -jnp.inf)
    logarithm_totals = jax.nn.logsumexp(scores, axis=-1)
    weights = jnp.exp(scores - logarithm_totals[..., None]).astype(jnp.bfloat16)
    attended = batched("hts,shd->thd", weights, value_reduced_precision).astype(jnp.bfloat16)
    return (attended, logarithm_totals)


def attend_back(
    rotated_query,
    rotated_key,
    value_reduced_precision,
    sequence_segment,
    logarithm_totals,
    grad_attended,
):
    scores = batched("thd,shd->hts", rotated_query, rotated_key)
    allowed = sequence_segment[:, None] == sequence_segment[None, :]
    scores = jnp.where(allowed[None], scores, -jnp.inf)
    probs_full = jnp.exp(scores - logarithm_totals[..., None])
    weights = probs_full.astype(jnp.bfloat16)
    grad_value = batched("hts,thd->shd", weights, grad_attended)
    grad_probs = batched("thd,shd->hts", grad_attended, value_reduced_precision)
    row_delta = jnp.sum(probs_full * grad_probs, axis=-1, keepdims=True)
    grad_scores = (probs_full * (grad_probs - row_delta)).astype(jnp.bfloat16)
    grad_query = batched("hts,shd->thd", grad_scores, rotated_key)
    grad_key = batched("hts,thd->shd", grad_scores, rotated_query)
    return (grad_query, grad_key, grad_value)


def forward(
    tokens, lengths, attention_norm_gain, w_qkv, w_attn_out, feedforward_norm_gain, w_in, w_out
):
    groups, row_count, embedding_width = tokens.shape
    head_count = embedding_width // HEAD_DIM
    hidden_units = w_in.shape[1] // 2
    sequence_segment, positions, valid = jax.vmap(
        lambda row_lengths: layout(row_lengths, row_count)
    )(lengths)
    cosine_table, sine_table = rotary(positions, HEAD_DIM)
    cosine_table = cosine_table[:, :, None, :]
    sine_table = sine_table[:, :, None, :]
    residual_input = tokens.reshape(groups * row_count, embedding_width).astype(jnp.float32)
    attention_standardized, attention_inverse_norm = norm_statistics(residual_input)
    attention_normed_input = (
        attention_standardized * attention_norm_gain.astype(jnp.float32)
    ).astype(jnp.bfloat16)
    packed = matmul(attention_normed_input, w_qkv).reshape(
        groups, row_count, 3, head_count, HEAD_DIM
    )
    query_raw = packed[:, :, 0]
    key_raw = packed[:, :, 1]
    rotated_query = (
        (query_raw * cosine_table + rotate_half(query_raw) * sine_table) * HEAD_DIM ** (-0.5)
    ).astype(jnp.bfloat16)
    rotated_key = (key_raw * cosine_table + rotate_half(key_raw) * sine_table).astype(jnp.bfloat16)
    value_reduced_precision = packed[:, :, 2].astype(jnp.bfloat16)
    attended, logarithm_totals = jax.vmap(attend)(
        rotated_query, rotated_key, value_reduced_precision, sequence_segment
    )
    attention_rows_flat = attended.reshape(groups * row_count, embedding_width)
    hidden_residual = residual_input + matmul(attention_rows_flat, w_attn_out)
    feedforward_standardized, feedforward_inverse_norm = norm_statistics(hidden_residual)
    feedforward_normed_input = (
        feedforward_standardized * feedforward_norm_gain.astype(jnp.float32)
    ).astype(jnp.bfloat16)
    inner_proj = matmul(feedforward_normed_input, w_in)
    gate_projection = inner_proj[:, :hidden_units]
    up_projection = inner_proj[:, hidden_units:]
    activation_output = jax.nn.gelu(gate_projection, approximate=False)
    mixed_input = (activation_output * up_projection).astype(jnp.bfloat16)
    live_token_rows = valid.reshape(groups * row_count, 1)
    mlp_result = matmul_right_t(mixed_input, w_out)
    output = jnp.where(live_token_rows, hidden_residual + mlp_result, 0.0).astype(jnp.bfloat16)
    saved_residuals = (
        sequence_segment,
        live_token_rows,
        cosine_table,
        sine_table,
        attention_standardized,
        attention_inverse_norm,
        attention_normed_input,
        rotated_query,
        rotated_key,
        value_reduced_precision,
        logarithm_totals,
        attention_rows_flat,
        feedforward_standardized,
        feedforward_inverse_norm,
        feedforward_normed_input,
        gate_projection,
        up_projection,
        activation_output,
        mixed_input,
    )
    return (output, saved_residuals)


def backward(
    saved_residuals,
    cotangent,
    attention_norm_gain,
    w_qkv,
    w_attn_out,
    feedforward_norm_gain,
    w_in,
    w_out,
):
    (
        sequence_segment,
        live_token_rows,
        cosine_table,
        sine_table,
        attention_standardized,
        attention_inverse_norm,
        attention_normed_input,
        rotated_query,
        rotated_key,
        value_reduced_precision,
        logarithm_totals,
        attention_rows_flat,
        feedforward_standardized,
        feedforward_inverse_norm,
        feedforward_normed_input,
        gate_projection,
        up_projection,
        activation_output,
        mixed_input,
    ) = saved_residuals
    groups, row_count = sequence_segment.shape
    embedding_width = attention_standardized.shape[1]
    head_count = embedding_width // HEAD_DIM
    flat_cot = cotangent.reshape(groups * row_count, embedding_width)
    output_gradient = jnp.where(live_token_rows, flat_cot, jnp.zeros((), flat_cot.dtype))
    grad_mixed = matmul(output_gradient, w_out)
    slope = (
        0.5 * (1.0 + lax.erf(gate_projection * 0.7071067811865476))
        + gate_projection * jnp.exp(-0.5 * gate_projection * gate_projection) * 0.3989422804014327
    )
    grad_inner = jnp.concatenate(
        [grad_mixed * up_projection * slope, grad_mixed * activation_output], axis=1
    ).astype(jnp.bfloat16)
    feedforward_normed_gradient = matmul_right_t(grad_inner, w_in)
    hidden_gradient = output_gradient.astype(jnp.float32) + norm_backward_pass(
        feedforward_normed_gradient,
        feedforward_norm_gain,
        feedforward_standardized,
        feedforward_inverse_norm,
    )
    grad_hidden_low = hidden_gradient.astype(jnp.bfloat16)
    grad_attended = matmul_right_t(grad_hidden_low, w_attn_out).astype(jnp.bfloat16)
    grad_attended = grad_attended.reshape(groups, row_count, head_count, HEAD_DIM)
    grad_query, grad_key, grad_value = jax.vmap(attend_back)(
        rotated_query,
        rotated_key,
        value_reduced_precision,
        sequence_segment,
        logarithm_totals,
        grad_attended,
    )
    grad_query = grad_query * HEAD_DIM ** (-0.5)
    grad_query = grad_query * cosine_table + rotate_back(grad_query * sine_table)
    grad_key = grad_key * cosine_table + rotate_back(grad_key * sine_table)
    grad_packed = jnp.stack([grad_query, grad_key, grad_value], axis=2)
    grad_packed = grad_packed.reshape(groups * row_count, 3 * embedding_width).astype(jnp.bfloat16)
    attention_normed_gradient = matmul_right_t(grad_packed, w_qkv)
    block_input_gradient = hidden_gradient + norm_backward_pass(
        attention_normed_gradient,
        attention_norm_gain,
        attention_standardized,
        attention_inverse_norm,
    )
    factors = (
        attention_normed_input,
        grad_packed,
        attention_rows_flat,
        grad_hidden_low,
        feedforward_normed_input,
        grad_inner,
        output_gradient,
        mixed_input,
        attention_normed_gradient,
        attention_standardized,
        feedforward_normed_gradient,
        feedforward_standardized,
    )
    return (block_input_gradient, factors)


def local_plain(
    tokens,
    seq_lengths,
    cotangent,
    attention_norm_gain,
    w_qkv,
    w_attn_out,
    feedforward_norm_gain,
    w_in,
    w_out,
):
    row_count, embedding_width = tokens.shape
    gathered = (
        lax.all_gather(attention_norm_gain, ("fsdp", "rep"), axis=0, tiled=True),
        lax.all_gather(w_qkv, ("fsdp", "rep"), axis=0, tiled=True),
        lax.all_gather(w_attn_out, ("fsdp", "rep"), axis=0, tiled=True),
        lax.all_gather(feedforward_norm_gain, ("fsdp", "rep"), axis=0, tiled=True),
        lax.all_gather(w_in, ("fsdp", "rep"), axis=0, tiled=True),
        lax.all_gather(w_out, ("fsdp", "rep"), axis=0, tiled=True),
    )
    output, saved_residuals = forward(
        tokens.reshape(1, row_count, embedding_width),
        seq_lengths,
        gathered[0],
        gathered[1],
        gathered[2],
        gathered[3],
        gathered[4],
        gathered[5],
    )
    second_copy = (
        lax.all_gather(attention_norm_gain, ("fsdp", "rep"), axis=0, tiled=True),
        lax.all_gather(w_qkv, ("fsdp", "rep"), axis=0, tiled=True),
        lax.all_gather(w_attn_out, ("fsdp", "rep"), axis=0, tiled=True),
        lax.all_gather(feedforward_norm_gain, ("fsdp", "rep"), axis=0, tiled=True),
        lax.all_gather(w_in, ("fsdp", "rep"), axis=0, tiled=True),
        lax.all_gather(w_out, ("fsdp", "rep"), axis=0, tiled=True),
    )
    block_input_gradient, factors = backward(
        saved_residuals,
        cotangent.reshape(1, row_count, embedding_width),
        second_copy[0],
        second_copy[1],
        second_copy[2],
        second_copy[3],
        second_copy[4],
        second_copy[5],
    )
    (
        normed_attn,
        grad_packed,
        attended_rows,
        grad_hidden_low,
        normed_mlp,
        grad_inner,
        grad_out,
        mixed_input,
        grad_normed_attn,
        standard_attn,
        grad_normed_mlp,
        standard_mlp,
    ) = factors
    qkv_width = w_qkv.shape[1]
    attn_width = w_attn_out.shape[1]
    inner_width = w_in.shape[1]
    outer_width = w_out.shape[1]
    qkv_term = matmul_left_t(normed_attn, grad_packed)
    attn_term = matmul_left_t(attended_rows, grad_hidden_low)
    inner_term = matmul_left_t(normed_mlp, grad_inner)
    outer_term = matmul_left_t(grad_out, mixed_input)
    attn_gain_term = jnp.sum(grad_normed_attn * standard_attn, axis=0)
    mlp_gain_term = jnp.sum(grad_normed_mlp * standard_mlp, axis=0)
    summed = lax.psum_scatter(
        jnp.concatenate(
            [
                qkv_term,
                attn_term,
                inner_term,
                outer_term,
                attn_gain_term[:, None],
                mlp_gain_term[:, None],
            ],
            axis=1,
        ),
        ("fsdp", "rep"),
        scatter_dimension=0,
        tiled=True,
    )
    edge_two = qkv_width + attn_width
    edge_three = edge_two + inner_width
    edge_four = edge_three + outer_width
    return (
        output,
        block_input_gradient,
        summed[:, edge_four],
        summed[:, :qkv_width],
        summed[:, qkv_width:edge_two],
        summed[:, edge_four + 1],
        summed[:, edge_two:edge_three],
        summed[:, edge_three:edge_four],
    )


AXES = ("fsdp", "rep")
LANES = 128
HALF = HEAD_DIM // 2


def tie(*values):
    return lax.optimization_barrier(values)


def wide(value):
    return value.astype(jnp.float32)


def low(value):
    return value.astype(jnp.bfloat16)


def split_columns(value, count):
    width = value.shape[1] // count
    return [value[:, k * width : (k + 1) * width] for k in range(count)]


def split_rows(value, count):
    width = value.shape[0] // count
    return [value[k * width : (k + 1) * width] for k in range(count)]


def columns(blocks):
    return jnp.concatenate(blocks, axis=1)


def rows(blocks):
    return jnp.concatenate(blocks, axis=0)


def swap(value, distance):
    return lax.ppermute(value, "rep", [(k, k ^ distance) for k in range(4)])


def rep_exchange(value):
    blocks = value.reshape(4, value.shape[0] // 4, value.shape[1])
    return lax.all_to_all(blocks, "rep", 0, 0, tiled=True).reshape(value.shape)


def up(value):
    return lax.ppermute(value, "fsdp", [(k, (k + 2) % 8) for k in range(8)])


def down(value):
    return lax.ppermute(value, "fsdp", [(k, (k - 2) % 8) for k in range(8)])


def over(value):
    return lax.ppermute(value, "fsdp", [(k, k ^ 1) for k in range(8)])


def relative(value, z, x):
    blocks = split_columns(value, 8)
    blocks = [jnp.where(x == 1, blocks[k ^ 1], blocks[k]) for k in range(8)]
    for bit in (1, 2):
        turn = (z & bit) != 0
        blocks = [jnp.where(turn, blocks[(k + 2 * bit) % 8], blocks[k]) for k in range(8)]
    return columns([blocks[2 * ((p + 1) % 4) + i] for i in range(2) for p in range(4)])


def absolute(value, z, x):
    blocks = split_columns(value, 8)
    blocks = [blocks[4 * i + (j - 1) % 4] for j in range(4) for i in range(2)]
    blocks = [jnp.where(x == 1, blocks[k ^ 1], blocks[k]) for k in range(8)]
    for bit in (1, 2):
        turn = (z & bit) != 0
        blocks = [jnp.where(turn, blocks[(k - 2 * bit) % 8], blocks[k]) for k in range(8)]
    return columns(blocks)


def place_of(place, step, side):
    z, x = place[0], place[1]
    return 2 * lax.rem(z + step + 1, 4) + (x if side == 0 else 1 - x)


def block_of(place, z_at, side):
    z, x = place[0], place[1]
    return 4 * (x if side == 0 else 1 - x) + lax.rem(z_at - z + 7, 4)


def turned(value):
    width = value.shape[1]
    lane = lax.broadcasted_iota(jnp.int32, value.shape, 1)
    return jnp.where(
        lane % HEAD_DIM < HALF,
        pltpu.roll(value, width - HALF, 1),
        pltpu.roll(value, HALF, 1),
    )


def head_masks(row_count):
    lane = lax.broadcasted_iota(jnp.int32, (row_count, LANES), 1)
    return [low(wide(lane < HEAD_DIM)), low(wide(lane >= HEAD_DIM))], lane < HEAD_DIM


def token_rows(mine, across, beside, first, step):
    count = 128
    return [
        mine[first : first + count],
        beside[first : first + count],
        across[first : first + count],
        beside[step + first : step + first + count],
    ]


def attention_forward(
    place, seg_col, seg_row, cosine, sine, mine, across, beside,
    first, second, third, own, others, other_second, other,
    normed, qkv, attn, query, key, value, probs, attended, send, keep,
):
    size = own.shape[0]
    blocks = [
        (first, 0), (second, 0), (third, 0), (own, 0),
        (others, 0), (other_second, 0), (others, size), (other, 0),
    ]
    part = size // 4
    for at, (ref, row) in enumerate(blocks):
        qkv[size * at : size * (at + 1), :] = ref[row : row + size, :768]
        target = pl.multiple_of(place_of(place, at % 4, at // 4) * part, part)
        for z_at in range(4):
            for side in range(2):
                lanes = pl.multiple_of(block_of(place, z_at, side) * LANES, LANES)
                attn[pl.ds(target, part), pl.ds(lanes, LANES)] = ref[
                    row + part * z_at : row + part * (z_at + 1),
                    768 + LANES * side : 768 + LANES * (side + 1),
                ]
    count = 128
    for at, ref in enumerate(token_rows(mine, across, beside, 0, mine.shape[0])):
        values = wide(ref)
        centred = values - jnp.mean(values, axis=1, keepdims=True)
        inverse = lax.rsqrt(jnp.mean(centred * centred, axis=1, keepdims=True) + norm_eps)
        normed[count * at : count * (at + 1), :] = low(centred * inverse)
    packed = matmul(normed[...], qkv[...])
    cos_all, sin_all = columns([cosine[...]] * 2), columns([sine[...]] * 2)
    raw = packed[:, :256]
    query[...] = low((raw * cos_all + turned(raw) * sin_all) * HEAD_DIM ** (-0.5))
    raw = packed[:, 256:512]
    key[...] = low(raw * cos_all + turned(raw) * sin_all)
    value[...] = low(packed[:, 512:])
    masks, is_first = head_masks(count)
    for at in range(4):
        here = slice(count * at, count * (at + 1))
        allowed = seg_col[here, :] == seg_row[at : at + 1, :]
        for pair in range(2):
            lanes = slice(LANES * pair, LANES * (pair + 1))
            made = []
            for head in range(2):
                scores = matmul_right_t(query[here, lanes] * masks[head], key[here, lanes])
                scores = jnp.where(allowed, scores, -jnp.inf)
                powers = jnp.exp(scores - jnp.max(scores, axis=1, keepdims=True))
                weights = powers / jnp.sum(powers, axis=1, keepdims=True)
                slot = count * (4 * at + 2 * pair + head)
                probs[slot : slot + count, :] = weights
                made.append(matmul(low(weights), value[here, lanes]))
            attended[here, lanes] = low(jnp.where(is_first, made[0], made[1]))
    total = low(matmul(attended[...], attn[...]))
    keep[:count, :], send[:count, :] = total[:count], total[count : 2 * count]
    keep[count:, :], send[count:, :] = total[2 * count : 3 * count], total[3 * count :]


def mlp(
    seg_col, norm_own, norm_across, norm_beside, mine, across, beside,
    first, second, third, own, other_first, other_second, other_third, other,
    normed, grad_out, mixed, grad_inner, send, keep, w_down,
    w_up, inner, grad_mixed,
):
    size, count, edge = own.shape[0], 128, w_up.shape[1]
    blocks = (first, second, third, own, other_first, other_second, other_third, other)
    for at, ref in enumerate(blocks):
        w_up[size * at : size * (at + 1), :] = ref[:, :edge]
        w_down[size * at : size * (at + 1), :] = ref[:, edge:]
    for at, ref in enumerate(
        (norm_own[...], norm_beside[:count, :], norm_across[...], norm_beside[count:, :])
    ):
        normed[count * at : count * (at + 1), :] = ref
    for at, ref in enumerate(token_rows(mine, across, beside, count, mine.shape[0])):
        live = wide(seg_col[count * at : count * (at + 1), :] < 8)
        grad_out[count * at : count * (at + 1), :] = low(wide(ref) * live)
    inner[...] = matmul(normed[...], w_up[...])
    grad_mixed[...] = matmul(grad_out[...], w_down[...])
    main = (w_down.shape[1] // LANES - 1) * LANES
    rest = 16

    def parts(gate):
        phi = 0.5 * (1.0 + lax.erf(gate * 0.7071067811865476))
        slope = phi + gate * jnp.exp(-0.5 * gate * gate) * 0.3989422804014327
        return gate * phi, slope

    @pl.loop(0, 8)
    def _(step):
        here = pl.ds(pl.multiple_of(step * 64, 64), 64)
        gate, up_part = inner[here, :main], inner[here, main : 2 * main]
        grad = grad_mixed[here, :main]
        activation, slope = parts(gate)
        mixed[here, :main] = low(activation * up_part)
        grad_inner[here, :main] = low(grad * up_part * slope)
        grad_inner[here, main : 2 * main] = low(grad * activation)
        tail = inner[here, 2 * main :]
        grad = grad_mixed[here, main:]
        activation, slope = parts(tail)
        tail_up = pltpu.roll(tail, LANES - rest, 1)
        mixed[here, main:] = low(activation * tail_up)
        grad_inner[here, 2 * main :] = low(
            grad * tail_up * slope + pltpu.roll(grad * activation, rest, 1)
        )

    total = low(matmul_right_t(grad_inner[...], w_up[...]))
    keep[:count, :], send[:count, :] = total[:count], total[count : 2 * count]
    keep[count:, :], send[count:, :] = total[2 * count : 3 * count], total[3 * count :]


def place_term(term, keep, pair, near, far, lanes):
    size = term.shape[0] // 8
    for at, (ref, row) in enumerate(
        [(keep, 0), (pair, 0), (keep, 1), (keep, 2), (near, 0), (pair, 1), (far, 0), (far, 1)]
    ):
        ref[size * row : size * (row + 1), lanes] = term[size * at : size * (at + 1)]


def mlp_terms(normed, grad_inner, grad_out, mixed, keep, pair, near, far):
    edge = grad_inner.shape[1]
    term = low(matmul_left_t(normed[...], grad_inner[...]))
    place_term(term, keep, pair, near, far, slice(0, edge))
    term = low(matmul_left_t(grad_out[...], mixed[...]))
    place_term(term, keep, pair, near, far, slice(edge, edge + mixed.shape[1]))


def attention_backward(
    place, cosine, sine, low_own, low_across, low_beside, attn, query, key, value, probs,
    attended, normed,
    grad_packed, keep, pair, near, far, grad_low, grad_attended, term_attn,
):
    count = 128
    for at, ref in enumerate(
        (low_own[...], low_beside[:count, :], low_across[...], low_beside[count:, :])
    ):
        grad_low[count * at : count * (at + 1), :] = ref
    grad_attended[...] = low(matmul_right_t(grad_low[...], attn[...]))
    masks, is_first = head_masks(count)
    for at in range(4):
        here = slice(count * at, count * (at + 1))
        cos, sin = cosine[here, :], sine[here, :]
        for half in range(2):
            lanes = slice(LANES * half, LANES * (half + 1))
            q, k, v = query[here, lanes], key[here, lanes], value[here, lanes]
            grad = grad_attended[here, lanes]
            made = []
            for head in range(2):
                slot = count * (4 * at + 2 * half + head)
                weights = probs[slot : slot + count, :]
                grad_value = matmul_left_t(low(weights), grad)
                grad_probs = matmul_right_t(grad * masks[head], v)
                delta = jnp.sum(weights * grad_probs, axis=1, keepdims=True)
                grad_scores = low(weights * (grad_probs - delta))
                made.append((matmul(grad_scores, k), matmul_left_t(grad_scores, q), grad_value))
            grad_q, grad_k, grad_v = (jnp.where(is_first, *both) for both in zip(*made))
            grad_q = grad_q * HEAD_DIM ** (-0.5)
            grad_packed[here, lanes] = low(grad_q * cos - turned(grad_q) * sin)
            lanes = slice(256 + LANES * half, 256 + LANES * (half + 1))
            grad_packed[here, lanes] = low(grad_k * cos - turned(grad_k) * sin)
            lanes = slice(512 + LANES * half, 512 + LANES * (half + 1))
            grad_packed[here, lanes] = low(grad_v)
    term = low(matmul_left_t(normed[...], grad_packed[...]))
    place_term(term, keep, pair, near, far, slice(0, 768))
    term_attn[...] = low(matmul_left_t(attended[...], grad_low[...]))
    size = term.shape[0] // 8
    part = size // 4
    targets = [
        (keep, 0), (pair, 0), (keep, size), (keep, 2 * size),
        (near, 0), (pair, size), (far, 0), (far, size),
    ]
    for at, (ref, row) in enumerate(targets):
        source = pl.multiple_of(place_of(place, at % 4, at // 4) * part, part)
        for z_at in range(4):
            for side in range(2):
                lanes = pl.multiple_of(block_of(place, z_at, side) * LANES, LANES)
                ref[
                    row + part * z_at : row + part * (z_at + 1),
                    768 + LANES * side : 768 + LANES * (side + 1),
                ] = term_attn[pl.ds(source, part), pl.ds(lanes, LANES)]


def projections(grad_packed, qkv, mixed, w_down, send, keep):
    count = 128
    for row, total in (
        (0, low(matmul_right_t(grad_packed[...], qkv[...]))),
        (count, low(matmul_right_t(mixed[...], w_down[...]))),
    ):
        keep[row : row + count, :] = total[:count]
        send[row : row + count, :] = total[count : 2 * count]
        keep[2 * count + row : 3 * count + row, :] = total[2 * count : 3 * count]
        send[2 * count + row : 3 * count + row, :] = total[3 * count :]


def unpack_rest(back, w_in, gain, grad_in, gain_grad, grad_out):
    size, hidden, part = w_in.shape[0], w_in.shape[1] // 2, w_in.shape[1] // 8
    main = part // LANES * LANES
    rest, edge = part - main, 2 * main + LANES
    total = jnp.zeros(gain_grad.shape, jnp.float32)
    for k in range(4):
        here = slice(size * k, size * (k + 1))
        for half in range(2):
            base = hidden * half + part * k
            for source, target, count in (
                (main * half, base, main),
                (2 * main + rest * half, base + main, rest),
            ):
                piece = wide(back[here, source : source + count])
                grad_in[:, target : target + count] = piece * gain[...]
                weights = wide(w_in[:, target : target + count])
                total += jnp.sum(piece * weights, axis=1, keepdims=True)
        grad_out[:, part * k : part * (k + 1)] = wide(back[here, edge : edge + part])
    gain_grad[...] = total


def unpack_qkv(back, w_qkv, gain, grad, gain_grad):
    size, part = w_qkv.shape[0], 256
    edge = back.shape[1] - 3 * part
    total = jnp.zeros(gain_grad.shape, jnp.float32)
    for k in range(4):
        for third in range(3):
            source = slice(edge + part * third, edge + part * (third + 1))
            piece = wide(back[size * k : size * (k + 1), source])
            lanes = slice(part * (4 * third + k), part * (4 * third + k + 1))
            grad[:, lanes] = piece * gain[...]
            total += jnp.sum(piece * wide(w_qkv[:, lanes]), axis=1, keepdims=True)
    gain_grad[...] = total


def kernel(body, outs, cost, *args, scratch=(), scalars=0):
    flops, transcendentals = cost
    shapes = [jax.ShapeDtypeStruct(shape, kind) for shape, kind in outs]
    moved = sum(arg.size * arg.dtype.itemsize for arg in (*args, *shapes))
    return pl.pallas_call(
        body,
        out_shape=shapes,
        in_specs=[
            pl.BlockSpec(memory_space=pltpu.SMEM if k < scalars else pltpu.VMEM)
            for k in range(len(args))
        ],
        out_specs=[pl.BlockSpec(memory_space=pltpu.VMEM)] * len(shapes),
        scratch_shapes=[pltpu.VMEM(shape, kind) for shape, kind in scratch],
        compiler_params=pltpu.CompilerParams(vmem_limit_bytes=28 * 2**20),
        cost_estimate=pl.CostEstimate(
            flops=flops, bytes_accessed=moved, transcendentals=transcendentals
        ),
        name=body.__name__,
    )(*args)


def scatter_last(send, keep):
    beside = split_rows(swap(send, 1), 2)
    kept = split_rows(keep, 2)
    sent = low(wide(kept[1]) + wide(beside[1]))
    return wide(kept[0]) + wide(beside[0]), sent


def local_ring(
    tokens,
    seq_lengths,
    cotangent,
    attention_norm_gain,
    w_qkv,
    w_attn_out,
    feedforward_norm_gain,
    w_in,
    w_out,
):
    count, width = tokens.shape
    index = lax.axis_index("fsdp")
    z, x = index // 2, index % 2
    place = jnp.stack([z, x]).astype(jnp.int32)
    hidden = w_in.shape[1] // 2
    part = hidden // 4
    main = part // LANES * LANES
    in_width, out_width = 2 * main + LANES, main + LANES
    f32, b16 = jnp.float32, jnp.bfloat16
    group = 4 * count

    gain_attn = wide(attention_norm_gain)[:, None]
    gain_mlp = wide(feedforward_norm_gain)[:, None]
    order = [(k, (k % 8) * 4 + k // 8) for k in range(32)]
    attn_own = lax.ppermute(w_attn_out, AXES, order)
    qkv_parts = split_columns(low(wide(w_qkv) * gain_attn), 12)
    size = w_qkv.shape[0]
    slots = seq_lengths.shape[1]
    lengths_low = jnp.pad(low(wide(seq_lengths)), ((0, size - 1), (0, LANES - slots)))
    exchanged = rep_exchange(rows([columns([*qkv_parts[k::4], lengths_low]) for k in range(4)]))
    first_own = columns([exchanged[:, :768], rows(split_columns(attn_own, 4))])
    lengths = rows([exchanged[size * k : size * k + 1, 768 : 768 + slots] for k in range(4)])
    lengths = wide(lengths).astype(jnp.int32)
    for bit in (1, 2):
        turned_rows = rows([lengths[k ^ bit : (k ^ bit) + 1] for k in range(4)])
        lengths = jnp.where((lax.axis_index("rep") & bit) != 0, turned_rows, lengths)

    scaled_in = low(wide(w_in) * gain_mlp)
    pieces = []
    for k in range(4):
        gate = scaled_in[:, part * k : part * (k + 1)]
        up_part = scaled_in[:, hidden + part * k : hidden + part * (k + 1)]
        out_part = w_out[:, part * k : part * (k + 1)]
        fill = [jnp.zeros((w_in.shape[0], n), b16) for n in (in_width - 2 * part, out_width - part)]
        pieces.append(
            columns(
                [gate[:, :main], up_part[:, :main], gate[:, main:], up_part[:, main:], fill[0]]
                + [out_part, fill[1]]
            )
        )
    mine = rows([relative(tokens, z, x), relative(cotangent, z, x)])
    first_own, rest, mine = tie(first_own, rows(pieces), mine)
    rest = rep_exchange(rest)

    third, first, other = up(first_own), down(first_own), over(first_own)
    third, first, other, mine, rest = tie(third, first, other, mine, rest)
    across = swap(mine, 2)
    second, others, rest_third = up(third), over(rows([first, third])), up(rest)
    second, others, across = tie(second, others, across)
    other_second = over(second)
    rest_first = down(tie(rest, rest_third)[0])
    beside = swap(rows([mine, across]), 1)
    rest_other = over(tie(rest, other_second)[0])

    step = mine.shape[0]
    segment, positions, _ = jax.vmap(lambda row: layout(row, count))(lengths)
    frequency = rope_base ** (-(lax.iota(f32, HALF) * (2.0 / HEAD_DIM)))
    angles = positions.reshape(group, 1).astype(f32) * frequency
    cosine, sine = jnp.cos(angles), jnp.sin(angles)
    cosine, sine = columns([cosine] * 4), columns([-sine, sine] * 2)
    seg_col = segment.reshape(group, 1)

    normed, qkv, attn, query, key, value, probs, attended, send, keep = kernel(
        attention_forward,
        [((group, width), b16), ((width, 768), b16), ((256, width), b16)]
        + [((group, 256), b16)] * 3
        + [((16 * count, count), f32), ((group, 256), b16)]
        + [((2 * count, width), b16)] * 2,
        (2 * group * width * (768 + 256) + 4 * 16 * count * count * LANES, 16 * count * count),
        place, seg_col, segment, cosine, sine, mine, across, beside,
        first, second, third, first_own, others, other_second, other,
        scalars=1,
    )
    rest_third, rest_first, rest_other, send = tie(rest_third, rest_first, rest_other, send)
    rest_second, rest_other_third = up(rest_third), over(rest_third)
    x_own = wide(mine[:count])
    kept, sent = scatter_last(send, keep)
    rest_other_first = over(tie(rest_first, rest_other_third)[0])
    hidden_sum = x_own + kept + wide(swap(sent, 2))
    standard_mlp, inverse_mlp = norm_statistics(hidden_sum)
    norm_own = low(standard_mlp)
    norm_across = swap(norm_own, 2)
    rest_second, rest_other_third, _ = tie(rest_second, rest_other_third, norm_own)
    rest_other_second = up(rest_other_third)
    norm_beside = swap(rows([norm_own, norm_across]), 1)

    normed_mlp, grad_out, mixed, grad_inner, send, keep, w_down = kernel(
        mlp,
        [((group, width), b16)] * 2
        + [((group, out_width), b16), ((group, in_width), b16)]
        + [((2 * count, width), b16)] * 2
        + [((width, out_width), b16)],
        (2 * group * width * (2 * in_width + out_width), 3 * group * part),
        seg_col, norm_own, norm_across, norm_beside, mine, across, beside,
        rest_first, rest_second, rest_third, rest,
        rest_other_first, rest_other_second, rest_other_third, rest_other,
        scratch=[
            ((width, in_width), b16),
            ((group, in_width), f32),
            ((group, out_width), f32),
        ],
    )
    all_width = in_width + out_width
    size = width // 8
    io_keep, io_pair, io_near, io_far = kernel(
        mlp_terms,
        [((size * n, all_width), b16) for n in (3, 2, 1, 2)],
        (2 * group * width * all_width, 0),
        normed_mlp, grad_inner, grad_out, mixed,
    )
    io_pair, io_far = up(io_pair), over(io_far)
    kept, sent = scatter_last(send, keep)
    scaled_mlp = kept + wide(tie(swap(sent, 2), io_keep)[0])
    grad_hidden = wide(grad_out[:count]) + norm_backward_pass(
        scaled_mlp, jnp.ones((), f32), standard_mlp, inverse_mlp
    )
    low_own = low(grad_hidden)
    low_across = swap(low_own, 2)
    low_beside = swap(rows([low_own, low_across]), 1)

    grad_packed, g_keep, g_pair, g_near, g_far = kernel(
        attention_backward,
        [((group, 768), b16)] + [((size * n, width), b16) for n in (3, 2, 1, 2)],
        (2 * group * width * (768 + 512) + 10 * 16 * count * count * LANES, 0),
        place, cosine, sine, low_own, low_across, low_beside, attn, query, key, value, probs,
        attended, normed,
        scratch=[((group, width), b16), ((group, 256), b16), ((256, width), b16)],
        scalars=1,
    )
    g_pair, g_far = up(g_pair), over(g_far)
    io_pair, io_far, _ = tie(io_pair, io_far, g_near)
    io_kept, io_pair, io_far = split_rows(io_keep, 3), split_rows(io_pair, 2), split_rows(io_far, 2)
    io_near = over(low(wide(io_near) + wide(io_pair[1])))
    io_down = down(low(wide(io_kept[1]) + wide(io_far[0])))
    send, keep = kernel(
        projections,
        [((4 * count, width), b16)] * 2,
        (2 * group * width * (768 + out_width), 0),
        grad_packed, qkv, mixed, w_down,
    )
    io_near, io_down, g_pair, g_far, send = tie(io_near, io_down, g_pair, g_far, send)
    g_kept, g_pair, g_far = split_rows(g_keep, 3), split_rows(g_pair, 2), split_rows(g_far, 2)
    g_near = over(low(wide(g_near) + wide(g_pair[1])))
    g_down = down(low(wide(g_kept[1]) + wide(g_far[0])))
    kept, sent = scatter_last(send, keep)
    io_up = up(low(wide(io_kept[0]) + wide(io_pair[0]) + wide(io_near)))
    g_near, sent = tie(g_near, sent)
    g_up = up(low(wide(g_kept[0]) + wide(g_pair[0]) + wide(g_near)))
    last_across = swap(sent, 2)
    io_up, g_up, g_down = tie(io_up, g_up, g_down)
    sum_io = low(wide(io_kept[2]) + wide(io_far[1]) + wide(io_down) + wide(io_up))
    sum_g = low(wide(g_kept[2]) + wide(g_far[1]) + wide(g_down) + wide(g_up))
    back = rep_exchange(columns([sum_io, sum_g[:, :768]]))
    grad_w_attn_out = wide(
        lax.ppermute(
            columns(split_rows(sum_g[:, 768:], 4)),
            AXES,
            [(there, here) for here, there in order],
        )
    )
    grad_w_in, gain_in, grad_w_out = kernel(
        unpack_rest,
        [(w_in.shape, f32), (gain_mlp.shape, f32), (w_out.shape, f32)],
        (4 * w_in.size, 0),
        back, w_in, gain_mlp,
    )
    grad_w_qkv, gain_qkv = kernel(
        unpack_qkv,
        [(w_qkv.shape, f32), (gain_attn.shape, f32)],
        (4 * w_qkv.size, 0),
        back, w_qkv, gain_attn,
    )
    last = kept + wide(last_across)

    standard, inverse = norm_statistics(x_own)
    block_input_gradient = grad_hidden + norm_backward_pass(
        last[:count], jnp.ones((), f32), standard, inverse
    )
    output = low(jnp.where(seg_col[:count] < 8, hidden_sum + last[count:], 0.0))
    return (
        absolute(output, z, x),
        absolute(block_input_gradient, z, x),
        gain_qkv.reshape(-1),
        grad_w_qkv,
        grad_w_attn_out,
        gain_in.reshape(-1),
        grad_w_in,
        grad_w_out,
    )


def solution(mesh):
    ringed = dict(mesh.shape) == {"fsdp": 8, "rep": 4}
    return jax.shard_map(
        local_ring if ringed else local_plain,
        mesh=mesh,
        in_specs=(
            P(AXES, None),
            P(AXES, None),
            P(AXES, None),
            P(AXES),
            P(AXES, None),
            P(AXES, None),
            P(AXES),
            P(AXES, None),
            P(AXES, None),
        ),
        out_specs=(
            P(AXES, None),
            P(AXES, None),
            P(AXES),
            P(AXES, None),
            P(AXES, None),
            P(AXES),
            P(AXES, None),
            P(AXES, None),
        ),
        check_vma=False,
    )
```

```python
import jax
import jax.numpy as jnp
from jax import lax
from jax.experimental import pallas as pl
from jax.experimental.pallas import tpu as pltpu
from jax.sharding import PartitionSpec as P

HEAD_DIM = 64


norm_eps = 1e-05
rope_base = 160000.0


def matmul(left_side, right_side):
    return jnp.dot(left_side, right_side, preferred_element_type=jnp.float32)


def matmul_right_t(left_side, right_side):
    return lax.dot_general(
        left_side, right_side, (((1,), (1,)), ((), ())), preferred_element_type=jnp.float32
    )


def matmul_left_t(left_side, right_side):
    return lax.dot_general(
        left_side, right_side, (((0,), (0,)), ((), ())), preferred_element_type=jnp.float32
    )


def batched(form, left_side, right_side):
    return jnp.einsum(form, left_side, right_side, preferred_element_type=jnp.float32)


def layout(lengths, row_count):
    slot_ids = lax.iota(jnp.int32, lengths.shape[0])
    before = (slot_ids[:, None] <= slot_ids[None, :]).astype(jnp.int32)
    ends = jnp.sum(lengths[:, None] * before, axis=0)
    starts = ends - lengths
    places = lax.iota(jnp.int32, row_count)
    sequence_segment = jnp.sum((ends[None, :] <= places[:, None]).astype(jnp.int32), axis=1)
    first_row = jnp.sum(
        jnp.where(sequence_segment[:, None] == slot_ids[None, :], starts[None, :], 0), axis=1
    )
    return (sequence_segment, places - first_row, sequence_segment < lengths.shape[0])


def rotary(positions, head_size):
    half_size = head_size // 2
    frequency = rope_base ** (-(lax.iota(jnp.float32, half_size) * (2.0 / head_size)))
    angles = positions.astype(jnp.float32)[..., None] * frequency
    cosine_table = jnp.concatenate([jnp.cos(angles), jnp.cos(angles)], axis=-1)
    sine_table = jnp.concatenate([jnp.sin(angles), jnp.sin(angles)], axis=-1)
    return (cosine_table, sine_table)


def rotate_half(vector):
    half_size = vector.shape[-1] // 2
    return jnp.concatenate([-vector[..., half_size:], vector[..., :half_size]], axis=-1)


def rotate_back(vector):
    half_size = vector.shape[-1] // 2
    return jnp.concatenate([vector[..., half_size:], -vector[..., :half_size]], axis=-1)


def norm_statistics(values):
    average = jnp.mean(values, axis=-1, keepdims=True)
    centred = values - average
    inverse = lax.rsqrt(jnp.mean(centred * centred, axis=-1, keepdims=True) + norm_eps)
    return (centred * inverse, inverse)


def norm_backward_pass(grad_normed, gain_vec, normalized, inverse):
    scaled = grad_normed * gain_vec.astype(jnp.float32)
    return inverse * (
        scaled
        - jnp.mean(scaled, axis=-1, keepdims=True)
        - normalized * jnp.mean(scaled * normalized, axis=-1, keepdims=True)
    )


def attend(rotated_query, rotated_key, value_reduced_precision, sequence_segment):
    scores = batched("thd,shd->hts", rotated_query, rotated_key)
    allowed = sequence_segment[:, None] == sequence_segment[None, :]
    scores = jnp.where(allowed[None], scores, -jnp.inf)
    logarithm_totals = jax.nn.logsumexp(scores, axis=-1)
    weights = jnp.exp(scores - logarithm_totals[..., None]).astype(jnp.bfloat16)
    attended = batched("hts,shd->thd", weights, value_reduced_precision).astype(jnp.bfloat16)
    return (attended, logarithm_totals)


def attend_back(
    rotated_query,
    rotated_key,
    value_reduced_precision,
    sequence_segment,
    logarithm_totals,
    grad_attended,
):
    scores = batched("thd,shd->hts", rotated_query, rotated_key)
    allowed = sequence_segment[:, None] == sequence_segment[None, :]
    scores = jnp.where(allowed[None], scores, -jnp.inf)
    probs_full = jnp.exp(scores - logarithm_totals[..., None])
    weights = probs_full.astype(jnp.bfloat16)
    grad_value = batched("hts,thd->shd", weights, grad_attended)
    grad_probs = batched("thd,shd->hts", grad_attended, value_reduced_precision)
    row_delta = jnp.sum(probs_full * grad_probs, axis=-1, keepdims=True)
    grad_scores = (probs_full * (grad_probs - row_delta)).astype(jnp.bfloat16)
    grad_query = batched("hts,shd->thd", grad_scores, rotated_key)
    grad_key = batched("hts,thd->shd", grad_scores, rotated_query)
    return (grad_query, grad_key, grad_value)


def forward(
    tokens, lengths, attention_norm_gain, w_qkv, w_attn_out, feedforward_norm_gain, w_in, w_out
):
    groups, row_count, embedding_width = tokens.shape
    head_count = embedding_width // HEAD_DIM
    hidden_units = w_in.shape[1] // 2
    sequence_segment, positions, valid = jax.vmap(
        lambda row_lengths: layout(row_lengths, row_count)
    )(lengths)
    cosine_table, sine_table = rotary(positions, HEAD_DIM)
    cosine_table = cosine_table[:, :, None, :]
    sine_table = sine_table[:, :, None, :]
    residual_input = tokens.reshape(groups * row_count, embedding_width).astype(jnp.float32)
    attention_standardized, attention_inverse_norm = norm_statistics(residual_input)
    attention_normed_input = (
        attention_standardized * attention_norm_gain.astype(jnp.float32)
    ).astype(jnp.bfloat16)
    packed = matmul(attention_normed_input, w_qkv).reshape(
        groups, row_count, 3, head_count, HEAD_DIM
    )
    query_raw = packed[:, :, 0]
    key_raw = packed[:, :, 1]
    rotated_query = (
        (query_raw * cosine_table + rotate_half(query_raw) * sine_table) * HEAD_DIM ** (-0.5)
    ).astype(jnp.bfloat16)
    rotated_key = (key_raw * cosine_table + rotate_half(key_raw) * sine_table).astype(jnp.bfloat16)
    value_reduced_precision = packed[:, :, 2].astype(jnp.bfloat16)
    attended, logarithm_totals = jax.vmap(attend)(
        rotated_query, rotated_key, value_reduced_precision, sequence_segment
    )
    attention_rows_flat = attended.reshape(groups * row_count, embedding_width)
    hidden_residual = residual_input + matmul(attention_rows_flat, w_attn_out)
    feedforward_standardized, feedforward_inverse_norm = norm_statistics(hidden_residual)
    feedforward_normed_input = (
        feedforward_standardized * feedforward_norm_gain.astype(jnp.float32)
    ).astype(jnp.bfloat16)
    inner_proj = matmul(feedforward_normed_input, w_in)
    gate_projection = inner_proj[:, :hidden_units]
    up_projection = inner_proj[:, hidden_units:]
    activation_output = jax.nn.gelu(gate_projection, approximate=False)
    mixed_input = (activation_output * up_projection).astype(jnp.bfloat16)
    live_token_rows = valid.reshape(groups * row_count, 1)
    mlp_result = matmul_right_t(mixed_input, w_out)
    output = jnp.where(live_token_rows, hidden_residual + mlp_result, 0.0).astype(jnp.bfloat16)
    saved_residuals = (
        sequence_segment,
        live_token_rows,
        cosine_table,
        sine_table,
        attention_standardized,
        attention_inverse_norm,
        attention_normed_input,
        rotated_query,
        rotated_key,
        value_reduced_precision,
        logarithm_totals,
        attention_rows_flat,
        feedforward_standardized,
        feedforward_inverse_norm,
        feedforward_normed_input,
        gate_projection,
        up_projection,
        activation_output,
        mixed_input,
    )
    return (output, saved_residuals)


def backward(
    saved_residuals,
    cotangent,
    attention_norm_gain,
    w_qkv,
    w_attn_out,
    feedforward_norm_gain,
    w_in,
    w_out,
):
    (
        sequence_segment,
        live_token_rows,
        cosine_table,
        sine_table,
        attention_standardized,
        attention_inverse_norm,
        attention_normed_input,
        rotated_query,
        rotated_key,
        value_reduced_precision,
        logarithm_totals,
        attention_rows_flat,
        feedforward_standardized,
        feedforward_inverse_norm,
        feedforward_normed_input,
        gate_projection,
        up_projection,
        activation_output,
        mixed_input,
    ) = saved_residuals
    groups, row_count = sequence_segment.shape
    embedding_width = attention_standardized.shape[1]
    head_count = embedding_width // HEAD_DIM
    flat_cot = cotangent.reshape(groups * row_count, embedding_width)
    output_gradient = jnp.where(live_token_rows, flat_cot, jnp.zeros((), flat_cot.dtype))
    grad_mixed = matmul(output_gradient, w_out)
    slope = (
        0.5 * (1.0 + lax.erf(gate_projection * 0.7071067811865476))
        + gate_projection * jnp.exp(-0.5 * gate_projection * gate_projection) * 0.3989422804014327
    )
    grad_inner = jnp.concatenate(
        [grad_mixed * up_projection * slope, grad_mixed * activation_output], axis=1
    ).astype(jnp.bfloat16)
    feedforward_normed_gradient = matmul_right_t(grad_inner, w_in)
    hidden_gradient = output_gradient.astype(jnp.float32) + norm_backward_pass(
        feedforward_normed_gradient,
        feedforward_norm_gain,
        feedforward_standardized,
        feedforward_inverse_norm,
    )
    grad_hidden_low = hidden_gradient.astype(jnp.bfloat16)
    grad_attended = matmul_right_t(grad_hidden_low, w_attn_out).astype(jnp.bfloat16)
    grad_attended = grad_attended.reshape(groups, row_count, head_count, HEAD_DIM)
    grad_query, grad_key, grad_value = jax.vmap(attend_back)(
        rotated_query,
        rotated_key,
        value_reduced_precision,
        sequence_segment,
        logarithm_totals,
        grad_attended,
    )
    grad_query = grad_query * HEAD_DIM ** (-0.5)
    grad_query = grad_query * cosine_table + rotate_back(grad_query * sine_table)
    grad_key = grad_key * cosine_table + rotate_back(grad_key * sine_table)
    grad_packed = jnp.stack([grad_query, grad_key, grad_value], axis=2)
    grad_packed = grad_packed.reshape(groups * row_count, 3 * embedding_width).astype(jnp.bfloat16)
    attention_normed_gradient = matmul_right_t(grad_packed, w_qkv)
    block_input_gradient = hidden_gradient + norm_backward_pass(
        attention_normed_gradient,
        attention_norm_gain,
        attention_standardized,
        attention_inverse_norm,
    )
    factors = (
        attention_normed_input,
        grad_packed,
        attention_rows_flat,
        grad_hidden_low,
        feedforward_normed_input,
        grad_inner,
        output_gradient,
        mixed_input,
        attention_normed_gradient,
        attention_standardized,
        feedforward_normed_gradient,
        feedforward_standardized,
    )
    return (block_input_gradient, factors)


def local_plain(
    tokens,
    seq_lengths,
    cotangent,
    attention_norm_gain,
    w_qkv,
    w_attn_out,
    feedforward_norm_gain,
    w_in,
    w_out,
):
    row_count, embedding_width = tokens.shape
    gathered = (
        lax.all_gather(attention_norm_gain, ("fsdp", "rep"), axis=0, tiled=True),
        lax.all_gather(w_qkv, ("fsdp", "rep"), axis=0, tiled=True),
        lax.all_gather(w_attn_out, ("fsdp", "rep"), axis=0, tiled=True),
        lax.all_gather(feedforward_norm_gain, ("fsdp", "rep"), axis=0, tiled=True),
        lax.all_gather(w_in, ("fsdp", "rep"), axis=0, tiled=True),
        lax.all_gather(w_out, ("fsdp", "rep"), axis=0, tiled=True),
    )
    output, saved_residuals = forward(
        tokens.reshape(1, row_count, embedding_width),
        seq_lengths,
        gathered[0],
        gathered[1],
        gathered[2],
        gathered[3],
        gathered[4],
        gathered[5],
    )
    second_copy = (
        lax.all_gather(attention_norm_gain, ("fsdp", "rep"), axis=0, tiled=True),
        lax.all_gather(w_qkv, ("fsdp", "rep"), axis=0, tiled=True),
        lax.all_gather(w_attn_out, ("fsdp", "rep"), axis=0, tiled=True),
        lax.all_gather(feedforward_norm_gain, ("fsdp", "rep"), axis=0, tiled=True),
        lax.all_gather(w_in, ("fsdp", "rep"), axis=0, tiled=True),
        lax.all_gather(w_out, ("fsdp", "rep"), axis=0, tiled=True),
    )
    block_input_gradient, factors = backward(
        saved_residuals,
        cotangent.reshape(1, row_count, embedding_width),
        second_copy[0],
        second_copy[1],
        second_copy[2],
        second_copy[3],
        second_copy[4],
        second_copy[5],
    )
    (
        normed_attn,
        grad_packed,
        attended_rows,
        grad_hidden_low,
        normed_mlp,
        grad_inner,
        grad_out,
        mixed_input,
        grad_normed_attn,
        standard_attn,
        grad_normed_mlp,
        standard_mlp,
    ) = factors
    qkv_width = w_qkv.shape[1]
    attn_width = w_attn_out.shape[1]
    inner_width = w_in.shape[1]
    outer_width = w_out.shape[1]
    qkv_term = matmul_left_t(normed_attn, grad_packed)
    attn_term = matmul_left_t(attended_rows, grad_hidden_low)
    inner_term = matmul_left_t(normed_mlp, grad_inner)
    outer_term = matmul_left_t(grad_out, mixed_input)
    attn_gain_term = jnp.sum(grad_normed_attn * standard_attn, axis=0)
    mlp_gain_term = jnp.sum(grad_normed_mlp * standard_mlp, axis=0)
    summed = lax.psum_scatter(
        jnp.concatenate(
            [
                qkv_term,
                attn_term,
                inner_term,
                outer_term,
                attn_gain_term[:, None],
                mlp_gain_term[:, None],
            ],
            axis=1,
        ),
        ("fsdp", "rep"),
        scatter_dimension=0,
        tiled=True,
    )
    edge_two = qkv_width + attn_width
    edge_three = edge_two + inner_width
    edge_four = edge_three + outer_width
    return (
        output,
        block_input_gradient,
        summed[:, edge_four],
        summed[:, :qkv_width],
        summed[:, qkv_width:edge_two],
        summed[:, edge_four + 1],
        summed[:, edge_two:edge_three],
        summed[:, edge_three:edge_four],
    )


AXES = ("fsdp", "rep")
LANES = 128
HALF = HEAD_DIM // 2


def tie(*values):
    return lax.optimization_barrier(values)


def wide(value):
    return value.astype(jnp.float32)


def low(value):
    return value.astype(jnp.bfloat16)


def split_columns(value, count):
    width = value.shape[1] // count
    return [value[:, k * width : (k + 1) * width] for k in range(count)]


def split_rows(value, count):
    width = value.shape[0] // count
    return [value[k * width : (k + 1) * width] for k in range(count)]


def columns(blocks):
    return jnp.concatenate(blocks, axis=1)


def rows(blocks):
    return jnp.concatenate(blocks, axis=0)


def swap(value, distance):
    return lax.ppermute(value, "rep", [(k, k ^ distance) for k in range(4)])


def rep_exchange(value):
    blocks = value.reshape(4, value.shape[0] // 4, value.shape[1])
    return lax.all_to_all(blocks, "rep", 0, 0, tiled=True).reshape(value.shape)


def up(value):
    return lax.ppermute(value, "fsdp", [(k, (k + 2) % 8) for k in range(8)])


def down(value):
    return lax.ppermute(value, "fsdp", [(k, (k - 2) % 8) for k in range(8)])


def over(value):
    return lax.ppermute(value, "fsdp", [(k, k ^ 1) for k in range(8)])


def relative(value, z, x):
    blocks = split_columns(value, 8)
    blocks = [jnp.where(x == 1, blocks[k ^ 1], blocks[k]) for k in range(8)]
    for bit in (1, 2):
        turn = (z & bit) != 0
        blocks = [jnp.where(turn, blocks[(k + 2 * bit) % 8], blocks[k]) for k in range(8)]
    return columns([blocks[2 * ((p + 1) % 4) + i] for i in range(2) for p in range(4)])


def absolute(value, z, x):
    blocks = split_columns(value, 8)
    blocks = [blocks[4 * i + (j - 1) % 4] for j in range(4) for i in range(2)]
    blocks = [jnp.where(x == 1, blocks[k ^ 1], blocks[k]) for k in range(8)]
    for bit in (1, 2):
        turn = (z & bit) != 0
        blocks = [jnp.where(turn, blocks[(k - 2 * bit) % 8], blocks[k]) for k in range(8)]
    return columns(blocks)


def place_of(place, step, side):
    z, x = place[0], place[1]
    return 2 * lax.rem(z + step + 1, 4) + (x if side == 0 else 1 - x)


def block_of(place, z_at, side):
    z, x = place[0], place[1]
    return 4 * (x if side == 0 else 1 - x) + lax.rem(z_at - z + 7, 4)


def turned(value):
    width = value.shape[1]
    lane = lax.broadcasted_iota(jnp.int32, value.shape, 1)
    return jnp.where(
        lane % HEAD_DIM < HALF,
        pltpu.roll(value, width - HALF, 1),
        pltpu.roll(value, HALF, 1),
    )


def head_masks(row_count):
    lane = lax.broadcasted_iota(jnp.int32, (row_count, LANES), 1)
    return [low(wide(lane < HEAD_DIM)), low(wide(lane >= HEAD_DIM))], lane < HEAD_DIM


def token_rows(mine, across, beside, first, step):
    count = 128
    return [
        mine[first : first + count],
        beside[first : first + count],
        across[first : first + count],
        beside[step + first : step + first + count],
    ]


def attention_forward(
    place, seg_col, seg_row, cosine, sine, mine, across, beside,
    first, second, third, own, others, other_second, other,
    normed, qkv, attn, query, key, value, probs, attended, send, keep,
):
    size = own.shape[0]
    blocks = [
        (first, 0), (second, 0), (third, 0), (own, 0),
        (others, 0), (other_second, 0), (others, size), (other, 0),
    ]
    part = size // 4
    for at, (ref, row) in enumerate(blocks):
        qkv[size * at : size * (at + 1), :] = ref[row : row + size, :768]
        target = pl.multiple_of(place_of(place, at % 4, at // 4) * part, part)
        for z_at in range(4):
            for side in range(2):
                lanes = pl.multiple_of(block_of(place, z_at, side) * LANES, LANES)
                attn[pl.ds(target, part), pl.ds(lanes, LANES)] = ref[
                    row + part * z_at : row + part * (z_at + 1),
                    768 + LANES * side : 768 + LANES * (side + 1),
                ]
    count = 128
    for at, ref in enumerate(token_rows(mine, across, beside, 0, mine.shape[0])):
        values = wide(ref)
        centred = values - jnp.mean(values, axis=1, keepdims=True)
        inverse = lax.rsqrt(jnp.mean(centred * centred, axis=1, keepdims=True) + norm_eps)
        normed[count * at : count * (at + 1), :] = low(centred * inverse)
    packed = matmul(normed[...], qkv[...])
    cos_all, sin_all = columns([cosine[...]] * 2), columns([sine[...]] * 2)
    raw = packed[:, :256]
    query[...] = low((raw * cos_all + turned(raw) * sin_all) * HEAD_DIM ** (-0.5))
    raw = packed[:, 256:512]
    key[...] = low(raw * cos_all + turned(raw) * sin_all)
    value[...] = low(packed[:, 512:])
    masks, is_first = head_masks(count)
    for at in range(4):
        here = slice(count * at, count * (at + 1))
        allowed = seg_col[here, :] == seg_row[at : at + 1, :]
        for pair in range(2):
            lanes = slice(LANES * pair, LANES * (pair + 1))
            made = []
            for head in range(2):
                scores = matmul_right_t(query[here, lanes] * masks[head], key[here, lanes])
                scores = jnp.where(allowed, scores, -jnp.inf)
                powers = jnp.exp(scores - jnp.max(scores, axis=1, keepdims=True))
                weights = powers / jnp.sum(powers, axis=1, keepdims=True)
                slot = count * (4 * at + 2 * pair + head)
                probs[slot : slot + count, :] = weights
                made.append(matmul(low(weights), value[here, lanes]))
            attended[here, lanes] = low(jnp.where(is_first, made[0], made[1]))
    total = low(matmul(attended[...], attn[...]))
    keep[:count, :], send[:count, :] = total[:count], total[count : 2 * count]
    keep[count:, :], send[count:, :] = total[2 * count : 3 * count], total[3 * count :]


def mlp(
    seg_col, norm_own, norm_across, norm_beside, mine, across, beside,
    first, second, third, own, other_first, other_second, other_third, other,
    normed, grad_out, mixed, grad_inner, send, keep, w_down,
    w_up, inner, grad_mixed,
):
    size, count, edge = own.shape[0], 128, w_up.shape[1]
    blocks = (first, second, third, own, other_first, other_second, other_third, other)
    for at, ref in enumerate(blocks):
        w_up[size * at : size * (at + 1), :] = ref[:, :edge]
        w_down[size * at : size * (at + 1), :] = ref[:, edge:]
    for at, ref in enumerate(
        (norm_own[...], norm_beside[:count, :], norm_across[...], norm_beside[count:, :])
    ):
        normed[count * at : count * (at + 1), :] = ref
    for at, ref in enumerate(token_rows(mine, across, beside, count, mine.shape[0])):
        live = wide(seg_col[count * at : count * (at + 1), :] < 8)
        grad_out[count * at : count * (at + 1), :] = low(wide(ref) * live)
    inner[...] = matmul(normed[...], w_up[...])
    grad_mixed[...] = matmul(grad_out[...], w_down[...])
    main = (w_down.shape[1] // LANES - 1) * LANES
    rest = 16

    def parts(gate):
        phi = 0.5 * (1.0 + lax.erf(gate * 0.7071067811865476))
        slope = phi + gate * jnp.exp(-0.5 * gate * gate) * 0.3989422804014327
        return gate * phi, slope

    @pl.loop(0, 8)
    def _(step):
        here = pl.ds(pl.multiple_of(step * 64, 64), 64)
        gate, up_part = inner[here, :main], inner[here, main : 2 * main]
        grad = grad_mixed[here, :main]
        activation, slope = parts(gate)
        mixed[here, :main] = low(activation * up_part)
        grad_inner[here, :main] = low(grad * up_part * slope)
        grad_inner[here, main : 2 * main] = low(grad * activation)
        tail = inner[here, 2 * main :]
        grad = grad_mixed[here, main:]
        activation, slope = parts(tail)
        tail_up = pltpu.roll(tail, LANES - rest, 1)
        mixed[here, main:] = low(activation * tail_up)
        grad_inner[here, 2 * main :] = low(
            grad * tail_up * slope + pltpu.roll(grad * activation, rest, 1)
        )

    total = low(matmul_right_t(grad_inner[...], w_up[...]))
    keep[:count, :], send[:count, :] = total[:count], total[count : 2 * count]
    keep[count:, :], send[count:, :] = total[2 * count : 3 * count], total[3 * count :]


def place_term(term, keep, pair, near, far, lanes):
    size = term.shape[0] // 8
    for at, (ref, row) in enumerate(
        [(keep, 0), (pair, 0), (keep, 1), (keep, 2), (near, 0), (pair, 1), (far, 0), (far, 1)]
    ):
        ref[size * row : size * (row + 1), lanes] = term[size * at : size * (at + 1)]


def mlp_terms(normed, grad_inner, grad_out, mixed, keep, pair, near, far):
    edge = grad_inner.shape[1]
    term = low(matmul_left_t(normed[...], grad_inner[...]))
    place_term(term, keep, pair, near, far, slice(0, edge))
    term = low(matmul_left_t(grad_out[...], mixed[...]))
    place_term(term, keep, pair, near, far, slice(edge, edge + mixed.shape[1]))


def attention_backward(
    place, cosine, sine, low_own, low_across, low_beside, attn, query, key, value, probs,
    attended, normed,
    grad_packed, keep, pair, near, far, grad_low, grad_attended, term_attn,
):
    count = 128
    for at, ref in enumerate(
        (low_own[...], low_beside[:count, :], low_across[...], low_beside[count:, :])
    ):
        grad_low[count * at : count * (at + 1), :] = ref
    grad_attended[...] = low(matmul_right_t(grad_low[...], attn[...]))
    masks, is_first = head_masks(count)
    for at in range(4):
        here = slice(count * at, count * (at + 1))
        cos, sin = cosine[here, :], sine[here, :]
        for half in range(2):
            lanes = slice(LANES * half, LANES * (half + 1))
            q, k, v = query[here, lanes], key[here, lanes], value[here, lanes]
            grad = grad_attended[here, lanes]
            made = []
            for head in range(2):
                slot = count * (4 * at + 2 * half + head)
                weights = probs[slot : slot + count, :]
                grad_value = matmul_left_t(low(weights), grad)
                grad_probs = matmul_right_t(grad * masks[head], v)
                delta = jnp.sum(weights * grad_probs, axis=1, keepdims=True)
                grad_scores = low(weights * (grad_probs - delta))
                made.append((matmul(grad_scores, k), matmul_left_t(grad_scores, q), grad_value))
            grad_q, grad_k, grad_v = (jnp.where(is_first, *both) for both in zip(*made))
            grad_q = grad_q * HEAD_DIM ** (-0.5)
            grad_packed[here, lanes] = low(grad_q * cos - turned(grad_q) * sin)
            lanes = slice(256 + LANES * half, 256 + LANES * (half + 1))
            grad_packed[here, lanes] = low(grad_k * cos - turned(grad_k) * sin)
            lanes = slice(512 + LANES * half, 512 + LANES * (half + 1))
            grad_packed[here, lanes] = low(grad_v)
    term = low(matmul_left_t(normed[...], grad_packed[...]))
    place_term(term, keep, pair, near, far, slice(0, 768))
    term_attn[...] = low(matmul_left_t(attended[...], grad_low[...]))
    size = term.shape[0] // 8
    part = size // 4
    targets = [
        (keep, 0), (pair, 0), (keep, size), (keep, 2 * size),
        (near, 0), (pair, size), (far, 0), (far, size),
    ]
    for at, (ref, row) in enumerate(targets):
        source = pl.multiple_of(place_of(place, at % 4, at // 4) * part, part)
        for z_at in range(4):
            for side in range(2):
                lanes = pl.multiple_of(block_of(place, z_at, side) * LANES, LANES)
                ref[
                    row + part * z_at : row + part * (z_at + 1),
                    768 + LANES * side : 768 + LANES * (side + 1),
                ] = term_attn[pl.ds(source, part), pl.ds(lanes, LANES)]


def projections(grad_packed, qkv, mixed, w_down, send, keep):
    count = 128
    for row, total in (
        (0, low(matmul_right_t(grad_packed[...], qkv[...]))),
        (count, low(matmul_right_t(mixed[...], w_down[...]))),
    ):
        keep[row : row + count, :] = total[:count]
        send[row : row + count, :] = total[count : 2 * count]
        keep[2 * count + row : 3 * count + row, :] = total[2 * count : 3 * count]
        send[2 * count + row : 3 * count + row, :] = total[3 * count :]


def unpack_rest(back, w_in, gain, grad_in, gain_grad, grad_out):
    size, hidden, part = w_in.shape[0], w_in.shape[1] // 2, w_in.shape[1] // 8
    main = part // LANES * LANES
    rest, edge = part - main, 2 * main + LANES
    total = jnp.zeros(gain.shape, jnp.float32)
    for k in range(4):
        here = slice(size * k, size * (k + 1))
        for half in range(2):
            base = hidden * half + part * k
            for source, target, count in (
                (main * half, base, main),
                (2 * main + rest * half, base + main, rest),
            ):
                piece = wide(back[here, source : source + count])
                grad_in[:, target : target + count] = piece * gain[...]
                weights = wide(w_in[:, target : target + count])
                total += jnp.sum(piece * weights, axis=1, keepdims=True)
        grad_out[:, part * k : part * (k + 1)] = wide(back[here, edge : edge + part])
    gain_grad[...] = jnp.broadcast_to(total, (total.shape[0], LANES)).T[:1, :]


def unpack_qkv(back, w_qkv, gain, grad, gain_grad):
    size, part = w_qkv.shape[0], 256
    edge = back.shape[1] - 3 * part
    total = jnp.zeros(gain.shape, jnp.float32)
    for k in range(4):
        for third in range(3):
            source = slice(edge + part * third, edge + part * (third + 1))
            piece = wide(back[size * k : size * (k + 1), source])
            lanes = slice(part * (4 * third + k), part * (4 * third + k + 1))
            grad[:, lanes] = piece * gain[...]
            total += jnp.sum(piece * wide(w_qkv[:, lanes]), axis=1, keepdims=True)
    gain_grad[...] = jnp.broadcast_to(total, (total.shape[0], LANES)).T[:1, :]


def kernel(body, outs, cost, *args, scratch=(), scalars=0):
    flops, transcendentals = cost
    shapes = [jax.ShapeDtypeStruct(shape, kind) for shape, kind in outs]
    moved = sum(arg.size * arg.dtype.itemsize for arg in (*args, *shapes))
    return pl.pallas_call(
        body,
        out_shape=shapes,
        in_specs=[
            pl.BlockSpec(memory_space=pltpu.SMEM if k < scalars else pltpu.VMEM)
            for k in range(len(args))
        ],
        out_specs=[pl.BlockSpec(memory_space=pltpu.VMEM)] * len(shapes),
        scratch_shapes=[pltpu.VMEM(shape, kind) for shape, kind in scratch],
        compiler_params=pltpu.CompilerParams(vmem_limit_bytes=28 * 2**20),
        cost_estimate=pl.CostEstimate(
            flops=flops, bytes_accessed=moved, transcendentals=transcendentals
        ),
        name=body.__name__,
    )(*args)


def scatter_last(send, keep):
    beside = split_rows(swap(send, 1), 2)
    kept = split_rows(keep, 2)
    sent = low(wide(kept[1]) + wide(beside[1]))
    return wide(kept[0]) + wide(beside[0]), sent


def local_ring(
    tokens,
    seq_lengths,
    cotangent,
    attention_norm_gain,
    w_qkv,
    w_attn_out,
    feedforward_norm_gain,
    w_in,
    w_out,
):
    count, width = tokens.shape
    index = lax.axis_index("fsdp")
    z, x = index // 2, index % 2
    place = jnp.stack([z, x]).astype(jnp.int32)
    hidden = w_in.shape[1] // 2
    part = hidden // 4
    main = part // LANES * LANES
    in_width, out_width = 2 * main + LANES, main + LANES
    f32, b16 = jnp.float32, jnp.bfloat16
    group = 4 * count

    gain_attn = wide(attention_norm_gain)[:, None]
    gain_mlp = wide(feedforward_norm_gain)[:, None]
    order = [(k, (k % 8) * 4 + k // 8) for k in range(32)]
    attn_own = lax.ppermute(w_attn_out, AXES, order)
    qkv_parts = split_columns(low(wide(w_qkv) * gain_attn), 12)
    size = w_qkv.shape[0]
    slots = seq_lengths.shape[1]
    lengths_low = jnp.pad(low(wide(seq_lengths)), ((0, size - 1), (0, LANES - slots)))
    exchanged = rep_exchange(rows([columns([*qkv_parts[k::4], lengths_low]) for k in range(4)]))
    first_own = columns([exchanged[:, :768], rows(split_columns(attn_own, 4))])
    lengths = rows([exchanged[size * k : size * k + 1, 768 : 768 + slots] for k in range(4)])
    lengths = wide(lengths).astype(jnp.int32)
    for bit in (1, 2):
        turned_rows = rows([lengths[k ^ bit : (k ^ bit) + 1] for k in range(4)])
        lengths = jnp.where((lax.axis_index("rep") & bit) != 0, turned_rows, lengths)

    scaled_in = low(wide(w_in) * gain_mlp)
    pieces = []
    for k in range(4):
        gate = scaled_in[:, part * k : part * (k + 1)]
        up_part = scaled_in[:, hidden + part * k : hidden + part * (k + 1)]
        out_part = w_out[:, part * k : part * (k + 1)]
        fill = [jnp.zeros((w_in.shape[0], n), b16) for n in (in_width - 2 * part, out_width - part)]
        pieces.append(
            columns(
                [gate[:, :main], up_part[:, :main], gate[:, main:], up_part[:, main:], fill[0]]
                + [out_part, fill[1]]
            )
        )
    mine = rows([relative(tokens, z, x), relative(cotangent, z, x)])
    first_own, rest, mine = tie(first_own, rows(pieces), mine)
    rest = rep_exchange(rest)

    third, first, other = up(first_own), down(first_own), over(first_own)
    third, first, other, mine, rest = tie(third, first, other, mine, rest)
    across = swap(mine, 2)
    second, others, rest_third = up(third), over(rows([first, third])), up(rest)
    second, others, across = tie(second, others, across)
    other_second = over(second)
    rest_first = down(tie(rest, rest_third)[0])
    beside = swap(rows([mine, across]), 1)
    rest_other = over(tie(rest, other_second)[0])

    step = mine.shape[0]
    segment, positions, _ = jax.vmap(lambda row: layout(row, count))(lengths)
    frequency = rope_base ** (-(lax.iota(f32, HALF) * (2.0 / HEAD_DIM)))
    angles = positions.reshape(group, 1).astype(f32) * frequency
    cosine, sine = jnp.cos(angles), jnp.sin(angles)
    cosine, sine = columns([cosine] * 4), columns([-sine, sine] * 2)
    seg_col = segment.reshape(group, 1)

    normed, qkv, attn, query, key, value, probs, attended, send, keep = kernel(
        attention_forward,
        [((group, width), b16), ((width, 768), b16), ((256, width), b16)]
        + [((group, 256), b16)] * 3
        + [((16 * count, count), f32), ((group, 256), b16)]
        + [((2 * count, width), b16)] * 2,
        (2 * group * width * (768 + 256) + 4 * 16 * count * count * LANES, 16 * count * count),
        place, seg_col, segment, cosine, sine, mine, across, beside,
        first, second, third, first_own, others, other_second, other,
        scalars=1,
    )
    rest_third, rest_first, rest_other, send = tie(rest_third, rest_first, rest_other, send)
    rest_second, rest_other_third = up(rest_third), over(rest_third)
    x_own = wide(mine[:count])
    kept, sent = scatter_last(send, keep)
    rest_other_first = over(tie(rest_first, rest_other_third)[0])
    hidden_sum = x_own + kept + wide(swap(sent, 2))
    standard_mlp, inverse_mlp = norm_statistics(hidden_sum)
    norm_own = low(standard_mlp)
    norm_across = swap(norm_own, 2)
    rest_second, rest_other_third, _ = tie(rest_second, rest_other_third, norm_own)
    rest_other_second = up(rest_other_third)
    norm_beside = swap(rows([norm_own, norm_across]), 1)

    normed_mlp, grad_out, mixed, grad_inner, send, keep, w_down = kernel(
        mlp,
        [((group, width), b16)] * 2
        + [((group, out_width), b16), ((group, in_width), b16)]
        + [((2 * count, width), b16)] * 2
        + [((width, out_width), b16)],
        (2 * group * width * (2 * in_width + out_width), 3 * group * part),
        seg_col, norm_own, norm_across, norm_beside, mine, across, beside,
        rest_first, rest_second, rest_third, rest,
        rest_other_first, rest_other_second, rest_other_third, rest_other,
        scratch=[
            ((width, in_width), b16),
            ((group, in_width), f32),
            ((group, out_width), f32),
        ],
    )
    all_width = in_width + out_width
    size = width // 8
    io_keep, io_pair, io_near, io_far = kernel(
        mlp_terms,
        [((size * n, all_width), b16) for n in (3, 2, 1, 2)],
        (2 * group * width * all_width, 0),
        normed_mlp, grad_inner, grad_out, mixed,
    )
    io_pair, io_far = up(io_pair), over(io_far)
    kept, sent = scatter_last(send, keep)
    scaled_mlp = kept + wide(tie(swap(sent, 2), io_keep)[0])
    grad_hidden = wide(grad_out[:count]) + norm_backward_pass(
        scaled_mlp, jnp.ones((), f32), standard_mlp, inverse_mlp
    )
    low_own = low(grad_hidden)
    low_across = swap(low_own, 2)
    low_beside = swap(rows([low_own, low_across]), 1)

    grad_packed, g_keep, g_pair, g_near, g_far = kernel(
        attention_backward,
        [((group, 768), b16)] + [((size * n, width), b16) for n in (3, 2, 1, 2)],
        (2 * group * width * (768 + 512) + 10 * 16 * count * count * LANES, 0),
        place, cosine, sine, low_own, low_across, low_beside, attn, query, key, value, probs,
        attended, normed,
        scratch=[((group, width), b16), ((group, 256), b16), ((256, width), b16)],
        scalars=1,
    )
    g_pair, g_far = up(g_pair), over(g_far)
    io_pair, io_far, _ = tie(io_pair, io_far, g_near)
    io_kept, io_pair, io_far = split_rows(io_keep, 3), split_rows(io_pair, 2), split_rows(io_far, 2)
    io_near = over(low(wide(io_near) + wide(io_pair[1])))
    io_down = down(low(wide(io_kept[1]) + wide(io_far[0])))
    send, keep = kernel(
        projections,
        [((4 * count, width), b16)] * 2,
        (2 * group * width * (768 + out_width), 0),
        grad_packed, qkv, mixed, w_down,
    )
    io_near, io_down, g_pair, g_far, send = tie(io_near, io_down, g_pair, g_far, send)
    g_kept, g_pair, g_far = split_rows(g_keep, 3), split_rows(g_pair, 2), split_rows(g_far, 2)
    g_near = over(low(wide(g_near) + wide(g_pair[1])))
    g_down = down(low(wide(g_kept[1]) + wide(g_far[0])))
    kept, sent = scatter_last(send, keep)
    io_up = up(low(wide(io_kept[0]) + wide(io_pair[0]) + wide(io_near)))
    g_near, sent = tie(g_near, sent)
    g_up = up(low(wide(g_kept[0]) + wide(g_pair[0]) + wide(g_near)))
    last_across = swap(sent, 2)
    io_up, g_up, g_down = tie(io_up, g_up, g_down)
    sum_io = low(wide(io_kept[2]) + wide(io_far[1]) + wide(io_down) + wide(io_up))
    sum_g = low(wide(g_kept[2]) + wide(g_far[1]) + wide(g_down) + wide(g_up))
    back = rep_exchange(columns([sum_io, sum_g[:, :768]]))
    grad_w_in, gain_in, grad_w_out = kernel(
        unpack_rest,
        [(w_in.shape, f32), ((1, w_in.shape[0]), f32), (w_out.shape, f32)],
        (4 * w_in.size, 0),
        back, w_in, gain_mlp,
    )
    grad_w_qkv, gain_qkv = kernel(
        unpack_qkv,
        [(w_qkv.shape, f32), ((1, w_qkv.shape[0]), f32)],
        (4 * w_qkv.size, 0),
        back, w_qkv, gain_attn,
    )
    last = kept + wide(last_across)

    standard, inverse = norm_statistics(x_own)
    block_input_gradient = grad_hidden + norm_backward_pass(
        last[:count], jnp.ones((), f32), standard, inverse
    )
    output = low(jnp.where(seg_col[:count] < 8, hidden_sum + last[count:], 0.0))
    block_input_gradient = absolute(block_input_gradient, z, x)
    sum_attn, block_input_gradient = tie(sum_g[:, 768:], block_input_gradient)
    grad_w_attn_out = wide(
        lax.ppermute(
            columns(split_rows(sum_attn, 4)),
            AXES,
            [(there, here) for here, there in order],
        )
    )
    return (
        absolute(output, z, x),
        block_input_gradient,
        gain_qkv.reshape(-1),
        grad_w_qkv,
        grad_w_attn_out,
        gain_in.reshape(-1),
        grad_w_in,
        grad_w_out,
    )


def solution(mesh):
    ringed = dict(mesh.shape) == {"fsdp": 8, "rep": 4}
    return jax.shard_map(
        local_ring if ringed else local_plain,
        mesh=mesh,
        in_specs=(
            P(AXES, None),
            P(AXES, None),
            P(AXES, None),
            P(AXES),
            P(AXES, None),
            P(AXES, None),
            P(AXES),
            P(AXES, None),
            P(AXES, None),
        ),
        out_specs=(
            P(AXES, None),
            P(AXES, None),
            P(AXES),
            P(AXES, None),
            P(AXES, None),
            P(AXES),
            P(AXES, None),
            P(AXES, None),
        ),
        check_vma=False,
    )
```

```python
import jax
import jax.numpy as jnp
from jax import lax
from jax.experimental import pallas as pl
from jax.experimental.pallas import tpu as pltpu
from jax.sharding import PartitionSpec as P

HEAD_DIM = 64


norm_eps = 1e-05
rope_base = 160000.0


def matmul(left_side, right_side):
    return jnp.dot(left_side, right_side, preferred_element_type=jnp.float32)


def matmul_right_t(left_side, right_side):
    return lax.dot_general(
        left_side, right_side, (((1,), (1,)), ((), ())), preferred_element_type=jnp.float32
    )


def matmul_left_t(left_side, right_side):
    return lax.dot_general(
        left_side, right_side, (((0,), (0,)), ((), ())), preferred_element_type=jnp.float32
    )


def batched(form, left_side, right_side):
    return jnp.einsum(form, left_side, right_side, preferred_element_type=jnp.float32)


def layout(lengths, row_count):
    slot_ids = lax.iota(jnp.int32, lengths.shape[0])
    before = (slot_ids[:, None] <= slot_ids[None, :]).astype(jnp.int32)
    ends = jnp.sum(lengths[:, None] * before, axis=0)
    starts = ends - lengths
    places = lax.iota(jnp.int32, row_count)
    sequence_segment = jnp.sum((ends[None, :] <= places[:, None]).astype(jnp.int32), axis=1)
    first_row = jnp.sum(
        jnp.where(sequence_segment[:, None] == slot_ids[None, :], starts[None, :], 0), axis=1
    )
    return (sequence_segment, places - first_row, sequence_segment < lengths.shape[0])


def rotary(positions, head_size):
    half_size = head_size // 2
    frequency = rope_base ** (-(lax.iota(jnp.float32, half_size) * (2.0 / head_size)))
    angles = positions.astype(jnp.float32)[..., None] * frequency
    cosine_table = jnp.concatenate([jnp.cos(angles), jnp.cos(angles)], axis=-1)
    sine_table = jnp.concatenate([jnp.sin(angles), jnp.sin(angles)], axis=-1)
    return (cosine_table, sine_table)


def rotate_half(vector):
    half_size = vector.shape[-1] // 2
    return jnp.concatenate([-vector[..., half_size:], vector[..., :half_size]], axis=-1)


def rotate_back(vector):
    half_size = vector.shape[-1] // 2
    return jnp.concatenate([vector[..., half_size:], -vector[..., :half_size]], axis=-1)


def norm_statistics(values):
    average = jnp.mean(values, axis=-1, keepdims=True)
    centred = values - average
    inverse = lax.rsqrt(jnp.mean(centred * centred, axis=-1, keepdims=True) + norm_eps)
    return (centred * inverse, inverse)


def norm_backward_pass(grad_normed, gain_vec, normalized, inverse):
    scaled = grad_normed * gain_vec.astype(jnp.float32)
    return inverse * (
        scaled
        - jnp.mean(scaled, axis=-1, keepdims=True)
        - normalized * jnp.mean(scaled * normalized, axis=-1, keepdims=True)
    )


def attend(rotated_query, rotated_key, value_reduced_precision, sequence_segment):
    scores = batched("thd,shd->hts", rotated_query, rotated_key)
    allowed = sequence_segment[:, None] == sequence_segment[None, :]
    scores = jnp.where(allowed[None], scores, -jnp.inf)
    logarithm_totals = jax.nn.logsumexp(scores, axis=-1)
    weights = jnp.exp(scores - logarithm_totals[..., None]).astype(jnp.bfloat16)
    attended = batched("hts,shd->thd", weights, value_reduced_precision).astype(jnp.bfloat16)
    return (attended, logarithm_totals)


def attend_back(
    rotated_query,
    rotated_key,
    value_reduced_precision,
    sequence_segment,
    logarithm_totals,
    grad_attended,
):
    scores = batched("thd,shd->hts", rotated_query, rotated_key)
    allowed = sequence_segment[:, None] == sequence_segment[None, :]
    scores = jnp.where(allowed[None], scores, -jnp.inf)
    probs_full = jnp.exp(scores - logarithm_totals[..., None])
    weights = probs_full.astype(jnp.bfloat16)
    grad_value = batched("hts,thd->shd", weights, grad_attended)
    grad_probs = batched("thd,shd->hts", grad_attended, value_reduced_precision)
    row_delta = jnp.sum(probs_full * grad_probs, axis=-1, keepdims=True)
    grad_scores = (probs_full * (grad_probs - row_delta)).astype(jnp.bfloat16)
    grad_query = batched("hts,shd->thd", grad_scores, rotated_key)
    grad_key = batched("hts,thd->shd", grad_scores, rotated_query)
    return (grad_query, grad_key, grad_value)


def forward(
    tokens, lengths, attention_norm_gain, w_qkv, w_attn_out, feedforward_norm_gain, w_in, w_out
):
    groups, row_count, embedding_width = tokens.shape
    head_count = embedding_width // HEAD_DIM
    hidden_units = w_in.shape[1] // 2
    sequence_segment, positions, valid = jax.vmap(
        lambda row_lengths: layout(row_lengths, row_count)
    )(lengths)
    cosine_table, sine_table = rotary(positions, HEAD_DIM)
    cosine_table = cosine_table[:, :, None, :]
    sine_table = sine_table[:, :, None, :]
    residual_input = tokens.reshape(groups * row_count, embedding_width).astype(jnp.float32)
    attention_standardized, attention_inverse_norm = norm_statistics(residual_input)
    attention_normed_input = (
        attention_standardized * attention_norm_gain.astype(jnp.float32)
    ).astype(jnp.bfloat16)
    packed = matmul(attention_normed_input, w_qkv).reshape(
        groups, row_count, 3, head_count, HEAD_DIM
    )
    query_raw = packed[:, :, 0]
    key_raw = packed[:, :, 1]
    rotated_query = (
        (query_raw * cosine_table + rotate_half(query_raw) * sine_table) * HEAD_DIM ** (-0.5)
    ).astype(jnp.bfloat16)
    rotated_key = (key_raw * cosine_table + rotate_half(key_raw) * sine_table).astype(jnp.bfloat16)
    value_reduced_precision = packed[:, :, 2].astype(jnp.bfloat16)
    attended, logarithm_totals = jax.vmap(attend)(
        rotated_query, rotated_key, value_reduced_precision, sequence_segment
    )
    attention_rows_flat = attended.reshape(groups * row_count, embedding_width)
    hidden_residual = residual_input + matmul(attention_rows_flat, w_attn_out)
    feedforward_standardized, feedforward_inverse_norm = norm_statistics(hidden_residual)
    feedforward_normed_input = (
        feedforward_standardized * feedforward_norm_gain.astype(jnp.float32)
    ).astype(jnp.bfloat16)
    inner_proj = matmul(feedforward_normed_input, w_in)
    gate_projection = inner_proj[:, :hidden_units]
    up_projection = inner_proj[:, hidden_units:]
    activation_output = jax.nn.gelu(gate_projection, approximate=False)
    mixed_input = (activation_output * up_projection).astype(jnp.bfloat16)
    live_token_rows = valid.reshape(groups * row_count, 1)
    mlp_result = matmul_right_t(mixed_input, w_out)
    output = jnp.where(live_token_rows, hidden_residual + mlp_result, 0.0).astype(jnp.bfloat16)
    saved_residuals = (
        sequence_segment,
        live_token_rows,
        cosine_table,
        sine_table,
        attention_standardized,
        attention_inverse_norm,
        attention_normed_input,
        rotated_query,
        rotated_key,
        value_reduced_precision,
        logarithm_totals,
        attention_rows_flat,
        feedforward_standardized,
        feedforward_inverse_norm,
        feedforward_normed_input,
        gate_projection,
        up_projection,
        activation_output,
        mixed_input,
    )
    return (output, saved_residuals)


def backward(
    saved_residuals,
    cotangent,
    attention_norm_gain,
    w_qkv,
    w_attn_out,
    feedforward_norm_gain,
    w_in,
    w_out,
):
    (
        sequence_segment,
        live_token_rows,
        cosine_table,
        sine_table,
        attention_standardized,
        attention_inverse_norm,
        attention_normed_input,
        rotated_query,
        rotated_key,
        value_reduced_precision,
        logarithm_totals,
        attention_rows_flat,
        feedforward_standardized,
        feedforward_inverse_norm,
        feedforward_normed_input,
        gate_projection,
        up_projection,
        activation_output,
        mixed_input,
    ) = saved_residuals
    groups, row_count = sequence_segment.shape
    embedding_width = attention_standardized.shape[1]
    head_count = embedding_width // HEAD_DIM
    flat_cot = cotangent.reshape(groups * row_count, embedding_width)
    output_gradient = jnp.where(live_token_rows, flat_cot, jnp.zeros((), flat_cot.dtype))
    grad_mixed = matmul(output_gradient, w_out)
    slope = (
        0.5 * (1.0 + lax.erf(gate_projection * 0.7071067811865476))
        + gate_projection * jnp.exp(-0.5 * gate_projection * gate_projection) * 0.3989422804014327
    )
    grad_inner = jnp.concatenate(
        [grad_mixed * up_projection * slope, grad_mixed * activation_output], axis=1
    ).astype(jnp.bfloat16)
    feedforward_normed_gradient = matmul_right_t(grad_inner, w_in)
    hidden_gradient = output_gradient.astype(jnp.float32) + norm_backward_pass(
        feedforward_normed_gradient,
        feedforward_norm_gain,
        feedforward_standardized,
        feedforward_inverse_norm,
    )
    grad_hidden_low = hidden_gradient.astype(jnp.bfloat16)
    grad_attended = matmul_right_t(grad_hidden_low, w_attn_out).astype(jnp.bfloat16)
    grad_attended = grad_attended.reshape(groups, row_count, head_count, HEAD_DIM)
    grad_query, grad_key, grad_value = jax.vmap(attend_back)(
        rotated_query,
        rotated_key,
        value_reduced_precision,
        sequence_segment,
        logarithm_totals,
        grad_attended,
    )
    grad_query = grad_query * HEAD_DIM ** (-0.5)
    grad_query = grad_query * cosine_table + rotate_back(grad_query * sine_table)
    grad_key = grad_key * cosine_table + rotate_back(grad_key * sine_table)
    grad_packed = jnp.stack([grad_query, grad_key, grad_value], axis=2)
    grad_packed = grad_packed.reshape(groups * row_count, 3 * embedding_width).astype(jnp.bfloat16)
    attention_normed_gradient = matmul_right_t(grad_packed, w_qkv)
    block_input_gradient = hidden_gradient + norm_backward_pass(
        attention_normed_gradient,
        attention_norm_gain,
        attention_standardized,
        attention_inverse_norm,
    )
    factors = (
        attention_normed_input,
        grad_packed,
        attention_rows_flat,
        grad_hidden_low,
        feedforward_normed_input,
        grad_inner,
        output_gradient,
        mixed_input,
        attention_normed_gradient,
        attention_standardized,
        feedforward_normed_gradient,
        feedforward_standardized,
    )
    return (block_input_gradient, factors)


def local_plain(
    tokens,
    seq_lengths,
    cotangent,
    attention_norm_gain,
    w_qkv,
    w_attn_out,
    feedforward_norm_gain,
    w_in,
    w_out,
):
    row_count, embedding_width = tokens.shape
    gathered = (
        lax.all_gather(attention_norm_gain, ("fsdp", "rep"), axis=0, tiled=True),
        lax.all_gather(w_qkv, ("fsdp", "rep"), axis=0, tiled=True),
        lax.all_gather(w_attn_out, ("fsdp", "rep"), axis=0, tiled=True),
        lax.all_gather(feedforward_norm_gain, ("fsdp", "rep"), axis=0, tiled=True),
        lax.all_gather(w_in, ("fsdp", "rep"), axis=0, tiled=True),
        lax.all_gather(w_out, ("fsdp", "rep"), axis=0, tiled=True),
    )
    output, saved_residuals = forward(
        tokens.reshape(1, row_count, embedding_width),
        seq_lengths,
        gathered[0],
        gathered[1],
        gathered[2],
        gathered[3],
        gathered[4],
        gathered[5],
    )
    second_copy = (
        lax.all_gather(attention_norm_gain, ("fsdp", "rep"), axis=0, tiled=True),
        lax.all_gather(w_qkv, ("fsdp", "rep"), axis=0, tiled=True),
        lax.all_gather(w_attn_out, ("fsdp", "rep"), axis=0, tiled=True),
        lax.all_gather(feedforward_norm_gain, ("fsdp", "rep"), axis=0, tiled=True),
        lax.all_gather(w_in, ("fsdp", "rep"), axis=0, tiled=True),
        lax.all_gather(w_out, ("fsdp", "rep"), axis=0, tiled=True),
    )
    block_input_gradient, factors = backward(
        saved_residuals,
        cotangent.reshape(1, row_count, embedding_width),
        second_copy[0],
        second_copy[1],
        second_copy[2],
        second_copy[3],
        second_copy[4],
        second_copy[5],
    )
    (
        normed_attn,
        grad_packed,
        attended_rows,
        grad_hidden_low,
        normed_mlp,
        grad_inner,
        grad_out,
        mixed_input,
        grad_normed_attn,
        standard_attn,
        grad_normed_mlp,
        standard_mlp,
    ) = factors
    qkv_width = w_qkv.shape[1]
    attn_width = w_attn_out.shape[1]
    inner_width = w_in.shape[1]
    outer_width = w_out.shape[1]
    qkv_term = matmul_left_t(normed_attn, grad_packed)
    attn_term = matmul_left_t(attended_rows, grad_hidden_low)
    inner_term = matmul_left_t(normed_mlp, grad_inner)
    outer_term = matmul_left_t(grad_out, mixed_input)
    attn_gain_term = jnp.sum(grad_normed_attn * standard_attn, axis=0)
    mlp_gain_term = jnp.sum(grad_normed_mlp * standard_mlp, axis=0)
    summed = lax.psum_scatter(
        jnp.concatenate(
            [
                qkv_term,
                attn_term,
                inner_term,
                outer_term,
                attn_gain_term[:, None],
                mlp_gain_term[:, None],
            ],
            axis=1,
        ),
        ("fsdp", "rep"),
        scatter_dimension=0,
        tiled=True,
    )
    edge_two = qkv_width + attn_width
    edge_three = edge_two + inner_width
    edge_four = edge_three + outer_width
    return (
        output,
        block_input_gradient,
        summed[:, edge_four],
        summed[:, :qkv_width],
        summed[:, qkv_width:edge_two],
        summed[:, edge_four + 1],
        summed[:, edge_two:edge_three],
        summed[:, edge_three:edge_four],
    )


AXES = ("fsdp", "rep")
LANES = 128
HALF = HEAD_DIM // 2


def tie(*values):
    return lax.optimization_barrier(values)


def wide(value):
    return value.astype(jnp.float32)


def low(value):
    return value.astype(jnp.bfloat16)


def split_columns(value, count):
    width = value.shape[1] // count
    return [value[:, k * width : (k + 1) * width] for k in range(count)]


def split_rows(value, count):
    width = value.shape[0] // count
    return [value[k * width : (k + 1) * width] for k in range(count)]


def columns(blocks):
    return jnp.concatenate(blocks, axis=1)


def rows(blocks):
    return jnp.concatenate(blocks, axis=0)


def swap(value, distance):
    return lax.ppermute(value, "rep", [(k, k ^ distance) for k in range(4)])


def rep_exchange(value):
    blocks = value.reshape(4, value.shape[0] // 4, value.shape[1])
    return lax.all_to_all(blocks, "rep", 0, 0, tiled=True).reshape(value.shape)


def up(value):
    return lax.ppermute(value, "fsdp", [(k, (k + 2) % 8) for k in range(8)])


def down(value):
    return lax.ppermute(value, "fsdp", [(k, (k - 2) % 8) for k in range(8)])


def over(value):
    return lax.ppermute(value, "fsdp", [(k, k ^ 1) for k in range(8)])


def relative(value, z, x):
    blocks = split_columns(value, 8)
    blocks = [jnp.where(x == 1, blocks[k ^ 1], blocks[k]) for k in range(8)]
    for bit in (1, 2):
        turn = (z & bit) != 0
        blocks = [jnp.where(turn, blocks[(k + 2 * bit) % 8], blocks[k]) for k in range(8)]
    return columns([blocks[2 * ((p + 1) % 4) + i] for i in range(2) for p in range(4)])


def absolute(value, z, x):
    blocks = split_columns(value, 8)
    blocks = [blocks[4 * i + (j - 1) % 4] for j in range(4) for i in range(2)]
    blocks = [jnp.where(x == 1, blocks[k ^ 1], blocks[k]) for k in range(8)]
    for bit in (1, 2):
        turn = (z & bit) != 0
        blocks = [jnp.where(turn, blocks[(k - 2 * bit) % 8], blocks[k]) for k in range(8)]
    return columns(blocks)


def place_of(place, step, side):
    z, x = place[0], place[1]
    return 2 * lax.rem(z + step + 1, 4) + (x if side == 0 else 1 - x)


def block_of(place, z_at, side):
    z, x = place[0], place[1]
    return 4 * (x if side == 0 else 1 - x) + lax.rem(z_at - z + 7, 4)


def turned(value):
    width = value.shape[1]
    lane = lax.broadcasted_iota(jnp.int32, value.shape, 1)
    return jnp.where(
        lane % HEAD_DIM < HALF,
        pltpu.roll(value, width - HALF, 1),
        pltpu.roll(value, HALF, 1),
    )


def head_masks(row_count):
    lane = lax.broadcasted_iota(jnp.int32, (row_count, LANES), 1)
    return [low(wide(lane < HEAD_DIM)), low(wide(lane >= HEAD_DIM))], lane < HEAD_DIM


def token_rows(mine, across, beside, first, step):
    count = 128
    return [
        mine[first : first + count],
        beside[first : first + count],
        across[first : first + count],
        beside[step + first : step + first + count],
    ]


def attention_forward(
    place, seg_col, seg_row, cosine, sine, mine, across, beside,
    first, second, third, own, others, other_second, other,
    normed, qkv, attn, query, key, value, probs, attended, send, keep,
):
    size = own.shape[0]
    blocks = [
        (first, 0), (second, 0), (third, 0), (own, 0),
        (others, 0), (other_second, 0), (others, size), (other, 0),
    ]
    part = size // 4
    for at, (ref, row) in enumerate(blocks):
        qkv[size * at : size * (at + 1), :] = ref[row : row + size, :768]
        target = pl.multiple_of(place_of(place, at % 4, at // 4) * part, part)
        for z_at in range(4):
            for side in range(2):
                lanes = pl.multiple_of(block_of(place, z_at, side) * LANES, LANES)
                attn[pl.ds(target, part), pl.ds(lanes, LANES)] = ref[
                    row + part * z_at : row + part * (z_at + 1),
                    768 + LANES * side : 768 + LANES * (side + 1),
                ]
    count = 128
    for at, ref in enumerate(token_rows(mine, across, beside, 0, mine.shape[0])):
        values = wide(ref)
        centred = values - jnp.mean(values, axis=1, keepdims=True)
        inverse = lax.rsqrt(jnp.mean(centred * centred, axis=1, keepdims=True) + norm_eps)
        normed[count * at : count * (at + 1), :] = low(centred * inverse)
    packed = matmul(normed[...], qkv[...])
    cos_all, sin_all = columns([cosine[...]] * 2), columns([sine[...]] * 2)
    raw = packed[:, :256]
    query[...] = low((raw * cos_all + turned(raw) * sin_all) * HEAD_DIM ** (-0.5))
    raw = packed[:, 256:512]
    key[...] = low(raw * cos_all + turned(raw) * sin_all)
    value[...] = low(packed[:, 512:])
    masks, is_first = head_masks(count)
    for at in range(4):
        here = slice(count * at, count * (at + 1))
        allowed = seg_col[here, :] == seg_row[at : at + 1, :]
        for pair in range(2):
            lanes = slice(LANES * pair, LANES * (pair + 1))
            made = []
            for head in range(2):
                scores = matmul_right_t(query[here, lanes] * masks[head], key[here, lanes])
                scores = jnp.where(allowed, scores, -jnp.inf)
                powers = jnp.exp(scores - jnp.max(scores, axis=1, keepdims=True))
                weights = powers / jnp.sum(powers, axis=1, keepdims=True)
                slot = count * (4 * at + 2 * pair + head)
                probs[slot : slot + count, :] = weights
                made.append(matmul(low(weights), value[here, lanes]))
            attended[here, lanes] = low(jnp.where(is_first, made[0], made[1]))
    total = low(matmul(attended[...], attn[...]))
    keep[:count, :], send[:count, :] = total[:count], total[count : 2 * count]
    keep[count:, :], send[count:, :] = total[2 * count : 3 * count], total[3 * count :]


def mlp(
    seg_col, norm_own, norm_across, norm_beside, mine, across, beside,
    first, second, third, own, other_first, other_second, other_third, other,
    normed, grad_out, mixed, grad_inner, send, keep, w_down,
    w_up, inner, grad_mixed,
):
    size, count = own.shape[0], 128
    main, rest = w_down.shape[1] - LANES, 16
    lane = lax.broadcasted_iota(jnp.int32, (size, LANES), 1)
    blocks = (first, second, third, own, other_first, other_second, other_third, other)
    for at, ref in enumerate(blocks):
        here = slice(size * at, size * (at + 1))
        tail = wide(ref[:, 3 * main :])
        w_up[here, : 2 * main] = ref[:, : 2 * main]
        w_up[here, 2 * main :] = low(jnp.where(lane < 2 * rest, tail, 0.0))
        w_down[here, :main] = ref[:, 2 * main : 3 * main]
        tail = pltpu.roll(tail, LANES - 2 * rest, 1)
        w_down[here, main:] = low(jnp.where(lane < rest, tail, 0.0))
    for at, ref in enumerate(
        (norm_own[...], norm_beside[:count, :], norm_across[...], norm_beside[count:, :])
    ):
        normed[count * at : count * (at + 1), :] = ref
    for at, ref in enumerate(token_rows(mine, across, beside, count, mine.shape[0])):
        live = wide(seg_col[count * at : count * (at + 1), :] < 8)
        grad_out[count * at : count * (at + 1), :] = low(wide(ref) * live)
    inner[...] = matmul(normed[...], w_up[...])
    grad_mixed[...] = matmul(grad_out[...], w_down[...])

    def parts(gate):
        phi = 0.5 * (1.0 + lax.erf(gate * 0.7071067811865476))
        slope = phi + gate * jnp.exp(-0.5 * gate * gate) * 0.3989422804014327
        return gate * phi, slope

    @pl.loop(0, 8)
    def _(step):
        here = pl.ds(pl.multiple_of(step * 64, 64), 64)
        gate, up_part = inner[here, :main], inner[here, main : 2 * main]
        grad = grad_mixed[here, :main]
        activation, slope = parts(gate)
        mixed[here, :main] = low(activation * up_part)
        grad_inner[here, :main] = low(grad * up_part * slope)
        grad_inner[here, main : 2 * main] = low(grad * activation)
        tail = inner[here, 2 * main :]
        grad = grad_mixed[here, main:]
        activation, slope = parts(tail)
        tail_up = pltpu.roll(tail, LANES - rest, 1)
        mixed[here, main:] = low(activation * tail_up)
        grad_inner[here, 2 * main :] = low(
            grad * tail_up * slope + pltpu.roll(grad * activation, rest, 1)
        )

    total = low(matmul_right_t(grad_inner[...], w_up[...]))
    keep[:count, :], send[:count, :] = total[:count], total[count : 2 * count]
    keep[count:, :], send[count:, :] = total[2 * count : 3 * count], total[3 * count :]


def place_term(term, keep, pair, near, far, lanes):
    size = term.shape[0] // 8
    for at, (ref, row) in enumerate(
        [(keep, 0), (pair, 0), (keep, 1), (keep, 2), (near, 0), (pair, 1), (far, 0), (far, 1)]
    ):
        ref[size * row : size * (row + 1), lanes] = term[size * at : size * (at + 1)]


def mlp_terms(normed, grad_inner, grad_out, mixed, keep, pair, near, far):
    main, rest = mixed.shape[1] - LANES, 16
    term_in = matmul_left_t(normed[...], grad_inner[...])
    term_out = matmul_left_t(grad_out[...], mixed[...])
    tail = term_in[:, 2 * main :] + pltpu.roll(term_out[:, main:], 2 * rest, 1)
    place_term(low(term_in[:, : 2 * main]), keep, pair, near, far, slice(0, 2 * main))
    place_term(low(term_out[:, :main]), keep, pair, near, far, slice(2 * main, 3 * main))
    place_term(low(tail), keep, pair, near, far, slice(3 * main, 3 * main + LANES))


def attention_backward(
    place, cosine, sine, low_own, low_across, low_beside, attn, query, key, value, probs,
    attended, normed,
    grad_packed, keep, pair, near, far, grad_low, grad_attended, term_attn,
):
    count = 128
    for at, ref in enumerate(
        (low_own[...], low_beside[:count, :], low_across[...], low_beside[count:, :])
    ):
        grad_low[count * at : count * (at + 1), :] = ref
    grad_attended[...] = low(matmul_right_t(grad_low[...], attn[...]))
    masks, is_first = head_masks(count)
    for at in range(4):
        here = slice(count * at, count * (at + 1))
        cos, sin = cosine[here, :], sine[here, :]
        for half in range(2):
            lanes = slice(LANES * half, LANES * (half + 1))
            q, k, v = query[here, lanes], key[here, lanes], value[here, lanes]
            grad = grad_attended[here, lanes]
            made = []
            for head in range(2):
                slot = count * (4 * at + 2 * half + head)
                weights = probs[slot : slot + count, :]
                grad_value = matmul_left_t(low(weights), grad)
                grad_probs = matmul_right_t(grad * masks[head], v)
                delta = jnp.sum(weights * grad_probs, axis=1, keepdims=True)
                grad_scores = low(weights * (grad_probs - delta))
                made.append((matmul(grad_scores, k), matmul_left_t(grad_scores, q), grad_value))
            grad_q, grad_k, grad_v = (jnp.where(is_first, *both) for both in zip(*made))
            grad_q = grad_q * HEAD_DIM ** (-0.5)
            grad_packed[here, lanes] = low(grad_q * cos - turned(grad_q) * sin)
            lanes = slice(256 + LANES * half, 256 + LANES * (half + 1))
            grad_packed[here, lanes] = low(grad_k * cos - turned(grad_k) * sin)
            lanes = slice(512 + LANES * half, 512 + LANES * (half + 1))
            grad_packed[here, lanes] = low(grad_v)
    term = low(matmul_left_t(normed[...], grad_packed[...]))
    place_term(term, keep, pair, near, far, slice(0, 768))
    term_attn[...] = low(matmul_left_t(attended[...], grad_low[...]))
    size = term.shape[0] // 8
    part = size // 4
    targets = [
        (keep, 0), (pair, 0), (keep, size), (keep, 2 * size),
        (near, 0), (pair, size), (far, 0), (far, size),
    ]
    for at, (ref, row) in enumerate(targets):
        source = pl.multiple_of(place_of(place, at % 4, at // 4) * part, part)
        for z_at in range(4):
            for side in range(2):
                lanes = pl.multiple_of(block_of(place, z_at, side) * LANES, LANES)
                ref[
                    row + part * z_at : row + part * (z_at + 1),
                    768 + LANES * side : 768 + LANES * (side + 1),
                ] = term_attn[pl.ds(source, part), pl.ds(lanes, LANES)]


def projections(grad_packed, qkv, mixed, w_down, send, keep):
    count = 128
    for row, total in (
        (0, low(matmul_right_t(grad_packed[...], qkv[...]))),
        (count, low(matmul_right_t(mixed[...], w_down[...]))),
    ):
        keep[row : row + count, :] = total[:count]
        send[row : row + count, :] = total[count : 2 * count]
        keep[2 * count + row : 3 * count + row, :] = total[2 * count : 3 * count]
        send[2 * count + row : 3 * count + row, :] = total[3 * count :]


def unpack_rest(back, w_in, gain, grad_in, gain_grad, grad_out):
    size, hidden, part = w_in.shape[0], w_in.shape[1] // 2, w_in.shape[1] // 8
    main = part // LANES * LANES
    rest = part - main
    total = jnp.zeros(gain.shape, jnp.float32)
    for k in range(4):
        here = slice(size * k, size * (k + 1))
        for half in range(2):
            base = hidden * half + part * k
            for source, target, count in (
                (main * half, base, main),
                (3 * main + rest * half, base + main, rest),
            ):
                piece = wide(back[here, source : source + count])
                grad_in[:, target : target + count] = piece * gain[...]
                weights = wide(w_in[:, target : target + count])
                total += jnp.sum(piece * weights, axis=1, keepdims=True)
        base = part * k
        grad_out[:, base : base + main] = wide(back[here, 2 * main : 3 * main])
        source = 3 * main + 2 * rest
        grad_out[:, base + main : base + part] = wide(back[here, source : source + rest])
    gain_grad[...] = jnp.broadcast_to(total, (total.shape[0], LANES)).T[:1, :]


def unpack_qkv(back, w_qkv, gain, grad, gain_grad):
    size, part = w_qkv.shape[0], 256
    edge = back.shape[1] - 3 * part
    total = jnp.zeros(gain.shape, jnp.float32)
    for k in range(4):
        for third in range(3):
            source = slice(edge + part * third, edge + part * (third + 1))
            piece = wide(back[size * k : size * (k + 1), source])
            lanes = slice(part * (4 * third + k), part * (4 * third + k + 1))
            grad[:, lanes] = piece * gain[...]
            total += jnp.sum(piece * wide(w_qkv[:, lanes]), axis=1, keepdims=True)
    gain_grad[...] = jnp.broadcast_to(total, (total.shape[0], LANES)).T[:1, :]


def kernel(body, outs, cost, *args, scratch=(), scalars=0):
    flops, transcendentals = cost
    shapes = [jax.ShapeDtypeStruct(shape, kind) for shape, kind in outs]
    moved = sum(arg.size * arg.dtype.itemsize for arg in (*args, *shapes))
    return pl.pallas_call(
        body,
        out_shape=shapes,
        in_specs=[
            pl.BlockSpec(memory_space=pltpu.SMEM if k < scalars else pltpu.VMEM)
            for k in range(len(args))
        ],
        out_specs=[pl.BlockSpec(memory_space=pltpu.VMEM)] * len(shapes),
        scratch_shapes=[pltpu.VMEM(shape, kind) for shape, kind in scratch],
        compiler_params=pltpu.CompilerParams(vmem_limit_bytes=28 * 2**20),
        cost_estimate=pl.CostEstimate(
            flops=flops, bytes_accessed=moved, transcendentals=transcendentals
        ),
        name=body.__name__,
    )(*args)


def scatter_last(send, keep):
    beside = split_rows(swap(send, 1), 2)
    kept = split_rows(keep, 2)
    sent = low(wide(kept[1]) + wide(beside[1]))
    return wide(kept[0]) + wide(beside[0]), sent


def local_ring(
    tokens,
    seq_lengths,
    cotangent,
    attention_norm_gain,
    w_qkv,
    w_attn_out,
    feedforward_norm_gain,
    w_in,
    w_out,
):
    count, width = tokens.shape
    index = lax.axis_index("fsdp")
    z, x = index // 2, index % 2
    place = jnp.stack([z, x]).astype(jnp.int32)
    hidden = w_in.shape[1] // 2
    part = hidden // 4
    main = part // LANES * LANES
    in_width, out_width, all_width = 2 * main + LANES, main + LANES, 3 * main + LANES
    f32, b16 = jnp.float32, jnp.bfloat16
    group = 4 * count

    gain_attn = wide(attention_norm_gain)[:, None]
    gain_mlp = wide(feedforward_norm_gain)[:, None]
    order = [(k, (k % 8) * 4 + k // 8) for k in range(32)]
    attn_own = lax.ppermute(w_attn_out, AXES, order)
    qkv_parts = split_columns(low(wide(w_qkv) * gain_attn), 12)
    size = w_qkv.shape[0]
    slots = seq_lengths.shape[1]
    lengths_low = jnp.pad(low(wide(seq_lengths)), ((0, size - 1), (0, LANES - slots)))
    exchanged = rep_exchange(rows([columns([*qkv_parts[k::4], lengths_low]) for k in range(4)]))
    first_own = columns([exchanged[:, :768], rows(split_columns(attn_own, 4))])
    lengths = rows([exchanged[size * k : size * k + 1, 768 : 768 + slots] for k in range(4)])
    lengths = wide(lengths).astype(jnp.int32)
    for bit in (1, 2):
        turned_rows = rows([lengths[k ^ bit : (k ^ bit) + 1] for k in range(4)])
        lengths = jnp.where((lax.axis_index("rep") & bit) != 0, turned_rows, lengths)

    scaled_in = low(wide(w_in) * gain_mlp)
    pieces = []
    for k in range(4):
        gate = scaled_in[:, part * k : part * (k + 1)]
        up_part = scaled_in[:, hidden + part * k : hidden + part * (k + 1)]
        out_part = w_out[:, part * k : part * (k + 1)]
        fill = jnp.zeros((w_in.shape[0], all_width - 3 * part), b16)
        pieces.append(
            columns(
                [gate[:, :main], up_part[:, :main], out_part[:, :main]]
                + [gate[:, main:], up_part[:, main:], out_part[:, main:], fill]
            )
        )
    mine = rows([relative(tokens, z, x), relative(cotangent, z, x)])
    first_own, rest, mine = tie(first_own, rows(pieces), mine)
    rest = rep_exchange(rest)

    third, first, other = up(first_own), down(first_own), over(first_own)
    third, first, other, mine, rest = tie(third, first, other, mine, rest)
    across = swap(mine, 2)
    second, others, rest_third = up(third), over(rows([first, third])), up(rest)
    second, others, across = tie(second, others, across)
    other_second = over(second)
    rest_first = down(tie(rest, rest_third)[0])
    beside = swap(rows([mine, across]), 1)
    rest_other = over(tie(rest, other_second)[0])

    step = mine.shape[0]
    segment, positions, _ = jax.vmap(lambda row: layout(row, count))(lengths)
    frequency = rope_base ** (-(lax.iota(f32, HALF) * (2.0 / HEAD_DIM)))
    angles = positions.reshape(group, 1).astype(f32) * frequency
    cosine, sine = jnp.cos(angles), jnp.sin(angles)
    cosine, sine = columns([cosine] * 4), columns([-sine, sine] * 2)
    seg_col = segment.reshape(group, 1)

    normed, qkv, attn, query, key, value, probs, attended, send, keep = kernel(
        attention_forward,
        [((group, width), b16), ((width, 768), b16), ((256, width), b16)]
        + [((group, 256), b16)] * 3
        + [((16 * count, count), f32), ((group, 256), b16)]
        + [((2 * count, width), b16)] * 2,
        (2 * group * width * (768 + 256) + 4 * 16 * count * count * LANES, 16 * count * count),
        place, seg_col, segment, cosine, sine, mine, across, beside,
        first, second, third, first_own, others, other_second, other,
        scalars=1,
    )
    rest_third, rest_first, rest_other, send = tie(rest_third, rest_first, rest_other, send)
    rest_second, rest_other_third = up(rest_third), over(rest_third)
    x_own = wide(mine[:count])
    kept, sent = scatter_last(send, keep)
    rest_other_first = over(tie(rest_first, rest_other_third)[0])
    hidden_sum = x_own + kept + wide(swap(sent, 2))
    standard_mlp, inverse_mlp = norm_statistics(hidden_sum)
    norm_own = low(standard_mlp)
    norm_across = swap(norm_own, 2)
    rest_second, rest_other_third, _ = tie(rest_second, rest_other_third, norm_own)
    rest_other_second = up(rest_other_third)
    norm_beside = swap(rows([norm_own, norm_across]), 1)

    normed_mlp, grad_out, mixed, grad_inner, send, keep, w_down = kernel(
        mlp,
        [((group, width), b16)] * 2
        + [((group, out_width), b16), ((group, in_width), b16)]
        + [((2 * count, width), b16)] * 2
        + [((width, out_width), b16)],
        (2 * group * width * (2 * in_width + out_width), 3 * group * part),
        seg_col, norm_own, norm_across, norm_beside, mine, across, beside,
        rest_first, rest_second, rest_third, rest,
        rest_other_first, rest_other_second, rest_other_third, rest_other,
        scratch=[
            ((width, in_width), b16),
            ((group, in_width), f32),
            ((group, out_width), f32),
        ],
    )
    size = width // 8
    io_keep, io_pair, io_near, io_far = kernel(
        mlp_terms,
        [((size * n, all_width), b16) for n in (3, 2, 1, 2)],
        (2 * group * width * all_width, 0),
        normed_mlp, grad_inner, grad_out, mixed,
    )
    io_pair, io_far = up(io_pair), over(io_far)
    kept, sent = scatter_last(send, keep)
    scaled_mlp = kept + wide(tie(swap(sent, 2), io_keep)[0])
    grad_hidden = wide(grad_out[:count]) + norm_backward_pass(
        scaled_mlp, jnp.ones((), f32), standard_mlp, inverse_mlp
    )
    low_own = low(grad_hidden)
    low_across = swap(low_own, 2)
    low_beside = swap(rows([low_own, low_across]), 1)

    grad_packed, g_keep, g_pair, g_near, g_far = kernel(
        attention_backward,
        [((group, 768), b16)] + [((size * n, width), b16) for n in (3, 2, 1, 2)],
        (2 * group * width * (768 + 512) + 10 * 16 * count * count * LANES, 0),
        place, cosine, sine, low_own, low_across, low_beside, attn, query, key, value, probs,
        attended, normed,
        scratch=[((group, width), b16), ((group, 256), b16), ((256, width), b16)],
        scalars=1,
    )
    g_pair, g_far = up(g_pair), over(g_far)
    io_pair, io_far, _ = tie(io_pair, io_far, g_near)
    io_kept, io_pair, io_far = split_rows(io_keep, 3), split_rows(io_pair, 2), split_rows(io_far, 2)
    io_near = over(low(wide(io_near) + wide(io_pair[1])))
    io_down = down(low(wide(io_kept[1]) + wide(io_far[0])))
    send, keep = kernel(
        projections,
        [((4 * count, width), b16)] * 2,
        (2 * group * width * (768 + out_width), 0),
        grad_packed, qkv, mixed, w_down,
    )
    io_near, io_down, g_pair, g_far, send = tie(io_near, io_down, g_pair, g_far, send)
    g_kept, g_pair, g_far = split_rows(g_keep, 3), split_rows(g_pair, 2), split_rows(g_far, 2)
    g_near = over(low(wide(g_near) + wide(g_pair[1])))
    g_down = down(low(wide(g_kept[1]) + wide(g_far[0])))
    kept, sent = scatter_last(send, keep)
    io_up = up(low(wide(io_kept[0]) + wide(io_pair[0]) + wide(io_near)))
    g_near, sent = tie(g_near, sent)
    g_up = up(low(wide(g_kept[0]) + wide(g_pair[0]) + wide(g_near)))
    last_across = swap(sent, 2)
    io_up, g_up, g_down = tie(io_up, g_up, g_down)
    sum_io = low(wide(io_kept[2]) + wide(io_far[1]) + wide(io_down) + wide(io_up))
    sum_g = low(wide(g_kept[2]) + wide(g_far[1]) + wide(g_down) + wide(g_up))
    back = rep_exchange(columns([sum_io, sum_g[:, :768]]))
    grad_w_in, gain_in, grad_w_out = kernel(
        unpack_rest,
        [(w_in.shape, f32), ((1, w_in.shape[0]), f32), (w_out.shape, f32)],
        (4 * w_in.size, 0),
        back, w_in, gain_mlp,
    )
    grad_w_qkv, gain_qkv = kernel(
        unpack_qkv,
        [(w_qkv.shape, f32), ((1, w_qkv.shape[0]), f32)],
        (4 * w_qkv.size, 0),
        back, w_qkv, gain_attn,
    )
    last = kept + wide(last_across)

    standard, inverse = norm_statistics(x_own)
    block_input_gradient = grad_hidden + norm_backward_pass(
        last[:count], jnp.ones((), f32), standard, inverse
    )
    output = low(jnp.where(seg_col[:count] < 8, hidden_sum + last[count:], 0.0))
    block_input_gradient = absolute(block_input_gradient, z, x)
    sum_attn, block_input_gradient = tie(sum_g[:, 768:], block_input_gradient)
    grad_w_attn_out = wide(
        lax.ppermute(
            columns(split_rows(sum_attn, 4)),
            AXES,
            [(there, here) for here, there in order],
        )
    )
    return (
        absolute(output, z, x),
        block_input_gradient,
        gain_qkv.reshape(-1),
        grad_w_qkv,
        grad_w_attn_out,
        gain_in.reshape(-1),
        grad_w_in,
        grad_w_out,
    )


def solution(mesh):
    ringed = dict(mesh.shape) == {"fsdp": 8, "rep": 4}
    return jax.shard_map(
        local_ring if ringed else local_plain,
        mesh=mesh,
        in_specs=(
            P(AXES, None),
            P(AXES, None),
            P(AXES, None),
            P(AXES),
            P(AXES, None),
            P(AXES, None),
            P(AXES),
            P(AXES, None),
            P(AXES, None),
        ),
        out_specs=(
            P(AXES, None),
            P(AXES, None),
            P(AXES),
            P(AXES, None),
            P(AXES, None),
            P(AXES),
            P(AXES, None),
            P(AXES, None),
        ),
        check_vma=False,
    )
```

```python
import jax
import jax.numpy as jnp
from jax import lax
from jax.experimental import pallas as pl
from jax.experimental.pallas import tpu as pltpu
from jax.sharding import PartitionSpec as P

HEAD_DIM = 64


norm_eps = 1e-05
rope_base = 160000.0


def matmul(left_side, right_side):
    return jnp.dot(left_side, right_side, preferred_element_type=jnp.float32)


def matmul_right_t(left_side, right_side):
    return lax.dot_general(
        left_side, right_side, (((1,), (1,)), ((), ())), preferred_element_type=jnp.float32
    )


def matmul_left_t(left_side, right_side):
    return lax.dot_general(
        left_side, right_side, (((0,), (0,)), ((), ())), preferred_element_type=jnp.float32
    )


def batched(form, left_side, right_side):
    return jnp.einsum(form, left_side, right_side, preferred_element_type=jnp.float32)


def layout(lengths, row_count):
    slot_ids = lax.iota(jnp.int32, lengths.shape[0])
    before = (slot_ids[:, None] <= slot_ids[None, :]).astype(jnp.int32)
    ends = jnp.sum(lengths[:, None] * before, axis=0)
    starts = ends - lengths
    places = lax.iota(jnp.int32, row_count)
    sequence_segment = jnp.sum((ends[None, :] <= places[:, None]).astype(jnp.int32), axis=1)
    first_row = jnp.sum(
        jnp.where(sequence_segment[:, None] == slot_ids[None, :], starts[None, :], 0), axis=1
    )
    return (sequence_segment, places - first_row, sequence_segment < lengths.shape[0])


def rotary(positions, head_size):
    half_size = head_size // 2
    frequency = rope_base ** (-(lax.iota(jnp.float32, half_size) * (2.0 / head_size)))
    angles = positions.astype(jnp.float32)[..., None] * frequency
    cosine_table = jnp.concatenate([jnp.cos(angles), jnp.cos(angles)], axis=-1)
    sine_table = jnp.concatenate([jnp.sin(angles), jnp.sin(angles)], axis=-1)
    return (cosine_table, sine_table)


def rotate_half(vector):
    half_size = vector.shape[-1] // 2
    return jnp.concatenate([-vector[..., half_size:], vector[..., :half_size]], axis=-1)


def rotate_back(vector):
    half_size = vector.shape[-1] // 2
    return jnp.concatenate([vector[..., half_size:], -vector[..., :half_size]], axis=-1)


def norm_statistics(values):
    average = jnp.mean(values, axis=-1, keepdims=True)
    centred = values - average
    inverse = lax.rsqrt(jnp.mean(centred * centred, axis=-1, keepdims=True) + norm_eps)
    return (centred * inverse, inverse)


def norm_backward_pass(grad_normed, gain_vec, normalized, inverse):
    scaled = grad_normed * gain_vec.astype(jnp.float32)
    return inverse * (
        scaled
        - jnp.mean(scaled, axis=-1, keepdims=True)
        - normalized * jnp.mean(scaled * normalized, axis=-1, keepdims=True)
    )


def attend(rotated_query, rotated_key, value_reduced_precision, sequence_segment):
    scores = batched("thd,shd->hts", rotated_query, rotated_key)
    allowed = sequence_segment[:, None] == sequence_segment[None, :]
    scores = jnp.where(allowed[None], scores, -jnp.inf)
    logarithm_totals = jax.nn.logsumexp(scores, axis=-1)
    weights = jnp.exp(scores - logarithm_totals[..., None]).astype(jnp.bfloat16)
    attended = batched("hts,shd->thd", weights, value_reduced_precision).astype(jnp.bfloat16)
    return (attended, logarithm_totals)


def attend_back(
    rotated_query,
    rotated_key,
    value_reduced_precision,
    sequence_segment,
    logarithm_totals,
    grad_attended,
):
    scores = batched("thd,shd->hts", rotated_query, rotated_key)
    allowed = sequence_segment[:, None] == sequence_segment[None, :]
    scores = jnp.where(allowed[None], scores, -jnp.inf)
    probs_full = jnp.exp(scores - logarithm_totals[..., None])
    weights = probs_full.astype(jnp.bfloat16)
    grad_value = batched("hts,thd->shd", weights, grad_attended)
    grad_probs = batched("thd,shd->hts", grad_attended, value_reduced_precision)
    row_delta = jnp.sum(probs_full * grad_probs, axis=-1, keepdims=True)
    grad_scores = (probs_full * (grad_probs - row_delta)).astype(jnp.bfloat16)
    grad_query = batched("hts,shd->thd", grad_scores, rotated_key)
    grad_key = batched("hts,thd->shd", grad_scores, rotated_query)
    return (grad_query, grad_key, grad_value)


def forward(
    tokens, lengths, attention_norm_gain, w_qkv, w_attn_out, feedforward_norm_gain, w_in, w_out
):
    groups, row_count, embedding_width = tokens.shape
    head_count = embedding_width // HEAD_DIM
    hidden_units = w_in.shape[1] // 2
    sequence_segment, positions, valid = jax.vmap(
        lambda row_lengths: layout(row_lengths, row_count)
    )(lengths)
    cosine_table, sine_table = rotary(positions, HEAD_DIM)
    cosine_table = cosine_table[:, :, None, :]
    sine_table = sine_table[:, :, None, :]
    residual_input = tokens.reshape(groups * row_count, embedding_width).astype(jnp.float32)
    attention_standardized, attention_inverse_norm = norm_statistics(residual_input)
    attention_normed_input = (
        attention_standardized * attention_norm_gain.astype(jnp.float32)
    ).astype(jnp.bfloat16)
    packed = matmul(attention_normed_input, w_qkv).reshape(
        groups, row_count, 3, head_count, HEAD_DIM
    )
    query_raw = packed[:, :, 0]
    key_raw = packed[:, :, 1]
    rotated_query = (
        (query_raw * cosine_table + rotate_half(query_raw) * sine_table) * HEAD_DIM ** (-0.5)
    ).astype(jnp.bfloat16)
    rotated_key = (key_raw * cosine_table + rotate_half(key_raw) * sine_table).astype(jnp.bfloat16)
    value_reduced_precision = packed[:, :, 2].astype(jnp.bfloat16)
    attended, logarithm_totals = jax.vmap(attend)(
        rotated_query, rotated_key, value_reduced_precision, sequence_segment
    )
    attention_rows_flat = attended.reshape(groups * row_count, embedding_width)
    hidden_residual = residual_input + matmul(attention_rows_flat, w_attn_out)
    feedforward_standardized, feedforward_inverse_norm = norm_statistics(hidden_residual)
    feedforward_normed_input = (
        feedforward_standardized * feedforward_norm_gain.astype(jnp.float32)
    ).astype(jnp.bfloat16)
    inner_proj = matmul(feedforward_normed_input, w_in)
    gate_projection = inner_proj[:, :hidden_units]
    up_projection = inner_proj[:, hidden_units:]
    activation_output = jax.nn.gelu(gate_projection, approximate=False)
    mixed_input = (activation_output * up_projection).astype(jnp.bfloat16)
    live_token_rows = valid.reshape(groups * row_count, 1)
    mlp_result = matmul_right_t(mixed_input, w_out)
    output = jnp.where(live_token_rows, hidden_residual + mlp_result, 0.0).astype(jnp.bfloat16)
    saved_residuals = (
        sequence_segment,
        live_token_rows,
        cosine_table,
        sine_table,
        attention_standardized,
        attention_inverse_norm,
        attention_normed_input,
        rotated_query,
        rotated_key,
        value_reduced_precision,
        logarithm_totals,
        attention_rows_flat,
        feedforward_standardized,
        feedforward_inverse_norm,
        feedforward_normed_input,
        gate_projection,
        up_projection,
        activation_output,
        mixed_input,
    )
    return (output, saved_residuals)


def backward(
    saved_residuals,
    cotangent,
    attention_norm_gain,
    w_qkv,
    w_attn_out,
    feedforward_norm_gain,
    w_in,
    w_out,
):
    (
        sequence_segment,
        live_token_rows,
        cosine_table,
        sine_table,
        attention_standardized,
        attention_inverse_norm,
        attention_normed_input,
        rotated_query,
        rotated_key,
        value_reduced_precision,
        logarithm_totals,
        attention_rows_flat,
        feedforward_standardized,
        feedforward_inverse_norm,
        feedforward_normed_input,
        gate_projection,
        up_projection,
        activation_output,
        mixed_input,
    ) = saved_residuals
    groups, row_count = sequence_segment.shape
    embedding_width = attention_standardized.shape[1]
    head_count = embedding_width // HEAD_DIM
    flat_cot = cotangent.reshape(groups * row_count, embedding_width)
    output_gradient = jnp.where(live_token_rows, flat_cot, jnp.zeros((), flat_cot.dtype))
    grad_mixed = matmul(output_gradient, w_out)
    slope = (
        0.5 * (1.0 + lax.erf(gate_projection * 0.7071067811865476))
        + gate_projection * jnp.exp(-0.5 * gate_projection * gate_projection) * 0.3989422804014327
    )
    grad_inner = jnp.concatenate(
        [grad_mixed * up_projection * slope, grad_mixed * activation_output], axis=1
    ).astype(jnp.bfloat16)
    feedforward_normed_gradient = matmul_right_t(grad_inner, w_in)
    hidden_gradient = output_gradient.astype(jnp.float32) + norm_backward_pass(
        feedforward_normed_gradient,
        feedforward_norm_gain,
        feedforward_standardized,
        feedforward_inverse_norm,
    )
    grad_hidden_low = hidden_gradient.astype(jnp.bfloat16)
    grad_attended = matmul_right_t(grad_hidden_low, w_attn_out).astype(jnp.bfloat16)
    grad_attended = grad_attended.reshape(groups, row_count, head_count, HEAD_DIM)
    grad_query, grad_key, grad_value = jax.vmap(attend_back)(
        rotated_query,
        rotated_key,
        value_reduced_precision,
        sequence_segment,
        logarithm_totals,
        grad_attended,
    )
    grad_query = grad_query * HEAD_DIM ** (-0.5)
    grad_query = grad_query * cosine_table + rotate_back(grad_query * sine_table)
    grad_key = grad_key * cosine_table + rotate_back(grad_key * sine_table)
    grad_packed = jnp.stack([grad_query, grad_key, grad_value], axis=2)
    grad_packed = grad_packed.reshape(groups * row_count, 3 * embedding_width).astype(jnp.bfloat16)
    attention_normed_gradient = matmul_right_t(grad_packed, w_qkv)
    block_input_gradient = hidden_gradient + norm_backward_pass(
        attention_normed_gradient,
        attention_norm_gain,
        attention_standardized,
        attention_inverse_norm,
    )
    factors = (
        attention_normed_input,
        grad_packed,
        attention_rows_flat,
        grad_hidden_low,
        feedforward_normed_input,
        grad_inner,
        output_gradient,
        mixed_input,
        attention_normed_gradient,
        attention_standardized,
        feedforward_normed_gradient,
        feedforward_standardized,
    )
    return (block_input_gradient, factors)


def local_plain(
    tokens,
    seq_lengths,
    cotangent,
    attention_norm_gain,
    w_qkv,
    w_attn_out,
    feedforward_norm_gain,
    w_in,
    w_out,
):
    row_count, embedding_width = tokens.shape
    gathered = (
        lax.all_gather(attention_norm_gain, ("fsdp", "rep"), axis=0, tiled=True),
        lax.all_gather(w_qkv, ("fsdp", "rep"), axis=0, tiled=True),
        lax.all_gather(w_attn_out, ("fsdp", "rep"), axis=0, tiled=True),
        lax.all_gather(feedforward_norm_gain, ("fsdp", "rep"), axis=0, tiled=True),
        lax.all_gather(w_in, ("fsdp", "rep"), axis=0, tiled=True),
        lax.all_gather(w_out, ("fsdp", "rep"), axis=0, tiled=True),
    )
    output, saved_residuals = forward(
        tokens.reshape(1, row_count, embedding_width),
        seq_lengths,
        gathered[0],
        gathered[1],
        gathered[2],
        gathered[3],
        gathered[4],
        gathered[5],
    )
    second_copy = (
        lax.all_gather(attention_norm_gain, ("fsdp", "rep"), axis=0, tiled=True),
        lax.all_gather(w_qkv, ("fsdp", "rep"), axis=0, tiled=True),
        lax.all_gather(w_attn_out, ("fsdp", "rep"), axis=0, tiled=True),
        lax.all_gather(feedforward_norm_gain, ("fsdp", "rep"), axis=0, tiled=True),
        lax.all_gather(w_in, ("fsdp", "rep"), axis=0, tiled=True),
        lax.all_gather(w_out, ("fsdp", "rep"), axis=0, tiled=True),
    )
    block_input_gradient, factors = backward(
        saved_residuals,
        cotangent.reshape(1, row_count, embedding_width),
        second_copy[0],
        second_copy[1],
        second_copy[2],
        second_copy[3],
        second_copy[4],
        second_copy[5],
    )
    (
        normed_attn,
        grad_packed,
        attended_rows,
        grad_hidden_low,
        normed_mlp,
        grad_inner,
        grad_out,
        mixed_input,
        grad_normed_attn,
        standard_attn,
        grad_normed_mlp,
        standard_mlp,
    ) = factors
    qkv_width = w_qkv.shape[1]
    attn_width = w_attn_out.shape[1]
    inner_width = w_in.shape[1]
    outer_width = w_out.shape[1]
    qkv_term = matmul_left_t(normed_attn, grad_packed)
    attn_term = matmul_left_t(attended_rows, grad_hidden_low)
    inner_term = matmul_left_t(normed_mlp, grad_inner)
    outer_term = matmul_left_t(grad_out, mixed_input)
    attn_gain_term = jnp.sum(grad_normed_attn * standard_attn, axis=0)
    mlp_gain_term = jnp.sum(grad_normed_mlp * standard_mlp, axis=0)
    summed = lax.psum_scatter(
        jnp.concatenate(
            [
                qkv_term,
                attn_term,
                inner_term,
                outer_term,
                attn_gain_term[:, None],
                mlp_gain_term[:, None],
            ],
            axis=1,
        ),
        ("fsdp", "rep"),
        scatter_dimension=0,
        tiled=True,
    )
    edge_two = qkv_width + attn_width
    edge_three = edge_two + inner_width
    edge_four = edge_three + outer_width
    return (
        output,
        block_input_gradient,
        summed[:, edge_four],
        summed[:, :qkv_width],
        summed[:, qkv_width:edge_two],
        summed[:, edge_four + 1],
        summed[:, edge_two:edge_three],
        summed[:, edge_three:edge_four],
    )


AXES = ("fsdp", "rep")
LANES = 128
HALF = HEAD_DIM // 2


def tie(*values):
    return lax.optimization_barrier(values)


def wide(value):
    return value.astype(jnp.float32)


def low(value):
    return value.astype(jnp.bfloat16)


def split_columns(value, count):
    width = value.shape[1] // count
    return [value[:, k * width : (k + 1) * width] for k in range(count)]


def split_rows(value, count):
    width = value.shape[0] // count
    return [value[k * width : (k + 1) * width] for k in range(count)]


def columns(blocks):
    return jnp.concatenate(blocks, axis=1)


def rows(blocks):
    return jnp.concatenate(blocks, axis=0)


def swap(value, distance):
    return lax.ppermute(value, "rep", [(k, k ^ distance) for k in range(4)])


def rep_exchange(value):
    blocks = value.reshape(4, value.shape[0] // 4, value.shape[1])
    return lax.all_to_all(blocks, "rep", 0, 0, tiled=True).reshape(value.shape)


def up(value):
    return lax.ppermute(value, "fsdp", [(k, (k + 2) % 8) for k in range(8)])


def down(value):
    return lax.ppermute(value, "fsdp", [(k, (k - 2) % 8) for k in range(8)])


def over(value):
    return lax.ppermute(value, "fsdp", [(k, k ^ 1) for k in range(8)])


def relative(value, z, x):
    blocks = split_columns(value, 8)
    blocks = [jnp.where(x == 1, blocks[k ^ 1], blocks[k]) for k in range(8)]
    for bit in (1, 2):
        turn = (z & bit) != 0
        blocks = [jnp.where(turn, blocks[(k + 2 * bit) % 8], blocks[k]) for k in range(8)]
    return columns([blocks[2 * ((p + 1) % 4) + i] for i in range(2) for p in range(4)])


def absolute(value, z, x):
    blocks = split_columns(value, 8)
    blocks = [blocks[4 * i + (j - 1) % 4] for j in range(4) for i in range(2)]
    blocks = [jnp.where(x == 1, blocks[k ^ 1], blocks[k]) for k in range(8)]
    for bit in (1, 2):
        turn = (z & bit) != 0
        blocks = [jnp.where(turn, blocks[(k - 2 * bit) % 8], blocks[k]) for k in range(8)]
    return columns(blocks)


def place_of(place, step, side):
    z, x = place[0], place[1]
    return 2 * lax.rem(z + step + 1, 4) + (x if side == 0 else 1 - x)


def block_of(place, z_at, side):
    z, x = place[0], place[1]
    return 4 * (x if side == 0 else 1 - x) + lax.rem(z_at - z + 7, 4)


def turned(value):
    width = value.shape[1]
    lane = lax.broadcasted_iota(jnp.int32, value.shape, 1)
    return jnp.where(
        lane % HEAD_DIM < HALF,
        pltpu.roll(value, width - HALF, 1),
        pltpu.roll(value, HALF, 1),
    )


def head_masks(row_count):
    lane = lax.broadcasted_iota(jnp.int32, (row_count, LANES), 1)
    return [low(wide(lane < HEAD_DIM)), low(wide(lane >= HEAD_DIM))], lane < HEAD_DIM


def token_rows(mine, across, beside, first, step):
    count = 128
    return [
        mine[first : first + count],
        beside[first : first + count],
        across[first : first + count],
        beside[step + first : step + first + count],
    ]


def attention_forward(
    place, seg_col, seg_row, cosine, sine, mine, across, beside,
    first, second, third, own, others, other_second, other,
    normed, qkv, attn, query, key, value, probs, attended, send, keep,
):
    size = own.shape[0]
    blocks = [
        (first, 0), (second, 0), (third, 0), (own, 0),
        (others, 0), (other_second, 0), (others, size), (other, 0),
    ]
    part = size // 4
    for at, (ref, row) in enumerate(blocks):
        qkv[size * at : size * (at + 1), :] = ref[row : row + size, :768]
        target = pl.multiple_of(place_of(place, at % 4, at // 4) * part, part)
        for z_at in range(4):
            for side in range(2):
                lanes = pl.multiple_of(block_of(place, z_at, side) * LANES, LANES)
                attn[pl.ds(target, part), pl.ds(lanes, LANES)] = ref[
                    row + part * z_at : row + part * (z_at + 1),
                    768 + LANES * side : 768 + LANES * (side + 1),
                ]
    count = 128
    for at, ref in enumerate(token_rows(mine, across, beside, 0, mine.shape[0])):
        values = wide(ref)
        centred = values - jnp.mean(values, axis=1, keepdims=True)
        inverse = lax.rsqrt(jnp.mean(centred * centred, axis=1, keepdims=True) + norm_eps)
        normed[count * at : count * (at + 1), :] = low(centred * inverse)
    packed = matmul(normed[...], qkv[...])
    cos_all, sin_all = columns([cosine[...]] * 2), columns([sine[...]] * 2)
    raw = packed[:, :256]
    query[...] = low((raw * cos_all + turned(raw) * sin_all) * HEAD_DIM ** (-0.5))
    raw = packed[:, 256:512]
    key[...] = low(raw * cos_all + turned(raw) * sin_all)
    value[...] = low(packed[:, 512:])
    masks, is_first = head_masks(count)
    for at in range(4):
        here = slice(count * at, count * (at + 1))
        allowed = seg_col[here, :] == seg_row[at : at + 1, :]
        for pair in range(2):
            lanes = slice(LANES * pair, LANES * (pair + 1))
            made = []
            for head in range(2):
                scores = matmul_right_t(query[here, lanes] * masks[head], key[here, lanes])
                scores = jnp.where(allowed, scores, -jnp.inf)
                powers = jnp.exp(scores - jnp.max(scores, axis=1, keepdims=True))
                weights = powers / jnp.sum(powers, axis=1, keepdims=True)
                slot = count * (4 * at + 2 * pair + head)
                probs[slot : slot + count, :] = weights
                made.append(matmul(low(weights), value[here, lanes]))
            attended[here, lanes] = low(jnp.where(is_first, made[0], made[1]))
    total = low(matmul(attended[...], attn[...]))
    keep[:count, :], send[:count, :] = total[:count], total[count : 2 * count]
    keep[count:, :], send[count:, :] = total[2 * count : 3 * count], total[3 * count :]


def mlp(
    seg_col, norm_own, norm_across, norm_beside, mine, across, beside,
    first, second, third, own, other_first, other_second, other_third, other,
    normed, grad_out, mixed, grad_inner, send, keep, w_down,
    w_up, inner, grad_mixed,
):
    size, count = own.shape[0], 128
    main, rest = w_down.shape[1] - LANES, 16
    lane = lax.broadcasted_iota(jnp.int32, (size, LANES), 1)
    blocks = (first, second, third, own, other_first, other_second, other_third, other)
    for at, ref in enumerate(blocks):
        here = slice(size * at, size * (at + 1))
        tail = wide(ref[:, 3 * main :])
        w_up[here, : 2 * main] = ref[:, : 2 * main]
        w_up[here, 2 * main :] = low(jnp.where(lane < 2 * rest, tail, 0.0))
        w_down[here, :main] = ref[:, 2 * main : 3 * main]
        tail = pltpu.roll(tail, LANES - 2 * rest, 1)
        w_down[here, main:] = low(jnp.where(lane < rest, tail, 0.0))
    for at, ref in enumerate(
        (norm_own[...], norm_beside[:count, :], norm_across[...], norm_beside[count:, :])
    ):
        normed[count * at : count * (at + 1), :] = ref
    for at, ref in enumerate(token_rows(mine, across, beside, count, mine.shape[0])):
        live = wide(seg_col[count * at : count * (at + 1), :] < 8)
        grad_out[count * at : count * (at + 1), :] = low(wide(ref) * live)
    inner[...] = matmul(normed[...], w_up[...])
    grad_mixed[...] = matmul(grad_out[...], w_down[...])

    def parts(gate):
        phi = 0.5 * (1.0 + lax.erf(gate * 0.7071067811865476))
        slope = phi + gate * jnp.exp(-0.5 * gate * gate) * 0.3989422804014327
        return gate * phi, slope

    @pl.loop(0, 8)
    def _(step):
        here = pl.ds(pl.multiple_of(step * 64, 64), 64)
        gate, up_part = inner[here, :main], inner[here, main : 2 * main]
        grad = grad_mixed[here, :main]
        activation, slope = parts(gate)
        mixed[here, :main] = low(activation * up_part)
        grad_inner[here, :main] = low(grad * up_part * slope)
        grad_inner[here, main : 2 * main] = low(grad * activation)
        tail = inner[here, 2 * main :]
        grad = grad_mixed[here, main:]
        activation, slope = parts(tail)
        tail_up = pltpu.roll(tail, LANES - rest, 1)
        mixed[here, main:] = low(activation * tail_up)
        grad_inner[here, 2 * main :] = low(
            grad * tail_up * slope + pltpu.roll(grad * activation, rest, 1)
        )

    total = low(matmul_right_t(grad_inner[...], w_up[...]))
    keep[:count, :], send[:count, :] = total[:count], total[count : 2 * count]
    keep[count:, :], send[count:, :] = total[2 * count : 3 * count], total[3 * count :]


def place_term(term, keep, pair, near, far, lanes):
    size = term.shape[0] // 8
    for at, (ref, row) in enumerate(
        [(keep, 0), (pair, 0), (keep, 1), (keep, 2), (near, 0), (pair, 1), (far, 0), (far, 1)]
    ):
        ref[size * row : size * (row + 1), lanes] = term[size * at : size * (at + 1)]


def mlp_terms(normed, grad_inner, grad_out, mixed, keep, pair, near, far):
    main, rest = mixed.shape[1] - LANES, 16
    term_in = matmul_left_t(normed[...], grad_inner[...])
    term_out = matmul_left_t(grad_out[...], mixed[...])
    tail = term_in[:, 2 * main :] + pltpu.roll(term_out[:, main:], 2 * rest, 1)
    place_term(low(term_in[:, : 2 * main]), keep, pair, near, far, slice(0, 2 * main))
    place_term(low(term_out[:, :main]), keep, pair, near, far, slice(2 * main, 3 * main))
    place_term(low(tail), keep, pair, near, far, slice(3 * main, 3 * main + LANES))


def attention_backward(
    place, cosine, sine, low_own, low_across, low_beside, attn, query, key, value, probs,
    attended, normed,
    grad_packed, keep, pair, near, far, grad_low, grad_attended, term_attn,
):
    count = 128
    for at, ref in enumerate(
        (low_own[...], low_beside[:count, :], low_across[...], low_beside[count:, :])
    ):
        grad_low[count * at : count * (at + 1), :] = ref
    grad_attended[...] = low(matmul_right_t(grad_low[...], attn[...]))
    masks, is_first = head_masks(count)
    for at in range(4):
        here = slice(count * at, count * (at + 1))
        cos, sin = cosine[here, :], sine[here, :]
        for half in range(2):
            lanes = slice(LANES * half, LANES * (half + 1))
            q, k, v = query[here, lanes], key[here, lanes], value[here, lanes]
            grad = grad_attended[here, lanes]
            made = []
            for head in range(2):
                slot = count * (4 * at + 2 * half + head)
                weights = probs[slot : slot + count, :]
                grad_value = matmul_left_t(low(weights), grad)
                grad_probs = matmul_right_t(grad * masks[head], v)
                delta = jnp.sum(weights * grad_probs, axis=1, keepdims=True)
                grad_scores = low(weights * (grad_probs - delta))
                made.append((matmul(grad_scores, k), matmul_left_t(grad_scores, q), grad_value))
            grad_q, grad_k, grad_v = (jnp.where(is_first, *both) for both in zip(*made))
            grad_q = grad_q * HEAD_DIM ** (-0.5)
            grad_packed[here, lanes] = low(grad_q * cos - turned(grad_q) * sin)
            lanes = slice(256 + LANES * half, 256 + LANES * (half + 1))
            grad_packed[here, lanes] = low(grad_k * cos - turned(grad_k) * sin)
            lanes = slice(512 + LANES * half, 512 + LANES * (half + 1))
            grad_packed[here, lanes] = low(grad_v)
    term = low(matmul_left_t(normed[...], grad_packed[...]))
    place_term(term, keep, pair, near, far, slice(0, 768))
    term_attn[...] = low(matmul_left_t(attended[...], grad_low[...]))
    size = term.shape[0] // 8
    part = size // 4
    targets = [
        (keep, 0), (pair, 0), (keep, size), (keep, 2 * size),
        (near, 0), (pair, size), (far, 0), (far, size),
    ]
    for at, (ref, row) in enumerate(targets):
        source = pl.multiple_of(place_of(place, at % 4, at // 4) * part, part)
        for z_at in range(4):
            for side in range(2):
                lanes = pl.multiple_of(block_of(place, z_at, side) * LANES, LANES)
                ref[
                    row + part * z_at : row + part * (z_at + 1),
                    768 + LANES * side : 768 + LANES * (side + 1),
                ] = term_attn[pl.ds(source, part), pl.ds(lanes, LANES)]


def projections(grad_packed, qkv, mixed, w_down, send, keep):
    count = 128
    for row, total in (
        (0, low(matmul_right_t(grad_packed[...], qkv[...]))),
        (count, low(matmul_right_t(mixed[...], w_down[...]))),
    ):
        keep[row : row + count, :] = total[:count]
        send[row : row + count, :] = total[count : 2 * count]
        keep[2 * count + row : 3 * count + row, :] = total[2 * count : 3 * count]
        send[2 * count + row : 3 * count + row, :] = total[3 * count :]


def unpack_rest(back, w_in, gain, grad_in, gain_grad, grad_out):
    size, hidden, part = w_in.shape[0], w_in.shape[1] // 2, w_in.shape[1] // 8
    main = part // LANES * LANES
    rest = part - main
    total = jnp.zeros(gain.shape, jnp.float32)
    for k in range(4):
        here = slice(size * k, size * (k + 1))
        for half in range(2):
            base = hidden * half + part * k
            for source, target, count in (
                (main * half, base, main),
                (3 * main + rest * half, base + main, rest),
            ):
                piece = wide(back[here, source : source + count])
                grad_in[:, target : target + count] = piece * gain[...]
                weights = wide(w_in[:, target : target + count])
                total += jnp.sum(piece * weights, axis=1, keepdims=True)
        base = part * k
        grad_out[:, base : base + main] = wide(back[here, 2 * main : 3 * main])
        source = 3 * main + 2 * rest
        grad_out[:, base + main : base + part] = wide(back[here, source : source + rest])
    gain_grad[...] = jnp.broadcast_to(total, (total.shape[0], LANES)).T[:1, :]


def unpack_qkv(back, w_qkv, gain, grad, gain_grad):
    size, part = w_qkv.shape[0], 256
    edge = back.shape[1] - 3 * part
    total = jnp.zeros(gain.shape, jnp.float32)
    for k in range(4):
        for third in range(3):
            source = slice(edge + part * third, edge + part * (third + 1))
            piece = wide(back[size * k : size * (k + 1), source])
            lanes = slice(part * (4 * third + k), part * (4 * third + k + 1))
            grad[:, lanes] = piece * gain[...]
            total += jnp.sum(piece * wide(w_qkv[:, lanes]), axis=1, keepdims=True)
    gain_grad[...] = jnp.broadcast_to(total, (total.shape[0], LANES)).T[:1, :]


def kernel(body, outs, cost, *args, scratch=(), scalars=0):
    flops, transcendentals = cost
    shapes = [jax.ShapeDtypeStruct(shape, kind) for shape, kind in outs]
    moved = sum(arg.size * arg.dtype.itemsize for arg in (*args, *shapes))
    moved = moved // 4 if body is attention_backward else moved
    return pl.pallas_call(
        body,
        out_shape=shapes,
        in_specs=[
            pl.BlockSpec(memory_space=pltpu.SMEM if k < scalars else pltpu.VMEM)
            for k in range(len(args))
        ],
        out_specs=[pl.BlockSpec(memory_space=pltpu.VMEM)] * len(shapes),
        scratch_shapes=[pltpu.VMEM(shape, kind) for shape, kind in scratch],
        compiler_params=pltpu.CompilerParams(vmem_limit_bytes=28 * 2**20),
        cost_estimate=pl.CostEstimate(
            flops=flops, bytes_accessed=moved, transcendentals=transcendentals
        ),
        name=body.__name__,
    )(*args)


def scatter_last(send, keep):
    beside = split_rows(swap(send, 1), 2)
    kept = split_rows(keep, 2)
    sent = low(wide(kept[1]) + wide(beside[1]))
    return wide(kept[0]) + wide(beside[0]), sent


def local_ring(
    tokens,
    seq_lengths,
    cotangent,
    attention_norm_gain,
    w_qkv,
    w_attn_out,
    feedforward_norm_gain,
    w_in,
    w_out,
):
    count, width = tokens.shape
    index = lax.axis_index("fsdp")
    z, x = index // 2, index % 2
    place = jnp.stack([z, x]).astype(jnp.int32)
    hidden = w_in.shape[1] // 2
    part = hidden // 4
    main = part // LANES * LANES
    in_width, out_width, all_width = 2 * main + LANES, main + LANES, 3 * main + LANES
    f32, b16 = jnp.float32, jnp.bfloat16
    group = 4 * count

    gain_attn = wide(attention_norm_gain)[:, None]
    gain_mlp = wide(feedforward_norm_gain)[:, None]
    order = [(k, (k % 8) * 4 + k // 8) for k in range(32)]
    attn_own = lax.ppermute(w_attn_out, AXES, order)
    qkv_parts = split_columns(low(wide(w_qkv) * gain_attn), 12)
    size = w_qkv.shape[0]
    slots = seq_lengths.shape[1]
    lengths_low = jnp.pad(low(wide(seq_lengths)), ((0, size - 1), (0, LANES - slots)))
    exchanged = rep_exchange(rows([columns([*qkv_parts[k::4], lengths_low]) for k in range(4)]))
    first_own = columns([exchanged[:, :768], rows(split_columns(attn_own, 4))])
    lengths = rows([exchanged[size * k : size * k + 1, 768 : 768 + slots] for k in range(4)])
    lengths = wide(lengths).astype(jnp.int32)
    for bit in (1, 2):
        turned_rows = rows([lengths[k ^ bit : (k ^ bit) + 1] for k in range(4)])
        lengths = jnp.where((lax.axis_index("rep") & bit) != 0, turned_rows, lengths)

    scaled_in = low(wide(w_in) * gain_mlp)
    pieces = []
    for k in range(4):
        gate = scaled_in[:, part * k : part * (k + 1)]
        up_part = scaled_in[:, hidden + part * k : hidden + part * (k + 1)]
        out_part = w_out[:, part * k : part * (k + 1)]
        fill = jnp.zeros((w_in.shape[0], all_width - 3 * part), b16)
        pieces.append(
            columns(
                [gate[:, :main], up_part[:, :main], out_part[:, :main]]
                + [gate[:, main:], up_part[:, main:], out_part[:, main:], fill]
            )
        )
    mine = rows([relative(tokens, z, x), relative(cotangent, z, x)])
    first_own, rest, mine = tie(first_own, rows(pieces), mine)
    rest = rep_exchange(rest)

    third, first, other = up(first_own), down(first_own), over(first_own)
    third, first, other, mine, rest = tie(third, first, other, mine, rest)
    across = swap(mine, 2)
    second, others, rest_third = up(third), over(rows([first, third])), up(rest)
    second, others, across = tie(second, others, across)
    other_second = over(second)
    rest_first = down(tie(rest, rest_third)[0])
    beside = swap(rows([mine, across]), 1)
    rest_other = over(tie(rest, other_second)[0])

    step = mine.shape[0]
    segment, positions, _ = jax.vmap(lambda row: layout(row, count))(lengths)
    frequency = rope_base ** (-(lax.iota(f32, HALF) * (2.0 / HEAD_DIM)))
    angles = positions.reshape(group, 1).astype(f32) * frequency
    cosine, sine = jnp.cos(angles), jnp.sin(angles)
    cosine, sine = columns([cosine] * 4), columns([-sine, sine] * 2)
    seg_col = segment.reshape(group, 1)

    normed, qkv, attn, query, key, value, probs, attended, send, keep = kernel(
        attention_forward,
        [((group, width), b16), ((width, 768), b16), ((256, width), b16)]
        + [((group, 256), b16)] * 3
        + [((16 * count, count), f32), ((group, 256), b16)]
        + [((2 * count, width), b16)] * 2,
        (2 * group * width * (768 + 256) + 4 * 16 * count * count * LANES, 16 * count * count),
        place, seg_col, segment, cosine, sine, mine, across, beside,
        first, second, third, first_own, others, other_second, other,
        scalars=1,
    )
    rest_third, rest_first, rest_other, send = tie(rest_third, rest_first, rest_other, send)
    rest_second, rest_other_third = up(rest_third), over(rest_third)
    x_own = wide(mine[:count])
    kept, sent = scatter_last(send, keep)
    rest_other_first = over(tie(rest_first, rest_other_third)[0])
    hidden_sum = x_own + kept + wide(swap(sent, 2))
    standard_mlp, inverse_mlp = norm_statistics(hidden_sum)
    norm_own = low(standard_mlp)
    norm_across = swap(norm_own, 2)
    rest_second, rest_other_third, _ = tie(rest_second, rest_other_third, norm_own)
    rest_other_second = up(rest_other_third)
    norm_beside = swap(rows([norm_own, norm_across]), 1)

    normed_mlp, grad_out, mixed, grad_inner, send, keep, w_down = kernel(
        mlp,
        [((group, width), b16)] * 2
        + [((group, out_width), b16), ((group, in_width), b16)]
        + [((2 * count, width), b16)] * 2
        + [((width, out_width), b16)],
        (2 * group * width * (2 * in_width + out_width), 3 * group * part),
        seg_col, norm_own, norm_across, norm_beside, mine, across, beside,
        rest_first, rest_second, rest_third, rest,
        rest_other_first, rest_other_second, rest_other_third, rest_other,
        scratch=[
            ((width, in_width), b16),
            ((group, in_width), f32),
            ((group, out_width), f32),
        ],
    )
    size = width // 8
    io_keep, io_pair, io_near, io_far = kernel(
        mlp_terms,
        [((size * n, all_width), b16) for n in (3, 2, 1, 2)],
        (2 * group * width * all_width, 0),
        normed_mlp, grad_inner, grad_out, mixed,
    )
    io_pair, io_far = up(io_pair), over(io_far)
    kept, sent = scatter_last(send, keep)
    scaled_mlp = kept + wide(tie(swap(sent, 2), io_keep)[0])
    grad_hidden = wide(grad_out[:count]) + norm_backward_pass(
        scaled_mlp, jnp.ones((), f32), standard_mlp, inverse_mlp
    )
    low_own = low(grad_hidden)
    low_across = swap(low_own, 2)
    low_beside = swap(rows([low_own, low_across]), 1)

    grad_packed, g_keep, g_pair, g_near, g_far = kernel(
        attention_backward,
        [((group, 768), b16)] + [((size * n, width), b16) for n in (3, 2, 1, 2)],
        (group * width * (768 + 512), 0),
        place, cosine, sine, low_own, low_across, low_beside, attn, query, key, value, probs,
        attended, normed,
        scratch=[((group, width), b16), ((group, 256), b16), ((256, width), b16)],
        scalars=1,
    )
    g_pair, g_far = up(g_pair), over(g_far)
    io_pair, io_far, _ = tie(io_pair, io_far, g_near)
    io_kept, io_pair, io_far = split_rows(io_keep, 3), split_rows(io_pair, 2), split_rows(io_far, 2)
    io_near = over(low(wide(io_near) + wide(io_pair[1])))
    io_down = down(low(wide(io_kept[1]) + wide(io_far[0])))
    send, keep = kernel(
        projections,
        [((4 * count, width), b16)] * 2,
        (2 * group * width * (768 + out_width), 0),
        grad_packed, qkv, mixed, w_down,
    )
    io_near, io_down, g_pair, g_far, send = tie(io_near, io_down, g_pair, g_far, send)
    g_kept, g_pair, g_far = split_rows(g_keep, 3), split_rows(g_pair, 2), split_rows(g_far, 2)
    g_near = over(low(wide(g_near) + wide(g_pair[1])))
    g_down = down(low(wide(g_kept[1]) + wide(g_far[0])))
    kept, sent = scatter_last(send, keep)
    io_up = up(low(wide(io_kept[0]) + wide(io_pair[0]) + wide(io_near)))
    g_near, sent = tie(g_near, sent)
    g_up = up(low(wide(g_kept[0]) + wide(g_pair[0]) + wide(g_near)))
    last_across = swap(sent, 2)
    io_up, g_up, g_down = tie(io_up, g_up, g_down)
    sum_io = low(wide(io_kept[2]) + wide(io_far[1]) + wide(io_down) + wide(io_up))
    sum_g = low(wide(g_kept[2]) + wide(g_far[1]) + wide(g_down) + wide(g_up))
    back = rep_exchange(columns([sum_io, sum_g[:, :768]]))
    grad_w_in, gain_in, grad_w_out = kernel(
        unpack_rest,
        [(w_in.shape, f32), ((1, w_in.shape[0]), f32), (w_out.shape, f32)],
        (4 * w_in.size, 0),
        back, w_in, gain_mlp,
    )
    grad_w_qkv, gain_qkv = kernel(
        unpack_qkv,
        [(w_qkv.shape, f32), ((1, w_qkv.shape[0]), f32)],
        (4 * w_qkv.size, 0),
        back, w_qkv, gain_attn,
    )
    last = kept + wide(last_across)

    standard, inverse = norm_statistics(x_own)
    block_input_gradient = grad_hidden + norm_backward_pass(
        last[:count], jnp.ones((), f32), standard, inverse
    )
    output = low(jnp.where(seg_col[:count] < 8, hidden_sum + last[count:], 0.0))
    block_input_gradient = absolute(block_input_gradient, z, x)
    sum_attn, block_input_gradient = tie(sum_g[:, 768:], block_input_gradient)
    grad_w_attn_out = wide(
        lax.ppermute(
            columns(split_rows(sum_attn, 4)),
            AXES,
            [(there, here) for here, there in order],
        )
    )
    return (
        absolute(output, z, x),
        block_input_gradient,
        gain_qkv.reshape(-1),
        grad_w_qkv,
        grad_w_attn_out,
        gain_in.reshape(-1),
        grad_w_in,
        grad_w_out,
    )


def solution(mesh):
    ringed = dict(mesh.shape) == {"fsdp": 8, "rep": 4}
    return jax.shard_map(
        local_ring if ringed else local_plain,
        mesh=mesh,
        in_specs=(
            P(AXES, None),
            P(AXES, None),
            P(AXES, None),
            P(AXES),
            P(AXES, None),
            P(AXES, None),
            P(AXES),
            P(AXES, None),
            P(AXES, None),
        ),
        out_specs=(
            P(AXES, None),
            P(AXES, None),
            P(AXES),
            P(AXES, None),
            P(AXES, None),
            P(AXES),
            P(AXES, None),
            P(AXES, None),
        ),
        check_vma=False,
    )
```
